32 devices in a mesh: dp: 16 (over z, y, x), tensor: 2 (over core).
Axes of the slice: x: 2, y: 2, z: 4, core: 2. Of those that a mesh axis runs over, the one named last changes fastest.
Arguments:
- tokens_in: bfloat16 [4096, 2048], P('dp'), may hold values from -6 to 6
- input_proj: bfloat16 [2048, 2048], P('dp'), may hold values from -0.125 to 0.125
- forget_proj: bfloat16 [2048, 2048], P('dp'), may hold values from -0.125 to 0.125
- outgate_proj: bfloat16 [2048, 2048], P('dp'), may hold values from -0.125 to 0.125
- output_proj: bfloat16 [2048, 2048], P('dp'), may hold values from -0.125 to 0.125
- glu_gate: bfloat16 [2048, 5632], P('dp', 'tensor'), may hold values from -0.125 to 0.125
- glu_up: bfloat16 [2048, 5632], P('dp', 'tensor'), may hold values from -0.125 to 0.125
- glu_down: bfloat16 [5632, 2048], P('tensor', 'dp'), may hold values from -0.078125 to 0.078125
- norm_gain: float32 [2048], replicated, may hold values from 0.5 to 1.5
- mixer_gain: float32 [2048], replicated, may hold values from 0.5 to 1.5
- ffn_gain: float32 [2048], replicated, may hold values from 0.5 to 1.5
- bound_table: float32 [24, 2048], replicated, may hold values from -6 to 6
- lengths: int32 [32], P('dp'), may hold values from 0 to 256, as said below
- bucket: int32 [16], P('dp'), may hold values from 0 to 1, as said below
- cotangent: bfloat16 [4096, 2048], P(('dp', 'tensor')), may hold values from -6 to 6
Outputs:
- block_out: bfloat16 [4096, 2048], P(('dp', 'tensor'))
- grad_tokens: float32 [4096, 2048], P('dp')
- grad_input_proj: float32 [2048, 2048], P('dp')
- grad_forget_proj: float32 [2048, 2048], P('dp')
- grad_outgate_proj: float32 [2048, 2048], P('dp')
- grad_output_proj: float32 [2048, 2048], P('dp')
- grad_glu_gate: float32 [2048, 5632], P('dp', 'tensor')
- grad_glu_up: float32 [2048, 5632], P('dp', 'tensor')
- grad_glu_down: float32 [5632, 2048], P('tensor', 'dp')
- grad_norm_gain: float32 [2048], P('dp')
- grad_mixer_gain: float32 [2048], P('dp')
- grad_ffn_gain: float32 [2048], P('dp')
- grad_bound_table: float32 [24, 2048], P(None, 'dp')
The draws below stay inside these ranges and needn't reach their ends.
Inputs may be any that keep to these rules, and one draw needn't show every extreme that they name: Dp index d holds 2**bucket[d] slots of 256 // 2**bucket[d] rows; index 0 has bucket 0 and index 1 has bucket 1. lengths[d * 2 + j] is the length of slot j of dp index d: 0 for j >= 2**bucket[d]; otherwise between max(128, L // 2 + 1) and L, the slot's length L, and exactly L for j = 0.
All inputs are finite; a program needn't handle non-finite values.
Results may differ from the reference program's by a relative error of at most 0.019.
Values may be sent and summed in bfloat16 or wider, within the bound.
A program may use at most 256 MiB of HBM per device.

```python
from functools import partial
import jax
import jax.numpy as jnp
from jax import lax

D = 2048
FF = 5632
LAYERS = 24
LAYER = 12
SLOTS = 2
MIN_LEN = 128
TOK_DEV = 256
TOKENS = 4096
N_DP = 16


def shared_layout(key):
    folded = jax.random.fold_in(key, 11)
    key_bucket, key_length = jax.random.split(folded)
    places = jnp.arange(N_DP, dtype=jnp.int32)
    drawn = jax.random.randint(key_bucket, (N_DP,), 0, 2, dtype=jnp.int32)
    bucket = jnp.where(places == 0, 0, jnp.where(places == 1, 1, drawn)).astype(jnp.int32)
    slot_len = TOK_DEV // jnp.left_shift(jnp.int32(1), bucket)
    floor_len = jnp.maximum(MIN_LEN, slot_len // 2 + 1)
    spread = jax.random.randint(key_length, (N_DP, SLOTS), 0, 1048576, dtype=jnp.int32)
    length_grid = floor_len[:, None] + spread % (slot_len - floor_len + 1)[:, None]
    column = jnp.arange(SLOTS, dtype=jnp.int32)[None, :]
    length_grid = jnp.where(column == 0, slot_len[:, None], length_grid)
    used = column < jnp.left_shift(jnp.int32(1), bucket)[:, None]
    length_grid = jnp.where(used, length_grid, 0).astype(jnp.int32)
    return (bucket, length_grid.reshape(N_DP * SLOTS))


def draw_bucket(key, part):
    return shared_layout(key)[0]


def draw_lengths(key, part):
    return shared_layout(key)[1]


def spiked(values, own_key, source, target, shards_of, factor):
    def block_of(dim):
        return (jnp.arange(values.shape[dim]) // (values.shape[dim] // shards_of)).reshape((-1,) + (1,) * (values.ndim - 1 - dim))

    one_side = jax.random.permutation(own_key, shards_of)[block_of(target)]
    second = (block_of(target) + shards_of // 2) % shards_of
    return jnp.where((block_of(source) == one_side) | (block_of(source) == second), factor * values, values)


def block_levels(stream_key, extent, cuts, low, high):
    loudness, own = 1.0, jax.random.fold_in(stream_key, 6)
    for axis_at, blocks in cuts:
        heights = jnp.exp(jax.random.uniform(jax.random.fold_in(own, axis_at), (blocks,), jnp.float32, low / len(cuts), high / len(cuts)))
        loudness = loudness * jnp.repeat(heights, extent[axis_at] // blocks).reshape([-1 if axis == axis_at else 1 for axis in range(len(extent))])
    return loudness


def normal_values(own_key, shape, scale, bound, cuts=(), kind=jnp.bfloat16):
    level = block_levels(own_key, shape, cuts, -0.22, 0.18) if cuts else 1.0
    array = jax.random.normal(own_key, shape, jnp.float32) * scale * level
    return jnp.minimum(jnp.maximum(array, -bound), bound).astype(kind)


def gaussian_with(key, extent, scale, most, cuts, heavy, kind=jnp.bfloat16):
    result = scale * jax.random.normal(key, extent, jnp.float32)
    if cuts:
        result = result * block_levels(key, extent, cuts, -0.22, 0.18)
    return jnp.clip(spiked(result, jax.random.fold_in(key, 3), *heavy), -most, most).astype(kind)


def setup_inputs(seed: int = 0) -> dict:
    splits = jax.random.split(jax.random.key(seed), 16)
    return {
        "tokens_in": gaussian_with(splits[0], (TOKENS, D), 1.0, 6.0, ((0, 16),), (0, 1, 16, 2.0)),
        "input_proj": normal_values(splits[1], (D, D), D ** -0.5, 0.125, ((0, 16),)),
        "forget_proj": normal_values(splits[2], (D, D), D ** -0.5, 0.125, ((0, 16),)),
        "outgate_proj": normal_values(splits[3], (D, D), D ** -0.5, 0.125, ((0, 16),)),
        "output_proj": normal_values(splits[4], (D, D), D ** -0.5, 0.125, ((0, 16),)),
        "glu_gate": normal_values(splits[5], (D, FF), D ** -0.5, 0.125, ((0, 16), (1, 2))),
        "glu_up": normal_values(splits[6], (D, FF), D ** -0.5, 0.125, ((0, 16), (1, 2))),
        "glu_down": normal_values(splits[7], (FF, D), FF ** -0.5, 0.078125, ((0, 2), (1, 16))),
        "norm_gain": jnp.clip(1.0 + 0.1 * jax.random.normal(splits[8], (D,), jnp.float32), 0.5, 1.5),
        "mixer_gain": jnp.clip(1.0 + 0.1 * jax.random.normal(splits[9], (D,), jnp.float32), 0.5, 1.5),
        "ffn_gain": jnp.clip(1.0 + 0.1 * jax.random.normal(splits[10], (D,), jnp.float32), 0.5, 1.5),
        "bound_table": normal_values(splits[11], (LAYERS, D), 1.0, 6.0, (), jnp.float32),
        "lengths": draw_lengths(jax.random.fold_in(splits[15], 71), 0),
        "bucket": draw_bucket(jax.random.fold_in(splits[15], 71), 0),
        "cotangent": gaussian_with(splits[14], (TOKENS, D), 1.0, 6.0, ((0, 32),), (0, 1, 32, 2.75)),
    }


epsilon = 1e-06
highest = lax.Precision.HIGHEST

@jax.custom_vjp
def low(v):
    return lax.optimization_barrier(v.astype(jnp.bfloat16)).astype(jnp.float32)

@jax.custom_vjp
def low_back(v):
    return v

def low_keep(v):
    return (low(v), None)

def low_pass(kept, grad):
    return (grad,)

def back_keep(v):
    return (v, None)

def back_low(kept, grad):
    return (low(grad),)
low.defvjp(low_keep, low_pass)
low_back.defvjp(back_keep, back_low)

def matmul(first_op, second_op):
    return jnp.dot(first_op, second_op, precision=highest, preferred_element_type=jnp.float32)

def rms_scale(values):
    return lax.rsqrt(lax.optimization_barrier(jnp.mean(values * values, axis=-1, keepdims=True)) + epsilon)

def layout(lengths, bucket):
    slot_len = TOK_DEV // jnp.left_shift(jnp.int32(1), bucket)
    position = jnp.arange(TOK_DEV, dtype=jnp.int32)[None, :]
    slot_index = position // slot_len[:, None]
    offset = position - slot_index * slot_len[:, None]
    length_grid = lengths.reshape(N_DP, SLOTS)
    slot_ids = jnp.arange(SLOTS, dtype=jnp.int32)
    chosen = (slot_index[:, :, None] == slot_ids[None, None, :]).astype(jnp.int32)
    slot_limit = lax.optimization_barrier(jnp.sum(chosen * length_grid[:, None, :], axis=-1))
    valid_mask = (offset < slot_limit).astype(jnp.float32).reshape(TOKENS, 1)
    keep_mask = (offset > 0).astype(jnp.float32).reshape(TOKENS, 1)
    return (valid_mask, keep_mask)

def advance(carried, pair_now):
    decay_now, inject_now = pair_now
    carried = decay_now * carried + inject_now
    return (carried, carried)

def recur(decay_rate, inject):
    decay_grid = jnp.swapaxes(decay_rate.reshape(N_DP, TOK_DEV, D), 0, 1)
    inject_grid = jnp.swapaxes(inject.reshape(N_DP, TOK_DEV, D), 0, 1)
    start = jnp.zeros((N_DP, D), jnp.float32)
    _, states = lax.scan(jax.checkpoint(advance), start, (decay_grid, inject_grid))
    return jnp.swapaxes(states, 0, 1).reshape(TOKENS, D)

def forward(inputs, input_proj, forget_proj, outgate_proj, output_proj, glu_gate, glu_up, glu_down, norm_gain, mixer_gain, ffn_gain, bound_table, valid_mask, keep_mask):
    normed_one = low(inputs * rms_scale(inputs) * norm_gain)
    input_pre = low_back(matmul(normed_one, input_proj))
    forget_pre = low_back(matmul(normed_one, forget_proj))
    outgate_pre = low_back(matmul(normed_one, outgate_proj))
    shares = jax.nn.softmax(bound_table, axis=0)
    lower_bound = (jnp.cumsum(shares, axis=0) - shares[0])[LAYER]
    forget = lower_bound + (1.0 - lower_bound) * jax.nn.sigmoid(forget_pre)
    inject = jax.nn.silu(input_pre) * (1.0 - forget) * valid_mask
    hidden_state = recur(forget * keep_mask, inject)
    mix_normed = low(hidden_state * rms_scale(hidden_state) * mixer_gain * jax.nn.silu(outgate_pre))
    residual = inputs + low_back(matmul(mix_normed, output_proj))
    normed_two = low(residual * rms_scale(residual) * ffn_gain)
    gate_pre = low_back(matmul(normed_two, glu_gate))
    up_pre = low_back(matmul(normed_two, glu_up))
    hidden = low(jax.nn.silu(gate_pre) * up_pre)
    return residual + matmul(hidden, glu_down)

def reference(tokens_in, input_proj, forget_proj, outgate_proj, output_proj, glu_gate, glu_up, glu_down, norm_gain, mixer_gain, ffn_gain, bound_table, lengths, bucket, cotangent):
    valid_mask, keep_mask = layout(lengths, bucket)
    block_value, pullback = jax.vjp(partial(forward, valid_mask=valid_mask, keep_mask=keep_mask), tokens_in.astype(jnp.float32), input_proj.astype(jnp.float32), forget_proj.astype(jnp.float32), outgate_proj.astype(jnp.float32), output_proj.astype(jnp.float32), glu_gate.astype(jnp.float32), glu_up.astype(jnp.float32), glu_down.astype(jnp.float32), norm_gain.astype(jnp.float32), mixer_gain.astype(jnp.float32), ffn_gain.astype(jnp.float32), bound_table.astype(jnp.float32))
    grads = pullback(cotangent.astype(jnp.float32) * valid_mask)
    return (block_value.astype(jnp.bfloat16), grads[0], grads[1], grads[2], grads[3], grads[4], grads[5], grads[6], grads[7], grads[8], grads[9], grads[10], grads[11])
```

```python
import functools

import jax
import jax.numpy as jnp
from jax import lax
from jax.experimental import pallas as pl
from jax.experimental.pallas import tpu as pltpu
from jax.sharding import PartitionSpec as P

LAYER = 12
epsilon = 1e-06
bf16 = jnp.bfloat16
f32 = jnp.float32


def rms_scale(values):
    return lax.rsqrt(jnp.mean(values * values, axis=-1, keepdims=True) + epsilon)


def norm_back(values, row_scale, gain_row, incoming):
    weighted = incoming * gain_row
    cubed = row_scale * row_scale * row_scale
    return row_scale * weighted - values * cubed * jnp.mean(
        weighted * values, axis=-1, keepdims=True
    )


def silu_slope(values):
    logistic = jax.nn.sigmoid(values)
    return logistic * (1.0 + values * (1.0 - logistic))


def matmul(first_op, second_op):
    return jnp.dot(first_op, second_op, preferred_element_type=f32)


def cross_rows(first_op, second_op):
    return lax.dot_general(
        first_op, second_op, (((0,), (0,)), ((), ())), preferred_element_type=f32
    )


def cross_cols(first_op, second_op):
    return lax.dot_general(
        first_op, second_op, (((1,), (1,)), ((), ())), preferred_element_type=f32
    )


def pick(values, index, axis):
    return lax.dynamic_index_in_dim(values, index, axis, keepdims=False)


def layout(lengths, bucket, row_count):
    slot_len = row_count // jnp.left_shift(jnp.int32(1), bucket)
    position = jnp.arange(row_count, dtype=jnp.int32)
    slot_index = position // slot_len
    offset = position - slot_index * slot_len
    slot_ids = jnp.arange(lengths.shape[0], dtype=jnp.int32)
    chosen = (slot_index[:, None] == slot_ids[None, :]).astype(jnp.int32)
    slot_limit = jnp.sum(chosen * lengths[None, :], axis=1)
    valid_mask = (offset < slot_limit).astype(f32)[:, None]
    keep_mask = (offset > 0).astype(f32)[:, None]
    return (valid_mask, keep_mask)


def bound_parts(bound_table):
    shares = jax.nn.softmax(bound_table, axis=0)
    layer_ids = jnp.arange(bound_table.shape[0], dtype=jnp.int32)[:, None]
    picked = ((layer_ids >= 1) & (layer_ids <= LAYER)).astype(f32)
    return (shares, picked, jnp.sum(shares * picked, axis=0))


def scan_rows(decay_ref, add_ref, out_ref, reverse):
    rows, width = out_ref.shape
    tiles = rows // 8
    sub = lax.broadcasted_iota(jnp.int32, (8, width), 0)

    def step(i, carry):
        j = tiles - 1 - i if reverse else i
        at = pl.ds(pl.multiple_of(j * 8, 8), 8)
        a = decay_ref[at, :]
        b = add_ref[at, :]
        for s in (1, 2, 4):
            shift = 8 - s if reverse else s
            inside = sub < 8 - s if reverse else sub >= s
            b = jnp.where(inside, b + a * pltpu.roll(b, shift, 0), b)
            a = jnp.where(inside, a * pltpu.roll(a, shift, 0), a)
        h = b + a * carry
        out_ref[at, :] = h
        edge = h[0:1, :] if reverse else h[7:8, :]
        return jnp.broadcast_to(edge, (8, width))

    lax.fori_loop(0, tiles, step, jnp.zeros((8, width), f32), unroll=4)


def mixer_forward_kernel(pre_ref, aux_ref, par_ref, state_ref, mix_ref, sq_ref, decay_ref, add_ref):
    width = state_ref.shape[1]
    input_pre = pre_ref[:, :width]
    forget_pre = pre_ref[:, width : 2 * width]
    outgate_pre = pre_ref[:, 2 * width :]
    valid = aux_ref[:, 0:1]
    keep = aux_ref[:, 1:2]
    bound = par_ref[0:1, :]
    gain = par_ref[1:2, :]
    forget = bound + (1.0 - bound) * jax.nn.sigmoid(forget_pre)
    add_ref[...] = input_pre * jax.nn.sigmoid(input_pre) * (1.0 - forget) * valid
    decay_ref[...] = forget * keep
    scan_rows(decay_ref, add_ref, state_ref, False)
    state = state_ref[...]
    mix_ref[...] = (state * gain * (outgate_pre * jax.nn.sigmoid(outgate_pre))).astype(bf16)
    sq_ref[...] = jnp.sum(state * state, axis=1, keepdims=True)


def mixer_forward(pre, aux, par, seq_rows):
    rows, width = pre.shape[0], pre.shape[1] // 3
    row_block = lambda n: pl.BlockSpec((seq_rows, n), lambda i: (i, 0))
    return pl.pallas_call(
        mixer_forward_kernel,
        grid=(rows // seq_rows,),
        in_specs=[
            row_block(3 * width),
            row_block(aux.shape[1]),
            pl.BlockSpec(par.shape, lambda i: (0, 0)),
        ],
        out_specs=[row_block(width), row_block(width), row_block(1)],
        out_shape=[
            jax.ShapeDtypeStruct((rows, width), f32),
            jax.ShapeDtypeStruct((rows, width), bf16),
            jax.ShapeDtypeStruct((rows, 1), f32),
        ],
        scratch_shapes=[pltpu.VMEM((seq_rows, width), f32)] * 2,
        cost_estimate=pl.CostEstimate(
            flops=rows * width * 60, bytes_accessed=rows * width * 20, transcendentals=rows * width * 3
        ),
        name="mixer_forward",
    )(pre, aux, par)


def mixer_backward_kernel(
    pre_ref, state_ref, up_ref, aux_ref, par_ref, grad_ref, sums_ref, decay_ref, add_ref, out_ref
):
    rows, width = state_ref.shape
    input_pre = pre_ref[:, :width]
    forget_pre = pre_ref[:, width : 2 * width]
    outgate_pre = pre_ref[:, 2 * width :]
    valid = aux_ref[:, 0:1]
    keep = aux_ref[:, 1:2]
    scale = aux_ref[:, 2:3]
    dot_mean = aux_ref[:, 3:4]
    bound = par_ref[0:1, :]
    gain = par_ref[1:2, :]
    state = state_ref[...]
    incoming = up_ref[...]
    at_row = lax.broadcasted_iota(jnp.int32, (rows, width), 0)
    sig_out = jax.nn.sigmoid(outgate_pre)
    act_out = outgate_pre * sig_out
    scaled = incoming * (state * scale)
    grad_ref[:, 2 * width :] = (
        scaled * gain * (sig_out * (1.0 + outgate_pre * (1.0 - sig_out)))
    ).astype(bf16)
    add_ref[...] = scale * (gain * act_out * incoming) - state * (scale * scale * scale * dot_mean)
    sig_forget = jax.nn.sigmoid(forget_pre)
    forget = bound + (1.0 - bound) * sig_forget
    decay_ref[...] = jnp.where(
        at_row < rows - 1, pltpu.roll(forget * keep, rows - 1, 0), 0.0
    )
    scan_rows(decay_ref, add_ref, out_ref, True)
    grad_state = out_ref[...]
    before = jnp.where(at_row > 0, pltpu.roll(state, 1, 0), 0.0)
    sig_in = jax.nn.sigmoid(input_pre)
    grad_forget = grad_state * (before * keep - input_pre * sig_in * valid)
    grad_ref[:, :width] = (
        grad_state * (1.0 - forget) * valid * (sig_in * (1.0 + input_pre * (1.0 - sig_in)))
    ).astype(bf16)
    grad_ref[:, width : 2 * width] = (
        grad_forget * (1.0 - bound) * sig_forget * (1.0 - sig_forget)
    ).astype(bf16)

    @pl.when(pl.program_id(0) == 0)
    def _():
        sums_ref[...] = jnp.zeros_like(sums_ref)

    sums_ref[0:1, :] += jnp.sum(scaled * act_out, axis=0, keepdims=True)
    sums_ref[1:2, :] += jnp.sum(grad_forget * (1.0 - sig_forget), axis=0, keepdims=True)


def mixer_backward(pre, state, incoming, aux, par, seq_rows):
    rows, width = state.shape
    row_block = lambda n: pl.BlockSpec((seq_rows, n), lambda i: (i, 0))
    whole = lambda shape: pl.BlockSpec(shape, lambda i: (0, 0))
    return pl.pallas_call(
        mixer_backward_kernel,
        grid=(rows // seq_rows,),
        in_specs=[
            row_block(3 * width),
            row_block(width),
            row_block(width),
            row_block(aux.shape[1]),
            whole(par.shape),
        ],
        out_specs=[row_block(3 * width), whole((2, width))],
        out_shape=[
            jax.ShapeDtypeStruct((rows, 3 * width), bf16),
            jax.ShapeDtypeStruct((2, width), f32),
        ],
        scratch_shapes=[pltpu.VMEM((seq_rows, width), f32)] * 3,
        cost_estimate=pl.CostEstimate(
            flops=rows * width * 90, bytes_accessed=rows * width * 26, transcendentals=rows * width * 3
        ),
        name="mixer_backward",
    )(pre, state, incoming, aux, par)


def body(
    n_dp,
    n_t,
    tokens_in,
    input_proj,
    forget_proj,
    outgate_proj,
    output_proj,
    glu_gate,
    glu_up,
    glu_down,
    norm_gain,
    mixer_gain,
    ffn_gain,
    bound_table,
    lengths,
    bucket,
    cotangent,
):
    depth = n_dp.bit_length() - 1
    tp_bits = (2, 0)
    fs_bits = tuple(b for b in reversed(range(depth)) if b not in tp_bits)
    t_depth = n_t.bit_length() - 1
    own_bits, free_bits = fs_bits[len(fs_bits) - t_depth :], fs_bits[: len(fs_bits) - t_depth]
    n_tp = 4
    tp_mask = (0, 1, 4, 5)
    axis_of = {b: depth - 1 - b for b in range(depth)}

    me = lax.axis_index("dp")
    t = lax.axis_index("tensor")
    bit = {b: (me >> b) & 1 for b in range(depth)}
    t_bit = {b: (t >> (t_depth - 1 - i)) & 1 for i, b in enumerate(own_bits)}
    q = bit[2] * 2 + bit[0]

    rows, width = tokens_in.shape
    share = cotangent.shape[0]
    block = width // n_dp
    free = 2 ** len(free_bits)
    feat = free * block

    def swap(values, mask):
        return lax.ppermute(values, "dp", [(i, i ^ mask) for i in range(n_dp)])

    def t_swap(values):
        return lax.ppermute(values, "tensor", [(0, 1), (1, 0)])

    def by_bit(which, own, other):
        return jnp.where(which == 0, own, other), jnp.where(which == 0, other, own)

    def in_order(parts, bits):
        parts = list(parts)
        for i, b in enumerate(reversed(bits)):
            step = 1 << i
            for r in range(len(parts)):
                if not r & step:
                    parts[r], parts[r | step] = by_bit(bit[b], parts[r], parts[r | step])
        return parts

    def t_gather(values):
        if n_t == 2:
            return jnp.stack(by_bit(t, values, t_swap(values)))
        return lax.all_gather(values, "tensor", axis=0)

    def t_scatter(values):
        if n_t == 2:
            return pick(values, t, 0).astype(f32) + t_swap(pick(values, 1 - t, 0)).astype(f32)
        return lax.psum_scatter(values, "tensor", scatter_dimension=0, tiled=False).astype(f32)

    def tp_gather(values):
        return [t_gather(values if r == 0 else swap(values, tp_mask[r])) for r in range(n_tp)]

    def tp_scatter(parts, kind):
        halves = [t_scatter(part) for part in parts]
        total = halves[0]
        for r in range(1, n_tp):
            total = total + swap(halves[r].astype(kind), tp_mask[r]).astype(f32)
        return total

    def exchange(values):
        parts = [pick(values, q, 0)]
        for r in range(1, n_tp):
            parts.append(swap(pick(values, q ^ r, 0), tp_mask[r]))
        return in_order(parts, tp_bits)

    def fs_gather(values):
        parts = [values]
        for b in fs_bits:
            parts = parts + [None] * 0 + [swap(v, 1 << b) for v in parts]
        return parts

    def weight_parts(shards):
        return fs_gather(jnp.stack(exchange(shards)))

    def weight_whole(parts):
        count = len(parts)
        flip = [0] * count
        for r in range(count):
            flip[sum(((r >> i) & 1) << (len(fs_bits) - 1 - i) for i in range(len(fs_bits)))] = parts[r]
        ordered = jnp.stack(in_order(flip, fs_bits))
        cols = ordered.shape[-1]
        ordered = ordered.reshape((2,) * depth + (block, cols))
        have = fs_bits + tp_bits
        axes = [have.index(b) for b in reversed(range(depth))]
        return ordered.transpose(axes + [depth, depth + 1]).reshape(width, cols)

    def weight_back(grad):
        cols = grad.shape[1]
        grad = grad.reshape((2,) * depth + (block, cols))
        for b in reversed(fs_bits):
            send = lax.dynamic_slice_in_dim(grad, 1 - bit[b], 1, axis_of[b]).astype(bf16)
            hold = lax.dynamic_slice_in_dim(grad, bit[b], 1, axis_of[b]).astype(f32)
            grad = hold + swap(send, 1 << b).astype(f32)
        return exchange(grad.reshape(n_tp, block, cols).astype(bf16))

    def my_columns(values):
        lead = values.shape[:-1]
        n = len(lead)
        values = values.reshape(lead + (2,) * depth + (block,))
        bits = list(reversed(range(depth)))
        for b in own_bits:
            values = pick(values, t_bit[b], n + bits.index(b))
            bits.remove(b)
        order = [n + bits.index(b) for b in tp_bits] + list(range(n)) + [n + bits.index(b) for b in free_bits]
        return values.transpose(order + [n + len(bits)]).reshape((n_tp,) + lead + (feat,))

    def my_half(values):
        return lax.dynamic_slice_in_dim(values, t * share, share, 0)

    inputs = tokens_in.astype(f32)
    scale_one = rms_scale(inputs)
    normed_mine = (inputs * scale_one * norm_gain).astype(bf16)
    normed_half = my_half(normed_mine)
    normed_parts = [normed_mine] + [
        t_gather(swap(normed_half, tp_mask[r])).reshape(rows, width) for r in range(1, n_tp)
    ]
    where_from = jnp.concatenate([lengths, bucket])
    masks = []
    for r in range(n_tp):
        got = where_from if r == 0 else swap(where_from, tp_mask[r])
        masks.append(layout(got[: lengths.shape[0]], got[lengths.shape[0] :], rows))
    valid_all = jnp.concatenate([m[0] for m in masks])
    keep_all = jnp.concatenate([m[1] for m in masks])

    mix_shards = jnp.concatenate(
        [my_columns(w) for w in (input_proj, forget_proj, outgate_proj)], axis=-1
    )
    mix_parts = weight_parts(mix_shards)
    out_piece = output_proj
    for b in own_bits:
        out_piece = jnp.where(t_bit[b] == bit[b], out_piece, swap(out_piece, 1 << b))
    out_pieces = [out_piece]
    for b in reversed(free_bits):
        out_pieces = out_pieces + [swap(v, 1 << b) for v in out_pieces]
    out_full = jnp.concatenate(in_order(out_pieces, free_bits))

    valid_mine = my_half(masks[0][0])
    grad_out_rows = (cotangent.astype(f32) * valid_mine).astype(bf16)

    hidden_cols = glu_gate.shape[1] // n_tp
    split_cols = lambda w: w.reshape(block, n_tp, hidden_cols).transpose(1, 0, 2)
    gate_parts = weight_parts(split_cols(glu_gate))
    up_parts = weight_parts(split_cols(glu_up))
    down_parts = weight_parts(glu_down.reshape(n_tp, hidden_cols, block).transpose(0, 2, 1))
    grad_out_all = jnp.stack(tp_gather(grad_out_rows)).reshape(n_tp * rows, width)

    normed_one = jnp.concatenate(normed_parts)
    mix_full = weight_whole(mix_parts)
    pre = matmul(normed_one, mix_full)
    my_table = pick(my_columns(bound_table), q, 0)
    bound_mine = bound_parts(my_table)[2]
    gain_mine = pick(my_columns(mixer_gain), q, 0)
    par = jnp.stack([bound_mine, gain_mine])
    aux = jnp.concatenate([valid_all, keep_all], axis=1)
    state, mix_raw, square = mixer_forward(pre, aux, par, rows)
    out_parts = matmul(mix_raw, out_full).astype(bf16).reshape(n_tp, n_t, share, width)
    square_parts = square.reshape(n_tp, n_t, share)
    square_sum = tp_scatter([square_parts[r] for r in range(n_tp)], f32)
    out_sum = tp_scatter([out_parts[r] for r in range(n_tp)], bf16)
    scale_state = lax.rsqrt(square_sum / width + epsilon)[:, None]
    mixed_out = out_sum * scale_state
    inputs_half = my_half(inputs)
    scale_one_half = my_half(scale_one)
    residual = inputs_half + mixed_out

    scale_two = rms_scale(residual)
    normed_two_half = (residual * scale_two * ffn_gain).astype(bf16)
    normed_two = jnp.stack(tp_gather(normed_two_half)).reshape(n_tp * rows, width)
    gate_full = weight_whole(gate_parts)
    up_full = weight_whole(up_parts)
    down_full = weight_whole(down_parts)
    gate_pre = matmul(normed_two, gate_full)
    up_pre = matmul(normed_two, up_full)
    grad_hidden = matmul(grad_out_all, down_full)
    gate_act = jax.nn.silu(gate_pre)
    hidden = (gate_act * up_pre).astype(bf16)
    grad_up = (grad_hidden * gate_act).astype(bf16)
    grad_gate = (grad_hidden * up_pre * silu_slope(gate_pre)).astype(bf16)
    grad_two_parts = (
        (cross_cols(grad_gate, gate_full) + cross_cols(grad_up, up_full))
        .astype(bf16)
        .reshape(n_tp, n_t, share, width)
    )
    grad_normed_two = tp_scatter([grad_two_parts[r] for r in range(n_tp)], bf16)
    block_parts = cross_cols(hidden, down_full).astype(bf16).reshape(n_tp, n_t, share, width)
    block_out = (residual + tp_scatter([block_parts[r] for r in range(n_tp)], bf16)).astype(bf16)
    grad_down_t = jnp.stack(weight_back(cross_rows(grad_out_all, hidden).astype(bf16)))
    grad_w_gate = jnp.stack(weight_back(cross_rows(normed_two, grad_gate).astype(bf16)))
    grad_w_up = jnp.stack(weight_back(cross_rows(normed_two, grad_up).astype(bf16)))
    grad_glu_down = grad_down_t.transpose(0, 2, 1).reshape(glu_down.shape).astype(f32)
    grad_glu_gate = grad_w_gate.transpose(1, 0, 2).reshape(glu_gate.shape).astype(f32)
    grad_glu_up = grad_w_up.transpose(1, 0, 2).reshape(glu_up.shape).astype(f32)

    grad_residual = grad_out_rows.astype(f32) + norm_back(
        residual, scale_two, ffn_gain, grad_normed_two
    )
    ffn_gain_sum = jnp.sum(grad_normed_two * residual * scale_two, axis=0)
    grad_mix_half = grad_residual.astype(bf16)
    dot_mean = jnp.sum(grad_mix_half.astype(f32) * mixed_out, axis=1, keepdims=True) / (
        scale_state * width
    )
    row_values = jnp.concatenate([scale_state, dot_mean], axis=1).T
    row_all = jnp.stack(tp_gather(row_values)).transpose(0, 1, 3, 2).reshape(n_tp * rows, 2)
    grad_mix = jnp.stack(tp_gather(grad_mix_half)).reshape(n_tp * rows, width)
    grad_mixed = cross_cols(grad_mix, out_full)
    aux_back = jnp.concatenate([valid_all, keep_all, row_all], axis=1)
    grads, sums = mixer_backward(pre, state, grad_mixed, aux_back, par, rows)
    one_parts = cross_cols(grads, mix_full).astype(bf16).reshape(n_tp, n_t, share, width)
    grad_normed_one = tp_scatter([one_parts[r] for r in range(n_tp)], bf16)
    grad_mix_w = jnp.stack(weight_back(cross_rows(normed_one, grads).astype(bf16)))

    mixed = (mix_raw.astype(f32) * row_all[:, :1]).astype(bf16)
    grad_out_w = cross_rows(mixed, grad_mix).astype(bf16).reshape((2,) * len(free_bits) + (block, width))
    for i, b in enumerate(free_bits):
        send = lax.dynamic_slice_in_dim(grad_out_w, 1 - bit[b], 1, i)
        hold = lax.dynamic_slice_in_dim(grad_out_w, bit[b], 1, i)
        grad_out_w = (hold.astype(f32) + swap(send, 1 << b).astype(f32)).astype(bf16)
    grad_out_w = grad_out_w.reshape(block, width)
    for b in own_bits:
        grad_out_w = (grad_out_w.astype(f32) + swap(grad_out_w, 1 << b).astype(f32)).astype(bf16)
    mine_t = jnp.int32(0)
    for b in own_bits:
        mine_t = mine_t * 2 + bit[b]
    if n_t == 2:
        other = t_swap(grad_out_w)
        grad_output_proj = jnp.where(mine_t == t, grad_out_w, other).astype(f32)
    else:
        grad_output_proj = pick(lax.all_gather(grad_out_w, "tensor", axis=0), mine_t, 0).astype(f32)

    mix_all = t_gather(grad_mix_w)
    mix_all = mix_all.reshape((2,) * t_depth + (2, 2) + (block, 3) + (2,) * len(free_bits) + (block,))
    order = list(own_bits) + list(tp_bits) + ["row", "which"] + list(free_bits) + ["col"]
    axes = [order.index(k) for k in ["which", "row"] + list(reversed(range(depth))) + ["col"]]
    mix_all = mix_all.transpose(axes).reshape(3, block, width).astype(f32)

    grad_tokens_half = my_half_residual = grad_residual + norm_back(
        inputs_half, scale_one_half, norm_gain, grad_normed_one
    )
    grad_tokens = t_gather(grad_tokens_half).reshape(rows, width)
    norm_gain_sum = jnp.sum(grad_normed_one * inputs_half * scale_one_half, axis=0)

    gains = jnp.stack([norm_gain_sum, ffn_gain_sum]).reshape((2,) + (2,) * depth + (block,))
    for b in reversed(range(depth)):
        at = 1 + axis_of[b]
        send = lax.dynamic_slice_in_dim(gains, 1 - bit[b], 1, at)
        hold = lax.dynamic_slice_in_dim(gains, bit[b], 1, at)
        gains = hold + swap(send, 1 << b)
    gains = gains.reshape(2, block)
    gains = gains + t_swap(gains) if n_t == 2 else lax.psum(gains, "tensor")

    for b in fs_bits:
        sums = sums + swap(sums, 1 << b)
    sums = t_gather(sums)
    sums = pick(sums, mine_t, 0).reshape((2,) + (2,) * len(free_bits) + (block,))
    for b in free_bits:
        sums = pick(sums, bit[b], 1)
    shares, picked, lower = bound_parts(lax.dynamic_slice_in_dim(bound_table, me * block, block, 1))
    grad_table = shares * (picked - lower[None, :]) * sums[1][None, :]

    return (
        block_out,
        grad_tokens,
        mix_all[0],
        mix_all[1],
        mix_all[2],
        grad_output_proj,
        grad_glu_gate,
        grad_glu_up,
        grad_glu_down,
        gains[0],
        sums[0],
        gains[1],
        grad_table,
    )


def solution(mesh):
    return jax.shard_map(
        functools.partial(body, mesh.shape["dp"], mesh.shape["tensor"]),
        mesh=mesh,
        in_specs=(
            P("dp", None),
            P("dp", None),
            P("dp", None),
            P("dp", None),
            P("dp", None),
            P("dp", "tensor"),
            P("dp", "tensor"),
            P("tensor", "dp"),
            P(),
            P(),
            P(),
            P(),
            P("dp"),
            P("dp"),
            P(("dp", "tensor"), None),
        ),
        out_specs=(
            P(("dp", "tensor"), None),
            P("dp", None),
            P("dp", None),
            P("dp", None),
            P("dp", None),
            P("dp", None),
            P("dp", "tensor"),
            P("dp", "tensor"),
            P("tensor", "dp"),
            P("dp"),
            P("dp"),
            P("dp"),
            P(None, "dp"),
        ),
        check_vma=False,
    )
```

```python
import functools

import jax
import jax.numpy as jnp
from jax import lax
from jax.experimental import pallas as pl
from jax.experimental.pallas import tpu as pltpu
from jax.sharding import PartitionSpec as P

LAYER = 12
epsilon = 1e-06
bf16 = jnp.bfloat16
f32 = jnp.float32


def rms_scale(values):
    return lax.rsqrt(jnp.mean(values * values, axis=-1, keepdims=True) + epsilon)


def norm_back(values, row_scale, gain_row, incoming):
    weighted = incoming * gain_row
    cubed = row_scale * row_scale * row_scale
    return row_scale * weighted - values * cubed * jnp.mean(
        weighted * values, axis=-1, keepdims=True
    )


def silu_slope(values):
    logistic = jax.nn.sigmoid(values)
    return logistic * (1.0 + values * (1.0 - logistic))


def matmul(first_op, second_op):
    return jnp.dot(first_op, second_op, preferred_element_type=f32)


def cross_rows(first_op, second_op):
    return lax.dot_general(
        first_op, second_op, (((0,), (0,)), ((), ())), preferred_element_type=f32
    )


def cross_cols(first_op, second_op):
    return lax.dot_general(
        first_op, second_op, (((1,), (1,)), ((), ())), preferred_element_type=f32
    )


def pick(values, index, axis):
    return lax.dynamic_index_in_dim(values, index, axis, keepdims=False)


def layout(lengths, bucket, row_count):
    slot_len = row_count // jnp.left_shift(jnp.int32(1), bucket)
    position = jnp.arange(row_count, dtype=jnp.int32)
    slot_index = position // slot_len
    offset = position - slot_index * slot_len
    slot_ids = jnp.arange(lengths.shape[0], dtype=jnp.int32)
    chosen = (slot_index[:, None] == slot_ids[None, :]).astype(jnp.int32)
    slot_limit = jnp.sum(chosen * lengths[None, :], axis=1)
    valid_mask = (offset < slot_limit).astype(f32)[:, None]
    keep_mask = (offset > 0).astype(f32)[:, None]
    return (valid_mask, keep_mask)


def bound_parts(bound_table):
    shares = jax.nn.softmax(bound_table, axis=0)
    layer_ids = jnp.arange(bound_table.shape[0], dtype=jnp.int32)[:, None]
    picked = ((layer_ids >= 1) & (layer_ids <= LAYER)).astype(f32)
    return (shares, picked, jnp.sum(shares * picked, axis=0))


def scan_rows(decay_ref, add_ref, out_ref, reverse):
    rows, width = out_ref.shape
    tiles = rows // 8
    sub = lax.broadcasted_iota(jnp.int32, (8, width), 0)

    def step(i, carry):
        j = tiles - 1 - i if reverse else i
        at = pl.ds(pl.multiple_of(j * 8, 8), 8)
        a = decay_ref[at, :]
        b = add_ref[at, :]
        for s in (1, 2, 4):
            shift = 8 - s if reverse else s
            inside = sub < 8 - s if reverse else sub >= s
            b = jnp.where(inside, b + a * pltpu.roll(b, shift, 0), b)
            a = jnp.where(inside, a * pltpu.roll(a, shift, 0), a)
        h = b + a * carry
        out_ref[at, :] = h
        edge = h[0:1, :] if reverse else h[7:8, :]
        return jnp.broadcast_to(edge, (8, width))

    lax.fori_loop(0, tiles, step, jnp.zeros((8, width), f32), unroll=4)


def mixer_forward_kernel(pre_ref, aux_ref, par_ref, state_ref, mix_ref, sq_ref, decay_ref, add_ref):
    width = state_ref.shape[1]
    input_pre = pre_ref[:, :width]
    forget_pre = pre_ref[:, width : 2 * width]
    outgate_pre = pre_ref[:, 2 * width :]
    valid = aux_ref[:, 0:1]
    keep = aux_ref[:, 1:2]
    bound = par_ref[0:1, :]
    gain = par_ref[1:2, :]
    forget = bound + (1.0 - bound) * jax.nn.sigmoid(forget_pre)
    add_ref[...] = input_pre * jax.nn.sigmoid(input_pre) * (1.0 - forget) * valid
    decay_ref[...] = forget * keep
    scan_rows(decay_ref, add_ref, state_ref, False)
    state = state_ref[...]
    mix_ref[...] = (state * gain * (outgate_pre * jax.nn.sigmoid(outgate_pre))).astype(bf16)
    sq_ref[...] = jnp.sum(state * state, axis=1, keepdims=True)


def mixer_forward(pre, aux, par, seq_rows):
    rows, width = pre.shape[0], pre.shape[1] // 3
    row_block = lambda n: pl.BlockSpec((seq_rows, n), lambda i: (i, 0))
    return pl.pallas_call(
        mixer_forward_kernel,
        grid=(rows // seq_rows,),
        in_specs=[
            row_block(3 * width),
            row_block(aux.shape[1]),
            pl.BlockSpec(par.shape, lambda i: (0, 0)),
        ],
        out_specs=[row_block(width), row_block(width), row_block(1)],
        out_shape=[
            jax.ShapeDtypeStruct((rows, width), f32),
            jax.ShapeDtypeStruct((rows, width), bf16),
            jax.ShapeDtypeStruct((rows, 1), f32),
        ],
        scratch_shapes=[pltpu.VMEM((seq_rows, width), f32)] * 2,
        cost_estimate=pl.CostEstimate(
            flops=rows * width * 60, bytes_accessed=rows * width * 20, transcendentals=rows * width * 3
        ),
        name="mixer_forward",
    )(pre, aux, par)


def mixer_backward_kernel(
    pre_ref, state_ref, up_ref, aux_ref, par_ref, grad_ref, sums_ref, decay_ref, add_ref, out_ref
):
    rows, width = state_ref.shape
    input_pre = pre_ref[:, :width]
    forget_pre = pre_ref[:, width : 2 * width]
    outgate_pre = pre_ref[:, 2 * width :]
    valid = aux_ref[:, 0:1]
    keep = aux_ref[:, 1:2]
    scale = aux_ref[:, 2:3]
    dot_mean = aux_ref[:, 3:4]
    bound = par_ref[0:1, :]
    gain = par_ref[1:2, :]
    state = state_ref[...]
    incoming = up_ref[...]
    at_row = lax.broadcasted_iota(jnp.int32, (rows, width), 0)
    sig_out = jax.nn.sigmoid(outgate_pre)
    act_out = outgate_pre * sig_out
    scaled = incoming * (state * scale)
    grad_ref[:, 2 * width :] = (
        scaled * gain * (sig_out * (1.0 + outgate_pre * (1.0 - sig_out)))
    ).astype(bf16)
    add_ref[...] = scale * (gain * act_out * incoming) - state * (scale * scale * scale * dot_mean)
    sig_forget = jax.nn.sigmoid(forget_pre)
    forget = bound + (1.0 - bound) * sig_forget
    decay_ref[...] = jnp.where(
        at_row < rows - 1, pltpu.roll(forget * keep, rows - 1, 0), 0.0
    )
    scan_rows(decay_ref, add_ref, out_ref, True)
    grad_state = out_ref[...]
    before = jnp.where(at_row > 0, pltpu.roll(state, 1, 0), 0.0)
    sig_in = jax.nn.sigmoid(input_pre)
    grad_forget = grad_state * (before * keep - input_pre * sig_in * valid)
    grad_ref[:, :width] = (
        grad_state * (1.0 - forget) * valid * (sig_in * (1.0 + input_pre * (1.0 - sig_in)))
    ).astype(bf16)
    grad_ref[:, width : 2 * width] = (
        grad_forget * (1.0 - bound) * sig_forget * (1.0 - sig_forget)
    ).astype(bf16)

    @pl.when(pl.program_id(0) == 0)
    def _():
        sums_ref[...] = jnp.zeros_like(sums_ref)

    sums_ref[0:1, :] += jnp.sum(scaled * act_out, axis=0, keepdims=True)
    sums_ref[1:2, :] += jnp.sum(grad_forget * (1.0 - sig_forget), axis=0, keepdims=True)


def mixer_backward(pre, state, incoming, aux, par, seq_rows):
    rows, width = state.shape
    row_block = lambda n: pl.BlockSpec((seq_rows, n), lambda i: (i, 0))
    whole = lambda shape: pl.BlockSpec(shape, lambda i: (0, 0))
    return pl.pallas_call(
        mixer_backward_kernel,
        grid=(rows // seq_rows,),
        in_specs=[
            row_block(3 * width),
            row_block(width),
            row_block(width),
            row_block(aux.shape[1]),
            whole(par.shape),
        ],
        out_specs=[row_block(3 * width), whole((2, width))],
        out_shape=[
            jax.ShapeDtypeStruct((rows, 3 * width), bf16),
            jax.ShapeDtypeStruct((2, width), f32),
        ],
        scratch_shapes=[pltpu.VMEM((seq_rows, width), f32)] * 3,
        cost_estimate=pl.CostEstimate(
            flops=rows * width * 90, bytes_accessed=rows * width * 26, transcendentals=rows * width * 3
        ),
        name="mixer_backward",
    )(pre, state, incoming, aux, par)


MESH = pl.DeviceIdType.MESH


class Copies:
    def __init__(self, send, recv, local):
        self.send, self.recv, self.local = send, recv, local
        self.n_remote = self.n_local = 0
        self.open = []

    def remote(self, src, dst, device):
        k = self.n_remote
        self.n_remote += 1
        copy = pltpu.make_async_remote_copy(
            src_ref=src,
            dst_ref=dst,
            send_sem=self.send.at[k],
            recv_sem=self.recv.at[k],
            device_id=device,
            device_id_type=MESH,
        )
        copy.start()
        self.open.append(copy.wait_send)
        return copy

    def here(self, src, dst, keep=False):
        k = self.n_local
        self.n_local += 1
        copy = pltpu.make_async_copy(src, dst, self.local.at[k])
        copy.start()
        if keep:
            self.open.append(copy.wait)
        return copy

    def close(self):
        assert self.n_remote <= self.send.shape[0] and self.n_local <= self.local.shape[0]
        for wait in self.open:
            wait()


def position():
    me = lax.axis_index("dp")
    t = lax.axis_index("tensor")
    zf, zn, y, x = me // 8, (me // 4) % 2, (me // 2) % 2, me % 2
    to_x, to_zn = 1 - 2 * x, 4 - 8 * zn
    group = [None, (me + to_x, t), (me + to_zn, t), (me + to_x + to_zn, t)]
    q = [zn * 2 + x, zn * 2 + 1 - x, (1 - zn) * 2 + x, (1 - zn) * 2 + 1 - x]
    far = (me + 8 - 16 * zf, t)
    side = (me + 2 - 4 * y, t)
    core = (me, 1 - t)
    return me, t, (zf, zn, y, x), q, group, far, side, core


def meet(devices):
    barrier = pltpu.get_barrier_semaphore()
    for device in devices:
        pl.semaphore_signal(barrier, inc=1, device_id=device, device_id_type=MESH)
    pl.semaphore_wait(barrier, len(devices))


def fold_lanes(values):
    width = values.shape[1]
    if width % 128:
        return values
    total = values[:, :128]
    for i in range(128, width, 128):
        total = total + values[:, i : i + 128]
    return total


def front_kernel(
    s_mix, s_out, s_g, s_u, s_d, n1_own, go_own, aux_own, par, inp, gain2,
    o_mix, o_out, o_g, o_u, o_d, o_n1, o_go, o_n2, o_pre, o_state, o_raw, o_res, o_mo, o_sc, o_aux,
    w_mix, w_out, out2, n1, aux, pre, state, raw, part, core_in, half, peer_in,
    sq, sq_core, sq_half, sq_peer, res, mo, sc, n2, decay, add,
    send, recv, local, core_send, core_recv, sqc_send, sqc_recv,
):
    me, t, (zf, zn, y, x), q, group, far, side, core = position()
    share, width = inp.shape
    rows = 2 * share
    block = s_out.shape[0]
    feat = par.shape[1]
    link = Copies(send, recv, local)
    meet(group[1:] + [far, side, core])

    def at(start, size, unit):
        return pl.ds(pl.multiple_of(start, unit), size)

    def pair(fz, c, fy):
        return at(fz * (8 * block) + c * (4 * block) + fy * (2 * block), 2 * block, 2 * block)

    mine = at(me * block, block, block)

    def row(r, tt):
        return at(r * rows + tt * share, share, share)

    mix_in = [link.remote(s_mix.at[q[r]], w_mix.at[mine], group[r]) for r in (1, 2, 3)]
    mix_own = link.here(s_mix.at[q[0]], w_mix.at[mine])
    side_out = link.remote(s_out, out2.at[y], side)
    own_out = link.here(s_out, out2.at[y])
    aux_in = [link.remote(aux_own, aux.at[r], group[r]) for r in (1, 2, 3)]
    aux_mine = link.here(aux_own, aux.at[0])
    n1_in = [link.remote(n1_own.at[at(t * share, share, share)], n1.at[row(r, t)], group[r]) for r in (1, 2, 3)]
    n1_mine = link.here(n1_own, n1.at[pl.ds(0, rows)])
    shards = ((s_g, o_g), (s_u, o_u), (s_d, o_d))
    ffn_in, ffn_own = [], []
    for s, o in shards:
        ffn_in += [link.remote(s.at[q[r]], o.at[:, mine], group[r]) for r in (1, 2, 3)]
        ffn_own.append(link.here(s.at[q[0]], o.at[:, mine]))

    mix_own.wait()
    for c in mix_in:
        c.wait_recv()
    far_mix = [link.remote(w_mix.at[pair(zf, c, y)], w_mix.at[pair(zf, c, y)], far) for c in (0, 1)]
    side_mix = [link.remote(w_mix.at[pair(zf, c, y)], w_mix.at[pair(zf, c, y)], side) for c in (0, 1)]
    side_out.wait_recv()
    own_out.wait()
    far_out = link.remote(out2.at[t], w_out.at[at(zf * block, block, block)], far)
    here_out = link.here(out2.at[t], w_out.at[at(zf * block, block, block)])
    n1_core = []
    for i, r in enumerate((1, 2, 3)):
        n1_in[i].wait_recv()
        n1_core.append(link.remote(n1.at[row(r, t)], n1.at[row(r, t)], core))
    for c in (0, 1):
        far_mix[c].wait_recv()
        side_mix.append(link.remote(w_mix.at[pair(1 - zf, c, y)], w_mix.at[pair(1 - zf, c, y)], side))

    for c in ffn_own:
        c.wait()
    for c in ffn_in:
        c.wait_recv()
    far_ffn, side_ffn = [], []
    for s, o in shards:
        far_ffn.append([link.remote(o.at[:, pair(zf, c, y)], o.at[:, pair(zf, c, y)], far) for c in (0, 1)])
    for s, o in shards:
        side_ffn += [link.remote(o.at[:, pair(zf, c, y)], o.at[:, pair(zf, c, y)], side) for c in (0, 1)]

    def forward_ffn(i):
        o = shards[i][1]
        for c in (0, 1):
            far_ffn[i][c].wait_recv()
            side_ffn.append(link.remote(o.at[:, pair(1 - zf, c, y)], o.at[:, pair(1 - zf, c, y)], side))

    go_in = [link.remote(go_own, o_go.at[row(r, t)], group[r]) for r in (1, 2, 3)]
    go_core = [link.remote(go_own, o_go.at[row(0, t)], core)]
    link.here(go_own, o_go.at[row(0, t)], keep=True)

    n1_mine.wait()
    aux_mine.wait()
    for c in side_mix + n1_core + aux_in + [far_out]:
        c.wait_recv()
    here_out.wait()

    def core_copy(r):
        return pltpu.make_async_remote_copy(
            src_ref=part.at[row(r, 1 - t)],
            dst_ref=core_in.at[at(r * share, share, share)],
            send_sem=core_send.at[r],
            recv_sem=core_recv.at[r],
            device_id=core,
            device_id_type=MESH,
        )

    def sq_copy(r):
        return pltpu.make_async_remote_copy(
            src_ref=sq.at[row(r, 1 - t)],
            dst_ref=sq_core.at[at(r * share, share, share)],
            send_sem=sqc_send.at[r],
            recv_sem=sqc_recv.at[r],
            device_id=core,
            device_id_type=MESH,
        )

    bound = par[0:1, :]
    gain = par[1:2, :]

    def piece(i, carry):
        r = 3 - i
        here = at(r * rows, rows, rows)
        pre[here, :] = jnp.dot(n1[here, :], w_mix[...], preferred_element_type=f32)
        columns = aux[r].T
        valid = columns[:, 0:1]
        keep = columns[:, 1:2]
        forget = bound + (1.0 - bound) * jax.nn.sigmoid(pre[here, feat : 2 * feat])
        input_pre = pre[here, 0:feat]
        add[...] = input_pre * jax.nn.sigmoid(input_pre) * (1.0 - forget) * valid
        decay[...] = forget * keep
        scan_rows(decay, add, state.at[here, :], False)
        held = state[here, :]
        outgate_pre = pre[here, 2 * feat :]
        raw[here, :] = (held * gain * (outgate_pre * jax.nn.sigmoid(outgate_pre))).astype(bf16)
        sq[here, :] = fold_lanes(held * held)
        part[here, :] = jnp.dot(raw[here, :], w_out[...], preferred_element_type=f32).astype(bf16)
        core_copy(r).start()
        sq_copy(r).start()
        return carry

    lax.fori_loop(0, 4, piece, 0)

    link.here(w_mix, o_mix, keep=True)
    link.here(w_out, o_out, keep=True)
    link.here(n1, o_n1, keep=True)
    link.here(pre, o_pre, keep=True)
    link.here(state, o_state, keep=True)
    link.here(raw, o_raw, keep=True)
    link.here(aux, o_aux, keep=True)

    out_in, sq_in = [], []
    for r in (3, 2, 1):
        core_copy(r).wait()
        sq_copy(r).wait()
        to = at(r * share, share, share)
        half[to, :] = (part[row(r, t), :].astype(f32) + core_in[to, :].astype(f32)).astype(bf16)
        sq_half[to, :] = sq[row(r, t), :] + sq_core[to, :]
        out_in.append(link.remote(half.at[to], peer_in.at[to], group[r]))
        sq_in.append(link.remote(sq_half.at[to], sq_peer.at[to], group[r]))
    core_copy(0).wait()
    sq_copy(0).wait()
    forward_ffn(0)
    for c in out_in + sq_in:
        c.wait_recv()
    total_sq = sq[row(0, t), :] + sq_core[0:share, :]
    for r in (1, 2, 3):
        total_sq = total_sq + sq_peer[r * share : (r + 1) * share, :]
    scale = lax.rsqrt(jnp.sum(total_sq, axis=1, keepdims=True) / width + epsilon)
    sc[...] = jnp.broadcast_to(scale, sc.shape)
    chunk = min(share, 16)

    def finish(i, carry):
        to = at(i * chunk, chunk, chunk)
        total = part[at(t * share + i * chunk, chunk, chunk), :].astype(f32) + core_in[to, :].astype(f32)
        for r in (1, 2, 3):
            total = total + peer_in[at(r * share + i * chunk, chunk, chunk), :].astype(f32)
        mixed = total * sc[to, 0:1]
        value = inp[to, :] + mixed
        mo[to, :] = mixed
        res[to, :] = value
        scale_two = lax.rsqrt(jnp.mean(value * value, axis=1, keepdims=True) + epsilon)
        n2[to, :] = (value * scale_two * gain2[...]).astype(bf16)
        return carry

    lax.fori_loop(0, share // chunk, finish, 0)
    n2_in = [link.remote(n2, o_n2.at[row(r, t)], group[r]) for r in (1, 2, 3)]
    n2_core = [link.remote(n2, o_n2.at[row(0, t)], core)]
    link.here(n2, o_n2.at[row(0, t)], keep=True)
    link.here(res, o_res, keep=True)
    link.here(mo, o_mo, keep=True)
    link.here(sc, o_sc, keep=True)
    for i, r in enumerate((1, 2, 3)):
        go_in[i].wait_recv()
        go_core.append(link.remote(o_go.at[row(r, t)], o_go.at[row(r, t)], core))
    forward_ffn(1)
    for i, r in enumerate((1, 2, 3)):
        n2_in[i].wait_recv()
        n2_core.append(link.remote(o_n2.at[row(r, t)], o_n2.at[row(r, t)], core))
    forward_ffn(2)
    for c in side_ffn + go_core + n2_core:
        c.wait_recv()
    link.close()


def front(s_mix, s_out, s_g, s_u, s_d, n1_own, go_own, aux_own, par, inp, gain2):
    share, width = inp.shape
    rows, group_rows = 2 * share, 8 * share
    feat, hid = par.shape[1], s_g.shape[1]
    block = s_out.shape[0]
    lanes = 128 if feat % 128 == 0 else feat
    any_spec = pl.BlockSpec(memory_space=pl.ANY)
    vmem_spec = pl.BlockSpec(memory_space=pltpu.VMEM)
    made = jax.ShapeDtypeStruct
    outs = [
        made((width, 3 * feat), bf16),
        made((feat, width), bf16),
        made((hid, width), bf16),
        made((hid, width), bf16),
        made((hid, width), bf16),
        made((group_rows, width), bf16),
        made((group_rows, width), bf16),
        made((group_rows, width), bf16),
        made((group_rows, 3 * feat), f32),
        made((group_rows, feat), f32),
        made((group_rows, feat), bf16),
        made((share, width), f32),
        made((share, width), f32),
        made((share, 128), f32),
        made((4,) + aux_own.shape, f32),
    ]
    scratch = [
        pltpu.VMEM((width, 3 * feat), bf16),
        pltpu.VMEM((feat, width), bf16),
        pltpu.VMEM((2, block, width), bf16),
        pltpu.VMEM((group_rows, width), bf16),
        pltpu.VMEM((4,) + aux_own.shape, f32),
        pltpu.VMEM((group_rows, 3 * feat), f32),
        pltpu.VMEM((group_rows, feat), f32),
        pltpu.VMEM((group_rows, feat), bf16),
        pltpu.VMEM((group_rows, width), bf16),
        pltpu.VMEM((4 * share, width), bf16),
        pltpu.VMEM((4 * share, width), bf16),
        pltpu.VMEM((4 * share, width), bf16),
        pltpu.VMEM((group_rows, lanes), f32),
        pltpu.VMEM((4 * share, lanes), f32),
        pltpu.VMEM((4 * share, lanes), f32),
        pltpu.VMEM((4 * share, lanes), f32),
        pltpu.VMEM((share, width), f32),
        pltpu.VMEM((share, width), f32),
        pltpu.VMEM((share, 128), f32),
        pltpu.VMEM((share, width), bf16),
        pltpu.VMEM((rows, feat), f32),
        pltpu.VMEM((rows, feat), f32),
        pltpu.SemaphoreType.DMA((68,)),
        pltpu.SemaphoreType.DMA((68,)),
        pltpu.SemaphoreType.DMA((24,)),
    ] + [pltpu.SemaphoreType.DMA((4,))] * 4
    return pl.pallas_call(
        front_kernel,
        in_specs=[any_spec] * 7 + [any_spec] + [vmem_spec] * 3,
        out_specs=[any_spec] * len(outs),
        out_shape=outs,
        scratch_shapes=scratch,
        compiler_params=pltpu.CompilerParams(
            collective_id=1, has_side_effects=True, vmem_limit_bytes=56 << 20
        ),
        name="front",
    )(s_mix, s_out, s_g, s_u, s_d, n1_own, go_own, aux_own, par, inp, gain2)


def body(
    n_dp,
    n_t,
    tokens_in,
    input_proj,
    forget_proj,
    outgate_proj,
    output_proj,
    glu_gate,
    glu_up,
    glu_down,
    norm_gain,
    mixer_gain,
    ffn_gain,
    bound_table,
    lengths,
    bucket,
    cotangent,
):
    depth = n_dp.bit_length() - 1
    tp_bits = (2, 0)
    fs_bits = tuple(b for b in reversed(range(depth)) if b not in tp_bits)
    t_depth = n_t.bit_length() - 1
    own_bits, free_bits = fs_bits[len(fs_bits) - t_depth :], fs_bits[: len(fs_bits) - t_depth]
    n_tp = 4
    tp_mask = (0, 1, 4, 5)
    axis_of = {b: depth - 1 - b for b in range(depth)}

    me = lax.axis_index("dp")
    t = lax.axis_index("tensor")
    bit = {b: (me >> b) & 1 for b in range(depth)}
    t_bit = {b: (t >> (t_depth - 1 - i)) & 1 for i, b in enumerate(own_bits)}
    q = bit[2] * 2 + bit[0]

    rows, width = tokens_in.shape
    share = cotangent.shape[0]
    block = width // n_dp
    free = 2 ** len(free_bits)
    feat = free * block

    def swap(values, mask):
        return lax.ppermute(values, "dp", [(i, i ^ mask) for i in range(n_dp)])

    def t_swap(values):
        return lax.ppermute(values, "tensor", [(0, 1), (1, 0)])

    def by_bit(which, own, other):
        return jnp.where(which == 0, own, other), jnp.where(which == 0, other, own)

    def in_order(parts, bits):
        parts = list(parts)
        for i, b in enumerate(reversed(bits)):
            step = 1 << i
            for r in range(len(parts)):
                if not r & step:
                    parts[r], parts[r | step] = by_bit(bit[b], parts[r], parts[r | step])
        return parts

    def t_gather(values):
        if n_t == 2:
            return jnp.stack(by_bit(t, values, t_swap(values)))
        return lax.all_gather(values, "tensor", axis=0)

    def t_scatter(values):
        if n_t == 2:
            return pick(values, t, 0).astype(f32) + t_swap(pick(values, 1 - t, 0)).astype(f32)
        return lax.psum_scatter(values, "tensor", scatter_dimension=0, tiled=False).astype(f32)

    def tp_gather(values):
        return [t_gather(values if r == 0 else swap(values, tp_mask[r])) for r in range(n_tp)]

    def tp_scatter(parts, kind):
        halves = [t_scatter(part) for part in parts]
        total = halves[0]
        for r in range(1, n_tp):
            total = total + swap(halves[r].astype(kind), tp_mask[r]).astype(f32)
        return total

    def exchange(values):
        parts = [pick(values, q, 0)]
        for r in range(1, n_tp):
            parts.append(swap(pick(values, q ^ r, 0), tp_mask[r]))
        return in_order(parts, tp_bits)

    def fs_gather(values):
        parts = [values]
        for b in fs_bits:
            parts = parts + [None] * 0 + [swap(v, 1 << b) for v in parts]
        return parts

    def weight_parts(shards):
        return fs_gather(jnp.stack(exchange(shards)))

    def weight_whole(parts):
        count = len(parts)
        flip = [0] * count
        for r in range(count):
            flip[sum(((r >> i) & 1) << (len(fs_bits) - 1 - i) for i in range(len(fs_bits)))] = parts[r]
        ordered = jnp.stack(in_order(flip, fs_bits))
        cols = ordered.shape[-1]
        ordered = ordered.reshape((2,) * depth + (block, cols))
        have = fs_bits + tp_bits
        axes = [have.index(b) for b in reversed(range(depth))]
        return ordered.transpose(axes + [depth, depth + 1]).reshape(width, cols)

    def weight_back(grad):
        cols = grad.shape[1]
        grad = grad.reshape((2,) * depth + (block, cols))
        for b in reversed(fs_bits):
            send = lax.dynamic_slice_in_dim(grad, 1 - bit[b], 1, axis_of[b]).astype(bf16)
            hold = lax.dynamic_slice_in_dim(grad, bit[b], 1, axis_of[b]).astype(f32)
            grad = hold + swap(send, 1 << b).astype(f32)
        return exchange(grad.reshape(n_tp, block, cols).astype(bf16))

    def my_columns(values):
        lead = values.shape[:-1]
        n = len(lead)
        values = values.reshape(lead + (2,) * depth + (block,))
        bits = list(reversed(range(depth)))
        for b in own_bits:
            values = pick(values, t_bit[b], n + bits.index(b))
            bits.remove(b)
        order = [n + bits.index(b) for b in tp_bits] + list(range(n)) + [n + bits.index(b) for b in free_bits]
        return values.transpose(order + [n + len(bits)]).reshape((n_tp,) + lead + (feat,))

    def my_half(values):
        return lax.dynamic_slice_in_dim(values, t * share, share, 0)

    inputs = tokens_in.astype(f32)
    scale_one = rms_scale(inputs)
    normed_mine = (inputs * scale_one * norm_gain).astype(bf16)
    inputs_half = my_half(inputs)
    scale_one_half = my_half(scale_one)
    mix_shards = jnp.concatenate(
        [my_columns(w) for w in (input_proj, forget_proj, outgate_proj)], axis=-1
    )
    hid = glu_gate.shape[1] // n_tp
    gate_shards = glu_gate.T.reshape(n_tp, hid, block)
    up_shards = glu_up.T.reshape(n_tp, hid, block)
    down_shards = glu_down.reshape(n_tp, hid, block)
    my_table = pick(my_columns(bound_table), q, 0)
    par = jnp.stack([bound_parts(my_table)[2], pick(my_columns(mixer_gain), q, 0)])
    valid_own, keep_own = layout(lengths, bucket, rows)
    grad_out_rows = (cotangent.astype(f32) * my_half(valid_own)).astype(bf16)
    if n_dp == 16 and n_t == 2:
        aux_own = jnp.concatenate([valid_own.T, keep_own.T, jnp.zeros((6, rows), f32)])
        (
            mix_full, out_full, gate_full, up_full, down_full, normed_one, grad_out_all, normed_two,
            pre, state, mix_raw, residual, mixed_out, scale_lanes, aux_rows,
        ) = front(
            mix_shards, output_proj, gate_shards, up_shards, down_shards, normed_mine, grad_out_rows,
            aux_own, par, inputs_half, ffn_gain[None, :],
        )
        scale_state = scale_lanes[:, :1]
        aux = aux_rows[:, :2].transpose(0, 2, 1).reshape(n_tp * rows, 2)
    else:
        normed_half = my_half(normed_mine)
        normed_parts = [normed_mine] + [
            t_gather(swap(normed_half, tp_mask[r])).reshape(rows, width) for r in range(1, n_tp)
        ]
        normed_one = jnp.concatenate(normed_parts)
        aux_own = jnp.concatenate([valid_own, keep_own], axis=1)
        aux = jnp.concatenate([aux_own] + [swap(aux_own, tp_mask[r]) for r in range(1, n_tp)])
        mix_full = weight_whole(weight_parts(mix_shards))
        out_piece = output_proj
        for b in own_bits:
            out_piece = jnp.where(t_bit[b] == bit[b], out_piece, swap(out_piece, 1 << b))
        out_pieces = [out_piece]
        for b in reversed(free_bits):
            out_pieces = out_pieces + [swap(v, 1 << b) for v in out_pieces]
        out_full = jnp.concatenate(in_order(out_pieces, free_bits))
        gate_full, up_full, down_full = (
            weight_whole(weight_parts(w.transpose(0, 2, 1))).T
            for w in (gate_shards, up_shards, down_shards)
        )
        grad_out_all = jnp.stack(tp_gather(grad_out_rows)).reshape(n_tp * rows, width)
        pre = matmul(normed_one, mix_full)
        state, mix_raw, square = mixer_forward(pre, aux, par, rows)
        out_parts = matmul(mix_raw, out_full).astype(bf16).reshape(n_tp, n_t, share, width)
        square_parts = square.reshape(n_tp, n_t, share)
        square_sum = tp_scatter([square_parts[r] for r in range(n_tp)], f32)
        out_sum = tp_scatter([out_parts[r] for r in range(n_tp)], bf16)
        scale_state = lax.rsqrt(square_sum / width + epsilon)[:, None]
        mixed_out = out_sum * scale_state
        residual = inputs_half + mixed_out
        normed_two_half = (residual * rms_scale(residual) * ffn_gain).astype(bf16)
        normed_two = jnp.stack(tp_gather(normed_two_half)).reshape(n_tp * rows, width)

    scale_two = rms_scale(residual)
    gate_pre = cross_cols(normed_two, gate_full)
    up_pre = cross_cols(normed_two, up_full)
    grad_hidden = cross_cols(grad_out_all, down_full)
    gate_act = jax.nn.silu(gate_pre)
    hidden = (gate_act * up_pre).astype(bf16)
    grad_up = (grad_hidden * gate_act).astype(bf16)
    grad_gate = (grad_hidden * up_pre * silu_slope(gate_pre)).astype(bf16)
    grad_two_parts = (
        (matmul(grad_gate, gate_full) + matmul(grad_up, up_full))
        .astype(bf16)
        .reshape(n_tp, n_t, share, width)
    )
    grad_normed_two = tp_scatter([grad_two_parts[r] for r in range(n_tp)], bf16)
    block_parts = matmul(hidden, down_full).astype(bf16).reshape(n_tp, n_t, share, width)
    block_out = (residual + tp_scatter([block_parts[r] for r in range(n_tp)], bf16)).astype(bf16)
    grad_down_t = jnp.stack(weight_back(cross_rows(grad_out_all, hidden).astype(bf16)))
    grad_w_gate = jnp.stack(weight_back(cross_rows(normed_two, grad_gate).astype(bf16)))
    grad_w_up = jnp.stack(weight_back(cross_rows(normed_two, grad_up).astype(bf16)))
    grad_glu_down = grad_down_t.transpose(0, 2, 1).reshape(glu_down.shape).astype(f32)
    grad_glu_gate = grad_w_gate.transpose(1, 0, 2).reshape(glu_gate.shape).astype(f32)
    grad_glu_up = grad_w_up.transpose(1, 0, 2).reshape(glu_up.shape).astype(f32)

    grad_residual = grad_out_rows.astype(f32) + norm_back(
        residual, scale_two, ffn_gain, grad_normed_two
    )
    ffn_gain_sum = jnp.sum(grad_normed_two * residual * scale_two, axis=0)
    grad_mix_half = grad_residual.astype(bf16)
    dot_mean = jnp.sum(grad_mix_half.astype(f32) * mixed_out, axis=1, keepdims=True) / (
        scale_state * width
    )
    row_values = jnp.concatenate([scale_state, dot_mean], axis=1).T
    row_all = jnp.stack(tp_gather(row_values)).transpose(0, 1, 3, 2).reshape(n_tp * rows, 2)
    grad_mix = jnp.stack(tp_gather(grad_mix_half)).reshape(n_tp * rows, width)
    grad_mixed = cross_cols(grad_mix, out_full)
    aux_back = jnp.concatenate([aux, row_all], axis=1)
    grads, sums = mixer_backward(pre, state, grad_mixed, aux_back, par, rows)
    one_parts = cross_cols(grads, mix_full).astype(bf16).reshape(n_tp, n_t, share, width)
    grad_normed_one = tp_scatter([one_parts[r] for r in range(n_tp)], bf16)
    grad_mix_w = jnp.stack(weight_back(cross_rows(normed_one, grads).astype(bf16)))

    mixed = (mix_raw.astype(f32) * row_all[:, :1]).astype(bf16)
    grad_out_w = cross_rows(mixed, grad_mix).astype(bf16).reshape((2,) * len(free_bits) + (block, width))
    for i, b in enumerate(free_bits):
        send = lax.dynamic_slice_in_dim(grad_out_w, 1 - bit[b], 1, i)
        hold = lax.dynamic_slice_in_dim(grad_out_w, bit[b], 1, i)
        grad_out_w = (hold.astype(f32) + swap(send, 1 << b).astype(f32)).astype(bf16)
    grad_out_w = grad_out_w.reshape(block, width)
    for b in own_bits:
        grad_out_w = (grad_out_w.astype(f32) + swap(grad_out_w, 1 << b).astype(f32)).astype(bf16)
    mine_t = jnp.int32(0)
    for b in own_bits:
        mine_t = mine_t * 2 + bit[b]
    if n_t == 2:
        other = t_swap(grad_out_w)
        grad_output_proj = jnp.where(mine_t == t, grad_out_w, other).astype(f32)
    else:
        grad_output_proj = pick(lax.all_gather(grad_out_w, "tensor", axis=0), mine_t, 0).astype(f32)

    mix_all = t_gather(grad_mix_w)
    mix_all = mix_all.reshape((2,) * t_depth + (2, 2) + (block, 3) + (2,) * len(free_bits) + (block,))
    order = list(own_bits) + list(tp_bits) + ["row", "which"] + list(free_bits) + ["col"]
    axes = [order.index(k) for k in ["which", "row"] + list(reversed(range(depth))) + ["col"]]
    mix_all = mix_all.transpose(axes).reshape(3, block, width).astype(f32)

    grad_tokens_half = my_half_residual = grad_residual + norm_back(
        inputs_half, scale_one_half, norm_gain, grad_normed_one
    )
    grad_tokens = t_gather(grad_tokens_half).reshape(rows, width)
    norm_gain_sum = jnp.sum(grad_normed_one * inputs_half * scale_one_half, axis=0)

    gains = jnp.stack([norm_gain_sum, ffn_gain_sum]).reshape((2,) + (2,) * depth + (block,))
    for b in reversed(range(depth)):
        at = 1 + axis_of[b]
        send = lax.dynamic_slice_in_dim(gains, 1 - bit[b], 1, at)
        hold = lax.dynamic_slice_in_dim(gains, bit[b], 1, at)
        gains = hold + swap(send, 1 << b)
    gains = gains.reshape(2, block)
    gains = gains + t_swap(gains) if n_t == 2 else lax.psum(gains, "tensor")

    for b in fs_bits:
        sums = sums + swap(sums, 1 << b)
    sums = t_gather(sums)
    sums = pick(sums, mine_t, 0).reshape((2,) + (2,) * len(free_bits) + (block,))
    for b in free_bits:
        sums = pick(sums, bit[b], 1)
    shares, picked, lower = bound_parts(lax.dynamic_slice_in_dim(bound_table, me * block, block, 1))
    grad_table = shares * (picked - lower[None, :]) * sums[1][None, :]

    return (
        block_out,
        grad_tokens,
        mix_all[0],
        mix_all[1],
        mix_all[2],
        grad_output_proj,
        grad_glu_gate,
        grad_glu_up,
        grad_glu_down,
        gains[0],
        sums[0],
        gains[1],
        grad_table,
    )


def solution(mesh):
    return jax.shard_map(
        functools.partial(body, mesh.shape["dp"], mesh.shape["tensor"]),
        mesh=mesh,
        in_specs=(
            P("dp", None),
            P("dp", None),
            P("dp", None),
            P("dp", None),
            P("dp", None),
            P("dp", "tensor"),
            P("dp", "tensor"),
            P("tensor", "dp"),
            P(),
            P(),
            P(),
            P(),
            P("dp"),
            P("dp"),
            P(("dp", "tensor"), None),
        ),
        out_specs=(
            P(("dp", "tensor"), None),
            P("dp", None),
            P("dp", None),
            P("dp", None),
            P("dp", None),
            P("dp", None),
            P("dp", "tensor"),
            P("dp", "tensor"),
            P("tensor", "dp"),
            P("dp"),
            P("dp"),
            P("dp"),
            P(None, "dp"),
        ),
        check_vma=False,
    )
```

```python
import functools

import jax
import jax.numpy as jnp
from jax import lax
from jax.experimental import pallas as pl
from jax.experimental.pallas import tpu as pltpu
from jax.sharding import PartitionSpec as P

LAYER = 12
epsilon = 1e-06
bf16 = jnp.bfloat16
f32 = jnp.float32


def rms_scale(values):
    return lax.rsqrt(jnp.mean(values * values, axis=-1, keepdims=True) + epsilon)


def norm_back(values, row_scale, gain_row, incoming):
    weighted = incoming * gain_row
    cubed = row_scale * row_scale * row_scale
    return row_scale * weighted - values * cubed * jnp.mean(
        weighted * values, axis=-1, keepdims=True
    )


def silu_slope(values):
    logistic = jax.nn.sigmoid(values)
    return logistic * (1.0 + values * (1.0 - logistic))


def matmul(first_op, second_op):
    return jnp.dot(first_op, second_op, preferred_element_type=f32)


def cross_rows(first_op, second_op):
    return lax.dot_general(
        first_op, second_op, (((0,), (0,)), ((), ())), preferred_element_type=f32
    )


def cross_cols(first_op, second_op):
    return lax.dot_general(
        first_op, second_op, (((1,), (1,)), ((), ())), preferred_element_type=f32
    )


def pick(values, index, axis):
    return lax.dynamic_index_in_dim(values, index, axis, keepdims=False)


def layout(lengths, bucket, row_count):
    slot_len = row_count // jnp.left_shift(jnp.int32(1), bucket)
    position = jnp.arange(row_count, dtype=jnp.int32)
    slot_index = position // slot_len
    offset = position - slot_index * slot_len
    slot_ids = jnp.arange(lengths.shape[0], dtype=jnp.int32)
    chosen = (slot_index[:, None] == slot_ids[None, :]).astype(jnp.int32)
    slot_limit = jnp.sum(chosen * lengths[None, :], axis=1)
    valid_mask = (offset < slot_limit).astype(f32)[:, None]
    keep_mask = (offset > 0).astype(f32)[:, None]
    return (valid_mask, keep_mask)


def bound_parts(bound_table):
    shares = jax.nn.softmax(bound_table, axis=0)
    layer_ids = jnp.arange(bound_table.shape[0], dtype=jnp.int32)[:, None]
    picked = ((layer_ids >= 1) & (layer_ids <= LAYER)).astype(f32)
    return (shares, picked, jnp.sum(shares * picked, axis=0))


def scan_rows(decay_ref, add_ref, out_ref, reverse):
    rows, width = out_ref.shape
    tiles = rows // 8
    sub = lax.broadcasted_iota(jnp.int32, (8, width), 0)

    def step(i, carry):
        j = tiles - 1 - i if reverse else i
        at = pl.ds(pl.multiple_of(j * 8, 8), 8)
        a = decay_ref[at, :]
        b = add_ref[at, :]
        for s in (1, 2, 4):
            shift = 8 - s if reverse else s
            inside = sub < 8 - s if reverse else sub >= s
            b = jnp.where(inside, b + a * pltpu.roll(b, shift, 0), b)
            a = jnp.where(inside, a * pltpu.roll(a, shift, 0), a)
        h = b + a * carry
        out_ref[at, :] = h
        edge = h[0:1, :] if reverse else h[7:8, :]
        return jnp.broadcast_to(edge, (8, width))

    lax.fori_loop(0, tiles, step, jnp.zeros((8, width), f32), unroll=4)


def mixer_forward_kernel(pre_ref, aux_ref, par_ref, state_ref, mix_ref, sq_ref, decay_ref, add_ref):
    width = state_ref.shape[1]
    input_pre = pre_ref[:, :width]
    forget_pre = pre_ref[:, width : 2 * width]
    outgate_pre = pre_ref[:, 2 * width :]
    valid = aux_ref[:, 0:1]
    keep = aux_ref[:, 1:2]
    bound = par_ref[0:1, :]
    gain = par_ref[1:2, :]
    forget = bound + (1.0 - bound) * jax.nn.sigmoid(forget_pre)
    add_ref[...] = input_pre * jax.nn.sigmoid(input_pre) * (1.0 - forget) * valid
    decay_ref[...] = forget * keep
    scan_rows(decay_ref, add_ref, state_ref, False)
    state = state_ref[...]
    mix_ref[...] = (state * gain * (outgate_pre * jax.nn.sigmoid(outgate_pre))).astype(bf16)
    sq_ref[...] = jnp.sum(state * state, axis=1, keepdims=True)


def mixer_forward(pre, aux, par, seq_rows):
    rows, width = pre.shape[0], pre.shape[1] // 3
    row_block = lambda n: pl.BlockSpec((seq_rows, n), lambda i: (i, 0))
    return pl.pallas_call(
        mixer_forward_kernel,
        grid=(rows // seq_rows,),
        in_specs=[
            row_block(3 * width),
            row_block(aux.shape[1]),
            pl.BlockSpec(par.shape, lambda i: (0, 0)),
        ],
        out_specs=[row_block(width), row_block(width), row_block(1)],
        out_shape=[
            jax.ShapeDtypeStruct((rows, width), f32),
            jax.ShapeDtypeStruct((rows, width), bf16),
            jax.ShapeDtypeStruct((rows, 1), f32),
        ],
        scratch_shapes=[pltpu.VMEM((seq_rows, width), f32)] * 2,
        cost_estimate=pl.CostEstimate(
            flops=rows * width * 60, bytes_accessed=rows * width * 20, transcendentals=rows * width * 3
        ),
        name="mixer_forward",
    )(pre, aux, par)


def mixer_backward_kernel(
    pre_ref, state_ref, up_ref, aux_ref, par_ref, grad_ref, sums_ref, decay_ref, add_ref, out_ref
):
    rows, width = state_ref.shape
    input_pre = pre_ref[:, :width]
    forget_pre = pre_ref[:, width : 2 * width]
    outgate_pre = pre_ref[:, 2 * width :]
    valid = aux_ref[:, 0:1]
    keep = aux_ref[:, 1:2]
    scale = aux_ref[:, 2:3]
    dot_mean = aux_ref[:, 3:4]
    bound = par_ref[0:1, :]
    gain = par_ref[1:2, :]
    state = state_ref[...]
    incoming = up_ref[...]
    at_row = lax.broadcasted_iota(jnp.int32, (rows, width), 0)
    sig_out = jax.nn.sigmoid(outgate_pre)
    act_out = outgate_pre * sig_out
    scaled = incoming * (state * scale)
    grad_ref[:, 2 * width :] = (
        scaled * gain * (sig_out * (1.0 + outgate_pre * (1.0 - sig_out)))
    ).astype(bf16)
    add_ref[...] = scale * (gain * act_out * incoming) - state * (scale * scale * scale * dot_mean)
    sig_forget = jax.nn.sigmoid(forget_pre)
    forget = bound + (1.0 - bound) * sig_forget
    decay_ref[...] = jnp.where(
        at_row < rows - 1, pltpu.roll(forget * keep, rows - 1, 0), 0.0
    )
    scan_rows(decay_ref, add_ref, out_ref, True)
    grad_state = out_ref[...]
    before = jnp.where(at_row > 0, pltpu.roll(state, 1, 0), 0.0)
    sig_in = jax.nn.sigmoid(input_pre)
    grad_forget = grad_state * (before * keep - input_pre * sig_in * valid)
    grad_ref[:, :width] = (
        grad_state * (1.0 - forget) * valid * (sig_in * (1.0 + input_pre * (1.0 - sig_in)))
    ).astype(bf16)
    grad_ref[:, width : 2 * width] = (
        grad_forget * (1.0 - bound) * sig_forget * (1.0 - sig_forget)
    ).astype(bf16)

    @pl.when(pl.program_id(0) == 0)
    def _():
        sums_ref[...] = jnp.zeros_like(sums_ref)

    sums_ref[0:1, :] += jnp.sum(scaled * act_out, axis=0, keepdims=True)
    sums_ref[1:2, :] += jnp.sum(grad_forget * (1.0 - sig_forget), axis=0, keepdims=True)


def mixer_backward(pre, state, incoming, aux, par, seq_rows):
    rows, width = state.shape
    row_block = lambda n: pl.BlockSpec((seq_rows, n), lambda i: (i, 0))
    whole = lambda shape: pl.BlockSpec(shape, lambda i: (0, 0))
    return pl.pallas_call(
        mixer_backward_kernel,
        grid=(rows // seq_rows,),
        in_specs=[
            row_block(3 * width),
            row_block(width),
            row_block(width),
            row_block(aux.shape[1]),
            whole(par.shape),
        ],
        out_specs=[row_block(3 * width), whole((2, width))],
        out_shape=[
            jax.ShapeDtypeStruct((rows, 3 * width), bf16),
            jax.ShapeDtypeStruct((2, width), f32),
        ],
        scratch_shapes=[pltpu.VMEM((seq_rows, width), f32)] * 3,
        cost_estimate=pl.CostEstimate(
            flops=rows * width * 90, bytes_accessed=rows * width * 26, transcendentals=rows * width * 3
        ),
        name="mixer_backward",
    )(pre, state, incoming, aux, par)


MESH = pl.DeviceIdType.MESH


class Copies:
    def __init__(self, send, recv, local):
        self.send, self.recv, self.local = send, recv, local
        self.n_remote = self.n_local = 0
        self.open = []

    def remote(self, src, dst, device):
        k = self.n_remote
        self.n_remote += 1
        copy = pltpu.make_async_remote_copy(
            src_ref=src,
            dst_ref=dst,
            send_sem=self.send.at[k],
            recv_sem=self.recv.at[k],
            device_id=device,
            device_id_type=MESH,
        )
        copy.start()
        self.open.append(copy.wait_send)
        return copy

    def here(self, src, dst, keep=False):
        k = self.n_local
        self.n_local += 1
        copy = pltpu.make_async_copy(src, dst, self.local.at[k])
        copy.start()
        if keep:
            self.open.append(copy.wait)
        return copy

    def sent(self, copies):
        for copy in copies:
            copy.wait_send()
            self.open.remove(copy.wait_send)

    def close(self):
        assert self.n_remote <= self.send.shape[0] and self.n_local <= self.local.shape[0]
        for wait in self.open:
            wait()


def position():
    me = lax.axis_index("dp")
    t = lax.axis_index("tensor")
    zf, zn, y, x = me // 8, (me // 4) % 2, (me // 2) % 2, me % 2
    to_x, to_zn = 1 - 2 * x, 4 - 8 * zn
    group = [None, (me + to_x, t), (me + to_zn, t), (me + to_x + to_zn, t)]
    q = [zn * 2 + x, zn * 2 + 1 - x, (1 - zn) * 2 + x, (1 - zn) * 2 + 1 - x]
    far = (me + 8 - 16 * zf, t)
    side = (me + 2 - 4 * y, t)
    core = (me, 1 - t)
    return me, t, (zf, zn, y, x), q, group, far, side, core


def meet(devices):
    barrier = pltpu.get_barrier_semaphore()
    for device in devices:
        pl.semaphore_signal(barrier, inc=1, device_id=device, device_id_type=MESH)
    pl.semaphore_wait(barrier, len(devices))


def fold_lanes(values):
    width = values.shape[1]
    if width % 128:
        return values
    total = values[:, :128]
    for i in range(128, width, 128):
        total = total + values[:, i : i + 128]
    return total


def front_kernel(
    s_mix, s_out, s_g, s_u, s_d, n1_own, go_own, aux_own, par, inp, gain2,
    o_mix, o_out, o_g, o_u, o_d, o_n1, o_go, o_n2, o_pre, o_state, o_raw, o_res, o_mo, o_sc, o_aux,
    w_mix, w_out, n1, aux, pre, state, raw, part, core_in, half, peer_in,
    sq, sq_core, sq_half, sq_peer, res, mo, sc, n2, decay, add,
    send, recv, local, core_send, core_recv, sqc_send, sqc_recv, out_send, out_recv,
):
    me, t, (zf, zn, y, x), q, group, far, side, core = position()
    share, width = inp.shape
    rows = 2 * share
    block = s_out.shape[0]
    feat = par.shape[1]
    link = Copies(send, recv, local)
    meet(group[1:] + [far, side, core])

    def at(start, size, unit):
        return pl.ds(pl.multiple_of(start, unit), size)

    def pair(fz, c, fy):
        return at(fz * (8 * block) + c * (4 * block) + fy * (2 * block), 2 * block, 2 * block)

    mine = at(me * block, block, block)

    def row(r, tt):
        return at(r * rows + tt * share, share, share)

    mix_in = [link.remote(s_mix.at[q[r]], w_mix.at[mine], group[r]) for r in (1, 2, 3)]
    mix_own = link.here(s_mix.at[q[0]], w_mix.at[mine])
    out_rows = [at(z * block, block, block) for z in (zf, 1 - zf)]

    def out_copy(k, src, dst, device):
        return pltpu.make_async_remote_copy(
            src_ref=src,
            dst_ref=w_out.at[dst],
            send_sem=out_send.at[k],
            recv_sem=out_recv.at[k],
            device_id=device,
            device_id_type=MESH,
        )

    out_far = out_copy(0, s_out, out_rows[0], far)
    out_side = out_copy(1, s_out, out_rows[0], side)
    out_next = out_copy(2, w_out.at[out_rows[1]], out_rows[1], side)
    out_here = pltpu.make_async_copy(s_out, w_out.at[out_rows[0]], out_send.at[3])

    @pl.when(t == y)
    def _():
        out_far.start()
        out_side.start()
        out_here.start()

    aux_in = [link.remote(aux_own, aux.at[r], group[r]) for r in (1, 2, 3)]
    aux_mine = link.here(aux_own, aux.at[0])
    n1_in = [link.remote(n1_own.at[at(t * share, share, share)], n1.at[row(r, t)], group[r]) for r in (1, 2)]
    n1_mine = link.here(n1_own, n1.at[pl.ds(0, rows)])
    mix_own.wait()
    for c in mix_in:
        c.wait_recv()
    far_mix = [link.remote(w_mix.at[pair(zf, c, y)], w_mix.at[pair(zf, c, y)], far) for c in (0, 1)]
    side_mix = [link.remote(w_mix.at[pair(zf, c, y)], w_mix.at[pair(zf, c, y)], side) for c in (0, 1)]
    n1_in[1].wait_recv()
    n1_in.append(link.remote(n1.at[row(2, t)], n1.at[row(3, t)], group[1]))
    n1_core = [link.remote(n1.at[row(2, t)], n1.at[row(2, t)], core)]
    n1_in[0].wait_recv()
    n1_core.append(link.remote(n1.at[row(1, t)], n1.at[row(1, t)], core))
    shards = ((s_g, o_g), (s_u, o_u), (s_d, o_d))
    ffn_in, ffn_own = [], []
    for s, o in shards:
        ffn_in += [link.remote(s.at[q[r]], o.at[:, mine], group[r]) for r in (1, 2, 3)]
        ffn_own.append(link.here(s.at[q[0]], o.at[:, mine]))
    n1_in[2].wait_recv()
    n1_core.append(link.remote(n1.at[row(3, t)], n1.at[row(3, t)], core))
    for c in (0, 1):
        far_mix[c].wait_recv()
        side_mix.append(link.remote(w_mix.at[pair(1 - zf, c, y)], w_mix.at[pair(1 - zf, c, y)], side))

    @pl.when(t == y)
    def _():
        out_far.wait_recv()
        out_next.start()
        out_far.wait_send()
        out_side.wait_send()
        out_here.wait()
        out_next.wait_send()

    @pl.when(t != y)
    def _():
        out_side.wait_recv()
        out_next.wait_recv()

    for c in ffn_own:
        c.wait()
    for c in ffn_in:
        c.wait_recv()
    far_ffn, side_ffn = [], []
    for s, o in shards:
        far_ffn.append([link.remote(o.at[:, pair(zf, c, y)], o.at[:, pair(zf, c, y)], far) for c in (0, 1)])
    for s, o in shards:
        side_ffn += [link.remote(o.at[:, pair(zf, c, y)], o.at[:, pair(zf, c, y)], side) for c in (0, 1)]

    def forward_ffn(i):
        o = shards[i][1]
        for c in (0, 1):
            far_ffn[i][c].wait_recv()
            side_ffn.append(link.remote(o.at[:, pair(1 - zf, c, y)], o.at[:, pair(1 - zf, c, y)], side))

    go_in = [link.remote(go_own, o_go.at[row(r, t)], group[r]) for r in (1, 2)]
    go_core = [link.remote(go_own, o_go.at[row(0, t)], core)]
    link.here(go_own, o_go.at[row(0, t)], keep=True)

    n1_mine.wait()
    aux_mine.wait()
    for c in side_mix + n1_core + aux_in:
        c.wait_recv()

    def core_copy(r):
        return pltpu.make_async_remote_copy(
            src_ref=part.at[row(r, 1 - t)],
            dst_ref=core_in.at[at(r * share, share, share)],
            send_sem=core_send.at[r],
            recv_sem=core_recv.at[r],
            device_id=core,
            device_id_type=MESH,
        )

    def sq_copy(r):
        return pltpu.make_async_remote_copy(
            src_ref=sq.at[row(r, 1 - t)],
            dst_ref=sq_core.at[at(r * share, share, share)],
            send_sem=sqc_send.at[r],
            recv_sem=sqc_recv.at[r],
            device_id=core,
            device_id_type=MESH,
        )

    bound = par[0:1, :]
    gain = par[1:2, :]

    def piece(i, carry):
        r = 3 - i
        here = at(r * rows, rows, rows)
        pre[here, :] = jnp.dot(n1[here, :], w_mix[...], preferred_element_type=f32)
        columns = aux[r].T
        valid = columns[:, 0:1]
        keep = columns[:, 1:2]
        forget = bound + (1.0 - bound) * jax.nn.sigmoid(pre[here, feat : 2 * feat])
        input_pre = pre[here, 0:feat]
        add[...] = input_pre * jax.nn.sigmoid(input_pre) * (1.0 - forget) * valid
        decay[...] = forget * keep
        scan_rows(decay, add, state.at[here, :], False)
        held = state[here, :]
        outgate_pre = pre[here, 2 * feat :]
        raw[here, :] = (held * gain * (outgate_pre * jax.nn.sigmoid(outgate_pre))).astype(bf16)
        sq[here, :] = fold_lanes(held * held)
        part[here, :] = jnp.dot(raw[here, :], w_out[...], preferred_element_type=f32).astype(bf16)
        core_copy(r).start()
        sq_copy(r).start()
        return carry

    lax.fori_loop(0, 4, piece, 0)

    link.here(w_mix, o_mix, keep=True)
    link.here(w_out, o_out, keep=True)
    link.here(n1, o_n1, keep=True)
    link.here(pre, o_pre, keep=True)
    link.here(state, o_state, keep=True)
    link.here(raw, o_raw, keep=True)
    link.here(aux, o_aux, keep=True)

    out_in, sq_in = [], []
    for r in (3, 2, 1):
        core_copy(r).wait()
        sq_copy(r).wait()
        to = at(r * share, share, share)
        half[to, :] = (part[row(r, t), :].astype(f32) + core_in[to, :].astype(f32)).astype(bf16)
        sq_half[to, :] = sq[row(r, t), :] + sq_core[to, :]
        out_in.append(link.remote(half.at[to], peer_in.at[to], group[r]))
        sq_in.append(link.remote(sq_half.at[to], sq_peer.at[to], group[r]))
    core_copy(0).wait()
    sq_copy(0).wait()
    forward_ffn(0)
    for c in out_in + sq_in:
        c.wait_recv()
    total_sq = sq[row(0, t), :] + sq_core[0:share, :]
    for r in (1, 2, 3):
        total_sq = total_sq + sq_peer[r * share : (r + 1) * share, :]
    scale = lax.rsqrt(jnp.sum(total_sq, axis=1, keepdims=True) / width + epsilon)
    sc[...] = jnp.broadcast_to(scale, sc.shape)
    chunk = min(share, 16)

    def finish(i, carry):
        to = at(i * chunk, chunk, chunk)
        total = part[at(t * share + i * chunk, chunk, chunk), :].astype(f32) + core_in[to, :].astype(f32)
        for r in (1, 2, 3):
            total = total + peer_in[at(r * share + i * chunk, chunk, chunk), :].astype(f32)
        mixed = total * sc[to, 0:1]
        value = inp[to, :] + mixed
        mo[to, :] = mixed
        res[to, :] = value
        scale_two = lax.rsqrt(jnp.mean(value * value, axis=1, keepdims=True) + epsilon)
        n2[to, :] = (value * scale_two * gain2[...]).astype(bf16)
        return carry

    lax.fori_loop(0, share // chunk, finish, 0)
    n2_in = [link.remote(n2, o_n2.at[row(r, t)], group[r]) for r in (1, 2)]
    n2_core = [link.remote(n2, o_n2.at[row(0, t)], core)]
    link.here(n2, o_n2.at[row(0, t)], keep=True)
    link.here(res, o_res, keep=True)
    link.here(mo, o_mo, keep=True)
    link.here(sc, o_sc, keep=True)

    def spread(o, incoming, cores):
        incoming[1].wait_recv()
        incoming.append(link.remote(o.at[row(2, t)], o.at[row(3, t)], group[1]))
        cores.append(link.remote(o.at[row(2, t)], o.at[row(2, t)], core))
        incoming[0].wait_recv()
        cores.append(link.remote(o.at[row(1, t)], o.at[row(1, t)], core))

    def spread_last(o, incoming, cores):
        incoming[2].wait_recv()
        cores.append(link.remote(o.at[row(3, t)], o.at[row(3, t)], core))

    spread(o_go, go_in, go_core)
    spread(o_n2, n2_in, n2_core)
    forward_ffn(1)
    spread_last(o_go, go_in, go_core)
    spread_last(o_n2, n2_in, n2_core)
    forward_ffn(2)
    for c in side_ffn + go_core + n2_core:
        c.wait_recv()
    link.close()


def front(s_mix, s_out, s_g, s_u, s_d, n1_own, go_own, aux_own, par, inp, gain2):
    share, width = inp.shape
    rows, group_rows = 2 * share, 8 * share
    feat, hid = par.shape[1], s_g.shape[1]
    block = s_out.shape[0]
    lanes = 128 if feat % 128 == 0 else feat
    any_spec = pl.BlockSpec(memory_space=pl.ANY)
    vmem_spec = pl.BlockSpec(memory_space=pltpu.VMEM)
    made = jax.ShapeDtypeStruct
    outs = [
        made((width, 3 * feat), bf16),
        made((feat, width), bf16),
        made((hid, width), bf16),
        made((hid, width), bf16),
        made((hid, width), bf16),
        made((group_rows, width), bf16),
        made((group_rows, width), bf16),
        made((group_rows, width), bf16),
        made((group_rows, 3 * feat), f32),
        made((group_rows, feat), f32),
        made((group_rows, feat), bf16),
        made((share, width), f32),
        made((share, width), f32),
        made((share, 128), f32),
        made((4,) + aux_own.shape, f32),
    ]
    scratch = [
        pltpu.VMEM((width, 3 * feat), bf16),
        pltpu.VMEM((feat, width), bf16),
        pltpu.VMEM((group_rows, width), bf16),
        pltpu.VMEM((4,) + aux_own.shape, f32),
        pltpu.VMEM((group_rows, 3 * feat), f32),
        pltpu.VMEM((group_rows, feat), f32),
        pltpu.VMEM((group_rows, feat), bf16),
        pltpu.VMEM((group_rows, width), bf16),
        pltpu.VMEM((4 * share, width), bf16),
        pltpu.VMEM((4 * share, width), bf16),
        pltpu.VMEM((4 * share, width), bf16),
        pltpu.VMEM((group_rows, lanes), f32),
        pltpu.VMEM((4 * share, lanes), f32),
        pltpu.VMEM((4 * share, lanes), f32),
        pltpu.VMEM((4 * share, lanes), f32),
        pltpu.VMEM((share, width), f32),
        pltpu.VMEM((share, width), f32),
        pltpu.VMEM((share, 128), f32),
        pltpu.VMEM((share, width), bf16),
        pltpu.VMEM((rows, feat), f32),
        pltpu.VMEM((rows, feat), f32),
        pltpu.SemaphoreType.DMA((68,)),
        pltpu.SemaphoreType.DMA((68,)),
        pltpu.SemaphoreType.DMA((24,)),
    ] + [pltpu.SemaphoreType.DMA((4,))] * 6
    return pl.pallas_call(
        front_kernel,
        in_specs=[any_spec] * 7 + [any_spec] + [vmem_spec] * 3,
        out_specs=[any_spec] * len(outs),
        out_shape=outs,
        scratch_shapes=scratch,
        compiler_params=pltpu.CompilerParams(
            collective_id=1, has_side_effects=True, vmem_limit_bytes=56 << 20
        ),
        name="front",
    )(s_mix, s_out, s_g, s_u, s_d, n1_own, go_own, aux_own, par, inp, gain2)


def back_kernel(
    h_d, h_g, h_u, n2, go, p_two, p_block, n1, w_mix_in, w_out_in, pre, state, raw, aux_in,
    par, inp, res, mo, sc, go_own, gains,
    o_g, o_u, o_d, o_mix, o_out, o_tok, o_blk, o_vec,
    left, right, gmix, dw_d, dw_g, dw_u, dw_mix, yr_d, yr_g, yr_u, yr_mix, zr_d, zr_g, zr_u, zr_mix,
    own, half, core_in, core_blk, peer_in, peer_blk, w_mix, w_out, aux, pre_b, state_b, raw_b,
    grads, grads_t, decay, add, hold, yr_out, zr_out, hid_a, hid_b,
    gres, gm_own, scalars, scal_all, sums, vec, vec_in,
    send, recv, local, core_send, core_recv, out_send, out_recv, piece_sem,
):
    me, t, (zf, zn, y, x), q, group, far, side, core = position()
    share, width = inp.shape
    rows = 2 * share
    block = width // 16
    feat = par.shape[1]
    link = Copies(send, recv, local)
    meet(group[1:] + [far, side, core])

    def at(start, size, unit):
        return pl.ds(pl.multiple_of(start, unit), size)

    def pair(fz, c, fy):
        return at(fz * (8 * block) + c * (4 * block) + fy * (2 * block), 2 * block, 2 * block)

    def row(r, tt):
        return at(r * rows + tt * share, share, share)

    def rel(r):
        return pl.ds(r * share, share)

    two_core = [link.remote(p_two.at[row(r, 1 - t)], core_in.at[rel(r)], core) for r in (3, 2, 1, 0)]
    two_own = [link.here(p_two.at[row(r, t)], own.at[rel(r)]) for r in (3, 2, 1, 0)]
    get_d = [link.here(h_d, hid_a), link.here(go, left)]
    get_g = [link.here(h_g, hid_b), link.here(n2, right)]
    get_aux = [link.here(aux_in, aux), link.here(w_out_in, w_out), link.here(w_mix_in, w_mix)]

    def over_cores(arrived, mine, source, peers):
        sent = []
        for i, r in enumerate((3, 2, 1)):
            for c in mine[i]:
                c.wait()
            arrived[i].wait_recv()

            def add_rows(j, carry):
                to = at(r * share + j * 16, 16, 16)
                half[to, :] = (source(r, j) + core_in_now[to, :].astype(f32)).astype(bf16)
                return carry

            lax.fori_loop(0, share // 16, add_rows, 0)
            sent.append(link.remote(half.at[rel(r)], peers.at[rel(r - 1)], group[r]))
        for c in mine[3]:
            c.wait()
        arrived[3].wait_recv()
        return sent

    def own_rows(r, j):
        return own[at(r * share + j * 16, 16, 16), :].astype(f32)

    core_in_now = core_in
    two_peer = over_cores(two_core, [[c] for c in two_own], own_rows, peer_in)

    def weight_grad(hid, other, dw, first, count):
        wide = 4 * block

        def columns(i, carry):
            to = at(((1 - zf) * 2 + i - (i // 2) * 4 * (1 - zf)) * wide, wide, wide)
            dw[:, to] = jnp.dot(hid[...], other[:, to], preferred_element_type=f32).astype(bf16)
            return carry

        lax.fori_loop(first, first + count, columns, 0)

    def side_send(dw, yr, slot):
        fz = 1 - zf if slot == 0 else zf
        return [
            link.remote(dw.at[:, pair(fz, c, 1 - y)], yr.at[:, pl.ds((slot * 2 + c) * 2 * block, 2 * block)], side)
            for c in (0, 1)
        ]

    def first_hop(hid, other, dw, yr):
        weight_grad(hid, other, dw, 0, 2)
        sent = [side_send(dw, yr, 0)]
        weight_grad(hid, other, dw, 2, 2)
        sent.append(side_send(dw, yr, 1))
        return sent

    for c in get_d:
        c.wait()
    hop_d = first_hop(hid_a, left, dw_d, yr_d)
    get_u = link.here(h_u, hid_a)
    get_n1 = link.here(n1, left)
    for c in get_g:
        c.wait()
    hop_g = first_hop(hid_b, right, dw_g, yr_g)

    for c in two_peer:
        c.wait_recv()
    gain_two = gains[1:2, :]
    sums[...] = jnp.zeros_like(sums)
    step = 16

    def residual_rows(j, carry):
        to = at(j * step, step, step)
        total = own[to, :].astype(f32) + core_in[to, :].astype(f32)
        for r in (0, 1, 2):
            total = total + peer_in[at(r * share + j * step, step, step), :].astype(f32)
        value = res[to, :]
        s = lax.rsqrt(jnp.mean(value * value, axis=1, keepdims=True) + epsilon)
        weighted = total * gain_two
        grad = (
            go_own[to, :].astype(f32)
            + s * weighted
            - value * (s * s * s) * jnp.mean(weighted * value, axis=1, keepdims=True)
        )
        gres[to, :] = grad
        low = grad.astype(bf16)
        gm_own[to, :] = low
        dot = jnp.sum(low.astype(f32) * mo[to, :], axis=1, keepdims=True)
        scale = sc[to, 0:1]
        sc[to, 1:2] = dot / (scale * width)
        sums[1:2, :] += jnp.sum(total * value * s, axis=0, keepdims=True)
        return carry

    lax.fori_loop(0, share // step, residual_rows, 0)
    scalars[...] = sc[...].T[0:8, :]

    def scal(r, tt):
        return scal_all.at[r * 2 + tt]

    gm_in = [link.remote(gm_own, gmix.at[row(r, t)], group[r]) for r in (1, 2)]
    sc_in = [link.remote(scalars, scal(r, t), group[r]) for r in (1, 2, 3)]
    gm_core = [link.remote(gm_own, gmix.at[row(0, t)], core), link.remote(scalars, scal(0, t), core)]
    gm_here = [link.here(gm_own, gmix.at[row(0, t)]), link.here(scalars, scal(0, t))]
    blk_core = [link.remote(p_block.at[row(r, 1 - t)], core_blk.at[rel(r)], core) for r in (3, 2, 1, 0)]

    get_u.wait()
    hop_u = first_hop(hid_a, right, dw_u, yr_u)

    def add_columns(dw, to, others):
        size = 64 if dw.shape[0] % 64 == 0 else dw.shape[0]

        def some(j, carry):
            at_rows = at(j * size, size, size)
            total = dw[at_rows, to].astype(f32)
            for ref, cols in others:
                total = total + ref[at_rows, cols].astype(f32)
            dw[at_rows, to] = total.astype(bf16)
            return carry

        lax.fori_loop(0, dw.shape[0] // size, some, 0)

    def part_of(i):
        return pl.ds(i * 2 * block, 2 * block)

    def second_hop(hop, dw, yr, zr):
        sent = []
        for c in (0, 1):
            hop[0][c].wait_recv()
            add_columns(dw, pair(1 - zf, c, y), [(yr, part_of(c))])
            sent.append(link.remote(dw.at[:, pair(1 - zf, c, y)], zr.at[:, part_of(c)], far))
        return sent

    def last_hop(hop, sent, dw, yr, zr, out):
        for c in (0, 1):
            hop[1][c].wait_recv()
            sent[c].wait_recv()
            add_columns(dw, pair(zf, c, y), [(yr, part_of(2 + c)), (zr, part_of(c))])

        def owner(r):
            fx = x if r in (0, 2) else 1 - x
            fzn = zn if r in (0, 1) else 1 - zn
            return at((zf * 8 + fzn * 4 + y * 2 + fx) * block, block, block)

        link.here(dw.at[:, owner(0)], out.at[q[0]], keep=True)
        return [link.remote(dw.at[:, owner(r)], out.at[q[0]], group[r]) for r in (1, 2, 3)]

    far_d = second_hop(hop_d, dw_d, yr_d, zr_d)

    gm_in[1].wait_recv()
    gm_in.append(link.remote(gmix.at[row(2, t)], gmix.at[row(3, t)], group[1]))
    gm_core.append(link.remote(gmix.at[row(2, t)], gmix.at[row(2, t)], core))
    gm_in[0].wait_recv()
    gm_core.append(link.remote(gmix.at[row(1, t)], gmix.at[row(1, t)], core))
    for i, r in enumerate((1, 2, 3)):
        sc_in[i].wait_recv()
        gm_core.append(link.remote(scal(r, t), scal(r, t), core))
    far_g = second_hop(hop_g, dw_g, yr_g, zr_g)
    gm_in[2].wait_recv()
    gm_core.append(link.remote(gmix.at[row(3, t)], gmix.at[row(3, t)], core))

    link.sent(two_peer)
    blk_own = [link.here(p_block.at[row(r, t)], own.at[rel(r)]) for r in (3, 2, 1, 0)]
    for c in get_aux + [get_n1] + gm_here:
        c.wait()
    for c in gm_core:
        c.wait_recv()

    def one_core(r):
        return pltpu.make_async_remote_copy(
            src_ref=right.at[row(r, 1 - t)],
            dst_ref=core_in.at[at(r * share, share, share)],
            send_sem=core_send.at[r],
            recv_sem=core_recv.at[r],
            device_id=core,
            device_id_type=MESH,
        )

    def fetch(r):
        here = at(r * rows, rows, rows)
        return [
            pltpu.make_async_copy(pre.at[here], pre_b, piece_sem.at[0]),
            pltpu.make_async_copy(state.at[here], state_b, piece_sem.at[1]),
            pltpu.make_async_copy(raw.at[here], raw_b, piece_sem.at[2]),
        ]

    bound = par[0:1, :]
    gain = par[1:2, :]
    gain_sums = sums.at[2:4, 0:feat]
    mixed_t = hid_b.at[0:feat]
    dw_out = w_out

    def piece(i, carry):
        r = 3 - i
        here = at(r * rows, rows, rows)
        copies = fetch(r)
        for c in copies:
            c.start()
        up = lax.dot_general(
            gmix[here, :], w_out[...], (((1,), (1,)), ((), ())), preferred_element_type=f32
        )
        masks = aux[r].T
        valid = masks[:, 0:1]
        keep = masks[:, 1:2]
        scale_parts = [scal_all[r * 2 + tt].T for tt in (0, 1)]
        scale = jnp.concatenate([p[:, 0:1] for p in scale_parts], axis=0)
        dot_mean = jnp.concatenate([p[:, 1:2] for p in scale_parts], axis=0)
        for c in copies:
            c.wait()
        at_row = lax.broadcasted_iota(jnp.int32, (rows, feat), 0)
        input_pre = pre_b[:, :feat]
        outgate_pre = pre_b[:, 2 * feat :]
        held = state_b[...]
        sig_out = jax.nn.sigmoid(outgate_pre)
        act_out = outgate_pre * sig_out
        scaled = up * (held * scale)
        grads[:, 2 * feat :] = scaled * gain * (sig_out * (1.0 + outgate_pre * (1.0 - sig_out)))
        add[...] = scale * (gain * act_out * up) - held * (scale * scale * scale * dot_mean)
        gain_sums[0:1, :] += jnp.sum(scaled * act_out, axis=0, keepdims=True)
        sig_forget = jax.nn.sigmoid(pre_b[:, feat : 2 * feat])
        forget = bound + (1.0 - bound) * sig_forget
        decay[...] = jnp.where(at_row < rows - 1, pltpu.roll(forget * keep, rows - 1, 0), 0.0)
        scan_rows(decay, add, hold, True)
        grad_state = hold[...]
        before = jnp.where(at_row > 0, pltpu.roll(held, 1, 0), 0.0)
        sig_in = jax.nn.sigmoid(input_pre)
        grad_forget = grad_state * (before * keep - input_pre * sig_in * valid)
        grads[:, :feat] = (
            grad_state * (1.0 - forget) * valid * (sig_in * (1.0 + input_pre * (1.0 - sig_in)))
        )
        grads[:, feat : 2 * feat] = grad_forget * (1.0 - bound) * sig_forget * (1.0 - sig_forget)
        gain_sums[1:2, :] += jnp.sum(grad_forget * (1.0 - sig_forget), axis=0, keepdims=True)
        low = grads[...].astype(bf16)
        right[here, :] = lax.dot_general(
            low, w_mix[...], (((1,), (1,)), ((), ())), preferred_element_type=f32
        ).astype(bf16)
        one_core(r).start()
        grads_t[:, here] = grads[...].T.astype(bf16)
        mixed_t[:, here] = (raw_b[...].astype(f32) * scale).T.astype(bf16)
        return carry

    lax.fori_loop(0, 4, piece, 0)

    core_in_now = core_in

    class Arrival:
        def __init__(self, copy):
            self.wait_recv = copy.wait_recv

    def one_rows(r, j):
        return right[at(r * rows + t * share + j * 16, 16, 16), :].astype(f32)

    one_arrived = [Arrival(one_core(r)) for r in (3, 2, 1, 0)]
    one_peer = over_cores(one_arrived, [[], [], [], []], one_rows, peer_in)
    for r in (3, 2, 1, 0):
        one_core(r).wait_send()

    hop_mix = first_hop(grads_t, left, dw_mix, yr_mix)

    def out_columns(i, carry):
        to = at(i * (4 * block), 4 * block, 4 * block)
        dw_out[:, to] = jnp.dot(mixed_t[...], gmix[:, to], preferred_element_type=f32).astype(bf16)
        return carry

    lax.fori_loop(0, 4, out_columns, 0)
    near_rows = at(zf * block, block, block)
    far_rows = at((1 - zf) * block, block, block)

    def out_copy(k, src, dst, device):
        return pltpu.make_async_remote_copy(
            src_ref=src,
            dst_ref=dst,
            send_sem=out_send.at[k],
            recv_sem=out_recv.at[k],
            device_id=device,
            device_id_type=MESH,
        )

    out_side = out_copy(0, dw_out, yr_out, side)
    out_far = out_copy(1, dw_out.at[far_rows], zr_out, far)
    out_core = out_copy(2, dw_out.at[near_rows], o_out, core)
    out_here = pltpu.make_async_copy(dw_out.at[near_rows], o_out, out_send.at[3])

    @pl.when(t != y)
    def _():
        out_side.start()

    far_u = second_hop(hop_u, dw_u, yr_u, zr_u)
    back_d = last_hop(hop_d, far_d, dw_d, yr_d, zr_d, o_d)

    for c in one_peer:
        c.wait_recv()
    gain_one = gains[0:1, :]

    def token_rows(j, carry):
        to = at(j * step, step, step)
        total = one_rows(0, j) + core_in[to, :].astype(f32)
        for r in (0, 1, 2):
            total = total + peer_in[at(r * share + j * step, step, step), :].astype(f32)
        value = inp[to, :]
        s = lax.rsqrt(jnp.mean(value * value, axis=1, keepdims=True) + epsilon)
        weighted = total * gain_one
        gres[to, :] = (
            gres[to, :]
            + s * weighted
            - value * (s * s * s) * jnp.mean(weighted * value, axis=1, keepdims=True)
        )
        sums[0:1, :] += jnp.sum(total * value * s, axis=0, keepdims=True)
        return carry

    lax.fori_loop(0, share // step, token_rows, 0)
    tok_rows = at(t * share, share, share)
    tok_core = link.remote(gres, o_tok.at[tok_rows], core)
    link.here(gres, o_tok.at[tok_rows], keep=True)

    vec[0] = jnp.zeros(vec.shape[1:], f32)
    for k in (0, 1):
        for i in range(16):
            vec[0, k * 16 + i : k * 16 + i + 1, :] = sums[k : k + 1, i * block : (i + 1) * block]
    for k in (2, 3):
        for i in (0, 1):
            vec[0, pl.ds(k * 16 + i * 8 + zn * 4 + t * 2 + x, 1), :] = sums[
                k : k + 1, i * block : (i + 1) * block
            ]
    partners = [group[1], group[2], side, far, core]
    turn = [link.remote(vec.at[0], vec_in.at[0], partners[0])]

    def next_turn():
        k = len(turn)
        turn[k - 1].wait_recv()
        vec[k] = vec[k - 1] + vec_in[k - 1]
        if k < len(partners):
            turn.append(link.remote(vec.at[k], vec_in.at[k], partners[k]))

    link.sent(one_peer)
    core_in_now = core_blk
    blk_peer = over_cores(blk_core, [[c] for c in blk_own], own_rows, peer_blk)
    next_turn()
    far_mix = second_hop(hop_mix, dw_mix, yr_mix, zr_mix)

    @pl.when(t == y)
    def _():
        out_side.wait_recv()
        add_columns(dw_out, pl.ds(0, width), [(yr_out, pl.ds(0, width))])
        out_far.start()

    next_turn()
    back_g = last_hop(hop_g, far_g, dw_g, yr_g, zr_g, o_g)
    next_turn()
    for c in blk_peer:
        c.wait_recv()

    def block_rows(j, carry):
        to = at(j * step, step, step)
        total = own_rows(0, j) + core_blk[to, :].astype(f32)
        for r in (0, 1, 2):
            total = total + peer_blk[at(r * share + j * step, step, step), :].astype(f32)
        gm_own[to, :] = (res[to, :] + total).astype(bf16)
        return carry

    link.sent(gm_in[:2] + gm_core[:1])
    lax.fori_loop(0, share // step, block_rows, 0)
    link.here(gm_own, o_blk, keep=True)
    next_turn()
    back_u = last_hop(hop_u, far_u, dw_u, yr_u, zr_u, o_u)
    next_turn()
    link.here(vec.at[5], o_vec, keep=True)
    back_mix = last_hop(hop_mix, far_mix, dw_mix, yr_mix, zr_mix, o_mix)

    @pl.when(t == y)
    def _():
        out_far.wait_recv()

        def some(j, carry):
            to = at(zf * block + j * 16, 16, 16)
            dw_out[to, :] = (
                dw_out[to, :].astype(f32) + zr_out[at(j * 16, 16, 16), :].astype(f32)
            ).astype(bf16)
            return carry

        lax.fori_loop(0, block // 16, some, 0)
        out_core.start()
        out_here.start()
        out_far.wait_send()
        out_core.wait_send()
        out_here.wait()

    @pl.when(t != y)
    def _():
        out_side.wait_send()
        out_core.wait_recv()

    for c in back_d + back_g + back_u + back_mix + [tok_core]:
        c.wait_recv()
    link.close()


def back(*arrays):
    par, inp = arrays[14], arrays[15]
    share, width = inp.shape
    rows, group_rows = 2 * share, 8 * share
    feat, hid, block = par.shape[1], arrays[0].shape[0], width // 16
    made = jax.ShapeDtypeStruct
    vm = pltpu.VMEM
    outs = [
        made((4, hid, block), bf16),
        made((4, hid, block), bf16),
        made((4, hid, block), bf16),
        made((4, 3 * feat, block), bf16),
        made((block, width), bf16),
        made((rows, width), f32),
        made((share, width), bf16),
        made((64, block), f32),
    ]
    scratch = (
        [vm((group_rows, width), bf16)] * 3
        + [vm((hid, width), bf16)] * 3
        + [vm((3 * feat, width), bf16)]
        + [vm((hid, width // 2), bf16)] * 3
        + [vm((3 * feat, width // 2), bf16)]
        + [vm((hid, width // 4), bf16)] * 3
        + [vm((3 * feat, width // 4), bf16)]
        + [vm((4 * share, width), bf16)] * 4
        + [vm((3 * share, width), bf16)] * 2
        + [
            vm((width, 3 * feat), bf16),
            vm((feat, width), bf16),
            vm(arrays[13].shape, f32),
            vm((rows, 3 * feat), f32),
            vm((rows, feat), f32),
            vm((rows, feat), bf16),
            vm((rows, 3 * feat), f32),
            vm((3 * feat, group_rows), bf16),
            vm((rows, feat), f32),
            vm((rows, feat), f32),
            vm((rows, feat), f32),
            vm((feat, width), bf16),
            vm((block, width), bf16),
            vm((hid, group_rows), bf16),
            vm((hid, group_rows), bf16),
            vm((share, width), f32),
            vm((share, width), bf16),
            vm((8, share), f32),
            vm((8, 8, share), f32),
            vm((4, width), f32),
            vm((6, 64, block), f32),
            vm((5, 64, block), f32),
            pltpu.SemaphoreType.DMA((96,)),
            pltpu.SemaphoreType.DMA((96,)),
            pltpu.SemaphoreType.DMA((32,)),
        ]
        + [pltpu.SemaphoreType.DMA((4,))] * 5
    )
    any_spec = pl.BlockSpec(memory_space=pl.ANY)
    vmem_spec = pl.BlockSpec(memory_space=pltpu.VMEM)
    return pl.pallas_call(
        back_kernel,
        in_specs=[any_spec] * 14 + [vmem_spec] * 7,
        out_specs=[any_spec] * len(outs),
        out_shape=outs,
        scratch_shapes=scratch,
        compiler_params=pltpu.CompilerParams(
            collective_id=2, has_side_effects=True, vmem_limit_bytes=62 << 20
        ),
        name="back",
    )(*arrays)


def body(
    n_dp,
    n_t,
    tokens_in,
    input_proj,
    forget_proj,
    outgate_proj,
    output_proj,
    glu_gate,
    glu_up,
    glu_down,
    norm_gain,
    mixer_gain,
    ffn_gain,
    bound_table,
    lengths,
    bucket,
    cotangent,
):
    depth = n_dp.bit_length() - 1
    tp_bits = (2, 0)
    fs_bits = tuple(b for b in reversed(range(depth)) if b not in tp_bits)
    t_depth = n_t.bit_length() - 1
    own_bits, free_bits = fs_bits[len(fs_bits) - t_depth :], fs_bits[: len(fs_bits) - t_depth]
    n_tp = 4
    tp_mask = (0, 1, 4, 5)
    axis_of = {b: depth - 1 - b for b in range(depth)}

    me = lax.axis_index("dp")
    t = lax.axis_index("tensor")
    bit = {b: (me >> b) & 1 for b in range(depth)}
    t_bit = {b: (t >> (t_depth - 1 - i)) & 1 for i, b in enumerate(own_bits)}
    q = bit[2] * 2 + bit[0]

    rows, width = tokens_in.shape
    share = cotangent.shape[0]
    block = width // n_dp
    free = 2 ** len(free_bits)
    feat = free * block

    def swap(values, mask):
        return lax.ppermute(values, "dp", [(i, i ^ mask) for i in range(n_dp)])

    def t_swap(values):
        return lax.ppermute(values, "tensor", [(0, 1), (1, 0)])

    def by_bit(which, own, other):
        return jnp.where(which == 0, own, other), jnp.where(which == 0, other, own)

    def in_order(parts, bits):
        parts = list(parts)
        for i, b in enumerate(reversed(bits)):
            step = 1 << i
            for r in range(len(parts)):
                if not r & step:
                    parts[r], parts[r | step] = by_bit(bit[b], parts[r], parts[r | step])
        return parts

    def t_gather(values):
        if n_t == 2:
            return jnp.stack(by_bit(t, values, t_swap(values)))
        return lax.all_gather(values, "tensor", axis=0)

    def t_scatter(values):
        if n_t == 2:
            return pick(values, t, 0).astype(f32) + t_swap(pick(values, 1 - t, 0)).astype(f32)
        return lax.psum_scatter(values, "tensor", scatter_dimension=0, tiled=False).astype(f32)

    def tp_gather(values):
        return [t_gather(values if r == 0 else swap(values, tp_mask[r])) for r in range(n_tp)]

    def tp_scatter(parts, kind):
        halves = [t_scatter(part) for part in parts]
        total = halves[0]
        for r in range(1, n_tp):
            total = total + swap(halves[r].astype(kind), tp_mask[r]).astype(f32)
        return total

    def exchange(values):
        parts = [pick(values, q, 0)]
        for r in range(1, n_tp):
            parts.append(swap(pick(values, q ^ r, 0), tp_mask[r]))
        return in_order(parts, tp_bits)

    def fs_gather(values):
        parts = [values]
        for b in fs_bits:
            parts = parts + [None] * 0 + [swap(v, 1 << b) for v in parts]
        return parts

    def weight_parts(shards):
        return fs_gather(jnp.stack(exchange(shards)))

    def weight_whole(parts):
        count = len(parts)
        flip = [0] * count
        for r in range(count):
            flip[sum(((r >> i) & 1) << (len(fs_bits) - 1 - i) for i in range(len(fs_bits)))] = parts[r]
        ordered = jnp.stack(in_order(flip, fs_bits))
        cols = ordered.shape[-1]
        ordered = ordered.reshape((2,) * depth + (block, cols))
        have = fs_bits + tp_bits
        axes = [have.index(b) for b in reversed(range(depth))]
        return ordered.transpose(axes + [depth, depth + 1]).reshape(width, cols)

    def weight_back(grad):
        cols = grad.shape[1]
        grad = grad.reshape((2,) * depth + (block, cols))
        for b in reversed(fs_bits):
            send = lax.dynamic_slice_in_dim(grad, 1 - bit[b], 1, axis_of[b]).astype(bf16)
            hold = lax.dynamic_slice_in_dim(grad, bit[b], 1, axis_of[b]).astype(f32)
            grad = hold + swap(send, 1 << b).astype(f32)
        return exchange(grad.reshape(n_tp, block, cols).astype(bf16))

    def my_columns(values):
        lead = values.shape[:-1]
        n = len(lead)
        values = values.reshape(lead + (2,) * depth + (block,))
        bits = list(reversed(range(depth)))
        for b in own_bits:
            values = pick(values, t_bit[b], n + bits.index(b))
            bits.remove(b)
        order = [n + bits.index(b) for b in tp_bits] + list(range(n)) + [n + bits.index(b) for b in free_bits]
        return values.transpose(order + [n + len(bits)]).reshape((n_tp,) + lead + (feat,))

    def my_half(values):
        return lax.dynamic_slice_in_dim(values, t * share, share, 0)

    inputs = tokens_in.astype(f32)
    scale_one = rms_scale(inputs)
    normed_mine = (inputs * scale_one * norm_gain).astype(bf16)
    inputs_half = my_half(inputs)
    scale_one_half = my_half(scale_one)
    mix_shards = jnp.concatenate(
        [my_columns(w) for w in (input_proj, forget_proj, outgate_proj)], axis=-1
    )
    hid = glu_gate.shape[1] // n_tp
    gate_shards = glu_gate.T.reshape(n_tp, hid, block)
    up_shards = glu_up.T.reshape(n_tp, hid, block)
    down_shards = glu_down.reshape(n_tp, hid, block)
    my_table = pick(my_columns(bound_table), q, 0)
    par = jnp.stack([bound_parts(my_table)[2], pick(my_columns(mixer_gain), q, 0)])
    valid_own, keep_own = layout(lengths, bucket, rows)
    grad_out_rows = (cotangent.astype(f32) * my_half(valid_own)).astype(bf16)
    if n_dp == 16 and n_t == 2:
        aux_own = jnp.concatenate([valid_own.T, keep_own.T, jnp.zeros((6, rows), f32)])
        (
            mix_full, out_full, gate_full, up_full, down_full, normed_one, grad_out_all, normed_two,
            pre, state, mix_raw, residual, mixed_out, scale_lanes, aux_rows,
        ) = front(
            mix_shards, output_proj, gate_shards, up_shards, down_shards, normed_mine, grad_out_rows,
            aux_own, par, inputs_half, ffn_gain[None, :],
        )
        scale_state = scale_lanes[:, :1]
        aux = aux_rows[:, :2].transpose(0, 2, 1).reshape(n_tp * rows, 2)
    else:
        normed_half = my_half(normed_mine)
        normed_parts = [normed_mine] + [
            t_gather(swap(normed_half, tp_mask[r])).reshape(rows, width) for r in range(1, n_tp)
        ]
        normed_one = jnp.concatenate(normed_parts)
        aux_own = jnp.concatenate([valid_own, keep_own], axis=1)
        aux = jnp.concatenate([aux_own] + [swap(aux_own, tp_mask[r]) for r in range(1, n_tp)])
        mix_full = weight_whole(weight_parts(mix_shards))
        out_piece = output_proj
        for b in own_bits:
            out_piece = jnp.where(t_bit[b] == bit[b], out_piece, swap(out_piece, 1 << b))
        out_pieces = [out_piece]
        for b in reversed(free_bits):
            out_pieces = out_pieces + [swap(v, 1 << b) for v in out_pieces]
        out_full = jnp.concatenate(in_order(out_pieces, free_bits))
        gate_full, up_full, down_full = (
            weight_whole(weight_parts(w.transpose(0, 2, 1))).T
            for w in (gate_shards, up_shards, down_shards)
        )
        grad_out_all = jnp.stack(tp_gather(grad_out_rows)).reshape(n_tp * rows, width)
        pre = matmul(normed_one, mix_full)
        state, mix_raw, square = mixer_forward(pre, aux, par, rows)
        out_parts = matmul(mix_raw, out_full).astype(bf16).reshape(n_tp, n_t, share, width)
        square_parts = square.reshape(n_tp, n_t, share)
        square_sum = tp_scatter([square_parts[r] for r in range(n_tp)], f32)
        out_sum = tp_scatter([out_parts[r] for r in range(n_tp)], bf16)
        scale_state = lax.rsqrt(square_sum / width + epsilon)[:, None]
        mixed_out = out_sum * scale_state
        residual = inputs_half + mixed_out
        normed_two_half = (residual * rms_scale(residual) * ffn_gain).astype(bf16)
        normed_two = jnp.stack(tp_gather(normed_two_half)).reshape(n_tp * rows, width)

    if n_dp == 16 and n_t == 2:
        gate_pre = cross_cols(gate_full, normed_two)
        up_pre = cross_cols(up_full, normed_two)
        grad_hidden = cross_cols(down_full, grad_out_all)
        gate_act = jax.nn.silu(gate_pre)
        hidden = (gate_act * up_pre).astype(bf16)
        grad_up = (grad_hidden * gate_act).astype(bf16)
        grad_gate = (grad_hidden * up_pre * silu_slope(gate_pre)).astype(bf16)
        two_parts = (cross_rows(grad_gate, gate_full) + cross_rows(grad_up, up_full)).astype(bf16)
        block_parts = cross_rows(hidden, down_full).astype(bf16)
        grad_g, grad_u, grad_d, grad_mix_w, grad_out_w, grad_tokens, block_out, vec = back(
            hidden, grad_gate, grad_up, normed_two, grad_out_all, two_parts, block_parts, normed_one,
            mix_full, out_full, pre, state, mix_raw, aux_rows, par, inputs_half, residual, mixed_out,
            scale_lanes, grad_out_rows, jnp.stack([norm_gain, ffn_gain]),
        )
        mix_all = t_gather(grad_mix_w).reshape((2, 2, 2, 3, 2, block, block))
        mix_all = mix_all.transpose((3, 6, 4, 1, 0, 2, 5)).reshape(3, block, width).astype(f32)
        mine = lambda k: lax.dynamic_slice_in_dim(vec, k * n_dp + me, 1, 0)
        shares, picked, lower = bound_parts(
            lax.dynamic_slice_in_dim(bound_table, me * block, block, 1)
        )
        return (
            block_out,
            grad_tokens,
            mix_all[0],
            mix_all[1],
            mix_all[2],
            grad_out_w.astype(f32),
            grad_g.reshape(n_tp * hid, block).T.astype(f32),
            grad_u.reshape(n_tp * hid, block).T.astype(f32),
            grad_d.reshape(n_tp * hid, block).astype(f32),
            mine(0)[0],
            mine(2)[0],
            mine(1)[0],
            shares * (picked - lower[None, :]) * mine(3),
        )

    scale_two = rms_scale(residual)
    gate_pre = cross_cols(normed_two, gate_full)
    up_pre = cross_cols(normed_two, up_full)
    grad_hidden = cross_cols(grad_out_all, down_full)
    gate_act = jax.nn.silu(gate_pre)
    hidden = (gate_act * up_pre).astype(bf16)
    grad_up = (grad_hidden * gate_act).astype(bf16)
    grad_gate = (grad_hidden * up_pre * silu_slope(gate_pre)).astype(bf16)
    grad_two_parts = (
        (matmul(grad_gate, gate_full) + matmul(grad_up, up_full))
        .astype(bf16)
        .reshape(n_tp, n_t, share, width)
    )
    grad_normed_two = tp_scatter([grad_two_parts[r] for r in range(n_tp)], bf16)
    block_parts = matmul(hidden, down_full).astype(bf16).reshape(n_tp, n_t, share, width)
    block_out = (residual + tp_scatter([block_parts[r] for r in range(n_tp)], bf16)).astype(bf16)
    grad_down_t = jnp.stack(weight_back(cross_rows(grad_out_all, hidden).astype(bf16)))
    grad_w_gate = jnp.stack(weight_back(cross_rows(normed_two, grad_gate).astype(bf16)))
    grad_w_up = jnp.stack(weight_back(cross_rows(normed_two, grad_up).astype(bf16)))
    grad_glu_down = grad_down_t.transpose(0, 2, 1).reshape(glu_down.shape).astype(f32)
    grad_glu_gate = grad_w_gate.transpose(1, 0, 2).reshape(glu_gate.shape).astype(f32)
    grad_glu_up = grad_w_up.transpose(1, 0, 2).reshape(glu_up.shape).astype(f32)

    grad_residual = grad_out_rows.astype(f32) + norm_back(
        residual, scale_two, ffn_gain, grad_normed_two
    )
    ffn_gain_sum = jnp.sum(grad_normed_two * residual * scale_two, axis=0)
    grad_mix_half = grad_residual.astype(bf16)
    dot_mean = jnp.sum(grad_mix_half.astype(f32) * mixed_out, axis=1, keepdims=True) / (
        scale_state * width
    )
    row_values = jnp.concatenate([scale_state, dot_mean], axis=1).T
    row_all = jnp.stack(tp_gather(row_values)).transpose(0, 1, 3, 2).reshape(n_tp * rows, 2)
    grad_mix = jnp.stack(tp_gather(grad_mix_half)).reshape(n_tp * rows, width)
    grad_mixed = cross_cols(grad_mix, out_full)
    aux_back = jnp.concatenate([aux, row_all], axis=1)
    grads, sums = mixer_backward(pre, state, grad_mixed, aux_back, par, rows)
    one_parts = cross_cols(grads, mix_full).astype(bf16).reshape(n_tp, n_t, share, width)
    grad_normed_one = tp_scatter([one_parts[r] for r in range(n_tp)], bf16)
    grad_mix_w = jnp.stack(weight_back(cross_rows(normed_one, grads).astype(bf16)))

    mixed = (mix_raw.astype(f32) * row_all[:, :1]).astype(bf16)
    grad_out_w = cross_rows(mixed, grad_mix).astype(bf16).reshape((2,) * len(free_bits) + (block, width))
    for i, b in enumerate(free_bits):
        send = lax.dynamic_slice_in_dim(grad_out_w, 1 - bit[b], 1, i)
        hold = lax.dynamic_slice_in_dim(grad_out_w, bit[b], 1, i)
        grad_out_w = (hold.astype(f32) + swap(send, 1 << b).astype(f32)).astype(bf16)
    grad_out_w = grad_out_w.reshape(block, width)
    for b in own_bits:
        grad_out_w = (grad_out_w.astype(f32) + swap(grad_out_w, 1 << b).astype(f32)).astype(bf16)
    mine_t = jnp.int32(0)
    for b in own_bits:
        mine_t = mine_t * 2 + bit[b]
    if n_t == 2:
        other = t_swap(grad_out_w)
        grad_output_proj = jnp.where(mine_t == t, grad_out_w, other).astype(f32)
    else:
        grad_output_proj = pick(lax.all_gather(grad_out_w, "tensor", axis=0), mine_t, 0).astype(f32)

    mix_all = t_gather(grad_mix_w)
    mix_all = mix_all.reshape((2,) * t_depth + (2, 2) + (block, 3) + (2,) * len(free_bits) + (block,))
    order = list(own_bits) + list(tp_bits) + ["row", "which"] + list(free_bits) + ["col"]
    axes = [order.index(k) for k in ["which", "row"] + list(reversed(range(depth))) + ["col"]]
    mix_all = mix_all.transpose(axes).reshape(3, block, width).astype(f32)

    grad_tokens_half = my_half_residual = grad_residual + norm_back(
        inputs_half, scale_one_half, norm_gain, grad_normed_one
    )
    grad_tokens = t_gather(grad_tokens_half).reshape(rows, width)
    norm_gain_sum = jnp.sum(grad_normed_one * inputs_half * scale_one_half, axis=0)

    gains = jnp.stack([norm_gain_sum, ffn_gain_sum]).reshape((2,) + (2,) * depth + (block,))
    for b in reversed(range(depth)):
        at = 1 + axis_of[b]
        send = lax.dynamic_slice_in_dim(gains, 1 - bit[b], 1, at)
        hold = lax.dynamic_slice_in_dim(gains, bit[b], 1, at)
        gains = hold + swap(send, 1 << b)
    gains = gains.reshape(2, block)
    gains = gains + t_swap(gains) if n_t == 2 else lax.psum(gains, "tensor")

    for b in fs_bits:
        sums = sums + swap(sums, 1 << b)
    sums = t_gather(sums)
    sums = pick(sums, mine_t, 0).reshape((2,) + (2,) * len(free_bits) + (block,))
    for b in free_bits:
        sums = pick(sums, bit[b], 1)
    shares, picked, lower = bound_parts(lax.dynamic_slice_in_dim(bound_table, me * block, block, 1))
    grad_table = shares * (picked - lower[None, :]) * sums[1][None, :]

    return (
        block_out,
        grad_tokens,
        mix_all[0],
        mix_all[1],
        mix_all[2],
        grad_output_proj,
        grad_glu_gate,
        grad_glu_up,
        grad_glu_down,
        gains[0],
        sums[0],
        gains[1],
        grad_table,
    )


def solution(mesh):
    return jax.shard_map(
        functools.partial(body, mesh.shape["dp"], mesh.shape["tensor"]),
        mesh=mesh,
        in_specs=(
            P("dp", None),
            P("dp", None),
            P("dp", None),
            P("dp", None),
            P("dp", None),
            P("dp", "tensor"),
            P("dp", "tensor"),
            P("tensor", "dp"),
            P(),
            P(),
            P(),
            P(),
            P("dp"),
            P("dp"),
            P(("dp", "tensor"), None),
        ),
        out_specs=(
            P(("dp", "tensor"), None),
            P("dp", None),
            P("dp", None),
            P("dp", None),
            P("dp", None),
            P("dp", None),
            P("dp", "tensor"),
            P("dp", "tensor"),
            P("tensor", "dp"),
            P("dp"),
            P("dp"),
            P("dp"),
            P(None, "dp"),
        ),
        check_vma=False,
    )
```

```python
import functools

import jax
import jax.numpy as jnp
from jax import lax
from jax.experimental import pallas as pl
from jax.experimental.pallas import tpu as pltpu
from jax.sharding import PartitionSpec as P

LAYER = 12
epsilon = 1e-06
bf16 = jnp.bfloat16
f32 = jnp.float32


def rms_scale(values):
    return lax.rsqrt(jnp.mean(values * values, axis=-1, keepdims=True) + epsilon)


def norm_back(values, row_scale, gain_row, incoming):
    weighted = incoming * gain_row
    cubed = row_scale * row_scale * row_scale
    return row_scale * weighted - values * cubed * jnp.mean(
        weighted * values, axis=-1, keepdims=True
    )


def silu_slope(values):
    logistic = jax.nn.sigmoid(values)
    return logistic * (1.0 + values * (1.0 - logistic))


def matmul(first_op, second_op):
    return jnp.dot(first_op, second_op, preferred_element_type=f32)


def cross_rows(first_op, second_op):
    return lax.dot_general(
        first_op, second_op, (((0,), (0,)), ((), ())), preferred_element_type=f32
    )


def cross_cols(first_op, second_op):
    return lax.dot_general(
        first_op, second_op, (((1,), (1,)), ((), ())), preferred_element_type=f32
    )


def pick(values, index, axis):
    return lax.dynamic_index_in_dim(values, index, axis, keepdims=False)


def layout(lengths, bucket, row_count):
    slot_len = row_count // jnp.left_shift(jnp.int32(1), bucket)
    position = jnp.arange(row_count, dtype=jnp.int32)
    slot_index = position // slot_len
    offset = position - slot_index * slot_len
    slot_ids = jnp.arange(lengths.shape[0], dtype=jnp.int32)
    chosen = (slot_index[:, None] == slot_ids[None, :]).astype(jnp.int32)
    slot_limit = jnp.sum(chosen * lengths[None, :], axis=1)
    valid_mask = (offset < slot_limit).astype(f32)[:, None]
    keep_mask = (offset > 0).astype(f32)[:, None]
    return (valid_mask, keep_mask)


def bound_parts(bound_table):
    shares = jax.nn.softmax(bound_table, axis=0)
    layer_ids = jnp.arange(bound_table.shape[0], dtype=jnp.int32)[:, None]
    picked = ((layer_ids >= 1) & (layer_ids <= LAYER)).astype(f32)
    return (shares, picked, jnp.sum(shares * picked, axis=0))


def scan_rows(decay_ref, add_ref, out_ref, reverse):
    rows, width = out_ref.shape
    tiles = rows // 8
    sub = lax.broadcasted_iota(jnp.int32, (8, width), 0)

    def step(i, carry):
        j = tiles - 1 - i if reverse else i
        at = pl.ds(pl.multiple_of(j * 8, 8), 8)
        a = decay_ref[at, :]
        b = add_ref[at, :]
        for s in (1, 2, 4):
            shift = 8 - s if reverse else s
            inside = sub < 8 - s if reverse else sub >= s
            b = jnp.where(inside, b + a * pltpu.roll(b, shift, 0), b)
            a = jnp.where(inside, a * pltpu.roll(a, shift, 0), a)
        h = b + a * carry
        out_ref[at, :] = h
        edge = h[0:1, :] if reverse else h[7:8, :]
        return jnp.broadcast_to(edge, (8, width))

    lax.fori_loop(0, tiles, step, jnp.zeros((8, width), f32), unroll=4)


def mixer_forward_kernel(pre_ref, aux_ref, par_ref, state_ref, mix_ref, sq_ref, decay_ref, add_ref):
    width = state_ref.shape[1]
    input_pre = pre_ref[:, :width]
    forget_pre = pre_ref[:, width : 2 * width]
    outgate_pre = pre_ref[:, 2 * width :]
    valid = aux_ref[:, 0:1]
    keep = aux_ref[:, 1:2]
    bound = par_ref[0:1, :]
    gain = par_ref[1:2, :]
    forget = bound + (1.0 - bound) * jax.nn.sigmoid(forget_pre)
    add_ref[...] = input_pre * jax.nn.sigmoid(input_pre) * (1.0 - forget) * valid
    decay_ref[...] = forget * keep
    scan_rows(decay_ref, add_ref, state_ref, False)
    state = state_ref[...]
    mix_ref[...] = (state * gain * (outgate_pre * jax.nn.sigmoid(outgate_pre))).astype(bf16)
    sq_ref[...] = jnp.sum(state * state, axis=1, keepdims=True)


def mixer_forward(pre, aux, par, seq_rows):
    rows, width = pre.shape[0], pre.shape[1] // 3
    row_block = lambda n: pl.BlockSpec((seq_rows, n), lambda i: (i, 0))
    return pl.pallas_call(
        mixer_forward_kernel,
        grid=(rows // seq_rows,),
        in_specs=[
            row_block(3 * width),
            row_block(aux.shape[1]),
            pl.BlockSpec(par.shape, lambda i: (0, 0)),
        ],
        out_specs=[row_block(width), row_block(width), row_block(1)],
        out_shape=[
            jax.ShapeDtypeStruct((rows, width), f32),
            jax.ShapeDtypeStruct((rows, width), bf16),
            jax.ShapeDtypeStruct((rows, 1), f32),
        ],
        scratch_shapes=[pltpu.VMEM((seq_rows, width), f32)] * 2,
        cost_estimate=pl.CostEstimate(
            flops=rows * width * 60, bytes_accessed=rows * width * 20, transcendentals=rows * width * 3
        ),
        name="mixer_forward",
    )(pre, aux, par)


def mixer_backward_kernel(
    pre_ref, state_ref, up_ref, aux_ref, par_ref, grad_ref, sums_ref, decay_ref, add_ref, out_ref
):
    rows, width = state_ref.shape
    input_pre = pre_ref[:, :width]
    forget_pre = pre_ref[:, width : 2 * width]
    outgate_pre = pre_ref[:, 2 * width :]
    valid = aux_ref[:, 0:1]
    keep = aux_ref[:, 1:2]
    scale = aux_ref[:, 2:3]
    dot_mean = aux_ref[:, 3:4]
    bound = par_ref[0:1, :]
    gain = par_ref[1:2, :]
    state = state_ref[...]
    incoming = up_ref[...]
    at_row = lax.broadcasted_iota(jnp.int32, (rows, width), 0)
    sig_out = jax.nn.sigmoid(outgate_pre)
    act_out = outgate_pre * sig_out
    scaled = incoming * (state * scale)
    grad_ref[:, 2 * width :] = (
        scaled * gain * (sig_out * (1.0 + outgate_pre * (1.0 - sig_out)))
    ).astype(bf16)
    add_ref[...] = scale * (gain * act_out * incoming) - state * (scale * scale * scale * dot_mean)
    sig_forget = jax.nn.sigmoid(forget_pre)
    forget = bound + (1.0 - bound) * sig_forget
    decay_ref[...] = jnp.where(
        at_row < rows - 1, pltpu.roll(forget * keep, rows - 1, 0), 0.0
    )
    scan_rows(decay_ref, add_ref, out_ref, True)
    grad_state = out_ref[...]
    before = jnp.where(at_row > 0, pltpu.roll(state, 1, 0), 0.0)
    sig_in = jax.nn.sigmoid(input_pre)
    grad_forget = grad_state * (before * keep - input_pre * sig_in * valid)
    grad_ref[:, :width] = (
        grad_state * (1.0 - forget) * valid * (sig_in * (1.0 + input_pre * (1.0 - sig_in)))
    ).astype(bf16)
    grad_ref[:, width : 2 * width] = (
        grad_forget * (1.0 - bound) * sig_forget * (1.0 - sig_forget)
    ).astype(bf16)

    @pl.when(pl.program_id(0) == 0)
    def _():
        sums_ref[...] = jnp.zeros_like(sums_ref)

    sums_ref[0:1, :] += jnp.sum(scaled * act_out, axis=0, keepdims=True)
    sums_ref[1:2, :] += jnp.sum(grad_forget * (1.0 - sig_forget), axis=0, keepdims=True)


def mixer_backward(pre, state, incoming, aux, par, seq_rows):
    rows, width = state.shape
    row_block = lambda n: pl.BlockSpec((seq_rows, n), lambda i: (i, 0))
    whole = lambda shape: pl.BlockSpec(shape, lambda i: (0, 0))
    return pl.pallas_call(
        mixer_backward_kernel,
        grid=(rows // seq_rows,),
        in_specs=[
            row_block(3 * width),
            row_block(width),
            row_block(width),
            row_block(aux.shape[1]),
            whole(par.shape),
        ],
        out_specs=[row_block(3 * width), whole((2, width))],
        out_shape=[
            jax.ShapeDtypeStruct((rows, 3 * width), bf16),
            jax.ShapeDtypeStruct((2, width), f32),
        ],
        scratch_shapes=[pltpu.VMEM((seq_rows, width), f32)] * 3,
        cost_estimate=pl.CostEstimate(
            flops=rows * width * 90, bytes_accessed=rows * width * 26, transcendentals=rows * width * 3
        ),
        name="mixer_backward",
    )(pre, state, incoming, aux, par)


MESH = pl.DeviceIdType.MESH


class Copies:
    def __init__(self, send, recv, local):
        self.send, self.recv, self.local = send, recv, local
        self.n_remote = self.n_local = 0
        self.open = []

    def remote(self, src, dst, device):
        k = self.n_remote
        self.n_remote += 1
        copy = pltpu.make_async_remote_copy(
            src_ref=src,
            dst_ref=dst,
            send_sem=self.send.at[k],
            recv_sem=self.recv.at[k],
            device_id=device,
            device_id_type=MESH,
        )
        copy.start()
        self.open.append(copy.wait_send)
        return copy

    def here(self, src, dst, keep=False):
        k = self.n_local
        self.n_local += 1
        copy = pltpu.make_async_copy(src, dst, self.local.at[k])
        copy.start()
        if keep:
            self.open.append(copy.wait)
        return copy

    def sent(self, copies):
        for copy in copies:
            copy.wait_send()
            self.open.remove(copy.wait_send)

    def close(self):
        assert self.n_remote <= self.send.shape[0] and self.n_local <= self.local.shape[0]
        for wait in self.open:
            wait()


def position():
    me = lax.axis_index("dp")
    t = lax.axis_index("tensor")
    zf, zn, y, x = me // 8, (me // 4) % 2, (me // 2) % 2, me % 2
    to_x, to_zn = 1 - 2 * x, 4 - 8 * zn
    group = [None, (me + to_x, t), (me + to_zn, t), (me + to_x + to_zn, t)]
    q = [zn * 2 + x, zn * 2 + 1 - x, (1 - zn) * 2 + x, (1 - zn) * 2 + 1 - x]
    far = (me + 8 - 16 * zf, t)
    side = (me + 2 - 4 * y, t)
    core = (me, 1 - t)
    return me, t, (zf, zn, y, x), q, group, far, side, core


def meet(devices):
    barrier = pltpu.get_barrier_semaphore()
    for device in devices:
        pl.semaphore_signal(barrier, inc=1, device_id=device, device_id_type=MESH)
    pl.semaphore_wait(barrier, len(devices))


def fold_lanes(values):
    width = values.shape[1]
    if width % 128:
        return values
    total = values[:, :128]
    for i in range(128, width, 128):
        total = total + values[:, i : i + 128]
    return total


def front_kernel(
    s_mix, s_out, s_g, s_u, s_d, n1_own, go_own, aux_own, par, inp, gain2,
    o_mix, o_out, o_g, o_u, o_d, o_n1, o_go, o_n2, o_pre, o_state, o_raw, o_res, o_mo, o_sc, o_aux,
    w_mix, w_out, n1, aux, pre, state, raw, part, core_in, half, peer_in,
    sq, sq_core, sq_half, sq_peer, res, mo, sc, n2, decay, add,
    send, recv, local, core_send, core_recv, sqc_send, sqc_recv, out_send, out_recv,
):
    me, t, (zf, zn, y, x), q, group, far, side, core = position()
    share, width = inp.shape
    rows = 2 * share
    block = s_out.shape[0]
    feat = par.shape[1]
    link = Copies(send, recv, local)
    meet(group[1:] + [far, side, core])

    def at(start, size, unit):
        return pl.ds(pl.multiple_of(start, unit), size)

    def pair(fz, c, fy):
        return at(fz * (8 * block) + c * (4 * block) + fy * (2 * block), 2 * block, 2 * block)

    mine = at(me * block, block, block)

    def row(r, tt):
        return at(r * rows + tt * share, share, share)

    mix_in = [link.remote(s_mix.at[q[r]], w_mix.at[mine], group[r]) for r in (1, 2, 3)]
    mix_own = link.here(s_mix.at[q[0]], w_mix.at[mine])
    out_rows = [at(z * block, block, block) for z in (zf, 1 - zf)]

    def out_copy(k, src, dst, device):
        return pltpu.make_async_remote_copy(
            src_ref=src,
            dst_ref=w_out.at[dst],
            send_sem=out_send.at[k],
            recv_sem=out_recv.at[k],
            device_id=device,
            device_id_type=MESH,
        )

    out_far = out_copy(0, s_out, out_rows[0], far)
    out_side = out_copy(1, s_out, out_rows[0], side)
    out_next = out_copy(2, w_out.at[out_rows[1]], out_rows[1], side)
    out_here = pltpu.make_async_copy(s_out, w_out.at[out_rows[0]], out_send.at[3])

    @pl.when(t == y)
    def _():
        out_far.start()
        out_side.start()
        out_here.start()

    aux_in = [link.remote(aux_own, aux.at[r], group[r]) for r in (1, 2, 3)]
    aux_mine = link.here(aux_own, aux.at[0])
    n1_in = [link.remote(n1_own.at[at(t * share, share, share)], n1.at[row(r, t)], group[r]) for r in (1, 2)]
    n1_mine = link.here(n1_own, n1.at[pl.ds(0, rows)])
    mix_own.wait()
    for c in mix_in:
        c.wait_recv()
    far_mix = [link.remote(w_mix.at[pair(zf, c, y)], w_mix.at[pair(zf, c, y)], far) for c in (0, 1)]
    side_mix = [link.remote(w_mix.at[pair(zf, c, y)], w_mix.at[pair(zf, c, y)], side) for c in (0, 1)]
    n1_in[1].wait_recv()
    n1_in.append(link.remote(n1.at[row(2, t)], n1.at[row(3, t)], group[1]))
    n1_core = [link.remote(n1.at[row(2, t)], n1.at[row(2, t)], core)]
    n1_in[0].wait_recv()
    n1_core.append(link.remote(n1.at[row(1, t)], n1.at[row(1, t)], core))
    shards = ((s_g, o_g), (s_u, o_u), (s_d, o_d))
    ffn_in, ffn_own = [], []
    for s, o in shards:
        ffn_in += [link.remote(s.at[q[r]], o.at[:, mine], group[r]) for r in (1, 2, 3)]
        ffn_own.append(link.here(s.at[q[0]], o.at[:, mine]))
    n1_in[2].wait_recv()
    n1_core.append(link.remote(n1.at[row(3, t)], n1.at[row(3, t)], core))
    for c in (0, 1):
        far_mix[c].wait_recv()
        side_mix.append(link.remote(w_mix.at[pair(1 - zf, c, y)], w_mix.at[pair(1 - zf, c, y)], side))

    @pl.when(t == y)
    def _():
        out_far.wait_recv()
        out_next.start()
        out_far.wait_send()
        out_side.wait_send()
        out_here.wait()
        out_next.wait_send()

    @pl.when(t != y)
    def _():
        out_side.wait_recv()
        out_next.wait_recv()

    far_ffn, side_ffn = [], []

    def start_ffn(i):
        o = shards[i][1]
        ffn_own[i].wait()
        for c in ffn_in[3 * i : 3 * i + 3]:
            c.wait_recv()
        far_ffn.append([link.remote(o.at[:, pair(zf, c, y)], o.at[:, pair(zf, c, y)], far) for c in (0, 1)])
        side_ffn.extend(link.remote(o.at[:, pair(zf, c, y)], o.at[:, pair(zf, c, y)], side) for c in (0, 1))

    def forward_ffn(i):
        o = shards[i][1]
        for c in (0, 1):
            far_ffn[i][c].wait_recv()
            side_ffn.append(link.remote(o.at[:, pair(1 - zf, c, y)], o.at[:, pair(1 - zf, c, y)], side))

    start_ffn(0)
    go_in = [link.remote(go_own, o_go.at[row(r, t)], group[r]) for r in (1, 2)]
    go_core = [link.remote(go_own, o_go.at[row(0, t)], core)]
    link.here(go_own, o_go.at[row(0, t)], keep=True)

    n1_mine.wait()
    aux_mine.wait()
    for c in side_mix + n1_core + aux_in:
        c.wait_recv()

    def core_copy(r):
        return pltpu.make_async_remote_copy(
            src_ref=part.at[row(r, 1 - t)],
            dst_ref=core_in.at[at(r * share, share, share)],
            send_sem=core_send.at[r],
            recv_sem=core_recv.at[r],
            device_id=core,
            device_id_type=MESH,
        )

    def sq_copy(r):
        return pltpu.make_async_remote_copy(
            src_ref=sq.at[row(r, 1 - t)],
            dst_ref=sq_core.at[at(r * share, share, share)],
            send_sem=sqc_send.at[r],
            recv_sem=sqc_recv.at[r],
            device_id=core,
            device_id_type=MESH,
        )

    bound = par[0:1, :]
    gain = par[1:2, :]

    def piece(i, carry):
        r = 3 - i
        here = at(r * rows, rows, rows)
        pre[here, :] = jnp.dot(n1[here, :], w_mix[...], preferred_element_type=f32)
        columns = aux[r].T
        valid = columns[:, 0:1]
        keep = columns[:, 1:2]
        forget = bound + (1.0 - bound) * jax.nn.sigmoid(pre[here, feat : 2 * feat])
        input_pre = pre[here, 0:feat]
        add[...] = input_pre * jax.nn.sigmoid(input_pre) * (1.0 - forget) * valid
        decay[...] = forget * keep
        scan_rows(decay, add, state.at[here, :], False)
        held = state[here, :]
        outgate_pre = pre[here, 2 * feat :]
        raw[here, :] = (held * gain * (outgate_pre * jax.nn.sigmoid(outgate_pre))).astype(bf16)
        sq[here, :] = fold_lanes(held * held)
        part[here, :] = jnp.dot(raw[here, :], w_out[...], preferred_element_type=f32).astype(bf16)
        core_copy(r).start()
        sq_copy(r).start()
        return carry

    lax.fori_loop(0, 4, piece, 0)

    link.here(w_mix, o_mix, keep=True)
    link.here(w_out, o_out, keep=True)
    link.here(n1, o_n1, keep=True)
    link.here(pre, o_pre, keep=True)
    link.here(state, o_state, keep=True)
    link.here(raw, o_raw, keep=True)
    link.here(aux, o_aux, keep=True)

    def spread(o, incoming, cores):
        incoming[1].wait_recv()
        incoming.append(link.remote(o.at[row(2, t)], o.at[row(3, t)], group[1]))
        cores.append(link.remote(o.at[row(2, t)], o.at[row(2, t)], core))
        incoming[0].wait_recv()
        cores.append(link.remote(o.at[row(1, t)], o.at[row(1, t)], core))

    def spread_last(o, incoming, cores):
        incoming[2].wait_recv()
        cores.append(link.remote(o.at[row(3, t)], o.at[row(3, t)], core))

    out_in, sq_in = [], []
    for r in (3, 2, 1):
        core_copy(r).wait()
        sq_copy(r).wait()
        to = at(r * share, share, share)
        half[to, :] = (part[row(r, t), :].astype(f32) + core_in[to, :].astype(f32)).astype(bf16)
        sq_half[to, :] = sq[row(r, t), :] + sq_core[to, :]
        out_in.append(link.remote(half.at[to], peer_in.at[to], group[r]))
        sq_in.append(link.remote(sq_half.at[to], sq_peer.at[to], group[r]))
    core_copy(0).wait()
    sq_copy(0).wait()
    start_ffn(1)
    spread(o_go, go_in, go_core)
    forward_ffn(0)
    for c in out_in + sq_in:
        c.wait_recv()
    total_sq = sq[row(0, t), :] + sq_core[0:share, :]
    for r in (1, 2, 3):
        total_sq = total_sq + sq_peer[r * share : (r + 1) * share, :]
    scale = lax.rsqrt(jnp.sum(total_sq, axis=1, keepdims=True) / width + epsilon)
    sc[...] = jnp.broadcast_to(scale, sc.shape)
    chunk = min(share, 16)

    def finish(i, carry):
        to = at(i * chunk, chunk, chunk)
        total = part[at(t * share + i * chunk, chunk, chunk), :].astype(f32) + core_in[to, :].astype(f32)
        for r in (1, 2, 3):
            total = total + peer_in[at(r * share + i * chunk, chunk, chunk), :].astype(f32)
        mixed = total * sc[to, 0:1]
        value = inp[to, :] + mixed
        mo[to, :] = mixed
        res[to, :] = value
        scale_two = lax.rsqrt(jnp.mean(value * value, axis=1, keepdims=True) + epsilon)
        n2[to, :] = (value * scale_two * gain2[...]).astype(bf16)
        return carry

    lax.fori_loop(0, share // chunk, finish, 0)
    n2_in = [link.remote(n2, o_n2.at[row(r, t)], group[r]) for r in (1, 2)]
    n2_core = [link.remote(n2, o_n2.at[row(0, t)], core)]
    link.here(n2, o_n2.at[row(0, t)], keep=True)
    link.here(res, o_res, keep=True)
    link.here(mo, o_mo, keep=True)
    link.here(sc, o_sc, keep=True)
    start_ffn(2)
    spread_last(o_go, go_in, go_core)
    forward_ffn(1)
    spread(o_n2, n2_in, n2_core)
    spread_last(o_n2, n2_in, n2_core)
    forward_ffn(2)
    for c in side_ffn + go_core + n2_core:
        c.wait_recv()
    link.close()


def front(s_mix, s_out, s_g, s_u, s_d, n1_own, go_own, aux_own, par, inp, gain2):
    share, width = inp.shape
    rows, group_rows = 2 * share, 8 * share
    feat, hid = par.shape[1], s_g.shape[1]
    block = s_out.shape[0]
    lanes = 128 if feat % 128 == 0 else feat
    any_spec = pl.BlockSpec(memory_space=pl.ANY)
    vmem_spec = pl.BlockSpec(memory_space=pltpu.VMEM)
    made = jax.ShapeDtypeStruct
    outs = [
        made((width, 3 * feat), bf16),
        made((feat, width), bf16),
        made((hid, width), bf16),
        made((hid, width), bf16),
        made((hid, width), bf16),
        made((group_rows, width), bf16),
        made((group_rows, width), bf16),
        made((group_rows, width), bf16),
        made((group_rows, 3 * feat), f32),
        made((group_rows, feat), f32),
        made((group_rows, feat), bf16),
        made((share, width), f32),
        made((share, width), f32),
        made((share, 128), f32),
        made((4,) + aux_own.shape, f32),
    ]
    scratch = [
        pltpu.VMEM((width, 3 * feat), bf16),
        pltpu.VMEM((feat, width), bf16),
        pltpu.VMEM((group_rows, width), bf16),
        pltpu.VMEM((4,) + aux_own.shape, f32),
        pltpu.VMEM((group_rows, 3 * feat), f32),
        pltpu.VMEM((group_rows, feat), f32),
        pltpu.VMEM((group_rows, feat), bf16),
        pltpu.VMEM((group_rows, width), bf16),
        pltpu.VMEM((4 * share, width), bf16),
        pltpu.VMEM((4 * share, width), bf16),
        pltpu.VMEM((4 * share, width), bf16),
        pltpu.VMEM((group_rows, lanes), f32),
        pltpu.VMEM((4 * share, lanes), f32),
        pltpu.VMEM((4 * share, lanes), f32),
        pltpu.VMEM((4 * share, lanes), f32),
        pltpu.VMEM((share, width), f32),
        pltpu.VMEM((share, width), f32),
        pltpu.VMEM((share, 128), f32),
        pltpu.VMEM((share, width), bf16),
        pltpu.VMEM((rows, feat), f32),
        pltpu.VMEM((rows, feat), f32),
        pltpu.SemaphoreType.DMA((68,)),
        pltpu.SemaphoreType.DMA((68,)),
        pltpu.SemaphoreType.DMA((24,)),
    ] + [pltpu.SemaphoreType.DMA((4,))] * 6
    return pl.pallas_call(
        front_kernel,
        in_specs=[any_spec] * 7 + [any_spec] + [vmem_spec] * 3,
        out_specs=[any_spec] * len(outs),
        out_shape=outs,
        scratch_shapes=scratch,
        compiler_params=pltpu.CompilerParams(
            collective_id=1, has_side_effects=True, vmem_limit_bytes=56 << 20
        ),
        name="front",
    )(s_mix, s_out, s_g, s_u, s_d, n1_own, go_own, aux_own, par, inp, gain2)


def back_kernel(
    h_d, h_g, h_u, n2, go, p_two, p_block, n1, w_mix_in, w_out_in, pre, state, raw, aux_in,
    par, inp, res, mo, sc, go_own, gains,
    o_g, o_u, o_d, o_mix, o_out, o_tok, o_blk, o_vec,
    left, right, gmix, dw_d, dw_g, dw_u, dw_mix, yr_d, yr_g, yr_u, yr_mix, zr_d, zr_g, zr_u, zr_mix,
    own, half, core_in, core_blk, peer_in, peer_blk, w_mix, w_out, aux, pre_b, state_b, raw_b,
    grads, grads_t, decay, add, hold, yr_out, zr_out, hid_a, hid_b,
    gres, gm_own, scalars, scal_all, sums, vec, vec_in,
    send, recv, local, core_send, core_recv, out_send, out_recv, piece_sem,
):
    me, t, (zf, zn, y, x), q, group, far, side, core = position()
    share, width = inp.shape
    rows = 2 * share
    block = width // 16
    feat = par.shape[1]
    link = Copies(send, recv, local)
    meet(group[1:] + [far, side, core])

    def at(start, size, unit):
        return pl.ds(pl.multiple_of(start, unit), size)

    def pair(fz, c, fy):
        return at(fz * (8 * block) + c * (4 * block) + fy * (2 * block), 2 * block, 2 * block)

    def row(r, tt):
        return at(r * rows + tt * share, share, share)

    def rel(r):
        return pl.ds(r * share, share)

    two_core = [link.remote(p_two.at[row(r, 1 - t)], core_in.at[rel(r)], core) for r in (3, 2, 1, 0)]
    two_own = [link.here(p_two.at[row(r, t)], own.at[rel(r)]) for r in (3, 2, 1, 0)]
    get_d = [link.here(h_d, hid_a), link.here(go, left)]
    get_g = [link.here(h_g, hid_b), link.here(n2, right)]
    get_aux = [link.here(aux_in, aux), link.here(w_out_in, w_out), link.here(w_mix_in, w_mix)]

    def over_cores(arrived, mine, source, peers):
        sent = []
        for i, r in enumerate((3, 2, 1)):
            for c in mine[i]:
                c.wait()
            arrived[i].wait_recv()

            def add_rows(j, carry):
                to = at(r * share + j * 16, 16, 16)
                half[to, :] = (source(r, j) + core_in_now[to, :].astype(f32)).astype(bf16)
                return carry

            lax.fori_loop(0, share // 16, add_rows, 0)
            sent.append(link.remote(half.at[rel(r)], peers.at[rel(r - 1)], group[r]))
        for c in mine[3]:
            c.wait()
        arrived[3].wait_recv()
        return sent

    def own_rows(r, j):
        return own[at(r * share + j * 16, 16, 16), :].astype(f32)

    core_in_now = core_in
    two_peer = over_cores(two_core, [[c] for c in two_own], own_rows, peer_in)

    def weight_grad(hid, other, dw, first, count):
        wide = 4 * block

        def columns(i, carry):
            to = at(((1 - zf) * 2 + i - (i // 2) * 4 * (1 - zf)) * wide, wide, wide)
            dw[:, to] = jnp.dot(hid[...], other[:, to], preferred_element_type=f32).astype(bf16)
            return carry

        lax.fori_loop(first, first + count, columns, 0)

    def side_send(dw, yr, slot):
        fz = 1 - zf if slot == 0 else zf
        return [
            link.remote(dw.at[:, pair(fz, c, 1 - y)], yr.at[:, pl.ds((slot * 2 + c) * 2 * block, 2 * block)], side)
            for c in (0, 1)
        ]

    def add_columns(dw, to, others):
        size = 64 if dw.shape[0] % 64 == 0 else dw.shape[0]

        def some(j, carry):
            at_rows = at(j * size, size, size)
            total = dw[at_rows, to].astype(f32)
            for ref, cols in others:
                total = total + ref[at_rows, cols].astype(f32)
            dw[at_rows, to] = total.astype(bf16)
            return carry

        lax.fori_loop(0, dw.shape[0] // size, some, 0)

    def part_of(i):
        return pl.ds(i * 2 * block, 2 * block)

    def second_hop(hop, dw, yr, zr):
        sent = []
        for c in (0, 1):
            hop[c].wait_recv()
            add_columns(dw, pair(1 - zf, c, y), [(yr, part_of(c))])
            sent.append(link.remote(dw.at[:, pair(1 - zf, c, y)], zr.at[:, part_of(c)], far))
        return sent

    def last_hop(near, sent, dw, yr, zr, out):
        for c in (0, 1):
            near[c].wait_recv()
            sent[c].wait_recv()
            add_columns(dw, pair(zf, c, y), [(yr, part_of(2 + c)), (zr, part_of(c))])

        def owner(r):
            fx = x if r in (0, 2) else 1 - x
            fzn = zn if r in (0, 1) else 1 - zn
            return at((zf * 8 + fzn * 4 + y * 2 + fx) * block, block, block)

        link.here(dw.at[:, owner(0)], out.at[q[0]], keep=True)
        return [link.remote(dw.at[:, owner(r)], out.at[q[0]], group[r]) for r in (1, 2, 3)]

    for c in get_d:
        c.wait()
    weight_grad(hid_a, left, dw_d, 0, 2)
    hop_d = side_send(dw_d, yr_d, 0)
    weight_grad(hid_a, left, dw_d, 2, 2)
    get_u = link.here(h_u, hid_a)
    get_n1 = link.here(n1, left)
    for c in get_g:
        c.wait()
    weight_grad(hid_b, right, dw_g, 0, 2)
    hop_g = side_send(dw_g, yr_g, 0)
    weight_grad(hid_b, right, dw_g, 2, 2)
    get_u.wait()
    weight_grad(hid_a, right, dw_u, 0, 4)
    far_d = second_hop(hop_d, dw_d, yr_d, zr_d)
    hop_u = side_send(dw_u, yr_u, 0)

    for c in two_peer:
        c.wait_recv()
    gain_two = gains[1:2, :]
    sums[...] = jnp.zeros_like(sums)
    step = 16

    def residual_rows(j, carry):
        to = at(j * step, step, step)
        total = own[to, :].astype(f32) + core_in[to, :].astype(f32)
        for r in (0, 1, 2):
            total = total + peer_in[at(r * share + j * step, step, step), :].astype(f32)
        value = res[to, :]
        s = lax.rsqrt(jnp.mean(value * value, axis=1, keepdims=True) + epsilon)
        weighted = total * gain_two
        grad = (
            go_own[to, :].astype(f32)
            + s * weighted
            - value * (s * s * s) * jnp.mean(weighted * value, axis=1, keepdims=True)
        )
        gres[to, :] = grad
        low = grad.astype(bf16)
        gm_own[to, :] = low
        dot = jnp.sum(low.astype(f32) * mo[to, :], axis=1, keepdims=True)
        scale = sc[to, 0:1]
        sc[to, 1:2] = dot / (scale * width)
        sums[1:2, :] += jnp.sum(total * value * s, axis=0, keepdims=True)
        return carry

    lax.fori_loop(0, share // step, residual_rows, 0)
    scalars[...] = sc[...].T[0:8, :]

    def scal(r, tt):
        return scal_all.at[r * 2 + tt]

    gm_in = [link.remote(gm_own, gmix.at[row(r, t)], group[r]) for r in (1, 2)]
    sc_in = [link.remote(scalars, scal(r, t), group[r]) for r in (1, 2, 3)]
    gm_core = [link.remote(gm_own, gmix.at[row(0, t)], core), link.remote(scalars, scal(0, t), core)]
    gm_here = [link.here(gm_own, gmix.at[row(0, t)]), link.here(scalars, scal(0, t))]
    blk_core = [link.remote(p_block.at[row(r, 1 - t)], core_blk.at[rel(r)], core) for r in (3, 2, 1, 0)]

    far_g = second_hop(hop_g, dw_g, yr_g, zr_g)
    near_d = side_send(dw_d, yr_d, 1)
    gm_in[1].wait_recv()
    gm_in.append(link.remote(gmix.at[row(2, t)], gmix.at[row(3, t)], group[1]))
    gm_core.append(link.remote(gmix.at[row(2, t)], gmix.at[row(2, t)], core))
    gm_in[0].wait_recv()
    gm_core.append(link.remote(gmix.at[row(1, t)], gmix.at[row(1, t)], core))
    for i, r in enumerate((1, 2, 3)):
        sc_in[i].wait_recv()
        gm_core.append(link.remote(scal(r, t), scal(r, t), core))
    near_g = side_send(dw_g, yr_g, 1)
    far_u = second_hop(hop_u, dw_u, yr_u, zr_u)
    gm_in[2].wait_recv()
    gm_core.append(link.remote(gmix.at[row(3, t)], gmix.at[row(3, t)], core))
    near_u = side_send(dw_u, yr_u, 1)

    link.sent(two_peer)
    blk_own = [link.here(p_block.at[row(r, t)], own.at[rel(r)]) for r in (3, 2, 1, 0)]
    for c in get_aux + [get_n1] + gm_here:
        c.wait()
    for c in gm_core:
        c.wait_recv()

    def one_core(r):
        return pltpu.make_async_remote_copy(
            src_ref=right.at[row(r, 1 - t)],
            dst_ref=core_in.at[at(r * share, share, share)],
            send_sem=core_send.at[r],
            recv_sem=core_recv.at[r],
            device_id=core,
            device_id_type=MESH,
        )

    def fetch(r):
        here = at(r * rows, rows, rows)
        return [
            pltpu.make_async_copy(pre.at[here], pre_b, piece_sem.at[0]),
            pltpu.make_async_copy(state.at[here], state_b, piece_sem.at[1]),
            pltpu.make_async_copy(raw.at[here], raw_b, piece_sem.at[2]),
        ]

    bound = par[0:1, :]
    gain = par[1:2, :]
    gain_sums = sums.at[2:4, 0:feat]
    mixed_t = hid_b.at[0:feat]
    dw_out = w_out

    def piece(i, carry):
        r = 3 - i
        here = at(r * rows, rows, rows)
        copies = fetch(r)
        for c in copies:
            c.start()
        up = lax.dot_general(
            gmix[here, :], w_out[...], (((1,), (1,)), ((), ())), preferred_element_type=f32
        )
        masks = aux[r].T
        valid = masks[:, 0:1]
        keep = masks[:, 1:2]
        scale_parts = [scal_all[r * 2 + tt].T for tt in (0, 1)]
        scale = jnp.concatenate([p[:, 0:1] for p in scale_parts], axis=0)
        dot_mean = jnp.concatenate([p[:, 1:2] for p in scale_parts], axis=0)
        for c in copies:
            c.wait()
        at_row = lax.broadcasted_iota(jnp.int32, (rows, feat), 0)
        input_pre = pre_b[:, :feat]
        outgate_pre = pre_b[:, 2 * feat :]
        held = state_b[...]
        sig_out = jax.nn.sigmoid(outgate_pre)
        act_out = outgate_pre * sig_out
        scaled = up * (held * scale)
        grads[:, 2 * feat :] = scaled * gain * (sig_out * (1.0 + outgate_pre * (1.0 - sig_out)))
        add[...] = scale * (gain * act_out * up) - held * (scale * scale * scale * dot_mean)
        gain_sums[0:1, :] += jnp.sum(scaled * act_out, axis=0, keepdims=True)
        sig_forget = jax.nn.sigmoid(pre_b[:, feat : 2 * feat])
        forget = bound + (1.0 - bound) * sig_forget
        decay[...] = jnp.where(at_row < rows - 1, pltpu.roll(forget * keep, rows - 1, 0), 0.0)
        scan_rows(decay, add, hold, True)
        grad_state = hold[...]
        before = jnp.where(at_row > 0, pltpu.roll(held, 1, 0), 0.0)
        sig_in = jax.nn.sigmoid(input_pre)
        grad_forget = grad_state * (before * keep - input_pre * sig_in * valid)
        grads[:, :feat] = (
            grad_state * (1.0 - forget) * valid * (sig_in * (1.0 + input_pre * (1.0 - sig_in)))
        )
        grads[:, feat : 2 * feat] = grad_forget * (1.0 - bound) * sig_forget * (1.0 - sig_forget)
        gain_sums[1:2, :] += jnp.sum(grad_forget * (1.0 - sig_forget), axis=0, keepdims=True)
        low = grads[...].astype(bf16)
        right[here, :] = lax.dot_general(
            low, w_mix[...], (((1,), (1,)), ((), ())), preferred_element_type=f32
        ).astype(bf16)
        one_core(r).start()
        grads_t[:, here] = grads[...].T.astype(bf16)
        mixed_t[:, here] = (raw_b[...].astype(f32) * scale).T.astype(bf16)
        return carry

    lax.fori_loop(0, 4, piece, 0)

    core_in_now = core_in

    class Arrival:
        def __init__(self, copy):
            self.wait_recv = copy.wait_recv

    def one_rows(r, j):
        return right[at(r * rows + t * share + j * 16, 16, 16), :].astype(f32)

    one_arrived = [Arrival(one_core(r)) for r in (3, 2, 1, 0)]
    one_peer = over_cores(one_arrived, [[], [], [], []], one_rows, peer_in)
    for r in (3, 2, 1, 0):
        one_core(r).wait_send()

    weight_grad(grads_t, left, dw_mix, 0, 2)
    hop_mix = side_send(dw_mix, yr_mix, 0)
    weight_grad(grads_t, left, dw_mix, 2, 2)

    def out_columns(i, carry):
        to = at(i * (4 * block), 4 * block, 4 * block)
        dw_out[:, to] = jnp.dot(mixed_t[...], gmix[:, to], preferred_element_type=f32).astype(bf16)
        return carry

    lax.fori_loop(0, 4, out_columns, 0)
    near_rows = at(zf * block, block, block)
    far_rows = at((1 - zf) * block, block, block)

    def out_copy(k, src, dst, device):
        return pltpu.make_async_remote_copy(
            src_ref=src,
            dst_ref=dst,
            send_sem=out_send.at[k],
            recv_sem=out_recv.at[k],
            device_id=device,
            device_id_type=MESH,
        )

    out_side = out_copy(0, dw_out, yr_out, side)
    out_far = out_copy(1, dw_out.at[far_rows], zr_out, far)
    out_core = out_copy(2, dw_out.at[near_rows], o_out, core)
    out_here = pltpu.make_async_copy(dw_out.at[near_rows], o_out, out_send.at[3])

    @pl.when(t != y)
    def _():
        out_side.start()

    near_mix = side_send(dw_mix, yr_mix, 1)
    back_d = last_hop(near_d, far_d, dw_d, yr_d, zr_d, o_d)
    back_g = last_hop(near_g, far_g, dw_g, yr_g, zr_g, o_g)
    far_mix = second_hop(hop_mix, dw_mix, yr_mix, zr_mix)

    @pl.when(t == y)
    def _():
        out_side.wait_recv()
        add_columns(dw_out, pl.ds(0, width), [(yr_out, pl.ds(0, width))])
        out_far.start()

    for c in one_peer:
        c.wait_recv()
    gain_one = gains[0:1, :]

    def token_rows(j, carry):
        to = at(j * step, step, step)
        total = one_rows(0, j) + core_in[to, :].astype(f32)
        for r in (0, 1, 2):
            total = total + peer_in[at(r * share + j * step, step, step), :].astype(f32)
        value = inp[to, :]
        s = lax.rsqrt(jnp.mean(value * value, axis=1, keepdims=True) + epsilon)
        weighted = total * gain_one
        gres[to, :] = (
            gres[to, :]
            + s * weighted
            - value * (s * s * s) * jnp.mean(weighted * value, axis=1, keepdims=True)
        )
        sums[0:1, :] += jnp.sum(total * value * s, axis=0, keepdims=True)
        return carry

    lax.fori_loop(0, share // step, token_rows, 0)
    tok_rows = at(t * share, share, share)
    tok_core = link.remote(gres, o_tok.at[tok_rows], core)
    link.here(gres, o_tok.at[tok_rows], keep=True)

    vec[0] = jnp.zeros(vec.shape[1:], f32)
    for k in (0, 1):
        for i in range(16):
            vec[0, k * 16 + i : k * 16 + i + 1, :] = sums[k : k + 1, i * block : (i + 1) * block]
    for k in (2, 3):
        for i in (0, 1):
            vec[0, pl.ds(k * 16 + i * 8 + zn * 4 + t * 2 + x, 1), :] = sums[
                k : k + 1, i * block : (i + 1) * block
            ]
    partners = [group[1], group[2], side, far, core]
    turn = [link.remote(vec.at[0], vec_in.at[0], partners[0])]

    def next_turn():
        k = len(turn)
        turn[k - 1].wait_recv()
        vec[k] = vec[k - 1] + vec_in[k - 1]
        if k < len(partners):
            turn.append(link.remote(vec.at[k], vec_in.at[k], partners[k]))

    link.sent(one_peer)
    core_in_now = core_blk
    blk_peer = over_cores(blk_core, [[c] for c in blk_own], own_rows, peer_blk)
    next_turn()
    back_u = last_hop(near_u, far_u, dw_u, yr_u, zr_u, o_u)
    next_turn()
    next_turn()
    for c in blk_peer:
        c.wait_recv()

    def block_rows(j, carry):
        to = at(j * step, step, step)
        total = own_rows(0, j) + core_blk[to, :].astype(f32)
        for r in (0, 1, 2):
            total = total + peer_blk[at(r * share + j * step, step, step), :].astype(f32)
        gm_own[to, :] = (res[to, :] + total).astype(bf16)
        return carry

    link.sent(gm_in[:2] + gm_core[:1])
    lax.fori_loop(0, share // step, block_rows, 0)
    link.here(gm_own, o_blk, keep=True)
    next_turn()
    next_turn()
    link.here(vec.at[5], o_vec, keep=True)
    back_mix = last_hop(near_mix, far_mix, dw_mix, yr_mix, zr_mix, o_mix)

    @pl.when(t == y)
    def _():
        out_far.wait_recv()

        def some(j, carry):
            to = at(zf * block + j * 16, 16, 16)
            dw_out[to, :] = (
                dw_out[to, :].astype(f32) + zr_out[at(j * 16, 16, 16), :].astype(f32)
            ).astype(bf16)
            return carry

        lax.fori_loop(0, block // 16, some, 0)
        out_core.start()
        out_here.start()
        out_far.wait_send()
        out_core.wait_send()
        out_here.wait()

    @pl.when(t != y)
    def _():
        out_side.wait_send()
        out_core.wait_recv()

    for c in back_d + back_g + back_u + back_mix + [tok_core]:
        c.wait_recv()
    link.close()


def back(*arrays):
    par, inp = arrays[14], arrays[15]
    share, width = inp.shape
    rows, group_rows = 2 * share, 8 * share
    feat, hid, block = par.shape[1], arrays[0].shape[0], width // 16
    made = jax.ShapeDtypeStruct
    vm = pltpu.VMEM
    outs = [
        made((4, hid, block), bf16),
        made((4, hid, block), bf16),
        made((4, hid, block), bf16),
        made((4, 3 * feat, block), bf16),
        made((block, width), bf16),
        made((rows, width), f32),
        made((share, width), bf16),
        made((64, block), f32),
    ]
    scratch = (
        [vm((group_rows, width), bf16)] * 3
        + [vm((hid, width), bf16)] * 3
        + [vm((3 * feat, width), bf16)]
        + [vm((hid, width // 2), bf16)] * 3
        + [vm((3 * feat, width // 2), bf16)]
        + [vm((hid, width // 4), bf16)] * 3
        + [vm((3 * feat, width // 4), bf16)]
        + [vm((4 * share, width), bf16)] * 4
        + [vm((3 * share, width), bf16)] * 2
        + [
            vm((width, 3 * feat), bf16),
            vm((feat, width), bf16),
            vm(arrays[13].shape, f32),
            vm((rows, 3 * feat), f32),
            vm((rows, feat), f32),
            vm((rows, feat), bf16),
            vm((rows, 3 * feat), f32),
            vm((3 * feat, group_rows), bf16),
            vm((rows, feat), f32),
            vm((rows, feat), f32),
            vm((rows, feat), f32),
            vm((feat, width), bf16),
            vm((block, width), bf16),
            vm((hid, group_rows), bf16),
            vm((hid, group_rows), bf16),
            vm((share, width), f32),
            vm((share, width), bf16),
            vm((8, share), f32),
            vm((8, 8, share), f32),
            vm((4, width), f32),
            vm((6, 64, block), f32),
            vm((5, 64, block), f32),
            pltpu.SemaphoreType.DMA((96,)),
            pltpu.SemaphoreType.DMA((96,)),
            pltpu.SemaphoreType.DMA((32,)),
        ]
        + [pltpu.SemaphoreType.DMA((4,))] * 5
    )
    any_spec = pl.BlockSpec(memory_space=pl.ANY)
    vmem_spec = pl.BlockSpec(memory_space=pltpu.VMEM)
    return pl.pallas_call(
        back_kernel,
        in_specs=[any_spec] * 14 + [vmem_spec] * 7,
        out_specs=[any_spec] * len(outs),
        out_shape=outs,
        scratch_shapes=scratch,
        compiler_params=pltpu.CompilerParams(
            collective_id=2, has_side_effects=True, vmem_limit_bytes=62 << 20
        ),
        name="back",
    )(*arrays)


def body(
    n_dp,
    n_t,
    tokens_in,
    input_proj,
    forget_proj,
    outgate_proj,
    output_proj,
    glu_gate,
    glu_up,
    glu_down,
    norm_gain,
    mixer_gain,
    ffn_gain,
    bound_table,
    lengths,
    bucket,
    cotangent,
):
    depth = n_dp.bit_length() - 1
    tp_bits = (2, 0)
    fs_bits = tuple(b for b in reversed(range(depth)) if b not in tp_bits)
    t_depth = n_t.bit_length() - 1
    own_bits, free_bits = fs_bits[len(fs_bits) - t_depth :], fs_bits[: len(fs_bits) - t_depth]
    n_tp = 4
    tp_mask = (0, 1, 4, 5)
    axis_of = {b: depth - 1 - b for b in range(depth)}

    me = lax.axis_index("dp")
    t = lax.axis_index("tensor")
    bit = {b: (me >> b) & 1 for b in range(depth)}
    t_bit = {b: (t >> (t_depth - 1 - i)) & 1 for i, b in enumerate(own_bits)}
    q = bit[2] * 2 + bit[0]

    rows, width = tokens_in.shape
    share = cotangent.shape[0]
    block = width // n_dp
    free = 2 ** len(free_bits)
    feat = free * block

    def swap(values, mask):
        return lax.ppermute(values, "dp", [(i, i ^ mask) for i in range(n_dp)])

    def t_swap(values):
        return lax.ppermute(values, "tensor", [(0, 1), (1, 0)])

    def by_bit(which, own, other):
        return jnp.where(which == 0, own, other), jnp.where(which == 0, other, own)

    def in_order(parts, bits):
        parts = list(parts)
        for i, b in enumerate(reversed(bits)):
            step = 1 << i
            for r in range(len(parts)):
                if not r & step:
                    parts[r], parts[r | step] = by_bit(bit[b], parts[r], parts[r | step])
        return parts

    def t_gather(values):
        if n_t == 2:
            return jnp.stack(by_bit(t, values, t_swap(values)))
        return lax.all_gather(values, "tensor", axis=0)

    def t_scatter(values):
        if n_t == 2:
            return pick(values, t, 0).astype(f32) + t_swap(pick(values, 1 - t, 0)).astype(f32)
        return lax.psum_scatter(values, "tensor", scatter_dimension=0, tiled=False).astype(f32)

    def tp_gather(values):
        return [t_gather(values if r == 0 else swap(values, tp_mask[r])) for r in range(n_tp)]

    def tp_scatter(parts, kind):
        halves = [t_scatter(part) for part in parts]
        total = halves[0]
        for r in range(1, n_tp):
            total = total + swap(halves[r].astype(kind), tp_mask[r]).astype(f32)
        return total

    def exchange(values):
        parts = [pick(values, q, 0)]
        for r in range(1, n_tp):
            parts.append(swap(pick(values, q ^ r, 0), tp_mask[r]))
        return in_order(parts, tp_bits)

    def fs_gather(values):
        parts = [values]
        for b in fs_bits:
            parts = parts + [None] * 0 + [swap(v, 1 << b) for v in parts]
        return parts

    def weight_parts(shards):
        return fs_gather(jnp.stack(exchange(shards)))

    def weight_whole(parts):
        count = len(parts)
        flip = [0] * count
        for r in range(count):
            flip[sum(((r >> i) & 1) << (len(fs_bits) - 1 - i) for i in range(len(fs_bits)))] = parts[r]
        ordered = jnp.stack(in_order(flip, fs_bits))
        cols = ordered.shape[-1]
        ordered = ordered.reshape((2,) * depth + (block, cols))
        have = fs_bits + tp_bits
        axes = [have.index(b) for b in reversed(range(depth))]
        return ordered.transpose(axes + [depth, depth + 1]).reshape(width, cols)

    def weight_back(grad):
        cols = grad.shape[1]
        grad = grad.reshape((2,) * depth + (block, cols))
        for b in reversed(fs_bits):
            send = lax.dynamic_slice_in_dim(grad, 1 - bit[b], 1, axis_of[b]).astype(bf16)
            hold = lax.dynamic_slice_in_dim(grad, bit[b], 1, axis_of[b]).astype(f32)
            grad = hold + swap(send, 1 << b).astype(f32)
        return exchange(grad.reshape(n_tp, block, cols).astype(bf16))

    def my_columns(values):
        lead = values.shape[:-1]
        n = len(lead)
        values = values.reshape(lead + (2,) * depth + (block,))
        bits = list(reversed(range(depth)))
        for b in own_bits:
            values = pick(values, t_bit[b], n + bits.index(b))
            bits.remove(b)
        order = [n + bits.index(b) for b in tp_bits] + list(range(n)) + [n + bits.index(b) for b in free_bits]
        return values.transpose(order + [n + len(bits)]).reshape((n_tp,) + lead + (feat,))

    def my_half(values):
        return lax.dynamic_slice_in_dim(values, t * share, share, 0)

    inputs = tokens_in.astype(f32)
    scale_one = rms_scale(inputs)
    normed_mine = (inputs * scale_one * norm_gain).astype(bf16)
    inputs_half = my_half(inputs)
    scale_one_half = my_half(scale_one)
    mix_shards = jnp.concatenate(
        [my_columns(w) for w in (input_proj, forget_proj, outgate_proj)], axis=-1
    )
    hid = glu_gate.shape[1] // n_tp
    gate_shards = glu_gate.T.reshape(n_tp, hid, block)
    up_shards = glu_up.T.reshape(n_tp, hid, block)
    down_shards = glu_down.reshape(n_tp, hid, block)
    my_table = pick(my_columns(bound_table), q, 0)
    par = jnp.stack([bound_parts(my_table)[2], pick(my_columns(mixer_gain), q, 0)])
    valid_own, keep_own = layout(lengths, bucket, rows)
    grad_out_rows = (cotangent.astype(f32) * my_half(valid_own)).astype(bf16)
    if n_dp == 16 and n_t == 2:
        aux_own = jnp.concatenate([valid_own.T, keep_own.T, jnp.zeros((6, rows), f32)])
        (
            mix_full, out_full, gate_full, up_full, down_full, normed_one, grad_out_all, normed_two,
            pre, state, mix_raw, residual, mixed_out, scale_lanes, aux_rows,
        ) = front(
            mix_shards, output_proj, gate_shards, up_shards, down_shards, normed_mine, grad_out_rows,
            aux_own, par, inputs_half, ffn_gain[None, :],
        )
        scale_state = scale_lanes[:, :1]
        aux = aux_rows[:, :2].transpose(0, 2, 1).reshape(n_tp * rows, 2)
    else:
        normed_half = my_half(normed_mine)
        normed_parts = [normed_mine] + [
            t_gather(swap(normed_half, tp_mask[r])).reshape(rows, width) for r in range(1, n_tp)
        ]
        normed_one = jnp.concatenate(normed_parts)
        aux_own = jnp.concatenate([valid_own, keep_own], axis=1)
        aux = jnp.concatenate([aux_own] + [swap(aux_own, tp_mask[r]) for r in range(1, n_tp)])
        mix_full = weight_whole(weight_parts(mix_shards))
        out_piece = output_proj
        for b in own_bits:
            out_piece = jnp.where(t_bit[b] == bit[b], out_piece, swap(out_piece, 1 << b))
        out_pieces = [out_piece]
        for b in reversed(free_bits):
            out_pieces = out_pieces + [swap(v, 1 << b) for v in out_pieces]
        out_full = jnp.concatenate(in_order(out_pieces, free_bits))
        gate_full, up_full, down_full = (
            weight_whole(weight_parts(w.transpose(0, 2, 1))).T
            for w in (gate_shards, up_shards, down_shards)
        )
        grad_out_all = jnp.stack(tp_gather(grad_out_rows)).reshape(n_tp * rows, width)
        pre = matmul(normed_one, mix_full)
        state, mix_raw, square = mixer_forward(pre, aux, par, rows)
        out_parts = matmul(mix_raw, out_full).astype(bf16).reshape(n_tp, n_t, share, width)
        square_parts = square.reshape(n_tp, n_t, share)
        square_sum = tp_scatter([square_parts[r] for r in range(n_tp)], f32)
        out_sum = tp_scatter([out_parts[r] for r in range(n_tp)], bf16)
        scale_state = lax.rsqrt(square_sum / width + epsilon)[:, None]
        mixed_out = out_sum * scale_state
        residual = inputs_half + mixed_out
        normed_two_half = (residual * rms_scale(residual) * ffn_gain).astype(bf16)
        normed_two = jnp.stack(tp_gather(normed_two_half)).reshape(n_tp * rows, width)

    if n_dp == 16 and n_t == 2:
        gate_pre = cross_cols(gate_full, normed_two)
        up_pre = cross_cols(up_full, normed_two)
        grad_hidden = cross_cols(down_full, grad_out_all)
        gate_act = jax.nn.silu(gate_pre)
        hidden = (gate_act * up_pre).astype(bf16)
        grad_up = (grad_hidden * gate_act).astype(bf16)
        grad_gate = (grad_hidden * up_pre * silu_slope(gate_pre)).astype(bf16)
        two_parts = (cross_rows(grad_gate, gate_full) + cross_rows(grad_up, up_full)).astype(bf16)
        block_parts = cross_rows(hidden, down_full).astype(bf16)
        grad_g, grad_u, grad_d, grad_mix_w, grad_out_w, grad_tokens, block_out, vec = back(
            hidden, grad_gate, grad_up, normed_two, grad_out_all, two_parts, block_parts, normed_one,
            mix_full, out_full, pre, state, mix_raw, aux_rows, par, inputs_half, residual, mixed_out,
            scale_lanes, grad_out_rows, jnp.stack([norm_gain, ffn_gain]),
        )
        mix_all = t_gather(grad_mix_w).reshape((2, 2, 2, 3, 2, block, block))
        mix_all = mix_all.transpose((3, 6, 4, 1, 0, 2, 5)).reshape(3, block, width).astype(f32)
        mine = lambda k: lax.dynamic_slice_in_dim(vec, k * n_dp + me, 1, 0)
        shares, picked, lower = bound_parts(
            lax.dynamic_slice_in_dim(bound_table, me * block, block, 1)
        )
        return (
            block_out,
            grad_tokens,
            mix_all[0],
            mix_all[1],
            mix_all[2],
            grad_out_w.astype(f32),
            grad_g.reshape(n_tp * hid, block).T.astype(f32),
            grad_u.reshape(n_tp * hid, block).T.astype(f32),
            grad_d.reshape(n_tp * hid, block).astype(f32),
            mine(0)[0],
            mine(2)[0],
            mine(1)[0],
            shares * (picked - lower[None, :]) * mine(3),
        )

    scale_two = rms_scale(residual)
    gate_pre = cross_cols(normed_two, gate_full)
    up_pre = cross_cols(normed_two, up_full)
    grad_hidden = cross_cols(grad_out_all, down_full)
    gate_act = jax.nn.silu(gate_pre)
    hidden = (gate_act * up_pre).astype(bf16)
    grad_up = (grad_hidden * gate_act).astype(bf16)
    grad_gate = (grad_hidden * up_pre * silu_slope(gate_pre)).astype(bf16)
    grad_two_parts = (
        (matmul(grad_gate, gate_full) + matmul(grad_up, up_full))
        .astype(bf16)
        .reshape(n_tp, n_t, share, width)
    )
    grad_normed_two = tp_scatter([grad_two_parts[r] for r in range(n_tp)], bf16)
    block_parts = matmul(hidden, down_full).astype(bf16).reshape(n_tp, n_t, share, width)
    block_out = (residual + tp_scatter([block_parts[r] for r in range(n_tp)], bf16)).astype(bf16)
    grad_down_t = jnp.stack(weight_back(cross_rows(grad_out_all, hidden).astype(bf16)))
    grad_w_gate = jnp.stack(weight_back(cross_rows(normed_two, grad_gate).astype(bf16)))
    grad_w_up = jnp.stack(weight_back(cross_rows(normed_two, grad_up).astype(bf16)))
    grad_glu_down = grad_down_t.transpose(0, 2, 1).reshape(glu_down.shape).astype(f32)
    grad_glu_gate = grad_w_gate.transpose(1, 0, 2).reshape(glu_gate.shape).astype(f32)
    grad_glu_up = grad_w_up.transpose(1, 0, 2).reshape(glu_up.shape).astype(f32)

    grad_residual = grad_out_rows.astype(f32) + norm_back(
        residual, scale_two, ffn_gain, grad_normed_two
    )
    ffn_gain_sum = jnp.sum(grad_normed_two * residual * scale_two, axis=0)
    grad_mix_half = grad_residual.astype(bf16)
    dot_mean = jnp.sum(grad_mix_half.astype(f32) * mixed_out, axis=1, keepdims=True) / (
        scale_state * width
    )
    row_values = jnp.concatenate([scale_state, dot_mean], axis=1).T
    row_all = jnp.stack(tp_gather(row_values)).transpose(0, 1, 3, 2).reshape(n_tp * rows, 2)
    grad_mix = jnp.stack(tp_gather(grad_mix_half)).reshape(n_tp * rows, width)
    grad_mixed = cross_cols(grad_mix, out_full)
    aux_back = jnp.concatenate([aux, row_all], axis=1)
    grads, sums = mixer_backward(pre, state, grad_mixed, aux_back, par, rows)
    one_parts = cross_cols(grads, mix_full).astype(bf16).reshape(n_tp, n_t, share, width)
    grad_normed_one = tp_scatter([one_parts[r] for r in range(n_tp)], bf16)
    grad_mix_w = jnp.stack(weight_back(cross_rows(normed_one, grads).astype(bf16)))

    mixed = (mix_raw.astype(f32) * row_all[:, :1]).astype(bf16)
    grad_out_w = cross_rows(mixed, grad_mix).astype(bf16).reshape((2,) * len(free_bits) + (block, width))
    for i, b in enumerate(free_bits):
        send = lax.dynamic_slice_in_dim(grad_out_w, 1 - bit[b], 1, i)
        hold = lax.dynamic_slice_in_dim(grad_out_w, bit[b], 1, i)
        grad_out_w = (hold.astype(f32) + swap(send, 1 << b).astype(f32)).astype(bf16)
    grad_out_w = grad_out_w.reshape(block, width)
    for b in own_bits:
        grad_out_w = (grad_out_w.astype(f32) + swap(grad_out_w, 1 << b).astype(f32)).astype(bf16)
    mine_t = jnp.int32(0)
    for b in own_bits:
        mine_t = mine_t * 2 + bit[b]
    if n_t == 2:
        other = t_swap(grad_out_w)
        grad_output_proj = jnp.where(mine_t == t, grad_out_w, other).astype(f32)
    else:
        grad_output_proj = pick(lax.all_gather(grad_out_w, "tensor", axis=0), mine_t, 0).astype(f32)

    mix_all = t_gather(grad_mix_w)
    mix_all = mix_all.reshape((2,) * t_depth + (2, 2) + (block, 3) + (2,) * len(free_bits) + (block,))
    order = list(own_bits) + list(tp_bits) + ["row", "which"] + list(free_bits) + ["col"]
    axes = [order.index(k) for k in ["which", "row"] + list(reversed(range(depth))) + ["col"]]
    mix_all = mix_all.transpose(axes).reshape(3, block, width).astype(f32)

    grad_tokens_half = my_half_residual = grad_residual + norm_back(
        inputs_half, scale_one_half, norm_gain, grad_normed_one
    )
    grad_tokens = t_gather(grad_tokens_half).reshape(rows, width)
    norm_gain_sum = jnp.sum(grad_normed_one * inputs_half * scale_one_half, axis=0)

    gains = jnp.stack([norm_gain_sum, ffn_gain_sum]).reshape((2,) + (2,) * depth + (block,))
    for b in reversed(range(depth)):
        at = 1 + axis_of[b]
        send = lax.dynamic_slice_in_dim(gains, 1 - bit[b], 1, at)
        hold = lax.dynamic_slice_in_dim(gains, bit[b], 1, at)
        gains = hold + swap(send, 1 << b)
    gains = gains.reshape(2, block)
    gains = gains + t_swap(gains) if n_t == 2 else lax.psum(gains, "tensor")

    for b in fs_bits:
        sums = sums + swap(sums, 1 << b)
    sums = t_gather(sums)
    sums = pick(sums, mine_t, 0).reshape((2,) + (2,) * len(free_bits) + (block,))
    for b in free_bits:
        sums = pick(sums, bit[b], 1)
    shares, picked, lower = bound_parts(lax.dynamic_slice_in_dim(bound_table, me * block, block, 1))
    grad_table = shares * (picked - lower[None, :]) * sums[1][None, :]

    return (
        block_out,
        grad_tokens,
        mix_all[0],
        mix_all[1],
        mix_all[2],
        grad_output_proj,
        grad_glu_gate,
        grad_glu_up,
        grad_glu_down,
        gains[0],
        sums[0],
        gains[1],
        grad_table,
    )


def solution(mesh):
    return jax.shard_map(
        functools.partial(body, mesh.shape["dp"], mesh.shape["tensor"]),
        mesh=mesh,
        in_specs=(
            P("dp", None),
            P("dp", None),
            P("dp", None),
            P("dp", None),
            P("dp", None),
            P("dp", "tensor"),
            P("dp", "tensor"),
            P("tensor", "dp"),
            P(),
            P(),
            P(),
            P(),
            P("dp"),
            P("dp"),
            P(("dp", "tensor"), None),
        ),
        out_specs=(
            P(("dp", "tensor"), None),
            P("dp", None),
            P("dp", None),
            P("dp", None),
            P("dp", None),
            P("dp", None),
            P("dp", "tensor"),
            P("dp", "tensor"),
            P("tensor", "dp"),
            P("dp"),
            P("dp"),
            P("dp"),
            P(None, "dp"),
        ),
        check_vma=False,
    )
```

```python
import functools

import jax
import jax.numpy as jnp
from jax import lax
from jax.experimental import pallas as pl
from jax.experimental.pallas import tpu as pltpu
from jax.sharding import PartitionSpec as P

LAYER = 12
epsilon = 1e-06
bf16 = jnp.bfloat16
f32 = jnp.float32


def rms_scale(values):
    return lax.rsqrt(jnp.mean(values * values, axis=-1, keepdims=True) + epsilon)


def norm_back(values, row_scale, gain_row, incoming):
    weighted = incoming * gain_row
    cubed = row_scale * row_scale * row_scale
    return row_scale * weighted - values * cubed * jnp.mean(
        weighted * values, axis=-1, keepdims=True
    )


def silu_slope(values):
    logistic = jax.nn.sigmoid(values)
    return logistic * (1.0 + values * (1.0 - logistic))


def matmul(first_op, second_op):
    return jnp.dot(first_op, second_op, preferred_element_type=f32)


def cross_rows(first_op, second_op):
    return lax.dot_general(
        first_op, second_op, (((0,), (0,)), ((), ())), preferred_element_type=f32
    )


def cross_cols(first_op, second_op):
    return lax.dot_general(
        first_op, second_op, (((1,), (1,)), ((), ())), preferred_element_type=f32
    )


def pick(values, index, axis):
    return lax.dynamic_index_in_dim(values, index, axis, keepdims=False)


def layout(lengths, bucket, row_count):
    slot_len = row_count // jnp.left_shift(jnp.int32(1), bucket)
    position = jnp.arange(row_count, dtype=jnp.int32)
    slot_index = position // slot_len
    offset = position - slot_index * slot_len
    slot_ids = jnp.arange(lengths.shape[0], dtype=jnp.int32)
    chosen = (slot_index[:, None] == slot_ids[None, :]).astype(jnp.int32)
    slot_limit = jnp.sum(chosen * lengths[None, :], axis=1)
    valid_mask = (offset < slot_limit).astype(f32)[:, None]
    keep_mask = (offset > 0).astype(f32)[:, None]
    return (valid_mask, keep_mask)


def bound_parts(bound_table):
    shares = jax.nn.softmax(bound_table, axis=0)
    layer_ids = jnp.arange(bound_table.shape[0], dtype=jnp.int32)[:, None]
    picked = ((layer_ids >= 1) & (layer_ids <= LAYER)).astype(f32)
    return (shares, picked, jnp.sum(shares * picked, axis=0))


def scan_rows(decay_ref, add_ref, out_ref, reverse):
    rows, width = out_ref.shape
    tiles = rows // 8
    sub = lax.broadcasted_iota(jnp.int32, (8, width), 0)

    def step(i, carry):
        j = tiles - 1 - i if reverse else i
        at = pl.ds(pl.multiple_of(j * 8, 8), 8)
        a = decay_ref[at, :]
        b = add_ref[at, :]
        for s in (1, 2, 4):
            shift = 8 - s if reverse else s
            inside = sub < 8 - s if reverse else sub >= s
            b = jnp.where(inside, b + a * pltpu.roll(b, shift, 0), b)
            a = jnp.where(inside, a * pltpu.roll(a, shift, 0), a)
        h = b + a * carry
        out_ref[at, :] = h
        edge = h[0:1, :] if reverse else h[7:8, :]
        return jnp.broadcast_to(edge, (8, width))

    lax.fori_loop(0, tiles, step, jnp.zeros((8, width), f32), unroll=4)


def mixer_forward_kernel(pre_ref, aux_ref, par_ref, state_ref, mix_ref, sq_ref, decay_ref, add_ref):
    width = state_ref.shape[1]
    input_pre = pre_ref[:, :width]
    forget_pre = pre_ref[:, width : 2 * width]
    outgate_pre = pre_ref[:, 2 * width :]
    valid = aux_ref[:, 0:1]
    keep = aux_ref[:, 1:2]
    bound = par_ref[0:1, :]
    gain = par_ref[1:2, :]
    forget = bound + (1.0 - bound) * jax.nn.sigmoid(forget_pre)
    add_ref[...] = input_pre * jax.nn.sigmoid(input_pre) * (1.0 - forget) * valid
    decay_ref[...] = forget * keep
    scan_rows(decay_ref, add_ref, state_ref, False)
    state = state_ref[...]
    mix_ref[...] = (state * gain * (outgate_pre * jax.nn.sigmoid(outgate_pre))).astype(bf16)
    sq_ref[...] = jnp.sum(state * state, axis=1, keepdims=True)


def mixer_forward(pre, aux, par, seq_rows):
    rows, width = pre.shape[0], pre.shape[1] // 3
    row_block = lambda n: pl.BlockSpec((seq_rows, n), lambda i: (i, 0))
    return pl.pallas_call(
        mixer_forward_kernel,
        grid=(rows // seq_rows,),
        in_specs=[
            row_block(3 * width),
            row_block(aux.shape[1]),
            pl.BlockSpec(par.shape, lambda i: (0, 0)),
        ],
        out_specs=[row_block(width), row_block(width), row_block(1)],
        out_shape=[
            jax.ShapeDtypeStruct((rows, width), f32),
            jax.ShapeDtypeStruct((rows, width), bf16),
            jax.ShapeDtypeStruct((rows, 1), f32),
        ],
        scratch_shapes=[pltpu.VMEM((seq_rows, width), f32)] * 2,
        cost_estimate=pl.CostEstimate(
            flops=rows * width * 60, bytes_accessed=rows * width * 20, transcendentals=rows * width * 3
        ),
        name="mixer_forward",
    )(pre, aux, par)


def mixer_backward_kernel(
    pre_ref, state_ref, up_ref, aux_ref, par_ref, grad_ref, sums_ref, decay_ref, add_ref, out_ref
):
    rows, width = state_ref.shape
    input_pre = pre_ref[:, :width]
    forget_pre = pre_ref[:, width : 2 * width]
    outgate_pre = pre_ref[:, 2 * width :]
    valid = aux_ref[:, 0:1]
    keep = aux_ref[:, 1:2]
    scale = aux_ref[:, 2:3]
    dot_mean = aux_ref[:, 3:4]
    bound = par_ref[0:1, :]
    gain = par_ref[1:2, :]
    state = state_ref[...]
    incoming = up_ref[...]
    at_row = lax.broadcasted_iota(jnp.int32, (rows, width), 0)
    sig_out = jax.nn.sigmoid(outgate_pre)
    act_out = outgate_pre * sig_out
    scaled = incoming * (state * scale)
    grad_ref[:, 2 * width :] = (
        scaled * gain * (sig_out * (1.0 + outgate_pre * (1.0 - sig_out)))
    ).astype(bf16)
    add_ref[...] = scale * (gain * act_out * incoming) - state * (scale * scale * scale * dot_mean)
    sig_forget = jax.nn.sigmoid(forget_pre)
    forget = bound + (1.0 - bound) * sig_forget
    decay_ref[...] = jnp.where(
        at_row < rows - 1, pltpu.roll(forget * keep, rows - 1, 0), 0.0
    )
    scan_rows(decay_ref, add_ref, out_ref, True)
    grad_state = out_ref[...]
    before = jnp.where(at_row > 0, pltpu.roll(state, 1, 0), 0.0)
    sig_in = jax.nn.sigmoid(input_pre)
    grad_forget = grad_state * (before * keep - input_pre * sig_in * valid)
    grad_ref[:, :width] = (
        grad_state * (1.0 - forget) * valid * (sig_in * (1.0 + input_pre * (1.0 - sig_in)))
    ).astype(bf16)
    grad_ref[:, width : 2 * width] = (
        grad_forget * (1.0 - bound) * sig_forget * (1.0 - sig_forget)
    ).astype(bf16)

    @pl.when(pl.program_id(0) == 0)
    def _():
        sums_ref[...] = jnp.zeros_like(sums_ref)

    sums_ref[0:1, :] += jnp.sum(scaled * act_out, axis=0, keepdims=True)
    sums_ref[1:2, :] += jnp.sum(grad_forget * (1.0 - sig_forget), axis=0, keepdims=True)


def mixer_backward(pre, state, incoming, aux, par, seq_rows):
    rows, width = state.shape
    row_block = lambda n: pl.BlockSpec((seq_rows, n), lambda i: (i, 0))
    whole = lambda shape: pl.BlockSpec(shape, lambda i: (0, 0))
    return pl.pallas_call(
        mixer_backward_kernel,
        grid=(rows // seq_rows,),
        in_specs=[
            row_block(3 * width),
            row_block(width),
            row_block(width),
            row_block(aux.shape[1]),
            whole(par.shape),
        ],
        out_specs=[row_block(3 * width), whole((2, width))],
        out_shape=[
            jax.ShapeDtypeStruct((rows, 3 * width), bf16),
            jax.ShapeDtypeStruct((2, width), f32),
        ],
        scratch_shapes=[pltpu.VMEM((seq_rows, width), f32)] * 3,
        cost_estimate=pl.CostEstimate(
            flops=rows * width * 90, bytes_accessed=rows * width * 26, transcendentals=rows * width * 3
        ),
        name="mixer_backward",
    )(pre, state, incoming, aux, par)


MESH = pl.DeviceIdType.MESH


class Copies:
    def __init__(self, send, recv, local):
        self.send, self.recv, self.local = send, recv, local
        self.n_remote = self.n_local = 0
        self.open = []

    def remote(self, src, dst, device):
        k = self.n_remote
        self.n_remote += 1
        copy = pltpu.make_async_remote_copy(
            src_ref=src,
            dst_ref=dst,
            send_sem=self.send.at[k],
            recv_sem=self.recv.at[k],
            device_id=device,
            device_id_type=MESH,
        )
        copy.start()
        self.open.append(copy.wait_send)
        return copy

    def here(self, src, dst, keep=False):
        k = self.n_local
        self.n_local += 1
        copy = pltpu.make_async_copy(src, dst, self.local.at[k])
        copy.start()
        if keep:
            self.open.append(copy.wait)
        return copy

    def sent(self, copies):
        for copy in copies:
            copy.wait_send()
            self.open.remove(copy.wait_send)

    def close(self):
        assert self.n_remote <= self.send.shape[0] and self.n_local <= self.local.shape[0]
        for wait in self.open:
            wait()


def position():
    me = lax.axis_index("dp")
    t = lax.axis_index("tensor")
    zf, zn, y, x = me // 8, (me // 4) % 2, (me // 2) % 2, me % 2
    to_x, to_zn = 1 - 2 * x, 4 - 8 * zn
    group = [None, (me + to_x, t), (me + to_zn, t), (me + to_x + to_zn, t)]
    q = [zn * 2 + x, zn * 2 + 1 - x, (1 - zn) * 2 + x, (1 - zn) * 2 + 1 - x]
    far = (me + 8 - 16 * zf, t)
    side = (me + 2 - 4 * y, t)
    core = (me, 1 - t)
    return me, t, (zf, zn, y, x), q, group, far, side, core


def meet(devices):
    barrier = pltpu.get_barrier_semaphore()
    for device in devices:
        pl.semaphore_signal(barrier, inc=1, device_id=device, device_id_type=MESH)
    pl.semaphore_wait(barrier, len(devices))


def fold_lanes(values):
    width = values.shape[1]
    if width % 128:
        return values
    total = values[:, :128]
    for i in range(128, width, 128):
        total = total + values[:, i : i + 128]
    return total


def front_kernel(
    s_in, s_fg, s_og, s_out, w_g, w_u, s_d, cot, tok, gains, table, sizes,
    o_mix, o_out, o_g, o_u, o_d, o_n1, o_go, o_n2, o_pre, o_state, o_raw, o_res, o_mo, o_sc, o_aux, o_par,
    w_mix, w_out, n1, aux, pre, state, raw, part, core_in, half, peer_in, par, wide_g, wide_u, s_g, s_u, go_own, bound_row,
    sq, sq_core, sq_half, sq_peer, res, mo, sc, n2, decay, add,
    send, recv, local, core_send, core_recv, sqc_send, sqc_recv, out_send, out_recv,
):
    me, t, (zf, zn, y, x), q, group, far, side, core = position()
    rows, width = tok.shape
    share = rows // 2
    block = s_out.shape[0]
    feat = par.shape[1]
    hid = s_d.shape[0] // 4
    link = Copies(send, recv, local)
    get_g, get_u, get_cot = link.here(w_g, wide_g), link.here(w_u, wide_u), link.here(cot, go_own)
    meet(group[1:] + [far, side, core])

    def at(start, size, unit):
        return pl.ds(pl.multiple_of(start, unit), size)

    def pair(fz, c, fy):
        return at(fz * (8 * block) + c * (4 * block) + fy * (2 * block), 2 * block, 2 * block)

    mine = at(me * block, block, block)

    def row(r, tt):
        return at(r * rows + tt * share, share, share)

    def columns(r, fz):
        fx = x if r in (0, 2) else 1 - x
        fzn = zn if r in (0, 1) else 1 - zn
        return at((fz * 8 + fzn * 4 + t * 2 + fx) * block, block, block)

    mix_in, mix_own = [], []
    for k, s in enumerate((s_in, s_fg, s_og)):
        for fz in (0, 1):
            to = w_mix.at[mine, pl.ds(k * feat + fz * block, block)]
            mix_in += [link.remote(s.at[:, columns(r, fz)], to, group[r]) for r in (1, 2, 3)]
            mix_own.append(link.here(s.at[:, columns(0, fz)], to))
    out_rows = [at(z * block, block, block) for z in (zf, 1 - zf)]

    def out_copy(k, src, dst, device):
        return pltpu.make_async_remote_copy(
            src_ref=src,
            dst_ref=w_out.at[dst],
            send_sem=out_send.at[k],
            recv_sem=out_recv.at[k],
            device_id=device,
            device_id_type=MESH,
        )

    out_far = out_copy(0, s_out, out_rows[0], far)
    out_side = out_copy(1, s_out, out_rows[0], side)
    out_next = out_copy(2, w_out.at[out_rows[1]], out_rows[1], side)
    out_here = pltpu.make_async_copy(s_out, w_out.at[out_rows[0]], out_send.at[3])

    @pl.when(t == y)
    def _():
        out_far.start()
        out_side.start()
        out_here.start()

    norm_row = gains[0:1, :]

    def norm_rows(first):
        def some(j, carry):
            to = at(first + j * 16, 16, 16)
            value = tok[to, :].astype(f32)
            s = lax.rsqrt(jnp.mean(value * value, axis=1, keepdims=True) + epsilon)
            n1[to, :] = (value * s * norm_row).astype(bf16)
            return carry

        lax.fori_loop(0, share // 16, some, 0)

    norm_rows(t * share)
    n1_in = [link.remote(n1.at[row(0, t)], n1.at[row(r, t)], group[r]) for r in (1, 2)]

    count = sizes.shape[0] - 1
    slot_len = lax.shift_right_logical(jnp.int32(rows), sizes[count])
    position_row = lax.broadcasted_iota(jnp.int32, (1, rows), 1)
    slot = jnp.zeros((1, rows), jnp.int32)
    for j in range(1, count):
        slot = slot + (position_row >= j * slot_len).astype(jnp.int32)
    limit = jnp.zeros((1, rows), jnp.int32)
    for j in range(count):
        limit = limit + jnp.where(slot == j, sizes[j], 0)
    offset = position_row - slot * slot_len
    aux[0] = jnp.zeros(aux.shape[1:], f32)
    aux[0, 0:1, :] = (offset < limit).astype(f32)
    aux[0, 1:2, :] = (offset > 0).astype(f32)
    aux_in = [link.remote(aux.at[0], aux.at[r], group[r]) for r in (1, 2, 3)]

    norm_rows((1 - t) * share)
    for c in mix_own:
        c.wait()
    for c in mix_in:
        c.wait_recv()
    far_mix = [link.remote(w_mix.at[pair(zf, c, y)], w_mix.at[pair(zf, c, y)], far) for c in (0, 1)]
    side_mix = [link.remote(w_mix.at[pair(zf, c, y)], w_mix.at[pair(zf, c, y)], side) for c in (0, 1)]
    n1_in[1].wait_recv()
    n1_in.append(link.remote(n1.at[row(2, t)], n1.at[row(3, t)], group[1]))
    n1_core = [link.remote(n1.at[row(2, t)], n1.at[row(2, t)], core)]
    n1_in[0].wait_recv()
    n1_core.append(link.remote(n1.at[row(1, t)], n1.at[row(1, t)], core))
    shards = ((s_g, o_g), (s_u, o_u), (s_d, o_d))
    ffn_in, ffn_own = [], []

    def turn_round(wide, tall):
        size = min(128, wide.shape[1])

        def some(j, carry):
            to = at(j * size, size, size)
            tall[to, :] = wide[:, to].astype(f32).T.astype(bf16)
            return carry

        lax.fori_loop(0, wide.shape[1] // size, some, 0)

    def leave(s, o):
        units = [at(q[r] * hid, hid, 16) for r in range(4)]
        ffn_in.extend(link.remote(s.at[units[r]], o.at[:, mine], group[r]) for r in (1, 2, 3))
        ffn_own.append(link.here(s.at[units[0]], o.at[:, mine]))

    get_g.wait()
    turn_round(wide_g, s_g)
    leave(s_g, o_g)
    get_u.wait()
    turn_round(wide_u, s_u)
    leave(s_u, o_u)
    leave(s_d, o_d)

    logits = table[...]
    powers = jnp.exp(logits - jnp.max(logits, axis=0, keepdims=True))
    layer_ids = lax.broadcasted_iota(jnp.int32, logits.shape, 0)
    picked = jnp.where((layer_ids >= 1) & (layer_ids <= LAYER), powers, 0.0)
    bound_row[0:1, :] = jnp.sum(picked, axis=0, keepdims=True) / jnp.sum(powers, axis=0, keepdims=True)
    for fz in (0, 1):
        par[0:1, fz * block : (fz + 1) * block] = bound_row[0:1, columns(0, fz)]
        par[1:2, fz * block : (fz + 1) * block] = gains[1:2, columns(0, fz)]
    get_cot.wait()
    valid_rows = aux[0].T[:, 0:1]
    first_half = lax.broadcasted_iota(jnp.int32, (share, 1), 0) * 0 + t
    valid_half = jnp.where(first_half == 0, valid_rows[:share], valid_rows[share:])
    go_own[...] = (go_own[...].astype(f32) * valid_half).astype(bf16)
    n1_in[2].wait_recv()
    n1_core.append(link.remote(n1.at[row(3, t)], n1.at[row(3, t)], core))
    for c in (0, 1):
        far_mix[c].wait_recv()
        side_mix.append(link.remote(w_mix.at[pair(1 - zf, c, y)], w_mix.at[pair(1 - zf, c, y)], side))

    @pl.when(t == y)
    def _():
        out_far.wait_recv()
        out_next.start()
        out_far.wait_send()
        out_side.wait_send()
        out_here.wait()
        out_next.wait_send()

    @pl.when(t != y)
    def _():
        out_side.wait_recv()
        out_next.wait_recv()

    far_ffn, side_ffn = [], []

    def start_ffn(i):
        o = shards[i][1]
        ffn_own[i].wait()
        for c in ffn_in[3 * i : 3 * i + 3]:
            c.wait_recv()
        far_ffn.append([link.remote(o.at[:, pair(zf, c, y)], o.at[:, pair(zf, c, y)], far) for c in (0, 1)])
        side_ffn.extend(link.remote(o.at[:, pair(zf, c, y)], o.at[:, pair(zf, c, y)], side) for c in (0, 1))

    def forward_ffn(i):
        o = shards[i][1]
        for c in (0, 1):
            far_ffn[i][c].wait_recv()
            side_ffn.append(link.remote(o.at[:, pair(1 - zf, c, y)], o.at[:, pair(1 - zf, c, y)], side))

    start_ffn(0)
    go_in = [link.remote(go_own, o_go.at[row(r, t)], group[r]) for r in (1, 2)]
    go_core = [link.remote(go_own, o_go.at[row(0, t)], core)]
    link.here(go_own, o_go.at[row(0, t)], keep=True)

    for c in side_mix + n1_core + aux_in:
        c.wait_recv()

    def core_copy(r):
        return pltpu.make_async_remote_copy(
            src_ref=part.at[row(r, 1 - t)],
            dst_ref=core_in.at[at(r * share, share, share)],
            send_sem=core_send.at[r],
            recv_sem=core_recv.at[r],
            device_id=core,
            device_id_type=MESH,
        )

    def sq_copy(r):
        return pltpu.make_async_remote_copy(
            src_ref=sq.at[row(r, 1 - t)],
            dst_ref=sq_core.at[at(r * share, share, share)],
            send_sem=sqc_send.at[r],
            recv_sem=sqc_recv.at[r],
            device_id=core,
            device_id_type=MESH,
        )

    bound = par[0:1, :]
    gain = par[1:2, :]

    def piece(i, carry):
        r = 3 - i
        here = at(r * rows, rows, rows)
        pre[here, :] = jnp.dot(n1[here, :], w_mix[...], preferred_element_type=f32)
        columns = aux[r].T
        valid = columns[:, 0:1]
        keep = columns[:, 1:2]
        forget = bound + (1.0 - bound) * jax.nn.sigmoid(pre[here, feat : 2 * feat])
        input_pre = pre[here, 0:feat]
        add[...] = input_pre * jax.nn.sigmoid(input_pre) * (1.0 - forget) * valid
        decay[...] = forget * keep
        scan_rows(decay, add, state.at[here, :], False)
        held = state[here, :]
        outgate_pre = pre[here, 2 * feat :]
        raw[here, :] = (held * gain * (outgate_pre * jax.nn.sigmoid(outgate_pre))).astype(bf16)
        sq[here, :] = fold_lanes(held * held)
        part[here, :] = jnp.dot(raw[here, :], w_out[...], preferred_element_type=f32).astype(bf16)
        core_copy(r).start()
        sq_copy(r).start()
        return carry

    lax.fori_loop(0, 4, piece, 0)

    link.here(w_mix, o_mix, keep=True)
    link.here(w_out, o_out, keep=True)
    link.here(n1, o_n1, keep=True)
    link.here(pre, o_pre, keep=True)
    link.here(state, o_state, keep=True)
    link.here(raw, o_raw, keep=True)
    link.here(aux, o_aux, keep=True)
    link.here(par, o_par, keep=True)

    def spread(o, incoming, cores):
        incoming[1].wait_recv()
        incoming.append(link.remote(o.at[row(2, t)], o.at[row(3, t)], group[1]))
        cores.append(link.remote(o.at[row(2, t)], o.at[row(2, t)], core))
        incoming[0].wait_recv()
        cores.append(link.remote(o.at[row(1, t)], o.at[row(1, t)], core))

    def spread_last(o, incoming, cores):
        incoming[2].wait_recv()
        cores.append(link.remote(o.at[row(3, t)], o.at[row(3, t)], core))

    out_in, sq_in = [], []
    for r in (3, 2, 1):
        core_copy(r).wait()
        sq_copy(r).wait()
        to = at(r * share, share, share)
        half[to, :] = (part[row(r, t), :].astype(f32) + core_in[to, :].astype(f32)).astype(bf16)
        sq_half[to, :] = sq[row(r, t), :] + sq_core[to, :]
        out_in.append(link.remote(half.at[to], peer_in.at[to], group[r]))
        sq_in.append(link.remote(sq_half.at[to], sq_peer.at[to], group[r]))
    core_copy(0).wait()
    sq_copy(0).wait()
    start_ffn(1)
    spread(o_go, go_in, go_core)
    forward_ffn(0)
    for c in out_in + sq_in:
        c.wait_recv()
    total_sq = sq[row(0, t), :] + sq_core[0:share, :]
    for r in (1, 2, 3):
        total_sq = total_sq + sq_peer[r * share : (r + 1) * share, :]
    scale = lax.rsqrt(jnp.sum(total_sq, axis=1, keepdims=True) / width + epsilon)
    sc[...] = jnp.broadcast_to(scale, sc.shape)
    chunk = min(share, 16)

    def finish(i, carry):
        to = at(i * chunk, chunk, chunk)
        total = part[at(t * share + i * chunk, chunk, chunk), :].astype(f32) + core_in[to, :].astype(f32)
        for r in (1, 2, 3):
            total = total + peer_in[at(r * share + i * chunk, chunk, chunk), :].astype(f32)
        mixed = total * sc[to, 0:1]
        value = tok[at(t * share + i * chunk, chunk, chunk), :].astype(f32) + mixed
        mo[to, :] = mixed
        res[to, :] = value
        scale_two = lax.rsqrt(jnp.mean(value * value, axis=1, keepdims=True) + epsilon)
        n2[to, :] = (value * scale_two * gains[2:3, :]).astype(bf16)
        return carry

    lax.fori_loop(0, share // chunk, finish, 0)
    n2_in = [link.remote(n2, o_n2.at[row(r, t)], group[r]) for r in (1, 2)]
    n2_core = [link.remote(n2, o_n2.at[row(0, t)], core)]
    link.here(n2, o_n2.at[row(0, t)], keep=True)
    link.here(res, o_res, keep=True)
    link.here(mo, o_mo, keep=True)
    link.here(sc, o_sc, keep=True)
    start_ffn(2)
    spread_last(o_go, go_in, go_core)
    forward_ffn(1)
    spread(o_n2, n2_in, n2_core)
    spread_last(o_n2, n2_in, n2_core)
    forward_ffn(2)
    for c in side_ffn + go_core + n2_core:
        c.wait_recv()
    link.close()


def front(s_in, s_fg, s_og, s_out, w_g, w_u, s_d, cot, tok, gains, table, sizes):
    rows, width = tok.shape
    share, group_rows = rows // 2, 4 * rows
    block = s_out.shape[0]
    feat, hid = 2 * block, s_d.shape[0] // 4
    lanes = 128 if feat % 128 == 0 else feat
    any_spec = pl.BlockSpec(memory_space=pl.ANY)
    vmem_spec = pl.BlockSpec(memory_space=pltpu.VMEM)
    made = jax.ShapeDtypeStruct
    outs = [
        made((width, 3 * feat), bf16),
        made((feat, width), bf16),
        made((hid, width), bf16),
        made((hid, width), bf16),
        made((hid, width), bf16),
        made((group_rows, width), bf16),
        made((group_rows, width), bf16),
        made((group_rows, width), bf16),
        made((group_rows, 3 * feat), f32),
        made((group_rows, feat), f32),
        made((group_rows, feat), bf16),
        made((share, width), f32),
        made((share, width), f32),
        made((share, 128), f32),
        made((4, 8, rows), f32),
        made((2, feat), f32),
    ]
    scratch = [
        pltpu.VMEM((width, 3 * feat), bf16),
        pltpu.VMEM((feat, width), bf16),
        pltpu.VMEM((group_rows, width), bf16),
        pltpu.VMEM((4, 8, rows), f32),
        pltpu.VMEM((group_rows, 3 * feat), f32),
        pltpu.VMEM((group_rows, feat), f32),
        pltpu.VMEM((group_rows, feat), bf16),
        pltpu.VMEM((group_rows, width), bf16),
        pltpu.VMEM((4 * share, width), bf16),
        pltpu.VMEM((4 * share, width), bf16),
        pltpu.VMEM((4 * share, width), bf16),
        pltpu.VMEM((2, feat), f32),
        pltpu.VMEM(w_g.shape, bf16),
        pltpu.VMEM(w_u.shape, bf16),
        pltpu.VMEM((4 * hid, block), bf16),
        pltpu.VMEM((4 * hid, block), bf16),
        pltpu.VMEM((share, width), bf16),
        pltpu.VMEM((8, width), f32),
        pltpu.VMEM((group_rows, lanes), f32),
        pltpu.VMEM((4 * share, lanes), f32),
        pltpu.VMEM((4 * share, lanes), f32),
        pltpu.VMEM((4 * share, lanes), f32),
        pltpu.VMEM((share, width), f32),
        pltpu.VMEM((share, width), f32),
        pltpu.VMEM((share, 128), f32),
        pltpu.VMEM((share, width), bf16),
        pltpu.VMEM((rows, feat), f32),
        pltpu.VMEM((rows, feat), f32),
        pltpu.SemaphoreType.DMA((88,)),
        pltpu.SemaphoreType.DMA((88,)),
        pltpu.SemaphoreType.DMA((32,)),
    ] + [pltpu.SemaphoreType.DMA((4,))] * 6
    return pl.pallas_call(
        front_kernel,
        in_specs=[any_spec] * 8 + [vmem_spec] * 3 + [pl.BlockSpec(memory_space=pltpu.SMEM)],
        out_specs=[any_spec] * len(outs),
        out_shape=outs,
        scratch_shapes=scratch,
        compiler_params=pltpu.CompilerParams(
            collective_id=1, has_side_effects=True, vmem_limit_bytes=56 << 20
        ),
        name="front",
    )(s_in, s_fg, s_og, s_out, w_g, w_u, s_d, cot, tok, gains, table, sizes)


def back_kernel(
    h_d, h_g, h_u, n2, go, p_two, p_block, n1, w_mix_in, w_out_in, pre, state, raw, aux_in,
    par, tok, res, mo, sc, gains,
    o_g, o_u, o_d, o_mix, o_out, o_tok, o_blk, o_vec,
    left, right, gmix, dw_d, dw_g, dw_u, dw_mix, yr_d, yr_g, yr_u, yr_mix, zr_d, zr_g, zr_u, zr_mix,
    own, half, core_in, core_blk, peer_in, peer_blk, w_mix, w_out, aux, pre_b, state_b, raw_b,
    grads, grads_t, decay, add, hold, yr_out, zr_out, hid_a, hid_b,
    gres, gm_own, go_own, scalars, scal_all, sums, vec, vec_in,
    send, recv, local, core_send, core_recv, out_send, out_recv, piece_sem,
):
    me, t, (zf, zn, y, x), q, group, far, side, core = position()
    rows, width = tok.shape
    share = rows // 2
    block = width // 16
    feat = par.shape[1]
    link = Copies(send, recv, local)
    meet(group[1:] + [far, side, core])

    def at(start, size, unit):
        return pl.ds(pl.multiple_of(start, unit), size)

    def pair(fz, c, fy):
        return at(fz * (8 * block) + c * (4 * block) + fy * (2 * block), 2 * block, 2 * block)

    def row(r, tt):
        return at(r * rows + tt * share, share, share)

    def rel(r):
        return pl.ds(r * share, share)

    two_core = [link.remote(p_two.at[row(r, 1 - t)], core_in.at[rel(r)], core) for r in (3, 2, 1, 0)]
    two_own = [link.here(p_two.at[row(r, t)], own.at[rel(r)]) for r in (3, 2, 1, 0)]
    get_d = [link.here(h_d, hid_a), link.here(go, left)]
    get_g = [link.here(h_g, hid_b), link.here(n2, right)]
    get_go = link.here(go.at[row(0, t)], go_own)
    get_aux = [link.here(aux_in, aux), link.here(w_out_in, w_out), link.here(w_mix_in, w_mix)]

    def over_cores(arrived, mine, source, peers):
        sent = []
        for i, r in enumerate((3, 2, 1)):
            for c in mine[i]:
                c.wait()
            arrived[i].wait_recv()

            def add_rows(j, carry):
                to = at(r * share + j * 16, 16, 16)
                half[to, :] = (source(r, j) + core_in_now[to, :].astype(f32)).astype(bf16)
                return carry

            lax.fori_loop(0, share // 16, add_rows, 0)
            sent.append(link.remote(half.at[rel(r)], peers.at[rel(r - 1)], group[r]))
        for c in mine[3]:
            c.wait()
        arrived[3].wait_recv()
        return sent

    def own_rows(r, j):
        return own[at(r * share + j * 16, 16, 16), :].astype(f32)

    core_in_now = core_in
    two_peer = over_cores(two_core, [[c] for c in two_own], own_rows, peer_in)

    def weight_grad(hid, other, dw, first, count):
        wide = 4 * block

        def columns(i, carry):
            to = at(((1 - zf) * 2 + i - (i // 2) * 4 * (1 - zf)) * wide, wide, wide)
            made = jnp.dot(hid[...], other[:, to], preferred_element_type=f32).astype(bf16)
            if len(dw.shape) == 2:
                dw[:, to] = made
            else:
                dw[:, :, :, to] = made.reshape(dw.shape[:3] + (wide,))
            return carry

        lax.fori_loop(first, first + count, columns, 0)

    def cut(ref, cols):
        return ref.at[:, cols] if len(ref.shape) == 2 else ref.at[:, :, :, cols]

    def side_send(dw, yr, slot):
        fz = 1 - zf if slot == 0 else zf
        return [
            link.remote(cut(dw, pair(fz, c, 1 - y)), cut(yr, pl.ds((slot * 2 + c) * 2 * block, 2 * block)), side)
            for c in (0, 1)
        ]

    def add_columns(dw, to, others):
        if len(dw.shape) == 2:
            size = 64 if dw.shape[0] % 64 == 0 else dw.shape[0]
            steps = dw.shape[0] // size
        else:
            steps = dw.shape[0] * dw.shape[1]

        def some(j, carry):
            if len(dw.shape) == 2:
                lead = (at(j * size, size, size),)
            else:
                lead = (j // dw.shape[1], j % dw.shape[1], slice(None))
            total = dw[lead + (to,)].astype(f32)
            for ref, cols in others:
                total = total + ref[lead + (cols,)].astype(f32)
            dw[lead + (to,)] = total.astype(bf16)
            return carry

        lax.fori_loop(0, steps, some, 0)

    def part_of(i):
        return pl.ds(i * 2 * block, 2 * block)

    def second_hop(hop, dw, yr, zr):
        sent = []
        for c in (0, 1):
            hop[c].wait_recv()
            add_columns(dw, pair(1 - zf, c, y), [(yr, part_of(c))])
            sent.append(link.remote(cut(dw, pair(1 - zf, c, y)), cut(zr, part_of(c)), far))
        return sent

    def last_hop(near, sent, dw, yr, zr, out):
        for c in (0, 1):
            near[c].wait_recv()
            sent[c].wait_recv()
            add_columns(dw, pair(zf, c, y), [(yr, part_of(2 + c)), (zr, part_of(c))])

        def owner(r):
            fx = x if r in (0, 2) else 1 - x
            fzn = zn if r in (0, 1) else 1 - zn
            return at((zf * 8 + fzn * 4 + y * 2 + fx) * block, block, block)

        if len(dw.shape) == 2:
            place = out.at[q[0]]
            link.here(dw.at[:, owner(0)], place, keep=True)
            return [link.remote(dw.at[:, owner(r)], place, group[r]) for r in (1, 2, 3)]
        place = out.at[:, :, zn, t, x]
        kept = link.here(cut(dw, owner(0)), place)
        sent = [link.remote(cut(dw, owner(r)), place, group[r]) for r in (1, 2, 3)]
        kept.wait()
        return sent

    for c in get_d:
        c.wait()
    weight_grad(hid_a, left, dw_d, 0, 2)
    hop_d = side_send(dw_d, yr_d, 0)
    weight_grad(hid_a, left, dw_d, 2, 2)
    get_u = link.here(h_u, hid_a)
    get_n1 = link.here(n1, left)
    for c in get_g:
        c.wait()
    weight_grad(hid_b, right, dw_g, 0, 2)
    hop_g = side_send(dw_g, yr_g, 0)
    weight_grad(hid_b, right, dw_g, 2, 2)
    get_u.wait()
    weight_grad(hid_a, right, dw_u, 0, 4)
    far_d = second_hop(hop_d, dw_d, yr_d, zr_d)
    hop_u = side_send(dw_u, yr_u, 0)

    for c in two_peer:
        c.wait_recv()
    get_go.wait()
    gain_two = gains[2:3, :]
    sums[...] = jnp.zeros_like(sums)
    step = 16

    def residual_rows(j, carry):
        to = at(j * step, step, step)
        total = own[to, :].astype(f32) + core_in[to, :].astype(f32)
        for r in (0, 1, 2):
            total = total + peer_in[at(r * share + j * step, step, step), :].astype(f32)
        value = res[to, :]
        s = lax.rsqrt(jnp.mean(value * value, axis=1, keepdims=True) + epsilon)
        weighted = total * gain_two
        grad = (
            go_own[to, :].astype(f32)
            + s * weighted
            - value * (s * s * s) * jnp.mean(weighted * value, axis=1, keepdims=True)
        )
        gres[to, :] = grad
        low = grad.astype(bf16)
        gm_own[to, :] = low
        dot = jnp.sum(low.astype(f32) * mo[to, :], axis=1, keepdims=True)
        scale = sc[to, 0:1]
        sc[to, 1:2] = dot / (scale * width)
        sums[1:2, :] += jnp.sum(total * value * s, axis=0, keepdims=True)
        return carry

    lax.fori_loop(0, share // step, residual_rows, 0)
    scalars[...] = sc[...].T[0:8, :]

    def scal(r, tt):
        return scal_all.at[r * 2 + tt]

    gm_in = [link.remote(gm_own, gmix.at[row(r, t)], group[r]) for r in (1, 2)]
    sc_in = [link.remote(scalars, scal(r, t), group[r]) for r in (1, 2, 3)]
    gm_core = [link.remote(gm_own, gmix.at[row(0, t)], core), link.remote(scalars, scal(0, t), core)]
    gm_here = [link.here(gm_own, gmix.at[row(0, t)]), link.here(scalars, scal(0, t))]
    blk_core = [link.remote(p_block.at[row(r, 1 - t)], core_blk.at[rel(r)], core) for r in (3, 2, 1, 0)]

    far_g = second_hop(hop_g, dw_g, yr_g, zr_g)
    near_d = side_send(dw_d, yr_d, 1)
    gm_in[1].wait_recv()
    gm_in.append(link.remote(gmix.at[row(2, t)], gmix.at[row(3, t)], group[1]))
    gm_core.append(link.remote(gmix.at[row(2, t)], gmix.at[row(2, t)], core))
    gm_in[0].wait_recv()
    gm_core.append(link.remote(gmix.at[row(1, t)], gmix.at[row(1, t)], core))
    for i, r in enumerate((1, 2, 3)):
        sc_in[i].wait_recv()
        gm_core.append(link.remote(scal(r, t), scal(r, t), core))
    near_g = side_send(dw_g, yr_g, 1)
    far_u = second_hop(hop_u, dw_u, yr_u, zr_u)
    gm_in[2].wait_recv()
    gm_core.append(link.remote(gmix.at[row(3, t)], gmix.at[row(3, t)], core))
    near_u = side_send(dw_u, yr_u, 1)

    link.sent(two_peer)
    blk_own = [link.here(p_block.at[row(r, t)], own.at[rel(r)]) for r in (3, 2, 1, 0)]
    for c in get_aux + [get_n1] + gm_here:
        c.wait()
    for c in gm_core:
        c.wait_recv()

    def one_core(r):
        return pltpu.make_async_remote_copy(
            src_ref=right.at[row(r, 1 - t)],
            dst_ref=core_in.at[at(r * share, share, share)],
            send_sem=core_send.at[r],
            recv_sem=core_recv.at[r],
            device_id=core,
            device_id_type=MESH,
        )

    def fetch(r):
        here = at(r * rows, rows, rows)
        return [
            pltpu.make_async_copy(pre.at[here], pre_b, piece_sem.at[0]),
            pltpu.make_async_copy(state.at[here], state_b, piece_sem.at[1]),
            pltpu.make_async_copy(raw.at[here], raw_b, piece_sem.at[2]),
        ]

    bound = par[0:1, :]
    gain = par[1:2, :]
    gain_sums = sums.at[2:4, 0:feat]
    mixed_t = hid_b.at[0:feat]
    dw_out = w_out

    def piece(i, carry):
        r = 3 - i
        here = at(r * rows, rows, rows)
        copies = fetch(r)
        for c in copies:
            c.start()
        up = lax.dot_general(
            gmix[here, :], w_out[...], (((1,), (1,)), ((), ())), preferred_element_type=f32
        )
        masks = aux[r].T
        valid = masks[:, 0:1]
        keep = masks[:, 1:2]
        scale_parts = [scal_all[r * 2 + tt].T for tt in (0, 1)]
        scale = jnp.concatenate([p[:, 0:1] for p in scale_parts], axis=0)
        dot_mean = jnp.concatenate([p[:, 1:2] for p in scale_parts], axis=0)
        for c in copies:
            c.wait()
        at_row = lax.broadcasted_iota(jnp.int32, (rows, feat), 0)
        input_pre = pre_b[:, :feat]
        outgate_pre = pre_b[:, 2 * feat :]
        held = state_b[...]
        sig_out = jax.nn.sigmoid(outgate_pre)
        act_out = outgate_pre * sig_out
        scaled = up * (held * scale)
        grads[:, 2 * feat :] = scaled * gain * (sig_out * (1.0 + outgate_pre * (1.0 - sig_out)))
        add[...] = scale * (gain * act_out * up) - held * (scale * scale * scale * dot_mean)
        gain_sums[0:1, :] += jnp.sum(scaled * act_out, axis=0, keepdims=True)
        sig_forget = jax.nn.sigmoid(pre_b[:, feat : 2 * feat])
        forget = bound + (1.0 - bound) * sig_forget
        decay[...] = jnp.where(at_row < rows - 1, pltpu.roll(forget * keep, rows - 1, 0), 0.0)
        scan_rows(decay, add, hold, True)
        grad_state = hold[...]
        before = jnp.where(at_row > 0, pltpu.roll(held, 1, 0), 0.0)
        sig_in = jax.nn.sigmoid(input_pre)
        grad_forget = grad_state * (before * keep - input_pre * sig_in * valid)
        grads[:, :feat] = (
            grad_state * (1.0 - forget) * valid * (sig_in * (1.0 + input_pre * (1.0 - sig_in)))
        )
        grads[:, feat : 2 * feat] = grad_forget * (1.0 - bound) * sig_forget * (1.0 - sig_forget)
        gain_sums[1:2, :] += jnp.sum(grad_forget * (1.0 - sig_forget), axis=0, keepdims=True)
        low = grads[...].astype(bf16)
        right[here, :] = lax.dot_general(
            low, w_mix[...], (((1,), (1,)), ((), ())), preferred_element_type=f32
        ).astype(bf16)
        one_core(r).start()
        grads_t[:, here] = grads[...].T.astype(bf16)
        mixed_t[:, here] = (raw_b[...].astype(f32) * scale).T.astype(bf16)
        return carry

    lax.fori_loop(0, 4, piece, 0)

    core_in_now = core_in

    class Arrival:
        def __init__(self, copy):
            self.wait_recv = copy.wait_recv

    def one_rows(r, j):
        return right[at(r * rows + t * share + j * 16, 16, 16), :].astype(f32)

    one_arrived = [Arrival(one_core(r)) for r in (3, 2, 1, 0)]
    one_peer = over_cores(one_arrived, [[], [], [], []], one_rows, peer_in)
    for r in (3, 2, 1, 0):
        one_core(r).wait_send()

    weight_grad(grads_t, left, dw_mix, 0, 2)
    hop_mix = side_send(dw_mix, yr_mix, 0)
    weight_grad(grads_t, left, dw_mix, 2, 2)

    def out_columns(i, carry):
        to = at(i * (4 * block), 4 * block, 4 * block)
        dw_out[:, to] = jnp.dot(mixed_t[...], gmix[:, to], preferred_element_type=f32).astype(bf16)
        return carry

    lax.fori_loop(0, 4, out_columns, 0)
    near_rows = at(zf * block, block, block)
    far_rows = at((1 - zf) * block, block, block)

    def out_copy(k, src, dst, device):
        return pltpu.make_async_remote_copy(
            src_ref=src,
            dst_ref=dst,
            send_sem=out_send.at[k],
            recv_sem=out_recv.at[k],
            device_id=device,
            device_id_type=MESH,
        )

    out_side = out_copy(0, dw_out, yr_out, side)
    out_far = out_copy(1, dw_out.at[far_rows], zr_out, far)
    out_core = out_copy(2, dw_out.at[near_rows], o_out, core)
    out_here = pltpu.make_async_copy(dw_out.at[near_rows], o_out, out_send.at[3])

    @pl.when(t != y)
    def _():
        out_side.start()

    near_mix = side_send(dw_mix, yr_mix, 1)
    back_d = last_hop(near_d, far_d, dw_d, yr_d, zr_d, o_d)
    back_g = last_hop(near_g, far_g, dw_g, yr_g, zr_g, o_g)
    far_mix = second_hop(hop_mix, dw_mix, yr_mix, zr_mix)

    @pl.when(t == y)
    def _():
        out_side.wait_recv()
        add_columns(dw_out, pl.ds(0, width), [(yr_out, pl.ds(0, width))])
        out_far.start()

    for c in one_peer:
        c.wait_recv()
    gain_one = gains[0:1, :]

    def token_rows(j, carry):
        to = at(j * step, step, step)
        total = one_rows(0, j) + core_in[to, :].astype(f32)
        for r in (0, 1, 2):
            total = total + peer_in[at(r * share + j * step, step, step), :].astype(f32)
        value = tok[at(t * share + j * step, step, step), :].astype(f32)
        s = lax.rsqrt(jnp.mean(value * value, axis=1, keepdims=True) + epsilon)
        weighted = total * gain_one
        gres[to, :] = (
            gres[to, :]
            + s * weighted
            - value * (s * s * s) * jnp.mean(weighted * value, axis=1, keepdims=True)
        )
        sums[0:1, :] += jnp.sum(total * value * s, axis=0, keepdims=True)
        return carry

    lax.fori_loop(0, share // step, token_rows, 0)
    tok_rows = at(t * share, share, share)
    tok_core = link.remote(gres, o_tok.at[tok_rows], core)
    link.here(gres, o_tok.at[tok_rows], keep=True)

    vec[0] = jnp.zeros(vec.shape[1:], f32)
    for k in (0, 1):
        for i in range(16):
            vec[0, k * 16 + i : k * 16 + i + 1, :] = sums[k : k + 1, i * block : (i + 1) * block]
    for k in (2, 3):
        for i in (0, 1):
            vec[0, pl.ds(k * 16 + i * 8 + zn * 4 + t * 2 + x, 1), :] = sums[
                k : k + 1, i * block : (i + 1) * block
            ]
    partners = [group[1], group[2], side, far, core]
    turn = [link.remote(vec.at[0], vec_in.at[0], partners[0])]

    def next_turn():
        k = len(turn)
        turn[k - 1].wait_recv()
        vec[k] = vec[k - 1] + vec_in[k - 1]
        if k < len(partners):
            turn.append(link.remote(vec.at[k], vec_in.at[k], partners[k]))

    link.sent(one_peer)
    core_in_now = core_blk
    blk_peer = over_cores(blk_core, [[c] for c in blk_own], own_rows, peer_blk)
    next_turn()
    back_u = last_hop(near_u, far_u, dw_u, yr_u, zr_u, o_u)
    next_turn()
    next_turn()
    for c in blk_peer:
        c.wait_recv()

    def block_rows(j, carry):
        to = at(j * step, step, step)
        total = own_rows(0, j) + core_blk[to, :].astype(f32)
        for r in (0, 1, 2):
            total = total + peer_blk[at(r * share + j * step, step, step), :].astype(f32)
        gm_own[to, :] = (res[to, :] + total).astype(bf16)
        return carry

    link.sent(gm_in[:2] + gm_core[:1])
    lax.fori_loop(0, share // step, block_rows, 0)
    link.here(gm_own, o_blk, keep=True)
    next_turn()
    next_turn()
    link.here(vec.at[5], o_vec, keep=True)
    back_mix = last_hop(near_mix, far_mix, dw_mix, yr_mix, zr_mix, o_mix)

    @pl.when(t == y)
    def _():
        out_far.wait_recv()

        def some(j, carry):
            to = at(zf * block + j * 16, 16, 16)
            dw_out[to, :] = (
                dw_out[to, :].astype(f32) + zr_out[at(j * 16, 16, 16), :].astype(f32)
            ).astype(bf16)
            return carry

        lax.fori_loop(0, block // 16, some, 0)
        out_core.start()
        out_here.start()
        out_far.wait_send()
        out_core.wait_send()
        out_here.wait()

    @pl.when(t != y)
    def _():
        out_side.wait_send()
        out_core.wait_recv()

    for c in back_mix:
        c.wait_recv()
    mix_core = link.remote(o_mix.at[:, :, :, t], o_mix.at[:, :, :, t], core)
    for c in back_d + back_g + back_u + [mix_core, tok_core]:
        c.wait_recv()
    link.close()


def back(*arrays):
    par, tok = arrays[14], arrays[15]
    rows, width = tok.shape
    share, group_rows = rows // 2, 4 * rows
    feat, hid, block = par.shape[1], arrays[0].shape[0], width // 16
    made = jax.ShapeDtypeStruct
    vm = pltpu.VMEM
    outs = [
        made((4, hid, block), bf16),
        made((4, hid, block), bf16),
        made((4, hid, block), bf16),
        made((3, 2, 2, 2, 2, block, block), bf16),
        made((block, width), bf16),
        made((rows, width), f32),
        made((share, width), bf16),
        made((64, block), f32),
    ]
    scratch = (
        [vm((group_rows, width), bf16)] * 3
        + [vm((hid, width), bf16)] * 3
        + [vm((3, 2, block, width), bf16)]
        + [vm((hid, width // 2), bf16)] * 3
        + [vm((3, 2, block, width // 2), bf16)]
        + [vm((hid, width // 4), bf16)] * 3
        + [vm((3, 2, block, width // 4), bf16)]
        + [vm((4 * share, width), bf16)] * 4
        + [vm((3 * share, width), bf16)] * 2
        + [
            vm((width, 3 * feat), bf16),
            vm((feat, width), bf16),
            vm(arrays[13].shape, f32),
            vm((rows, 3 * feat), f32),
            vm((rows, feat), f32),
            vm((rows, feat), bf16),
            vm((rows, 3 * feat), f32),
            vm((3 * feat, group_rows), bf16),
            vm((rows, feat), f32),
            vm((rows, feat), f32),
            vm((rows, feat), f32),
            vm((feat, width), bf16),
            vm((block, width), bf16),
            vm((hid, group_rows), bf16),
            vm((hid, group_rows), bf16),
            vm((share, width), f32),
            vm((share, width), bf16),
            vm((share, width), bf16),
            vm((8, share), f32),
            vm((8, 8, share), f32),
            vm((4, width), f32),
            vm((6, 64, block), f32),
            vm((5, 64, block), f32),
            pltpu.SemaphoreType.DMA((96,)),
            pltpu.SemaphoreType.DMA((96,)),
            pltpu.SemaphoreType.DMA((32,)),
        ]
        + [pltpu.SemaphoreType.DMA((4,))] * 5
    )
    any_spec = pl.BlockSpec(memory_space=pl.ANY)
    vmem_spec = pl.BlockSpec(memory_space=pltpu.VMEM)
    return pl.pallas_call(
        back_kernel,
        in_specs=[any_spec] * 14 + [vmem_spec] * 6,
        out_specs=[any_spec] * len(outs),
        out_shape=outs,
        scratch_shapes=scratch,
        compiler_params=pltpu.CompilerParams(
            collective_id=2, has_side_effects=True, vmem_limit_bytes=62 << 20
        ),
        name="back",
    )(*arrays)


def body(
    n_dp,
    n_t,
    tokens_in,
    input_proj,
    forget_proj,
    outgate_proj,
    output_proj,
    glu_gate,
    glu_up,
    glu_down,
    norm_gain,
    mixer_gain,
    ffn_gain,
    bound_table,
    lengths,
    bucket,
    cotangent,
):
    depth = n_dp.bit_length() - 1
    tp_bits = (2, 0)
    fs_bits = tuple(b for b in reversed(range(depth)) if b not in tp_bits)
    t_depth = n_t.bit_length() - 1
    own_bits, free_bits = fs_bits[len(fs_bits) - t_depth :], fs_bits[: len(fs_bits) - t_depth]
    n_tp = 4
    tp_mask = (0, 1, 4, 5)
    axis_of = {b: depth - 1 - b for b in range(depth)}

    me = lax.axis_index("dp")
    t = lax.axis_index("tensor")
    bit = {b: (me >> b) & 1 for b in range(depth)}
    t_bit = {b: (t >> (t_depth - 1 - i)) & 1 for i, b in enumerate(own_bits)}
    q = bit[2] * 2 + bit[0]

    rows, width = tokens_in.shape
    share = cotangent.shape[0]
    block = width // n_dp
    free = 2 ** len(free_bits)
    feat = free * block

    def swap(values, mask):
        return lax.ppermute(values, "dp", [(i, i ^ mask) for i in range(n_dp)])

    def t_swap(values):
        return lax.ppermute(values, "tensor", [(0, 1), (1, 0)])

    def by_bit(which, own, other):
        return jnp.where(which == 0, own, other), jnp.where(which == 0, other, own)

    def in_order(parts, bits):
        parts = list(parts)
        for i, b in enumerate(reversed(bits)):
            step = 1 << i
            for r in range(len(parts)):
                if not r & step:
                    parts[r], parts[r | step] = by_bit(bit[b], parts[r], parts[r | step])
        return parts

    def t_gather(values):
        if n_t == 2:
            return jnp.stack(by_bit(t, values, t_swap(values)))
        return lax.all_gather(values, "tensor", axis=0)

    def t_scatter(values):
        if n_t == 2:
            return pick(values, t, 0).astype(f32) + t_swap(pick(values, 1 - t, 0)).astype(f32)
        return lax.psum_scatter(values, "tensor", scatter_dimension=0, tiled=False).astype(f32)

    def tp_gather(values):
        return [t_gather(values if r == 0 else swap(values, tp_mask[r])) for r in range(n_tp)]

    def tp_scatter(parts, kind):
        halves = [t_scatter(part) for part in parts]
        total = halves[0]
        for r in range(1, n_tp):
            total = total + swap(halves[r].astype(kind), tp_mask[r]).astype(f32)
        return total

    def exchange(values):
        parts = [pick(values, q, 0)]
        for r in range(1, n_tp):
            parts.append(swap(pick(values, q ^ r, 0), tp_mask[r]))
        return in_order(parts, tp_bits)

    def fs_gather(values):
        parts = [values]
        for b in fs_bits:
            parts = parts + [None] * 0 + [swap(v, 1 << b) for v in parts]
        return parts

    def weight_parts(shards):
        return fs_gather(jnp.stack(exchange(shards)))

    def weight_whole(parts):
        count = len(parts)
        flip = [0] * count
        for r in range(count):
            flip[sum(((r >> i) & 1) << (len(fs_bits) - 1 - i) for i in range(len(fs_bits)))] = parts[r]
        ordered = jnp.stack(in_order(flip, fs_bits))
        cols = ordered.shape[-1]
        ordered = ordered.reshape((2,) * depth + (block, cols))
        have = fs_bits + tp_bits
        axes = [have.index(b) for b in reversed(range(depth))]
        return ordered.transpose(axes + [depth, depth + 1]).reshape(width, cols)

    def weight_back(grad):
        cols = grad.shape[1]
        grad = grad.reshape((2,) * depth + (block, cols))
        for b in reversed(fs_bits):
            send = lax.dynamic_slice_in_dim(grad, 1 - bit[b], 1, axis_of[b]).astype(bf16)
            hold = lax.dynamic_slice_in_dim(grad, bit[b], 1, axis_of[b]).astype(f32)
            grad = hold + swap(send, 1 << b).astype(f32)
        return exchange(grad.reshape(n_tp, block, cols).astype(bf16))

    def my_columns(values):
        lead = values.shape[:-1]
        n = len(lead)
        values = values.reshape(lead + (2,) * depth + (block,))
        bits = list(reversed(range(depth)))
        for b in own_bits:
            values = pick(values, t_bit[b], n + bits.index(b))
            bits.remove(b)
        order = [n + bits.index(b) for b in tp_bits] + list(range(n)) + [n + bits.index(b) for b in free_bits]
        return values.transpose(order + [n + len(bits)]).reshape((n_tp,) + lead + (feat,))

    def my_half(values):
        return lax.dynamic_slice_in_dim(values, t * share, share, 0)

    hid = glu_gate.shape[1] // n_tp
    if n_dp == 16 and n_t == 2:
        gains = jnp.stack([norm_gain, mixer_gain, ffn_gain])
        (
            mix_full, out_full, gate_full, up_full, down_full, normed_one, grad_out_all, normed_two,
            pre, state, mix_raw, residual, mixed_out, scale_lanes, aux_rows, par,
        ) = front(
            input_proj, forget_proj, outgate_proj, output_proj, glu_gate, glu_up, glu_down, cotangent,
            tokens_in, gains, bound_table, jnp.concatenate([lengths, bucket]),
        )
    else:
        inputs = tokens_in.astype(f32)
        scale_one = rms_scale(inputs)
        normed_mine = (inputs * scale_one * norm_gain).astype(bf16)
        inputs_half = my_half(inputs)
        scale_one_half = my_half(scale_one)
        mix_shards = jnp.concatenate(
            [my_columns(w) for w in (input_proj, forget_proj, outgate_proj)], axis=-1
        )
        gate_shards = glu_gate.T.reshape(n_tp, hid, block)
        up_shards = glu_up.T.reshape(n_tp, hid, block)
        down_shards = glu_down.reshape(n_tp, hid, block)
        my_table = pick(my_columns(bound_table), q, 0)
        par = jnp.stack([bound_parts(my_table)[2], pick(my_columns(mixer_gain), q, 0)])
        valid_own, keep_own = layout(lengths, bucket, rows)
        grad_out_rows = (cotangent.astype(f32) * my_half(valid_own)).astype(bf16)
        normed_half = my_half(normed_mine)
        normed_parts = [normed_mine] + [
            t_gather(swap(normed_half, tp_mask[r])).reshape(rows, width) for r in range(1, n_tp)
        ]
        normed_one = jnp.concatenate(normed_parts)
        aux_own = jnp.concatenate([valid_own, keep_own], axis=1)
        aux = jnp.concatenate([aux_own] + [swap(aux_own, tp_mask[r]) for r in range(1, n_tp)])
        mix_full = weight_whole(weight_parts(mix_shards))
        out_piece = output_proj
        for b in own_bits:
            out_piece = jnp.where(t_bit[b] == bit[b], out_piece, swap(out_piece, 1 << b))
        out_pieces = [out_piece]
        for b in reversed(free_bits):
            out_pieces = out_pieces + [swap(v, 1 << b) for v in out_pieces]
        out_full = jnp.concatenate(in_order(out_pieces, free_bits))
        gate_full, up_full, down_full = (
            weight_whole(weight_parts(w.transpose(0, 2, 1))).T
            for w in (gate_shards, up_shards, down_shards)
        )
        grad_out_all = jnp.stack(tp_gather(grad_out_rows)).reshape(n_tp * rows, width)
        pre = matmul(normed_one, mix_full)
        state, mix_raw, square = mixer_forward(pre, aux, par, rows)
        out_parts = matmul(mix_raw, out_full).astype(bf16).reshape(n_tp, n_t, share, width)
        square_parts = square.reshape(n_tp, n_t, share)
        square_sum = tp_scatter([square_parts[r] for r in range(n_tp)], f32)
        out_sum = tp_scatter([out_parts[r] for r in range(n_tp)], bf16)
        scale_state = lax.rsqrt(square_sum / width + epsilon)[:, None]
        mixed_out = out_sum * scale_state
        residual = inputs_half + mixed_out
        normed_two_half = (residual * rms_scale(residual) * ffn_gain).astype(bf16)
        normed_two = jnp.stack(tp_gather(normed_two_half)).reshape(n_tp * rows, width)

    if n_dp == 16 and n_t == 2:
        gate_pre = cross_cols(gate_full, normed_two)
        up_pre = cross_cols(up_full, normed_two)
        grad_hidden = cross_cols(down_full, grad_out_all)
        gate_act = jax.nn.silu(gate_pre)
        hidden = (gate_act * up_pre).astype(bf16)
        grad_up = (grad_hidden * gate_act).astype(bf16)
        grad_gate = (grad_hidden * up_pre * silu_slope(gate_pre)).astype(bf16)
        two_parts = (cross_rows(grad_gate, gate_full) + cross_rows(grad_up, up_full)).astype(bf16)
        block_parts = cross_rows(hidden, down_full).astype(bf16)
        grad_g, grad_u, grad_d, grad_mix_w, grad_out_w, grad_tokens, block_out, vec = back(
            hidden, grad_gate, grad_up, normed_two, grad_out_all, two_parts, block_parts, normed_one,
            mix_full, out_full, pre, state, mix_raw, aux_rows, par, tokens_in, residual, mixed_out,
            scale_lanes, gains,
        )
        mix_all = grad_mix_w.reshape(3, width, block)
        mine = lambda k: lax.dynamic_slice_in_dim(vec, k * n_dp + me, 1, 0)
        shares, picked, lower = bound_parts(
            lax.dynamic_slice_in_dim(bound_table, me * block, block, 1)
        )
        return (
            block_out,
            grad_tokens,
            mix_all[0].T.astype(f32),
            mix_all[1].T.astype(f32),
            mix_all[2].T.astype(f32),
            grad_out_w.astype(f32),
            grad_g.reshape(n_tp * hid, block).T.astype(f32),
            grad_u.reshape(n_tp * hid, block).T.astype(f32),
            grad_d.reshape(n_tp * hid, block).astype(f32),
            mine(0)[0],
            mine(2)[0],
            mine(1)[0],
            shares * (picked - lower[None, :]) * mine(3),
        )

    scale_two = rms_scale(residual)
    gate_pre = cross_cols(normed_two, gate_full)
    up_pre = cross_cols(normed_two, up_full)
    grad_hidden = cross_cols(grad_out_all, down_full)
    gate_act = jax.nn.silu(gate_pre)
    hidden = (gate_act * up_pre).astype(bf16)
    grad_up = (grad_hidden * gate_act).astype(bf16)
    grad_gate = (grad_hidden * up_pre * silu_slope(gate_pre)).astype(bf16)
    grad_two_parts = (
        (matmul(grad_gate, gate_full) + matmul(grad_up, up_full))
        .astype(bf16)
        .reshape(n_tp, n_t, share, width)
    )
    grad_normed_two = tp_scatter([grad_two_parts[r] for r in range(n_tp)], bf16)
    block_parts = matmul(hidden, down_full).astype(bf16).reshape(n_tp, n_t, share, width)
    block_out = (residual + tp_scatter([block_parts[r] for r in range(n_tp)], bf16)).astype(bf16)
    grad_down_t = jnp.stack(weight_back(cross_rows(grad_out_all, hidden).astype(bf16)))
    grad_w_gate = jnp.stack(weight_back(cross_rows(normed_two, grad_gate).astype(bf16)))
    grad_w_up = jnp.stack(weight_back(cross_rows(normed_two, grad_up).astype(bf16)))
    grad_glu_down = grad_down_t.transpose(0, 2, 1).reshape(glu_down.shape).astype(f32)
    grad_glu_gate = grad_w_gate.transpose(1, 0, 2).reshape(glu_gate.shape).astype(f32)
    grad_glu_up = grad_w_up.transpose(1, 0, 2).reshape(glu_up.shape).astype(f32)

    grad_residual = grad_out_rows.astype(f32) + norm_back(
        residual, scale_two, ffn_gain, grad_normed_two
    )
    ffn_gain_sum = jnp.sum(grad_normed_two * residual * scale_two, axis=0)
    grad_mix_half = grad_residual.astype(bf16)
    dot_mean = jnp.sum(grad_mix_half.astype(f32) * mixed_out, axis=1, keepdims=True) / (
        scale_state * width
    )
    row_values = jnp.concatenate([scale_state, dot_mean], axis=1).T
    row_all = jnp.stack(tp_gather(row_values)).transpose(0, 1, 3, 2).reshape(n_tp * rows, 2)
    grad_mix = jnp.stack(tp_gather(grad_mix_half)).reshape(n_tp * rows, width)
    grad_mixed = cross_cols(grad_mix, out_full)
    aux_back = jnp.concatenate([aux, row_all], axis=1)
    grads, sums = mixer_backward(pre, state, grad_mixed, aux_back, par, rows)
    one_parts = cross_cols(grads, mix_full).astype(bf16).reshape(n_tp, n_t, share, width)
    grad_normed_one = tp_scatter([one_parts[r] for r in range(n_tp)], bf16)
    grad_mix_w = jnp.stack(weight_back(cross_rows(normed_one, grads).astype(bf16)))

    mixed = (mix_raw.astype(f32) * row_all[:, :1]).astype(bf16)
    grad_out_w = cross_rows(mixed, grad_mix).astype(bf16).reshape((2,) * len(free_bits) + (block, width))
    for i, b in enumerate(free_bits):
        send = lax.dynamic_slice_in_dim(grad_out_w, 1 - bit[b], 1, i)
        hold = lax.dynamic_slice_in_dim(grad_out_w, bit[b], 1, i)
        grad_out_w = (hold.astype(f32) + swap(send, 1 << b).astype(f32)).astype(bf16)
    grad_out_w = grad_out_w.reshape(block, width)
    for b in own_bits:
        grad_out_w = (grad_out_w.astype(f32) + swap(grad_out_w, 1 << b).astype(f32)).astype(bf16)
    mine_t = jnp.int32(0)
    for b in own_bits:
        mine_t = mine_t * 2 + bit[b]
    if n_t == 2:
        other = t_swap(grad_out_w)
        grad_output_proj = jnp.where(mine_t == t, grad_out_w, other).astype(f32)
    else:
        grad_output_proj = pick(lax.all_gather(grad_out_w, "tensor", axis=0), mine_t, 0).astype(f32)

    mix_all = t_gather(grad_mix_w)
    mix_all = mix_all.reshape((2,) * t_depth + (2, 2) + (block, 3) + (2,) * len(free_bits) + (block,))
    order = list(own_bits) + list(tp_bits) + ["row", "which"] + list(free_bits) + ["col"]
    axes = [order.index(k) for k in ["which", "row"] + list(reversed(range(depth))) + ["col"]]
    mix_all = mix_all.transpose(axes).reshape(3, block, width).astype(f32)

    grad_tokens_half = my_half_residual = grad_residual + norm_back(
        inputs_half, scale_one_half, norm_gain, grad_normed_one
    )
    grad_tokens = t_gather(grad_tokens_half).reshape(rows, width)
    norm_gain_sum = jnp.sum(grad_normed_one * inputs_half * scale_one_half, axis=0)

    gains = jnp.stack([norm_gain_sum, ffn_gain_sum]).reshape((2,) + (2,) * depth + (block,))
    for b in reversed(range(depth)):
        at = 1 + axis_of[b]
        send = lax.dynamic_slice_in_dim(gains, 1 - bit[b], 1, at)
        hold = lax.dynamic_slice_in_dim(gains, bit[b], 1, at)
        gains = hold + swap(send, 1 << b)
    gains = gains.reshape(2, block)
    gains = gains + t_swap(gains) if n_t == 2 else lax.psum(gains, "tensor")

    for b in fs_bits:
        sums = sums + swap(sums, 1 << b)
    sums = t_gather(sums)
    sums = pick(sums, mine_t, 0).reshape((2,) + (2,) * len(free_bits) + (block,))
    for b in free_bits:
        sums = pick(sums, bit[b], 1)
    shares, picked, lower = bound_parts(lax.dynamic_slice_in_dim(bound_table, me * block, block, 1))
    grad_table = shares * (picked - lower[None, :]) * sums[1][None, :]

    return (
        block_out,
        grad_tokens,
        mix_all[0],
        mix_all[1],
        mix_all[2],
        grad_output_proj,
        grad_glu_gate,
        grad_glu_up,
        grad_glu_down,
        gains[0],
        sums[0],
        gains[1],
        grad_table,
    )


def solution(mesh):
    return jax.shard_map(
        functools.partial(body, mesh.shape["dp"], mesh.shape["tensor"]),
        mesh=mesh,
        in_specs=(
            P("dp", None),
            P("dp", None),
            P("dp", None),
            P("dp", None),
            P("dp", None),
            P("dp", "tensor"),
            P("dp", "tensor"),
            P("tensor", "dp"),
            P(),
            P(),
            P(),
            P(),
            P("dp"),
            P("dp"),
            P(("dp", "tensor"), None),
        ),
        out_specs=(
            P(("dp", "tensor"), None),
            P("dp", None),
            P("dp", None),
            P("dp", None),
            P("dp", None),
            P("dp", None),
            P("dp", "tensor"),
            P("dp", "tensor"),
            P("tensor", "dp"),
            P("dp"),
            P("dp"),
            P("dp"),
            P(None, "dp"),
        ),
        check_vma=False,
    )
```

```python
import functools

import jax
import jax.numpy as jnp
from jax import lax
from jax.experimental import pallas as pl
from jax.experimental.pallas import tpu as pltpu
from jax.sharding import PartitionSpec as P

LAYER = 12
epsilon = 1e-06
bf16 = jnp.bfloat16
f32 = jnp.float32


def rms_scale(values):
    return lax.rsqrt(jnp.mean(values * values, axis=-1, keepdims=True) + epsilon)


def norm_back(values, row_scale, gain_row, incoming):
    weighted = incoming * gain_row
    cubed = row_scale * row_scale * row_scale
    return row_scale * weighted - values * cubed * jnp.mean(
        weighted * values, axis=-1, keepdims=True
    )


def silu_slope(values):
    logistic = jax.nn.sigmoid(values)
    return logistic * (1.0 + values * (1.0 - logistic))


def matmul(first_op, second_op):
    return jnp.dot(first_op, second_op, preferred_element_type=f32)


def cross_rows(first_op, second_op):
    return lax.dot_general(
        first_op, second_op, (((0,), (0,)), ((), ())), preferred_element_type=f32
    )


def cross_cols(first_op, second_op):
    return lax.dot_general(
        first_op, second_op, (((1,), (1,)), ((), ())), preferred_element_type=f32
    )


def pick(values, index, axis):
    return lax.dynamic_index_in_dim(values, index, axis, keepdims=False)


def layout(lengths, bucket, row_count):
    slot_len = row_count // jnp.left_shift(jnp.int32(1), bucket)
    position = jnp.arange(row_count, dtype=jnp.int32)
    slot_index = position // slot_len
    offset = position - slot_index * slot_len
    slot_ids = jnp.arange(lengths.shape[0], dtype=jnp.int32)
    chosen = (slot_index[:, None] == slot_ids[None, :]).astype(jnp.int32)
    slot_limit = jnp.sum(chosen * lengths[None, :], axis=1)
    valid_mask = (offset < slot_limit).astype(f32)[:, None]
    keep_mask = (offset > 0).astype(f32)[:, None]
    return (valid_mask, keep_mask)


def bound_parts(bound_table):
    shares = jax.nn.softmax(bound_table, axis=0)
    layer_ids = jnp.arange(bound_table.shape[0], dtype=jnp.int32)[:, None]
    picked = ((layer_ids >= 1) & (layer_ids <= LAYER)).astype(f32)
    return (shares, picked, jnp.sum(shares * picked, axis=0))


def scan_rows(decay_ref, add_ref, out_ref, reverse):
    rows, width = out_ref.shape
    tiles = rows // 8
    sub = lax.broadcasted_iota(jnp.int32, (8, width), 0)

    def step(i, carry):
        j = tiles - 1 - i if reverse else i
        at = pl.ds(pl.multiple_of(j * 8, 8), 8)
        a = decay_ref[at, :]
        b = add_ref[at, :]
        for s in (1, 2, 4):
            shift = 8 - s if reverse else s
            inside = sub < 8 - s if reverse else sub >= s
            b = jnp.where(inside, b + a * pltpu.roll(b, shift, 0), b)
            a = jnp.where(inside, a * pltpu.roll(a, shift, 0), a)
        h = b + a * carry
        out_ref[at, :] = h
        edge = h[0:1, :] if reverse else h[7:8, :]
        return jnp.broadcast_to(edge, (8, width))

    lax.fori_loop(0, tiles, step, jnp.zeros((8, width), f32), unroll=4)


def mixer_forward_kernel(pre_ref, aux_ref, par_ref, state_ref, mix_ref, sq_ref, decay_ref, add_ref):
    width = state_ref.shape[1]
    input_pre = pre_ref[:, :width]
    forget_pre = pre_ref[:, width : 2 * width]
    outgate_pre = pre_ref[:, 2 * width :]
    valid = aux_ref[:, 0:1]
    keep = aux_ref[:, 1:2]
    bound = par_ref[0:1, :]
    gain = par_ref[1:2, :]
    forget = bound + (1.0 - bound) * jax.nn.sigmoid(forget_pre)
    add_ref[...] = input_pre * jax.nn.sigmoid(input_pre) * (1.0 - forget) * valid
    decay_ref[...] = forget * keep
    scan_rows(decay_ref, add_ref, state_ref, False)
    state = state_ref[...]
    mix_ref[...] = (state * gain * (outgate_pre * jax.nn.sigmoid(outgate_pre))).astype(bf16)
    sq_ref[...] = jnp.sum(state * state, axis=1, keepdims=True)


def mixer_forward(pre, aux, par, seq_rows):
    rows, width = pre.shape[0], pre.shape[1] // 3
    row_block = lambda n: pl.BlockSpec((seq_rows, n), lambda i: (i, 0))
    return pl.pallas_call(
        mixer_forward_kernel,
        grid=(rows // seq_rows,),
        in_specs=[
            row_block(3 * width),
            row_block(aux.shape[1]),
            pl.BlockSpec(par.shape, lambda i: (0, 0)),
        ],
        out_specs=[row_block(width), row_block(width), row_block(1)],
        out_shape=[
            jax.ShapeDtypeStruct((rows, width), f32),
            jax.ShapeDtypeStruct((rows, width), bf16),
            jax.ShapeDtypeStruct((rows, 1), f32),
        ],
        scratch_shapes=[pltpu.VMEM((seq_rows, width), f32)] * 2,
        cost_estimate=pl.CostEstimate(
            flops=rows * width * 60, bytes_accessed=rows * width * 20, transcendentals=rows * width * 3
        ),
        name="mixer_forward",
    )(pre, aux, par)


def mixer_backward_kernel(
    pre_ref, state_ref, up_ref, aux_ref, par_ref, grad_ref, sums_ref, decay_ref, add_ref, out_ref
):
    rows, width = state_ref.shape
    input_pre = pre_ref[:, :width]
    forget_pre = pre_ref[:, width : 2 * width]
    outgate_pre = pre_ref[:, 2 * width :]
    valid = aux_ref[:, 0:1]
    keep = aux_ref[:, 1:2]
    scale = aux_ref[:, 2:3]
    dot_mean = aux_ref[:, 3:4]
    bound = par_ref[0:1, :]
    gain = par_ref[1:2, :]
    state = state_ref[...]
    incoming = up_ref[...]
    at_row = lax.broadcasted_iota(jnp.int32, (rows, width), 0)
    sig_out = jax.nn.sigmoid(outgate_pre)
    act_out = outgate_pre * sig_out
    scaled = incoming * (state * scale)
    grad_ref[:, 2 * width :] = (
        scaled * gain * (sig_out * (1.0 + outgate_pre * (1.0 - sig_out)))
    ).astype(bf16)
    add_ref[...] = scale * (gain * act_out * incoming) - state * (scale * scale * scale * dot_mean)
    sig_forget = jax.nn.sigmoid(forget_pre)
    forget = bound + (1.0 - bound) * sig_forget
    decay_ref[...] = jnp.where(
        at_row < rows - 1, pltpu.roll(forget * keep, rows - 1, 0), 0.0
    )
    scan_rows(decay_ref, add_ref, out_ref, True)
    grad_state = out_ref[...]
    before = jnp.where(at_row > 0, pltpu.roll(state, 1, 0), 0.0)
    sig_in = jax.nn.sigmoid(input_pre)
    grad_forget = grad_state * (before * keep - input_pre * sig_in * valid)
    grad_ref[:, :width] = (
        grad_state * (1.0 - forget) * valid * (sig_in * (1.0 + input_pre * (1.0 - sig_in)))
    ).astype(bf16)
    grad_ref[:, width : 2 * width] = (
        grad_forget * (1.0 - bound) * sig_forget * (1.0 - sig_forget)
    ).astype(bf16)

    @pl.when(pl.program_id(0) == 0)
    def _():
        sums_ref[...] = jnp.zeros_like(sums_ref)

    sums_ref[0:1, :] += jnp.sum(scaled * act_out, axis=0, keepdims=True)
    sums_ref[1:2, :] += jnp.sum(grad_forget * (1.0 - sig_forget), axis=0, keepdims=True)


def mixer_backward(pre, state, incoming, aux, par, seq_rows):
    rows, width = state.shape
    row_block = lambda n: pl.BlockSpec((seq_rows, n), lambda i: (i, 0))
    whole = lambda shape: pl.BlockSpec(shape, lambda i: (0, 0))
    return pl.pallas_call(
        mixer_backward_kernel,
        grid=(rows // seq_rows,),
        in_specs=[
            row_block(3 * width),
            row_block(width),
            row_block(width),
            row_block(aux.shape[1]),
            whole(par.shape),
        ],
        out_specs=[row_block(3 * width), whole((2, width))],
        out_shape=[
            jax.ShapeDtypeStruct((rows, 3 * width), bf16),
            jax.ShapeDtypeStruct((2, width), f32),
        ],
        scratch_shapes=[pltpu.VMEM((seq_rows, width), f32)] * 3,
        cost_estimate=pl.CostEstimate(
            flops=rows * width * 90, bytes_accessed=rows * width * 26, transcendentals=rows * width * 3
        ),
        name="mixer_backward",
    )(pre, state, incoming, aux, par)


MESH = pl.DeviceIdType.MESH


class Copies:
    def __init__(self, send, recv, local):
        self.send, self.recv, self.local = send, recv, local
        self.n_remote = self.n_local = 0
        self.open = []

    def remote(self, src, dst, device):
        k = self.n_remote
        self.n_remote += 1
        copy = pltpu.make_async_remote_copy(
            src_ref=src,
            dst_ref=dst,
            send_sem=self.send.at[k],
            recv_sem=self.recv.at[k],
            device_id=device,
            device_id_type=MESH,
        )
        copy.start()
        self.open.append(copy.wait_send)
        return copy

    def here(self, src, dst, keep=False):
        k = self.n_local
        self.n_local += 1
        copy = pltpu.make_async_copy(src, dst, self.local.at[k])
        copy.start()
        if keep:
            self.open.append(copy.wait)
        return copy

    def sent(self, copies):
        for copy in copies:
            copy.wait_send()
            self.open.remove(copy.wait_send)

    def close(self):
        assert self.n_remote <= self.send.shape[0] and self.n_local <= self.local.shape[0]
        for wait in self.open:
            wait()


def position():
    me = lax.axis_index("dp")
    t = lax.axis_index("tensor")
    zf, zn, y, x = me // 8, (me // 4) % 2, (me // 2) % 2, me % 2
    to_x, to_zn = 1 - 2 * x, 4 - 8 * zn
    group = [None, (me + to_x, t), (me + to_zn, t), (me + to_x + to_zn, t)]
    q = [zn * 2 + x, zn * 2 + 1 - x, (1 - zn) * 2 + x, (1 - zn) * 2 + 1 - x]
    far = (me + 8 - 16 * zf, t)
    side = (me + 2 - 4 * y, t)
    core = (me, 1 - t)
    return me, t, (zf, zn, y, x), q, group, far, side, core


def meet(devices):
    barrier = pltpu.get_barrier_semaphore()
    for device in devices:
        pl.semaphore_signal(barrier, inc=1, device_id=device, device_id_type=MESH)
    pl.semaphore_wait(barrier, len(devices))


def fold_lanes(values):
    width = values.shape[1]
    if width % 128:
        return values
    total = values[:, :128]
    for i in range(128, width, 128):
        total = total + values[:, i : i + 128]
    return total


def front_kernel(
    s_in, s_fg, s_og, s_out, w_g, w_u, s_d, cot, tok, gains, table, sizes,
    o_mix, o_out, o_g, o_u, o_d, o_n1, o_go, o_n2, o_pre, o_state, o_raw, o_res, o_mo, o_sc, o_aux, o_par,
    w_mix, w_out, n1, aux, pre, state, raw, part, core_in, half, peer_in, par, wide_g, wide_u, s_g, s_u, go_own, bound_row,
    sq, sq_core, sq_half, sq_peer, res, mo, sc, n2, decay, add,
    send, recv, local, core_send, core_recv, sqc_send, sqc_recv, out_send, out_recv, x_send, x_recv,
):
    me, t, (zf, zn, y, x), q, group, far, side, core = position()
    rows, width = tok.shape
    share = rows // 2
    block = s_out.shape[0]
    feat = par.shape[1]
    hid = s_d.shape[0] // 4
    link = Copies(send, recv, local)
    get_g, get_u, get_cot = link.here(w_g, wide_g), link.here(w_u, wide_u), link.here(cot, go_own)
    meet(group[1:] + [far, side, core])

    def at(start, size, unit):
        return pl.ds(pl.multiple_of(start, unit), size)

    def pair(fz, c, fy):
        return at(fz * (8 * block) + c * (4 * block) + fy * (2 * block), 2 * block, 2 * block)

    mine = at(me * block, block, block)

    def row(r, tt):
        return at(r * rows + tt * share, share, share)

    def columns(r, fz):
        fx = x if r in (0, 2) else 1 - x
        fzn = zn if r in (0, 1) else 1 - zn
        return at((fz * 8 + fzn * 4 + t * 2 + fx) * block, block, block)

    mix_in, mix_own = [], []
    for k, s in enumerate((s_in, s_fg, s_og)):
        for fz in (0, 1):
            to = w_mix.at[mine, pl.ds(k * feat + fz * block, block)]
            mix_in += [link.remote(s.at[:, columns(r, fz)], to, group[r]) for r in (1, 2, 3)]
            mix_own.append(link.here(s.at[:, columns(0, fz)], to))
    out_rows = [at(z * block, block, block) for z in (zf, 1 - zf)]

    def out_copy(k, src, dst, device):
        return pltpu.make_async_remote_copy(
            src_ref=src,
            dst_ref=w_out.at[dst],
            send_sem=out_send.at[k],
            recv_sem=out_recv.at[k],
            device_id=device,
            device_id_type=MESH,
        )

    out_far = out_copy(0, s_out, out_rows[0], far)
    out_side = out_copy(1, s_out, out_rows[0], side)
    out_next = out_copy(2, w_out.at[out_rows[1]], out_rows[1], side)
    out_here = pltpu.make_async_copy(s_out, w_out.at[out_rows[0]], out_send.at[3])

    @pl.when(t == y)
    def _():
        out_far.start()
        out_side.start()
        out_here.start()

    norm_row = gains[0:1, :]

    def norm_rows(first):
        def some(j, carry):
            to = at(first + j * 16, 16, 16)
            value = tok[to, :].astype(f32)
            s = lax.rsqrt(jnp.mean(value * value, axis=1, keepdims=True) + epsilon)
            n1[to, :] = (value * s * norm_row).astype(bf16)
            return carry

        lax.fori_loop(0, share // 16, some, 0)

    norm_rows(t * share)
    n1_in = [link.remote(n1.at[row(0, t)], n1.at[row(r, t)], group[r]) for r in (1, 2)]

    count = sizes.shape[0] - 1
    slot_len = lax.shift_right_logical(jnp.int32(rows), sizes[count])
    position_row = lax.broadcasted_iota(jnp.int32, (1, rows), 1)
    slot = jnp.zeros((1, rows), jnp.int32)
    for j in range(1, count):
        slot = slot + (position_row >= j * slot_len).astype(jnp.int32)
    limit = jnp.zeros((1, rows), jnp.int32)
    for j in range(count):
        limit = limit + jnp.where(slot == j, sizes[j], 0)
    offset = position_row - slot * slot_len
    aux[0] = jnp.zeros(aux.shape[1:], f32)
    aux[0, 0:1, :] = (offset < limit).astype(f32)
    aux[0, 1:2, :] = (offset > 0).astype(f32)
    aux_in = [link.remote(aux.at[0], aux.at[r], group[r]) for r in (1, 2, 3)]

    norm_rows((1 - t) * share)
    for c in mix_own:
        c.wait()
    for c in mix_in:
        c.wait_recv()
    far_mix = [link.remote(w_mix.at[pair(zf, c, y)], w_mix.at[pair(zf, c, y)], far) for c in (0, 1)]
    side_mix = [link.remote(w_mix.at[pair(zf, c, y)], w_mix.at[pair(zf, c, y)], side) for c in (0, 1)]
    n1_in[1].wait_recv()
    n1_in.append(link.remote(n1.at[row(2, t)], n1.at[row(3, t)], group[1]))
    n1_core = [link.remote(n1.at[row(2, t)], n1.at[row(2, t)], core)]
    n1_in[0].wait_recv()
    n1_core.append(link.remote(n1.at[row(1, t)], n1.at[row(1, t)], core))
    shards = ((s_g, o_g), (s_u, o_u), (s_d, o_d))
    ffn_in, ffn_own = [], []

    def turn_round(wide, tall):
        size = min(128, wide.shape[1])

        def some(j, carry):
            to = at(j * size, size, size)
            tall[to, :] = wide[:, to].astype(f32).T.astype(bf16)
            return carry

        lax.fori_loop(0, wide.shape[1] // size, some, 0)

    def leave(s, o):
        units = [at(q[r] * hid, hid, 16) for r in range(4)]
        ffn_in.extend(link.remote(s.at[units[r]], o.at[:, mine], group[r]) for r in (1, 2, 3))
        ffn_own.append(link.here(s.at[units[0]], o.at[:, mine]))

    get_g.wait()
    turn_round(wide_g, s_g)
    leave(s_g, o_g)
    get_u.wait()
    turn_round(wide_u, s_u)
    leave(s_u, o_u)
    leave(s_d, o_d)

    logits = table[...]
    powers = jnp.exp(logits - jnp.max(logits, axis=0, keepdims=True))
    layer_ids = lax.broadcasted_iota(jnp.int32, logits.shape, 0)
    picked = jnp.where((layer_ids >= 1) & (layer_ids <= LAYER), powers, 0.0)
    bound_row[0:1, :] = jnp.sum(picked, axis=0, keepdims=True) / jnp.sum(powers, axis=0, keepdims=True)
    for fz in (0, 1):
        par[0:1, fz * block : (fz + 1) * block] = bound_row[0:1, columns(0, fz)]
        par[1:2, fz * block : (fz + 1) * block] = gains[1:2, columns(0, fz)]
    get_cot.wait()
    valid_rows = aux[0].T[:, 0:1]
    first_half = lax.broadcasted_iota(jnp.int32, (share, 1), 0) * 0 + t
    valid_half = jnp.where(first_half == 0, valid_rows[:share], valid_rows[share:])
    go_own[...] = (go_own[...].astype(f32) * valid_half).astype(bf16)
    n1_in[2].wait_recv()
    n1_core.append(link.remote(n1.at[row(3, t)], n1.at[row(3, t)], core))
    for c in (0, 1):
        far_mix[c].wait_recv()
        side_mix.append(link.remote(w_mix.at[pair(1 - zf, c, y)], w_mix.at[pair(1 - zf, c, y)], side))

    @pl.when(t == y)
    def _():
        out_far.wait_recv()
        out_next.start()
        out_far.wait_send()
        out_side.wait_send()
        out_here.wait()
        out_next.wait_send()

    @pl.when(t != y)
    def _():
        out_side.wait_recv()
        out_next.wait_recv()

    far_ffn, side_ffn = [], []

    def start_ffn(i):
        o = shards[i][1]
        ffn_own[i].wait()
        for c in ffn_in[3 * i : 3 * i + 3]:
            c.wait_recv()
        far_ffn.append([link.remote(o.at[:, pair(zf, c, y)], o.at[:, pair(zf, c, y)], far) for c in (0, 1)])
        side_ffn.extend(link.remote(o.at[:, pair(zf, c, y)], o.at[:, pair(zf, c, y)], side) for c in (0, 1))

    def forward_ffn(i):
        o = shards[i][1]
        for c in (0, 1):
            far_ffn[i][c].wait_recv()
            side_ffn.append(link.remote(o.at[:, pair(1 - zf, c, y)], o.at[:, pair(1 - zf, c, y)], side))

    start_ffn(0)
    go_in = [link.remote(go_own, o_go.at[row(r, t)], group[r]) for r in (1, 2)]
    go_core = [link.remote(go_own, o_go.at[row(0, t)], core)]
    link.here(go_own, o_go.at[row(0, t)], keep=True)

    for c in side_mix + n1_core + aux_in:
        c.wait_recv()

    def core_copy(r):
        return pltpu.make_async_remote_copy(
            src_ref=part.at[row(r, 1 - t)],
            dst_ref=core_in.at[at(r * share, share, share)],
            send_sem=core_send.at[r],
            recv_sem=core_recv.at[r],
            device_id=core,
            device_id_type=MESH,
        )

    def sq_copy(r):
        return pltpu.make_async_remote_copy(
            src_ref=sq.at[row(r, 1 - t)],
            dst_ref=sq_core.at[at(r * share, share, share)],
            send_sem=sqc_send.at[r],
            recv_sem=sqc_recv.at[r],
            device_id=core,
            device_id_type=MESH,
        )

    bound = par[0:1, :]
    gain = par[1:2, :]

    def to_x(slot, r):
        from_rows, to_rows = at(r * share, share, share), at(slot * share, share, share)
        return [
            pltpu.make_async_remote_copy(
                src_ref=a.at[from_rows],
                dst_ref=b.at[to_rows],
                send_sem=x_send.at[i * 2 + slot],
                recv_sem=x_recv.at[i * 2 + slot],
                device_id=group[1],
                device_id_type=MESH,
            )
            for i, (a, b) in enumerate(((half, peer_in), (sq_half, sq_peer)))
        ]

    def hand_over(r):
        core_copy(r).wait()
        sq_copy(r).wait()

        def some(j, carry):
            to = at(r * share + j * 16, 16, 16)
            mine_rows = at(r * rows + t * share + j * 16, 16, 16)
            half[to, :] = (part[mine_rows, :].astype(f32) + core_in[to, :].astype(f32)).astype(bf16)
            sq_half[to, :] = sq[mine_rows, :] + sq_core[to, :]
            return carry

        lax.fori_loop(0, share // 16, some, 0)

    def piece(i, carry):
        r = 3 - 2 * i + 3 * (i // 2)
        here = at(r * rows, rows, rows)
        pre[here, :] = jnp.dot(n1[here, :], w_mix[...], preferred_element_type=f32)
        masks = aux[r].T
        valid = masks[:, 0:1]
        keep = masks[:, 1:2]
        forget = bound + (1.0 - bound) * jax.nn.sigmoid(pre[here, feat : 2 * feat])
        input_pre = pre[here, 0:feat]
        add[...] = input_pre * jax.nn.sigmoid(input_pre) * (1.0 - forget) * valid
        decay[...] = forget * keep
        scan_rows(decay, add, state.at[here, :], False)
        held = state[here, :]
        outgate_pre = pre[here, 2 * feat :]
        raw[here, :] = (held * gain * (outgate_pre * jax.nn.sigmoid(outgate_pre))).astype(bf16)
        sq[here, :] = fold_lanes(held * held)
        part[here, :] = jnp.dot(raw[here, :], w_out[...], preferred_element_type=f32).astype(bf16)
        core_copy(r).start()
        sq_copy(r).start()

        @pl.when(i > 0)
        def _():
            before = 5 - 2 * i + 3 * ((i - 1) // 2)
            hand_over(before)

            @pl.when(i < 3)
            def _():
                for c in to_x(i - 1, before):
                    c.start()

        return carry

    lax.fori_loop(0, 4, piece, 0)
    start_ffn(1)

    link.here(w_mix, o_mix, keep=True)
    link.here(w_out, o_out, keep=True)
    link.here(n1, o_n1, keep=True)
    link.here(pre, o_pre, keep=True)
    link.here(state, o_state, keep=True)
    link.here(raw, o_raw, keep=True)
    link.here(aux, o_aux, keep=True)
    link.here(par, o_par, keep=True)

    def spread(o, incoming, cores):
        incoming[1].wait_recv()
        incoming.append(link.remote(o.at[row(2, t)], o.at[row(3, t)], group[1]))
        cores.append(link.remote(o.at[row(2, t)], o.at[row(2, t)], core))
        incoming[0].wait_recv()
        cores.append(link.remote(o.at[row(1, t)], o.at[row(1, t)], core))

    def spread_last(o, incoming, cores):
        incoming[2].wait_recv()
        cores.append(link.remote(o.at[row(3, t)], o.at[row(3, t)], core))

    hand_over(0)
    for c in to_x(0, 3):
        c.wait()

    def pass_on(j, carry):
        two = at(2 * share + j * 16, 16, 16)
        half[two, :] = (half[two, :].astype(f32) + peer_in[at(j * 16, 16, 16), :].astype(f32)).astype(bf16)
        sq_half[two, :] = sq_half[two, :] + sq_peer[at(j * 16, 16, 16), :]
        return carry

    lax.fori_loop(0, share // 16, pass_on, 0)
    third = pl.ds(2 * share, share)
    to_z = [
        link.remote(half.at[third], peer_in.at[third], group[2]),
        link.remote(sq_half.at[third], sq_peer.at[third], group[2]),
    ]
    spread(o_go, go_in, go_core)
    forward_ffn(0)
    for c in to_x(1, 1):
        c.wait()
    for c in to_z:
        c.wait_recv()
    total_sq = sq_half[0:share, :] + sq_peer[share : 2 * share, :] + sq_peer[2 * share : 3 * share, :]
    scale = lax.rsqrt(jnp.sum(total_sq, axis=1, keepdims=True) / width + epsilon)
    sc[...] = jnp.broadcast_to(scale, sc.shape)
    chunk = min(share, 16)

    def finish(i, carry):
        to = at(i * chunk, chunk, chunk)
        total = part[at(t * share + i * chunk, chunk, chunk), :].astype(f32) + core_in[to, :].astype(f32)
        for r in (1, 2):
            total = total + peer_in[at(r * share + i * chunk, chunk, chunk), :].astype(f32)
        mixed = total * sc[to, 0:1]
        value = tok[at(t * share + i * chunk, chunk, chunk), :].astype(f32) + mixed
        mo[to, :] = mixed
        res[to, :] = value
        scale_two = lax.rsqrt(jnp.mean(value * value, axis=1, keepdims=True) + epsilon)
        n2[to, :] = (value * scale_two * gains[2:3, :]).astype(bf16)
        return carry

    lax.fori_loop(0, share // chunk, finish, 0)
    n2_in = [link.remote(n2, o_n2.at[row(r, t)], group[r]) for r in (1, 2)]
    n2_core = [link.remote(n2, o_n2.at[row(0, t)], core)]
    link.here(n2, o_n2.at[row(0, t)], keep=True)
    link.here(res, o_res, keep=True)
    link.here(mo, o_mo, keep=True)
    link.here(sc, o_sc, keep=True)
    start_ffn(2)
    spread_last(o_go, go_in, go_core)
    forward_ffn(1)
    spread(o_n2, n2_in, n2_core)
    spread_last(o_n2, n2_in, n2_core)
    forward_ffn(2)
    for c in side_ffn + go_core + n2_core:
        c.wait_recv()
    link.close()


def front(s_in, s_fg, s_og, s_out, w_g, w_u, s_d, cot, tok, gains, table, sizes):
    rows, width = tok.shape
    share, group_rows = rows // 2, 4 * rows
    block = s_out.shape[0]
    feat, hid = 2 * block, s_d.shape[0] // 4
    lanes = 128 if feat % 128 == 0 else feat
    any_spec = pl.BlockSpec(memory_space=pl.ANY)
    vmem_spec = pl.BlockSpec(memory_space=pltpu.VMEM)
    made = jax.ShapeDtypeStruct
    outs = [
        made((width, 3 * feat), bf16),
        made((feat, width), bf16),
        made((hid, width), bf16),
        made((hid, width), bf16),
        made((hid, width), bf16),
        made((group_rows, width), bf16),
        made((group_rows, width), bf16),
        made((group_rows, width), bf16),
        made((group_rows, 3 * feat), f32),
        made((group_rows, feat), f32),
        made((group_rows, feat), bf16),
        made((share, width), f32),
        made((share, width), f32),
        made((share, 128), f32),
        made((4, 8, rows), f32),
        made((2, feat), f32),
    ]
    scratch = [
        pltpu.VMEM((width, 3 * feat), bf16),
        pltpu.VMEM((feat, width), bf16),
        pltpu.VMEM((group_rows, width), bf16),
        pltpu.VMEM((4, 8, rows), f32),
        pltpu.VMEM((group_rows, 3 * feat), f32),
        pltpu.VMEM((group_rows, feat), f32),
        pltpu.VMEM((group_rows, feat), bf16),
        pltpu.VMEM((group_rows, width), bf16),
        pltpu.VMEM((4 * share, width), bf16),
        pltpu.VMEM((4 * share, width), bf16),
        pltpu.VMEM((4 * share, width), bf16),
        pltpu.VMEM((2, feat), f32),
        pltpu.VMEM(w_g.shape, bf16),
        pltpu.VMEM(w_u.shape, bf16),
        pltpu.VMEM((4 * hid, block), bf16),
        pltpu.VMEM((4 * hid, block), bf16),
        pltpu.VMEM((share, width), bf16),
        pltpu.VMEM((8, width), f32),
        pltpu.VMEM((group_rows, lanes), f32),
        pltpu.VMEM((4 * share, lanes), f32),
        pltpu.VMEM((4 * share, lanes), f32),
        pltpu.VMEM((4 * share, lanes), f32),
        pltpu.VMEM((share, width), f32),
        pltpu.VMEM((share, width), f32),
        pltpu.VMEM((share, 128), f32),
        pltpu.VMEM((share, width), bf16),
        pltpu.VMEM((rows, feat), f32),
        pltpu.VMEM((rows, feat), f32),
        pltpu.SemaphoreType.DMA((88,)),
        pltpu.SemaphoreType.DMA((88,)),
        pltpu.SemaphoreType.DMA((32,)),
    ] + [pltpu.SemaphoreType.DMA((4,))] * 8
    return pl.pallas_call(
        front_kernel,
        in_specs=[any_spec] * 8 + [vmem_spec] * 3 + [pl.BlockSpec(memory_space=pltpu.SMEM)],
        out_specs=[any_spec] * len(outs),
        out_shape=outs,
        scratch_shapes=scratch,
        compiler_params=pltpu.CompilerParams(
            collective_id=1, has_side_effects=True, vmem_limit_bytes=56 << 20
        ),
        name="front",
    )(s_in, s_fg, s_og, s_out, w_g, w_u, s_d, cot, tok, gains, table, sizes)


def back_kernel(
    h_d, h_g, h_u, n2, go, p_two, p_block, n1, w_mix_in, w_out_in, pre, state, raw, aux_in,
    par, tok, res, mo, sc, gains,
    o_g, o_u, o_d, o_mix, o_out, o_tok, o_blk, o_vec,
    left, right, gmix, dw_d, dw_g, dw_u, dw_mix, yr_d, yr_g, yr_u, yr_mix, zr_d, zr_g, zr_u, zr_mix,
    own, half, core_in, core_blk, peer_in, peer_blk, w_mix, w_out, aux, pre_b, state_b, raw_b,
    grads, grads_t, decay, add, yr_out, zr_out, hid_a, hid_b,
    gres, gm_own, scalars, scal_all, sums, vec, vec_in,
    send, recv, local, core_send, core_recv, out_send, out_recv, piece_sem,
):
    me, t, (zf, zn, y, x), q, group, far, side, core = position()
    rows, width = tok.shape
    share = rows // 2
    block = width // 16
    feat = par.shape[1]
    link = Copies(send, recv, local)
    meet(group[1:] + [far, side, core])

    def at(start, size, unit):
        return pl.ds(pl.multiple_of(start, unit), size)

    def pair(fz, c, fy):
        return at(fz * (8 * block) + c * (4 * block) + fy * (2 * block), 2 * block, 2 * block)

    def row(r, tt):
        return at(r * rows + tt * share, share, share)

    def rel(r):
        return pl.ds(r * share, share)

    two_core = [link.remote(p_two.at[row(r, 1 - t)], core_in.at[rel(r)], core) for r in (3, 1, 2, 0)]
    two_own = [link.here(p_two.at[row(r, t)], own.at[rel(r)]) for r in (3, 1, 2, 0)]
    get_d = [link.here(h_d, hid_a), link.here(go, left)]
    get_g = [link.here(h_g, hid_b), link.here(n2, right)]
    get_go = link.here(go.at[row(0, t)], gm_own)
    get_aux = [link.here(aux_in, aux), link.here(w_out_in, w_out), link.here(w_mix_in, w_mix)]

    def own_rows(r, j):
        return own[at(r * share + j * 16, 16, 16), :].astype(f32)

    def add_half(r, source, incoming):
        def some(j, carry):
            to = at(r * share + j * 16, 16, 16)
            half[to, :] = (source(r, j) + incoming[to, :].astype(f32)).astype(bf16)
            return carry

        lax.fori_loop(0, share // 16, some, 0)

    def over_cores(arrived, mine, source, incoming, peers):
        sent = []
        for r in (3, 1, 2, 0):
            mine[r].wait()
            arrived[r].wait_recv()
            if r:
                add_half(r, source, incoming)
            if r % 2:
                sent.append(link.remote(half.at[rel(r)], peers.at[rel(len(sent))], group[1]))
        return sent

    def pass_on(sent, peers):
        sent[0].wait_recv()

        def some(j, carry):
            two = at(2 * share + j * 16, 16, 16)
            half[two, :] = (half[two, :].astype(f32) + peers[at(j * 16, 16, 16), :].astype(f32)).astype(bf16)
            return carry

        lax.fori_loop(0, share // 16, some, 0)
        sent.append(link.remote(half.at[rel(2)], peers.at[rel(2)], group[2]))

    def by_piece(copies):
        return dict(zip((3, 1, 2, 0), copies))

    two_peer = over_cores(by_piece(two_core), by_piece(two_own), own_rows, core_in, peer_in)

    def weight_grad(hid, other, dw, first, count):
        wide = 4 * block

        def columns(i, carry):
            to = at(((1 - zf) * 2 + i - (i // 2) * 4 * (1 - zf)) * wide, wide, wide)
            made = jnp.dot(hid[...], other[:, to], preferred_element_type=f32).astype(bf16)
            if len(dw.shape) == 2:
                dw[:, to] = made
            else:
                dw[:, :, :, to] = made.reshape(dw.shape[:3] + (wide,))
            return carry

        lax.fori_loop(first, first + count, columns, 0)

    def cut(ref, cols):
        return ref.at[:, cols] if len(ref.shape) == 2 else ref.at[:, :, :, cols]

    def side_send(dw, yr, slot):
        fz = 1 - zf if slot == 0 else zf
        return [
            link.remote(cut(dw, pair(fz, c, 1 - y)), cut(yr, pl.ds((slot * 2 + c) * 2 * block, 2 * block)), side)
            for c in (0, 1)
        ]

    def add_columns(dw, to, others):
        if len(dw.shape) == 2:
            size = 64 if dw.shape[0] % 64 == 0 else dw.shape[0]
            steps = dw.shape[0] // size
        else:
            steps = dw.shape[0] * dw.shape[1]

        def some(j, carry):
            if len(dw.shape) == 2:
                lead = (at(j * size, size, size),)
            else:
                lead = (j // dw.shape[1], j % dw.shape[1], slice(None))
            total = dw[lead + (to,)].astype(f32)
            for ref, cols in others:
                total = total + ref[lead + (cols,)].astype(f32)
            dw[lead + (to,)] = total.astype(bf16)
            return carry

        lax.fori_loop(0, steps, some, 0)

    def part_of(i):
        return pl.ds(i * 2 * block, 2 * block)

    def second_hop(hop, dw, yr, zr):
        sent = []
        for c in (0, 1):
            hop[c].wait_recv()
            add_columns(dw, pair(1 - zf, c, y), [(yr, part_of(c))])
            sent.append(link.remote(cut(dw, pair(1 - zf, c, y)), cut(zr, part_of(c)), far))
        return sent

    def last_hop(near, sent, dw, yr, zr, out):
        for c in (0, 1):
            near[c].wait_recv()
            sent[c].wait_recv()
            add_columns(dw, pair(zf, c, y), [(yr, part_of(2 + c)), (zr, part_of(c))])

        def owner(r):
            fx = x if r in (0, 2) else 1 - x
            fzn = zn if r in (0, 1) else 1 - zn
            return at((zf * 8 + fzn * 4 + y * 2 + fx) * block, block, block)

        if len(dw.shape) == 2:
            place = out.at[q[0]]
            link.here(dw.at[:, owner(0)], place, keep=True)
            return [link.remote(dw.at[:, owner(r)], place, group[r]) for r in (1, 2, 3)]
        place = out.at[:, :, zn, t, x]
        kept = link.here(cut(dw, owner(0)), place)
        sent = [link.remote(cut(dw, owner(r)), place, group[r]) for r in (1, 2, 3)]
        kept.wait()
        return sent

    for c in get_d:
        c.wait()
    weight_grad(hid_a, left, dw_d, 0, 2)
    hop_d = side_send(dw_d, yr_d, 0)
    weight_grad(hid_a, left, dw_d, 2, 2)
    get_u = link.here(h_u, hid_a)
    get_n1 = link.here(n1, left)
    for c in get_g:
        c.wait()
    weight_grad(hid_b, right, dw_g, 0, 2)
    hop_g = side_send(dw_g, yr_g, 0)
    weight_grad(hid_b, right, dw_g, 2, 2)
    pass_on(two_peer, peer_in)
    get_u.wait()
    weight_grad(hid_a, right, dw_u, 0, 4)
    far_d = second_hop(hop_d, dw_d, yr_d, zr_d)
    hop_u = side_send(dw_u, yr_u, 0)

    for c in two_peer[1:]:
        c.wait_recv()
    get_go.wait()
    gain_two = gains[2:3, :]
    sums[...] = jnp.zeros_like(sums)
    step = 16

    def residual_rows(j, carry):
        to = at(j * step, step, step)
        total = own[to, :].astype(f32) + core_in[to, :].astype(f32)
        for r in (1, 2):
            total = total + peer_in[at(r * share + j * step, step, step), :].astype(f32)
        value = res[to, :]
        s = lax.rsqrt(jnp.mean(value * value, axis=1, keepdims=True) + epsilon)
        weighted = total * gain_two
        grad = (
            gm_own[to, :].astype(f32)
            + s * weighted
            - value * (s * s * s) * jnp.mean(weighted * value, axis=1, keepdims=True)
        )
        gres[to, :] = grad
        low = grad.astype(bf16)
        gm_own[to, :] = low
        dot = jnp.sum(low.astype(f32) * mo[to, :], axis=1, keepdims=True)
        scale = sc[to, 0:1]
        sc[to, 1:2] = dot / (scale * width)
        sums[1:2, :] += jnp.sum(total * value * s, axis=0, keepdims=True)
        return carry

    lax.fori_loop(0, share // step, residual_rows, 0)
    scalars[...] = sc[...].T[0:8, :]

    def scal(r, tt):
        return scal_all.at[r * 2 + tt]

    gm_in = [link.remote(gm_own, gmix.at[row(r, t)], group[r]) for r in (1, 2)]
    sc_in = [link.remote(scalars, scal(r, t), group[r]) for r in (1, 2, 3)]
    gm_core = [link.remote(gm_own, gmix.at[row(0, t)], core), link.remote(scalars, scal(0, t), core)]
    gm_here = [link.here(gm_own, gmix.at[row(0, t)]), link.here(scalars, scal(0, t))]
    blk_core = [link.remote(p_block.at[row(r, 1 - t)], core_blk.at[rel(r)], core) for r in (3, 1, 2, 0)]

    far_g = second_hop(hop_g, dw_g, yr_g, zr_g)
    near_d = side_send(dw_d, yr_d, 1)
    gm_in[1].wait_recv()
    gm_in.append(link.remote(gmix.at[row(2, t)], gmix.at[row(3, t)], group[1]))
    gm_core.append(link.remote(gmix.at[row(2, t)], gmix.at[row(2, t)], core))
    gm_in[0].wait_recv()
    gm_core.append(link.remote(gmix.at[row(1, t)], gmix.at[row(1, t)], core))
    for i, r in enumerate((1, 2, 3)):
        sc_in[i].wait_recv()
        gm_core.append(link.remote(scal(r, t), scal(r, t), core))
    near_g = side_send(dw_g, yr_g, 1)
    far_u = second_hop(hop_u, dw_u, yr_u, zr_u)
    gm_in[2].wait_recv()
    gm_core.append(link.remote(gmix.at[row(3, t)], gmix.at[row(3, t)], core))
    near_u = side_send(dw_u, yr_u, 1)

    link.sent(two_peer)
    blk_own = [link.here(p_block.at[row(r, t)], own.at[rel(r)]) for r in (3, 1, 2, 0)]
    for c in get_aux + [get_n1] + gm_here:
        c.wait()
    for c in gm_core:
        c.wait_recv()

    def one_core(r):
        return pltpu.make_async_remote_copy(
            src_ref=right.at[row(r, 1 - t)],
            dst_ref=core_in.at[at(r * share, share, share)],
            send_sem=core_send.at[r],
            recv_sem=core_recv.at[r],
            device_id=core,
            device_id_type=MESH,
        )

    def fetch(r):
        here = at(r * rows, rows, rows)
        return [
            pltpu.make_async_copy(pre.at[here], pre_b, piece_sem.at[0]),
            pltpu.make_async_copy(state.at[here], state_b, piece_sem.at[1]),
            pltpu.make_async_copy(raw.at[here], raw_b, piece_sem.at[2]),
        ]

    bound = par[0:1, :]
    gain = par[1:2, :]
    gain_sums = sums.at[2:4, 0:feat]
    mixed_t = hid_b.at[0:feat]
    dw_out = w_out

    def one_rows(r, j):
        return right[at(r * rows + t * share + j * 16, 16, 16), :].astype(f32)

    def one_x(slot, r):
        return pltpu.make_async_remote_copy(
            src_ref=half.at[at(r * share, share, share)],
            dst_ref=peer_in.at[at(slot * share, share, share)],
            send_sem=core_send.at[4 + slot],
            recv_sem=core_recv.at[4 + slot],
            device_id=group[1],
            device_id_type=MESH,
        )

    def hand_over(r):
        one_core(r).wait()
        add_half(r, one_rows, core_in)

    def piece(i, carry):
        r = 3 - 2 * i + 3 * (i // 2)
        here = at(r * rows, rows, rows)
        copies = fetch(r)
        for c in copies:
            c.start()
        up = lax.dot_general(
            gmix[here, :], w_out[...], (((1,), (1,)), ((), ())), preferred_element_type=f32
        )
        masks = aux[r].T
        valid = masks[:, 0:1]
        keep = masks[:, 1:2]
        scale_parts = [scal_all[r * 2 + tt].T for tt in (0, 1)]
        scale = jnp.concatenate([p[:, 0:1] for p in scale_parts], axis=0)
        dot_mean = jnp.concatenate([p[:, 1:2] for p in scale_parts], axis=0)
        for c in copies:
            c.wait()
        at_row = lax.broadcasted_iota(jnp.int32, (rows, feat), 0)
        input_pre = pre_b[:, :feat]
        outgate_pre = pre_b[:, 2 * feat :]
        held = state_b[...]
        sig_out = jax.nn.sigmoid(outgate_pre)
        act_out = outgate_pre * sig_out
        scaled = up * (held * scale)
        grads[:, 2 * feat :] = scaled * gain * (sig_out * (1.0 + outgate_pre * (1.0 - sig_out)))
        add[...] = scale * (gain * act_out * up) - held * (scale * scale * scale * dot_mean)
        gain_sums[0:1, :] += jnp.sum(scaled * act_out, axis=0, keepdims=True)
        sig_forget = jax.nn.sigmoid(pre_b[:, feat : 2 * feat])
        forget = bound + (1.0 - bound) * sig_forget
        decay[...] = jnp.where(at_row < rows - 1, pltpu.roll(forget * keep, rows - 1, 0), 0.0)
        scan_rows(decay, add, add, True)
        grad_state = add[...]
        before = jnp.where(at_row > 0, pltpu.roll(held, 1, 0), 0.0)
        sig_in = jax.nn.sigmoid(input_pre)
        grad_forget = grad_state * (before * keep - input_pre * sig_in * valid)
        grads[:, :feat] = (
            grad_state * (1.0 - forget) * valid * (sig_in * (1.0 + input_pre * (1.0 - sig_in)))
        )
        grads[:, feat : 2 * feat] = grad_forget * (1.0 - bound) * sig_forget * (1.0 - sig_forget)
        gain_sums[1:2, :] += jnp.sum(grad_forget * (1.0 - sig_forget), axis=0, keepdims=True)
        low = grads[...].astype(bf16)
        right[here, :] = lax.dot_general(
            low, w_mix[...], (((1,), (1,)), ((), ())), preferred_element_type=f32
        ).astype(bf16)
        one_core(r).start()
        grads_t[:, here] = grads[...].T.astype(bf16)
        mixed_t[:, here] = (raw_b[...].astype(f32) * scale).T.astype(bf16)

        @pl.when(i > 0)
        def _():
            before_r = 5 - 2 * i + 3 * ((i - 1) // 2)
            hand_over(before_r)

            @pl.when(i < 3)
            def _():
                one_x(i - 1, before_r).start()

        return carry

    lax.fori_loop(0, 4, piece, 0)

    one_core(0).wait()

    weight_grad(grads_t, left, dw_mix, 0, 2)
    hop_mix = side_send(dw_mix, yr_mix, 0)
    weight_grad(grads_t, left, dw_mix, 2, 2)

    def out_columns(i, carry):
        to = at(i * (4 * block), 4 * block, 4 * block)
        dw_out[:, to] = jnp.dot(mixed_t[...], gmix[:, to], preferred_element_type=f32).astype(bf16)
        return carry

    lax.fori_loop(0, 4, out_columns, 0)
    near_rows = at(zf * block, block, block)
    far_rows = at((1 - zf) * block, block, block)

    def out_copy(k, src, dst, device):
        return pltpu.make_async_remote_copy(
            src_ref=src,
            dst_ref=dst,
            send_sem=out_send.at[k],
            recv_sem=out_recv.at[k],
            device_id=device,
            device_id_type=MESH,
        )

    out_side = out_copy(0, dw_out, yr_out, side)
    out_far = out_copy(1, dw_out.at[far_rows], zr_out, far)
    out_core = out_copy(2, dw_out.at[near_rows], o_out, core)
    out_here = pltpu.make_async_copy(dw_out.at[near_rows], o_out, out_send.at[3])

    @pl.when(t != y)
    def _():
        out_side.start()

    one_x(0, 3).wait()

    def one_on(j, carry):
        two = at(2 * share + j * 16, 16, 16)
        half[two, :] = (half[two, :].astype(f32) + peer_in[at(j * 16, 16, 16), :].astype(f32)).astype(bf16)
        return carry

    lax.fori_loop(0, share // 16, one_on, 0)
    one_z = link.remote(half.at[rel(2)], peer_in.at[rel(2)], group[2])
    near_mix = side_send(dw_mix, yr_mix, 1)
    back_d = last_hop(near_d, far_d, dw_d, yr_d, zr_d, o_d)
    back_g = last_hop(near_g, far_g, dw_g, yr_g, zr_g, o_g)
    far_mix = second_hop(hop_mix, dw_mix, yr_mix, zr_mix)

    @pl.when(t == y)
    def _():
        out_side.wait_recv()
        add_columns(dw_out, pl.ds(0, width), [(yr_out, pl.ds(0, width))])
        out_far.start()

    one_x(1, 1).wait()
    one_z.wait_recv()
    gain_one = gains[0:1, :]

    def token_rows(j, carry):
        to = at(j * step, step, step)
        total = one_rows(0, j) + core_in[to, :].astype(f32)
        for r in (1, 2):
            total = total + peer_in[at(r * share + j * step, step, step), :].astype(f32)
        value = tok[at(t * share + j * step, step, step), :].astype(f32)
        s = lax.rsqrt(jnp.mean(value * value, axis=1, keepdims=True) + epsilon)
        weighted = total * gain_one
        gres[to, :] = (
            gres[to, :]
            + s * weighted
            - value * (s * s * s) * jnp.mean(weighted * value, axis=1, keepdims=True)
        )
        sums[0:1, :] += jnp.sum(total * value * s, axis=0, keepdims=True)
        return carry

    lax.fori_loop(0, share // step, token_rows, 0)
    tok_rows = at(t * share, share, share)
    tok_core = link.remote(gres, o_tok.at[tok_rows], core)
    link.here(gres, o_tok.at[tok_rows], keep=True)

    vec[0] = jnp.zeros(vec.shape[1:], f32)
    for k in (0, 1):
        for i in range(16):
            vec[0, k * 16 + i : k * 16 + i + 1, :] = sums[k : k + 1, i * block : (i + 1) * block]
    for k in (2, 3):
        for i in (0, 1):
            vec[0, pl.ds(k * 16 + i * 8 + zn * 4 + t * 2 + x, 1), :] = sums[
                k : k + 1, i * block : (i + 1) * block
            ]
    partners = [group[1], group[2], side, far, core]
    turn = [link.remote(vec.at[0], vec_in.at[0], partners[0])]

    def next_turn():
        k = len(turn)
        turn[k - 1].wait_recv()
        vec[k] = vec[k - 1] + vec_in[k - 1]
        if k < len(partners):
            turn.append(link.remote(vec.at[k], vec_in.at[k], partners[k]))

    link.sent([one_z])
    blk_peer = over_cores(by_piece(blk_core), by_piece(blk_own), own_rows, core_blk, peer_blk)
    next_turn()
    back_u = last_hop(near_u, far_u, dw_u, yr_u, zr_u, o_u)
    pass_on(blk_peer, peer_blk)
    next_turn()
    next_turn()
    for c in blk_peer[1:]:
        c.wait_recv()

    def block_rows(j, carry):
        to = at(j * step, step, step)
        total = own_rows(0, j) + core_blk[to, :].astype(f32)
        for r in (1, 2):
            total = total + peer_blk[at(r * share + j * step, step, step), :].astype(f32)
        gm_own[to, :] = (res[to, :] + total).astype(bf16)
        return carry

    link.sent(gm_in[:2] + gm_core[:1])
    lax.fori_loop(0, share // step, block_rows, 0)
    link.here(gm_own, o_blk, keep=True)
    next_turn()
    next_turn()
    link.here(vec.at[5], o_vec, keep=True)
    back_mix = last_hop(near_mix, far_mix, dw_mix, yr_mix, zr_mix, o_mix)

    @pl.when(t == y)
    def _():
        out_far.wait_recv()

        def some(j, carry):
            to = at(zf * block + j * 16, 16, 16)
            dw_out[to, :] = (
                dw_out[to, :].astype(f32) + zr_out[at(j * 16, 16, 16), :].astype(f32)
            ).astype(bf16)
            return carry

        lax.fori_loop(0, block // 16, some, 0)
        out_core.start()
        out_here.start()
        out_far.wait_send()
        out_core.wait_send()
        out_here.wait()

    @pl.when(t != y)
    def _():
        out_side.wait_send()
        out_core.wait_recv()

    for c in back_mix:
        c.wait_recv()
    mix_core = link.remote(o_mix.at[:, :, :, t], o_mix.at[:, :, :, t], core)
    for c in back_d + back_g + back_u + [mix_core, tok_core]:
        c.wait_recv()
    link.close()


def back(*arrays):
    par, tok = arrays[14], arrays[15]
    rows, width = tok.shape
    share, group_rows = rows // 2, 4 * rows
    feat, hid, block = par.shape[1], arrays[0].shape[0], width // 16
    made = jax.ShapeDtypeStruct
    vm = pltpu.VMEM
    outs = [
        made((4, hid, block), bf16),
        made((4, hid, block), bf16),
        made((4, hid, block), bf16),
        made((3, 2, 2, 2, 2, block, block), bf16),
        made((block, width), bf16),
        made((rows, width), f32),
        made((share, width), bf16),
        made((64, block), f32),
    ]
    scratch = (
        [vm((group_rows, width), bf16)] * 3
        + [vm((hid, width), bf16)] * 3
        + [vm((3, 2, block, width), bf16)]
        + [vm((hid, width // 2), bf16)] * 3
        + [vm((3, 2, block, width // 2), bf16)]
        + [vm((hid, width // 4), bf16)] * 3
        + [vm((3, 2, block, width // 4), bf16)]
        + [vm((4 * share, width), bf16)] * 4
        + [vm((3 * share, width), bf16)] * 2
        + [
            vm((width, 3 * feat), bf16),
            vm((feat, width), bf16),
            vm(arrays[13].shape, f32),
            vm((rows, 3 * feat), f32),
            vm((rows, feat), f32),
            vm((rows, feat), bf16),
            vm((rows, 3 * feat), f32),
            vm((3 * feat, group_rows), bf16),
            vm((rows, feat), f32),
            vm((rows, feat), f32),
            vm((feat, width), bf16),
            vm((block, width), bf16),
            vm((hid, group_rows), bf16),
            vm((hid, group_rows), bf16),
            vm((share, width), f32),
            vm((share, width), bf16),
            vm((8, share), f32),
            vm((8, 8, share), f32),
            vm((4, width), f32),
            vm((6, 64, block), f32),
            vm((5, 64, block), f32),
            pltpu.SemaphoreType.DMA((96,)),
            pltpu.SemaphoreType.DMA((96,)),
            pltpu.SemaphoreType.DMA((32,)),
        ]
        + [pltpu.SemaphoreType.DMA((6,))] * 5
    )
    any_spec = pl.BlockSpec(memory_space=pl.ANY)
    vmem_spec = pl.BlockSpec(memory_space=pltpu.VMEM)
    return pl.pallas_call(
        back_kernel,
        in_specs=[any_spec] * 14 + [vmem_spec] * 6,
        out_specs=[any_spec] * len(outs),
        out_shape=outs,
        scratch_shapes=scratch,
        compiler_params=pltpu.CompilerParams(
            collective_id=2, has_side_effects=True, vmem_limit_bytes=63 << 20
        ),
        name="back",
    )(*arrays)


def body(
    n_dp,
    n_t,
    tokens_in,
    input_proj,
    forget_proj,
    outgate_proj,
    output_proj,
    glu_gate,
    glu_up,
    glu_down,
    norm_gain,
    mixer_gain,
    ffn_gain,
    bound_table,
    lengths,
    bucket,
    cotangent,
):
    depth = n_dp.bit_length() - 1
    tp_bits = (2, 0)
    fs_bits = tuple(b for b in reversed(range(depth)) if b not in tp_bits)
    t_depth = n_t.bit_length() - 1
    own_bits, free_bits = fs_bits[len(fs_bits) - t_depth :], fs_bits[: len(fs_bits) - t_depth]
    n_tp = 4
    tp_mask = (0, 1, 4, 5)
    axis_of = {b: depth - 1 - b for b in range(depth)}

    me = lax.axis_index("dp")
    t = lax.axis_index("tensor")
    bit = {b: (me >> b) & 1 for b in range(depth)}
    t_bit = {b: (t >> (t_depth - 1 - i)) & 1 for i, b in enumerate(own_bits)}
    q = bit[2] * 2 + bit[0]

    rows, width = tokens_in.shape
    share = cotangent.shape[0]
    block = width // n_dp
    free = 2 ** len(free_bits)
    feat = free * block

    def swap(values, mask):
        return lax.ppermute(values, "dp", [(i, i ^ mask) for i in range(n_dp)])

    def t_swap(values):
        return lax.ppermute(values, "tensor", [(0, 1), (1, 0)])

    def by_bit(which, own, other):
        return jnp.where(which == 0, own, other), jnp.where(which == 0, other, own)

    def in_order(parts, bits):
        parts = list(parts)
        for i, b in enumerate(reversed(bits)):
            step = 1 << i
            for r in range(len(parts)):
                if not r & step:
                    parts[r], parts[r | step] = by_bit(bit[b], parts[r], parts[r | step])
        return parts

    def t_gather(values):
        if n_t == 2:
            return jnp.stack(by_bit(t, values, t_swap(values)))
        return lax.all_gather(values, "tensor", axis=0)

    def t_scatter(values):
        if n_t == 2:
            return pick(values, t, 0).astype(f32) + t_swap(pick(values, 1 - t, 0)).astype(f32)
        return lax.psum_scatter(values, "tensor", scatter_dimension=0, tiled=False).astype(f32)

    def tp_gather(values):
        return [t_gather(values if r == 0 else swap(values, tp_mask[r])) for r in range(n_tp)]

    def tp_scatter(parts, kind):
        halves = [t_scatter(part) for part in parts]
        total = halves[0]
        for r in range(1, n_tp):
            total = total + swap(halves[r].astype(kind), tp_mask[r]).astype(f32)
        return total

    def exchange(values):
        parts = [pick(values, q, 0)]
        for r in range(1, n_tp):
            parts.append(swap(pick(values, q ^ r, 0), tp_mask[r]))
        return in_order(parts, tp_bits)

    def fs_gather(values):
        parts = [values]
        for b in fs_bits:
            parts = parts + [None] * 0 + [swap(v, 1 << b) for v in parts]
        return parts

    def weight_parts(shards):
        return fs_gather(jnp.stack(exchange(shards)))

    def weight_whole(parts):
        count = len(parts)
        flip = [0] * count
        for r in range(count):
            flip[sum(((r >> i) & 1) << (len(fs_bits) - 1 - i) for i in range(len(fs_bits)))] = parts[r]
        ordered = jnp.stack(in_order(flip, fs_bits))
        cols = ordered.shape[-1]
        ordered = ordered.reshape((2,) * depth + (block, cols))
        have = fs_bits + tp_bits
        axes = [have.index(b) for b in reversed(range(depth))]
        return ordered.transpose(axes + [depth, depth + 1]).reshape(width, cols)

    def weight_back(grad):
        cols = grad.shape[1]
        grad = grad.reshape((2,) * depth + (block, cols))
        for b in reversed(fs_bits):
            send = lax.dynamic_slice_in_dim(grad, 1 - bit[b], 1, axis_of[b]).astype(bf16)
            hold = lax.dynamic_slice_in_dim(grad, bit[b], 1, axis_of[b]).astype(f32)
            grad = hold + swap(send, 1 << b).astype(f32)
        return exchange(grad.reshape(n_tp, block, cols).astype(bf16))

    def my_columns(values):
        lead = values.shape[:-1]
        n = len(lead)
        values = values.reshape(lead + (2,) * depth + (block,))
        bits = list(reversed(range(depth)))
        for b in own_bits:
            values = pick(values, t_bit[b], n + bits.index(b))
            bits.remove(b)
        order = [n + bits.index(b) for b in tp_bits] + list(range(n)) + [n + bits.index(b) for b in free_bits]
        return values.transpose(order + [n + len(bits)]).reshape((n_tp,) + lead + (feat,))

    def my_half(values):
        return lax.dynamic_slice_in_dim(values, t * share, share, 0)

    hid = glu_gate.shape[1] // n_tp
    if n_dp == 16 and n_t == 2:
        gains = jnp.stack([norm_gain, mixer_gain, ffn_gain])
        (
            mix_full, out_full, gate_full, up_full, down_full, normed_one, grad_out_all, normed_two,
            pre, state, mix_raw, residual, mixed_out, scale_lanes, aux_rows, par,
        ) = front(
            input_proj, forget_proj, outgate_proj, output_proj, glu_gate, glu_up, glu_down, cotangent,
            tokens_in, gains, bound_table, jnp.concatenate([lengths, bucket]),
        )
    else:
        inputs = tokens_in.astype(f32)
        scale_one = rms_scale(inputs)
        normed_mine = (inputs * scale_one * norm_gain).astype(bf16)
        inputs_half = my_half(inputs)
        scale_one_half = my_half(scale_one)
        mix_shards = jnp.concatenate(
            [my_columns(w) for w in (input_proj, forget_proj, outgate_proj)], axis=-1
        )
        gate_shards = glu_gate.T.reshape(n_tp, hid, block)
        up_shards = glu_up.T.reshape(n_tp, hid, block)
        down_shards = glu_down.reshape(n_tp, hid, block)
        my_table = pick(my_columns(bound_table), q, 0)
        par = jnp.stack([bound_parts(my_table)[2], pick(my_columns(mixer_gain), q, 0)])
        valid_own, keep_own = layout(lengths, bucket, rows)
        grad_out_rows = (cotangent.astype(f32) * my_half(valid_own)).astype(bf16)
        normed_half = my_half(normed_mine)
        normed_parts = [normed_mine] + [
            t_gather(swap(normed_half, tp_mask[r])).reshape(rows, width) for r in range(1, n_tp)
        ]
        normed_one = jnp.concatenate(normed_parts)
        aux_own = jnp.concatenate([valid_own, keep_own], axis=1)
        aux = jnp.concatenate([aux_own] + [swap(aux_own, tp_mask[r]) for r in range(1, n_tp)])
        mix_full = weight_whole(weight_parts(mix_shards))
        out_piece = output_proj
        for b in own_bits:
            out_piece = jnp.where(t_bit[b] == bit[b], out_piece, swap(out_piece, 1 << b))
        out_pieces = [out_piece]
        for b in reversed(free_bits):
            out_pieces = out_pieces + [swap(v, 1 << b) for v in out_pieces]
        out_full = jnp.concatenate(in_order(out_pieces, free_bits))
        gate_full, up_full, down_full = (
            weight_whole(weight_parts(w.transpose(0, 2, 1))).T
            for w in (gate_shards, up_shards, down_shards)
        )
        grad_out_all = jnp.stack(tp_gather(grad_out_rows)).reshape(n_tp * rows, width)
        pre = matmul(normed_one, mix_full)
        state, mix_raw, square = mixer_forward(pre, aux, par, rows)
        out_parts = matmul(mix_raw, out_full).astype(bf16).reshape(n_tp, n_t, share, width)
        square_parts = square.reshape(n_tp, n_t, share)
        square_sum = tp_scatter([square_parts[r] for r in range(n_tp)], f32)
        out_sum = tp_scatter([out_parts[r] for r in range(n_tp)], bf16)
        scale_state = lax.rsqrt(square_sum / width + epsilon)[:, None]
        mixed_out = out_sum * scale_state
        residual = inputs_half + mixed_out
        normed_two_half = (residual * rms_scale(residual) * ffn_gain).astype(bf16)
        normed_two = jnp.stack(tp_gather(normed_two_half)).reshape(n_tp * rows, width)

    if n_dp == 16 and n_t == 2:
        gate_pre = cross_cols(gate_full, normed_two)
        up_pre = cross_cols(up_full, normed_two)
        grad_hidden = cross_cols(down_full, grad_out_all)
        gate_act = jax.nn.silu(gate_pre)
        hidden = (gate_act * up_pre).astype(bf16)
        grad_up = (grad_hidden * gate_act).astype(bf16)
        grad_gate = (grad_hidden * up_pre * silu_slope(gate_pre)).astype(bf16)
        two_parts = (cross_rows(grad_gate, gate_full) + cross_rows(grad_up, up_full)).astype(bf16)
        block_parts = cross_rows(hidden, down_full).astype(bf16)
        grad_g, grad_u, grad_d, grad_mix_w, grad_out_w, grad_tokens, block_out, vec = back(
            hidden, grad_gate, grad_up, normed_two, grad_out_all, two_parts, block_parts, normed_one,
            mix_full, out_full, pre, state, mix_raw, aux_rows, par, tokens_in, residual, mixed_out,
            scale_lanes, gains,
        )
        mix_all = grad_mix_w.reshape(3, width, block)
        mine = lambda k: lax.dynamic_slice_in_dim(vec, k * n_dp + me, 1, 0)
        shares, picked, lower = bound_parts(
            lax.dynamic_slice_in_dim(bound_table, me * block, block, 1)
        )
        return (
            block_out,
            grad_tokens,
            mix_all[0].T.astype(f32),
            mix_all[1].T.astype(f32),
            mix_all[2].T.astype(f32),
            grad_out_w.astype(f32),
            grad_g.reshape(n_tp * hid, block).T.astype(f32),
            grad_u.reshape(n_tp * hid, block).T.astype(f32),
            grad_d.reshape(n_tp * hid, block).astype(f32),
            mine(0)[0],
            mine(2)[0],
            mine(1)[0],
            shares * (picked - lower[None, :]) * mine(3),
        )

    scale_two = rms_scale(residual)
    gate_pre = cross_cols(normed_two, gate_full)
    up_pre = cross_cols(normed_two, up_full)
    grad_hidden = cross_cols(grad_out_all, down_full)
    gate_act = jax.nn.silu(gate_pre)
    hidden = (gate_act * up_pre).astype(bf16)
    grad_up = (grad_hidden * gate_act).astype(bf16)
    grad_gate = (grad_hidden * up_pre * silu_slope(gate_pre)).astype(bf16)
    grad_two_parts = (
        (matmul(grad_gate, gate_full) + matmul(grad_up, up_full))
        .astype(bf16)
        .reshape(n_tp, n_t, share, width)
    )
    grad_normed_two = tp_scatter([grad_two_parts[r] for r in range(n_tp)], bf16)
    block_parts = matmul(hidden, down_full).astype(bf16).reshape(n_tp, n_t, share, width)
    block_out = (residual + tp_scatter([block_parts[r] for r in range(n_tp)], bf16)).astype(bf16)
    grad_down_t = jnp.stack(weight_back(cross_rows(grad_out_all, hidden).astype(bf16)))
    grad_w_gate = jnp.stack(weight_back(cross_rows(normed_two, grad_gate).astype(bf16)))
    grad_w_up = jnp.stack(weight_back(cross_rows(normed_two, grad_up).astype(bf16)))
    grad_glu_down = grad_down_t.transpose(0, 2, 1).reshape(glu_down.shape).astype(f32)
    grad_glu_gate = grad_w_gate.transpose(1, 0, 2).reshape(glu_gate.shape).astype(f32)
    grad_glu_up = grad_w_up.transpose(1, 0, 2).reshape(glu_up.shape).astype(f32)

    grad_residual = grad_out_rows.astype(f32) + norm_back(
        residual, scale_two, ffn_gain, grad_normed_two
    )
    ffn_gain_sum = jnp.sum(grad_normed_two * residual * scale_two, axis=0)
    grad_mix_half = grad_residual.astype(bf16)
    dot_mean = jnp.sum(grad_mix_half.astype(f32) * mixed_out, axis=1, keepdims=True) / (
        scale_state * width
    )
    row_values = jnp.concatenate([scale_state, dot_mean], axis=1).T
    row_all = jnp.stack(tp_gather(row_values)).transpose(0, 1, 3, 2).reshape(n_tp * rows, 2)
    grad_mix = jnp.stack(tp_gather(grad_mix_half)).reshape(n_tp * rows, width)
    grad_mixed = cross_cols(grad_mix, out_full)
    aux_back = jnp.concatenate([aux, row_all], axis=1)
    grads, sums = mixer_backward(pre, state, grad_mixed, aux_back, par, rows)
    one_parts = cross_cols(grads, mix_full).astype(bf16).reshape(n_tp, n_t, share, width)
    grad_normed_one = tp_scatter([one_parts[r] for r in range(n_tp)], bf16)
    grad_mix_w = jnp.stack(weight_back(cross_rows(normed_one, grads).astype(bf16)))

    mixed = (mix_raw.astype(f32) * row_all[:, :1]).astype(bf16)
    grad_out_w = cross_rows(mixed, grad_mix).astype(bf16).reshape((2,) * len(free_bits) + (block, width))
    for i, b in enumerate(free_bits):
        send = lax.dynamic_slice_in_dim(grad_out_w, 1 - bit[b], 1, i)
        hold = lax.dynamic_slice_in_dim(grad_out_w, bit[b], 1, i)
        grad_out_w = (hold.astype(f32) + swap(send, 1 << b).astype(f32)).astype(bf16)
    grad_out_w = grad_out_w.reshape(block, width)
    for b in own_bits:
        grad_out_w = (grad_out_w.astype(f32) + swap(grad_out_w, 1 << b).astype(f32)).astype(bf16)
    mine_t = jnp.int32(0)
    for b in own_bits:
        mine_t = mine_t * 2 + bit[b]
    if n_t == 2:
        other = t_swap(grad_out_w)
        grad_output_proj = jnp.where(mine_t == t, grad_out_w, other).astype(f32)
    else:
        grad_output_proj = pick(lax.all_gather(grad_out_w, "tensor", axis=0), mine_t, 0).astype(f32)

    mix_all = t_gather(grad_mix_w)
    mix_all = mix_all.reshape((2,) * t_depth + (2, 2) + (block, 3) + (2,) * len(free_bits) + (block,))
    order = list(own_bits) + list(tp_bits) + ["row", "which"] + list(free_bits) + ["col"]
    axes = [order.index(k) for k in ["which", "row"] + list(reversed(range(depth))) + ["col"]]
    mix_all = mix_all.transpose(axes).reshape(3, block, width).astype(f32)

    grad_tokens_half = my_half_residual = grad_residual + norm_back(
        inputs_half, scale_one_half, norm_gain, grad_normed_one
    )
    grad_tokens = t_gather(grad_tokens_half).reshape(rows, width)
    norm_gain_sum = jnp.sum(grad_normed_one * inputs_half * scale_one_half, axis=0)

    gains = jnp.stack([norm_gain_sum, ffn_gain_sum]).reshape((2,) + (2,) * depth + (block,))
    for b in reversed(range(depth)):
        at = 1 + axis_of[b]
        send = lax.dynamic_slice_in_dim(gains, 1 - bit[b], 1, at)
        hold = lax.dynamic_slice_in_dim(gains, bit[b], 1, at)
        gains = hold + swap(send, 1 << b)
    gains = gains.reshape(2, block)
    gains = gains + t_swap(gains) if n_t == 2 else lax.psum(gains, "tensor")

    for b in fs_bits:
        sums = sums + swap(sums, 1 << b)
    sums = t_gather(sums)
    sums = pick(sums, mine_t, 0).reshape((2,) + (2,) * len(free_bits) + (block,))
    for b in free_bits:
        sums = pick(sums, bit[b], 1)
    shares, picked, lower = bound_parts(lax.dynamic_slice_in_dim(bound_table, me * block, block, 1))
    grad_table = shares * (picked - lower[None, :]) * sums[1][None, :]

    return (
        block_out,
        grad_tokens,
        mix_all[0],
        mix_all[1],
        mix_all[2],
        grad_output_proj,
        grad_glu_gate,
        grad_glu_up,
        grad_glu_down,
        gains[0],
        sums[0],
        gains[1],
        grad_table,
    )


def solution(mesh):
    return jax.shard_map(
        functools.partial(body, mesh.shape["dp"], mesh.shape["tensor"]),
        mesh=mesh,
        in_specs=(
            P("dp", None),
            P("dp", None),
            P("dp", None),
            P("dp", None),
            P("dp", None),
            P("dp", "tensor"),
            P("dp", "tensor"),
            P("tensor", "dp"),
            P(),
            P(),
            P(),
            P(),
            P("dp"),
            P("dp"),
            P(("dp", "tensor"), None),
        ),
        out_specs=(
            P(("dp", "tensor"), None),
            P("dp", None),
            P("dp", None),
            P("dp", None),
            P("dp", None),
            P("dp", None),
            P("dp", "tensor"),
            P("dp", "tensor"),
            P("tensor", "dp"),
            P("dp"),
            P("dp"),
            P("dp"),
            P(None, "dp"),
        ),
        check_vma=False,
    )
```

```python
import functools

import jax
import jax.numpy as jnp
from jax import lax
from jax.experimental import pallas as pl
from jax.experimental.pallas import tpu as pltpu
from jax.sharding import PartitionSpec as P

LAYER = 12
epsilon = 1e-06
bf16 = jnp.bfloat16
f32 = jnp.float32


def rms_scale(values):
    return lax.rsqrt(jnp.mean(values * values, axis=-1, keepdims=True) + epsilon)


def norm_back(values, row_scale, gain_row, incoming):
    weighted = incoming * gain_row
    cubed = row_scale * row_scale * row_scale
    return row_scale * weighted - values * cubed * jnp.mean(
        weighted * values, axis=-1, keepdims=True
    )


def silu_slope(values):
    logistic = jax.nn.sigmoid(values)
    return logistic * (1.0 + values * (1.0 - logistic))


def matmul(first_op, second_op):
    return jnp.dot(first_op, second_op, preferred_element_type=f32)


def cross_rows(first_op, second_op):
    return lax.dot_general(
        first_op, second_op, (((0,), (0,)), ((), ())), preferred_element_type=f32
    )


def cross_cols(first_op, second_op):
    return lax.dot_general(
        first_op, second_op, (((1,), (1,)), ((), ())), preferred_element_type=f32
    )


def pick(values, index, axis):
    return lax.dynamic_index_in_dim(values, index, axis, keepdims=False)


def layout(lengths, bucket, row_count):
    slot_len = row_count // jnp.left_shift(jnp.int32(1), bucket)
    position = jnp.arange(row_count, dtype=jnp.int32)
    slot_index = position // slot_len
    offset = position - slot_index * slot_len
    slot_ids = jnp.arange(lengths.shape[0], dtype=jnp.int32)
    chosen = (slot_index[:, None] == slot_ids[None, :]).astype(jnp.int32)
    slot_limit = jnp.sum(chosen * lengths[None, :], axis=1)
    valid_mask = (offset < slot_limit).astype(f32)[:, None]
    keep_mask = (offset > 0).astype(f32)[:, None]
    return (valid_mask, keep_mask)


def bound_parts(bound_table):
    shares = jax.nn.softmax(bound_table, axis=0)
    layer_ids = jnp.arange(bound_table.shape[0], dtype=jnp.int32)[:, None]
    picked = ((layer_ids >= 1) & (layer_ids <= LAYER)).astype(f32)
    return (shares, picked, jnp.sum(shares * picked, axis=0))


def scan_rows(decay_ref, add_ref, out_ref, reverse):
    rows, width = out_ref.shape
    tiles = rows // 8
    sub = lax.broadcasted_iota(jnp.int32, (8, width), 0)

    def step(i, carry):
        j = tiles - 1 - i if reverse else i
        at = pl.ds(pl.multiple_of(j * 8, 8), 8)
        a = decay_ref[at, :]
        b = add_ref[at, :]
        for s in (1, 2, 4):
            shift = 8 - s if reverse else s
            inside = sub < 8 - s if reverse else sub >= s
            b = jnp.where(inside, b + a * pltpu.roll(b, shift, 0), b)
            a = jnp.where(inside, a * pltpu.roll(a, shift, 0), a)
        h = b + a * carry
        out_ref[at, :] = h
        edge = h[0:1, :] if reverse else h[7:8, :]
        return jnp.broadcast_to(edge, (8, width))

    lax.fori_loop(0, tiles, step, jnp.zeros((8, width), f32), unroll=4)


def mixer_forward_kernel(pre_ref, aux_ref, par_ref, state_ref, mix_ref, sq_ref, decay_ref, add_ref):
    width = state_ref.shape[1]
    input_pre = pre_ref[:, :width]
    forget_pre = pre_ref[:, width : 2 * width]
    outgate_pre = pre_ref[:, 2 * width :]
    valid = aux_ref[:, 0:1]
    keep = aux_ref[:, 1:2]
    bound = par_ref[0:1, :]
    gain = par_ref[1:2, :]
    forget = bound + (1.0 - bound) * jax.nn.sigmoid(forget_pre)
    add_ref[...] = input_pre * jax.nn.sigmoid(input_pre) * (1.0 - forget) * valid
    decay_ref[...] = forget * keep
    scan_rows(decay_ref, add_ref, state_ref, False)
    state = state_ref[...]
    mix_ref[...] = (state * gain * (outgate_pre * jax.nn.sigmoid(outgate_pre))).astype(bf16)
    sq_ref[...] = jnp.sum(state * state, axis=1, keepdims=True)


def mixer_forward(pre, aux, par, seq_rows):
    rows, width = pre.shape[0], pre.shape[1] // 3
    row_block = lambda n: pl.BlockSpec((seq_rows, n), lambda i: (i, 0))
    return pl.pallas_call(
        mixer_forward_kernel,
        grid=(rows // seq_rows,),
        in_specs=[
            row_block(3 * width),
            row_block(aux.shape[1]),
            pl.BlockSpec(par.shape, lambda i: (0, 0)),
        ],
        out_specs=[row_block(width), row_block(width), row_block(1)],
        out_shape=[
            jax.ShapeDtypeStruct((rows, width), f32),
            jax.ShapeDtypeStruct((rows, width), bf16),
            jax.ShapeDtypeStruct((rows, 1), f32),
        ],
        scratch_shapes=[pltpu.VMEM((seq_rows, width), f32)] * 2,
        cost_estimate=pl.CostEstimate(
            flops=rows * width * 60, bytes_accessed=rows * width * 20, transcendentals=rows * width * 3
        ),
        name="mixer_forward",
    )(pre, aux, par)


def mixer_backward_kernel(
    pre_ref, state_ref, up_ref, aux_ref, par_ref, grad_ref, sums_ref, decay_ref, add_ref, out_ref
):
    rows, width = state_ref.shape
    input_pre = pre_ref[:, :width]
    forget_pre = pre_ref[:, width : 2 * width]
    outgate_pre = pre_ref[:, 2 * width :]
    valid = aux_ref[:, 0:1]
    keep = aux_ref[:, 1:2]
    scale = aux_ref[:, 2:3]
    dot_mean = aux_ref[:, 3:4]
    bound = par_ref[0:1, :]
    gain = par_ref[1:2, :]
    state = state_ref[...]
    incoming = up_ref[...]
    at_row = lax.broadcasted_iota(jnp.int32, (rows, width), 0)
    sig_out = jax.nn.sigmoid(outgate_pre)
    act_out = outgate_pre * sig_out
    scaled = incoming * (state * scale)
    grad_ref[:, 2 * width :] = (
        scaled * gain * (sig_out * (1.0 + outgate_pre * (1.0 - sig_out)))
    ).astype(bf16)
    add_ref[...] = scale * (gain * act_out * incoming) - state * (scale * scale * scale * dot_mean)
    sig_forget = jax.nn.sigmoid(forget_pre)
    forget = bound + (1.0 - bound) * sig_forget
    decay_ref[...] = jnp.where(
        at_row < rows - 1, pltpu.roll(forget * keep, rows - 1, 0), 0.0
    )
    scan_rows(decay_ref, add_ref, out_ref, True)
    grad_state = out_ref[...]
    before = jnp.where(at_row > 0, pltpu.roll(state, 1, 0), 0.0)
    sig_in = jax.nn.sigmoid(input_pre)
    grad_forget = grad_state * (before * keep - input_pre * sig_in * valid)
    grad_ref[:, :width] = (
        grad_state * (1.0 - forget) * valid * (sig_in * (1.0 + input_pre * (1.0 - sig_in)))
    ).astype(bf16)
    grad_ref[:, width : 2 * width] = (
        grad_forget * (1.0 - bound) * sig_forget * (1.0 - sig_forget)
    ).astype(bf16)

    @pl.when(pl.program_id(0) == 0)
    def _():
        sums_ref[...] = jnp.zeros_like(sums_ref)

    sums_ref[0:1, :] += jnp.sum(scaled * act_out, axis=0, keepdims=True)
    sums_ref[1:2, :] += jnp.sum(grad_forget * (1.0 - sig_forget), axis=0, keepdims=True)


def mixer_backward(pre, state, incoming, aux, par, seq_rows):
    rows, width = state.shape
    row_block = lambda n: pl.BlockSpec((seq_rows, n), lambda i: (i, 0))
    whole = lambda shape: pl.BlockSpec(shape, lambda i: (0, 0))
    return pl.pallas_call(
        mixer_backward_kernel,
        grid=(rows // seq_rows,),
        in_specs=[
            row_block(3 * width),
            row_block(width),
            row_block(width),
            row_block(aux.shape[1]),
            whole(par.shape),
        ],
        out_specs=[row_block(3 * width), whole((2, width))],
        out_shape=[
            jax.ShapeDtypeStruct((rows, 3 * width), bf16),
            jax.ShapeDtypeStruct((2, width), f32),
        ],
        scratch_shapes=[pltpu.VMEM((seq_rows, width), f32)] * 3,
        cost_estimate=pl.CostEstimate(
            flops=rows * width * 90, bytes_accessed=rows * width * 26, transcendentals=rows * width * 3
        ),
        name="mixer_backward",
    )(pre, state, incoming, aux, par)


MESH = pl.DeviceIdType.MESH


class Copies:
    def __init__(self, send, recv, local):
        self.send, self.recv, self.local = send, recv, local
        self.n_remote = self.n_local = 0
        self.open = []

    def remote(self, src, dst, device):
        k = self.n_remote
        self.n_remote += 1
        copy = pltpu.make_async_remote_copy(
            src_ref=src,
            dst_ref=dst,
            send_sem=self.send.at[k],
            recv_sem=self.recv.at[k],
            device_id=device,
            device_id_type=MESH,
        )
        copy.start()
        self.open.append(copy.wait_send)
        return copy

    def here(self, src, dst, keep=False):
        k = self.n_local
        self.n_local += 1
        copy = pltpu.make_async_copy(src, dst, self.local.at[k])
        copy.start()
        if keep:
            self.open.append(copy.wait)
        return copy

    def sent(self, copies):
        for copy in copies:
            copy.wait_send()
            self.open.remove(copy.wait_send)

    def close(self):
        assert self.n_remote <= self.send.shape[0] and self.n_local <= self.local.shape[0]
        for wait in self.open:
            wait()


def position():
    me = lax.axis_index("dp")
    t = lax.axis_index("tensor")
    zf, zn, y, x = me // 8, (me // 4) % 2, (me // 2) % 2, me % 2
    to_x, to_zn = 1 - 2 * x, 4 - 8 * zn
    group = [None, (me + to_x, t), (me + to_zn, t), (me + to_x + to_zn, t)]
    q = [zn * 2 + x, zn * 2 + 1 - x, (1 - zn) * 2 + x, (1 - zn) * 2 + 1 - x]
    far = (me + 8 - 16 * zf, t)
    side = (me + 2 - 4 * y, t)
    core = (me, 1 - t)
    return me, t, (zf, zn, y, x), q, group, far, side, core


def meet(devices):
    barrier = pltpu.get_barrier_semaphore()
    for device in devices:
        pl.semaphore_signal(barrier, inc=1, device_id=device, device_id_type=MESH)
    pl.semaphore_wait(barrier, len(devices))


def fold_lanes(values):
    width = values.shape[1]
    if width % 128:
        return values
    total = values[:, :128]
    for i in range(128, width, 128):
        total = total + values[:, i : i + 128]
    return total


def front_kernel(
    s_in, s_fg, s_og, s_out, w_g, w_u, s_d, cot, tok, gains, table, sizes,
    o_mix, o_out, o_g, o_u, o_d, o_n1, o_go, o_n2, o_pre, o_state, o_raw, o_res, o_mo, o_sc, o_aux, o_par, o_gate, o_up, o_coef,
    w_mix, w_out, n1, aux, pre, state, raw, part, core_in, half, peer_in, par, wide_g, wide_u, s_g, s_u, go_own, bound_row, full_g, full_u, gate, up, all_powers, coef,
    sq, sq_core, sq_half, sq_peer, res, mo, sc, n2, decay, add,
    send, recv, local, core_send, core_recv, sqc_send, sqc_recv, out_send, out_recv, x_send, x_recv,
):
    me, t, (zf, zn, y, x), q, group, far, side, core = position()
    rows, width = tok.shape
    share = rows // 2
    block = s_out.shape[0]
    feat = par.shape[1]
    hid = s_d.shape[0] // 4
    link = Copies(send, recv, local)
    get_g, get_u, get_cot = link.here(w_g, wide_g), link.here(w_u, wide_u), link.here(cot, go_own)
    meet(group[1:] + [far, side, core])

    def at(start, size, unit):
        return pl.ds(pl.multiple_of(start, unit), size)

    def pair(fz, c, fy):
        return at(fz * (8 * block) + c * (4 * block) + fy * (2 * block), 2 * block, 2 * block)

    mine = at(me * block, block, block)

    def row(r, tt):
        return at(r * rows + tt * share, share, share)

    def columns(r, fz):
        fx = x if r in (0, 2) else 1 - x
        fzn = zn if r in (0, 1) else 1 - zn
        return at((fz * 8 + fzn * 4 + t * 2 + fx) * block, block, block)

    mix_in, mix_own = [], []
    for k, s in enumerate((s_in, s_fg, s_og)):
        for fz in (0, 1):
            to = w_mix.at[mine, pl.ds(k * feat + fz * block, block)]
            mix_in += [link.remote(s.at[:, columns(r, fz)], to, group[r]) for r in (1, 2, 3)]
            mix_own.append(link.here(s.at[:, columns(0, fz)], to))
    out_rows = [at(z * block, block, block) for z in (zf, 1 - zf)]

    def out_copy(k, src, dst, device):
        return pltpu.make_async_remote_copy(
            src_ref=src,
            dst_ref=w_out.at[dst],
            send_sem=out_send.at[k],
            recv_sem=out_recv.at[k],
            device_id=device,
            device_id_type=MESH,
        )

    out_far = out_copy(0, s_out, out_rows[0], far)
    out_side = out_copy(1, s_out, out_rows[0], side)
    out_next = out_copy(2, w_out.at[out_rows[1]], out_rows[1], side)
    out_here = pltpu.make_async_copy(s_out, w_out.at[out_rows[0]], out_send.at[3])

    @pl.when(t == y)
    def _():
        out_far.start()
        out_side.start()
        out_here.start()

    norm_row = gains[0:1, :]

    def norm_rows(first):
        def some(j, carry):
            to = at(first + j * 16, 16, 16)
            value = tok[to, :].astype(f32)
            s = lax.rsqrt(jnp.mean(value * value, axis=1, keepdims=True) + epsilon)
            n1[to, :] = (value * s * norm_row).astype(bf16)
            return carry

        lax.fori_loop(0, share // 16, some, 0)

    norm_rows(t * share)
    n1_in = [link.remote(n1.at[row(0, t)], n1.at[row(r, t)], group[r]) for r in (1, 2)]

    count = sizes.shape[0] - 1
    slot_len = lax.shift_right_logical(jnp.int32(rows), sizes[count])
    position_row = lax.broadcasted_iota(jnp.int32, (1, rows), 1)
    slot = jnp.zeros((1, rows), jnp.int32)
    for j in range(1, count):
        slot = slot + (position_row >= j * slot_len).astype(jnp.int32)
    limit = jnp.zeros((1, rows), jnp.int32)
    for j in range(count):
        limit = limit + jnp.where(slot == j, sizes[j], 0)
    offset = position_row - slot * slot_len
    aux[0] = jnp.zeros(aux.shape[1:], f32)
    aux[0, 0:1, :] = (offset < limit).astype(f32)
    aux[0, 1:2, :] = (offset > 0).astype(f32)
    aux_in = [link.remote(aux.at[0], aux.at[r], group[r]) for r in (1, 2, 3)]

    norm_rows((1 - t) * share)
    for c in mix_own:
        c.wait()
    for c in mix_in:
        c.wait_recv()
    far_mix = [link.remote(w_mix.at[pair(zf, c, y)], w_mix.at[pair(zf, c, y)], far) for c in (0, 1)]
    side_mix = [link.remote(w_mix.at[pair(zf, c, y)], w_mix.at[pair(zf, c, y)], side) for c in (0, 1)]
    n1_in[1].wait_recv()
    n1_in.append(link.remote(n1.at[row(2, t)], n1.at[row(3, t)], group[1]))
    n1_core = [link.remote(n1.at[row(2, t)], n1.at[row(2, t)], core)]
    n1_in[0].wait_recv()
    n1_core.append(link.remote(n1.at[row(1, t)], n1.at[row(1, t)], core))
    shards = ((s_g, o_g), (s_u, o_u), (s_d, o_d))
    ffn_in, ffn_own = [], []

    def turn_round(wide, tall):
        size = min(128, wide.shape[1])

        def some(j, carry):
            to = at(j * size, size, size)
            tall[to, :] = wide[:, to].astype(f32).T.astype(bf16)
            return carry

        lax.fori_loop(0, wide.shape[1] // size, some, 0)

    def leave(s, o):
        units = [at(q[r] * hid, hid, 16) for r in range(4)]
        ffn_in.extend(link.remote(s.at[units[r]], o.at[:, mine], group[r]) for r in (1, 2, 3))
        ffn_own.append(link.here(s.at[units[0]], o.at[:, mine]))

    get_g.wait()
    turn_round(wide_g, s_g)
    leave(s_g, o_g)
    get_u.wait()
    turn_round(wide_u, s_u)
    leave(s_u, o_u)
    leave(s_d, o_d)

    logits = table[...]
    powers = jnp.exp(logits - jnp.max(logits, axis=0, keepdims=True))
    layer_ids = lax.broadcasted_iota(jnp.int32, logits.shape, 0)
    picked = jnp.where((layer_ids >= 1) & (layer_ids <= LAYER), powers, 0.0)
    bound_row[0:1, :] = jnp.sum(picked, axis=0, keepdims=True) / jnp.sum(powers, axis=0, keepdims=True)
    all_powers[...] = powers
    mine_powers = all_powers[:, mine]
    mine_shares = mine_powers / jnp.sum(mine_powers, axis=0, keepdims=True)
    ids = lax.broadcasted_iota(jnp.int32, mine_shares.shape, 0)
    mine_picked = ((ids >= 1) & (ids <= LAYER)).astype(f32)
    coef[...] = mine_shares * (mine_picked - jnp.sum(mine_shares * mine_picked, axis=0, keepdims=True))
    link.here(coef, o_coef, keep=True)
    for fz in (0, 1):
        par[0:1, fz * block : (fz + 1) * block] = bound_row[0:1, columns(0, fz)]
        par[1:2, fz * block : (fz + 1) * block] = gains[1:2, columns(0, fz)]
    get_cot.wait()
    valid_rows = aux[0].T[:, 0:1]
    first_half = lax.broadcasted_iota(jnp.int32, (share, 1), 0) * 0 + t
    valid_half = jnp.where(first_half == 0, valid_rows[:share], valid_rows[share:])
    go_own[...] = (go_own[...].astype(f32) * valid_half).astype(bf16)
    n1_in[2].wait_recv()
    n1_core.append(link.remote(n1.at[row(3, t)], n1.at[row(3, t)], core))
    for c in (0, 1):
        far_mix[c].wait_recv()
        side_mix.append(link.remote(w_mix.at[pair(1 - zf, c, y)], w_mix.at[pair(1 - zf, c, y)], side))

    @pl.when(t == y)
    def _():
        out_far.wait_recv()
        out_next.start()
        out_far.wait_send()
        out_side.wait_send()
        out_here.wait()
        out_next.wait_send()

    @pl.when(t != y)
    def _():
        out_side.wait_recv()
        out_next.wait_recv()

    far_ffn, side_ffn = [], ([], [], [])

    def start_ffn(i):
        o = shards[i][1]
        ffn_own[i].wait()
        for c in ffn_in[3 * i : 3 * i + 3]:
            c.wait_recv()
        far_ffn.append([link.remote(o.at[:, pair(zf, c, y)], o.at[:, pair(zf, c, y)], far) for c in (0, 1)])
        side_ffn[i].extend(link.remote(o.at[:, pair(zf, c, y)], o.at[:, pair(zf, c, y)], side) for c in (0, 1))

    def forward_ffn(i):
        o = shards[i][1]
        for c in (0, 1):
            far_ffn[i][c].wait_recv()
            side_ffn[i].append(link.remote(o.at[:, pair(1 - zf, c, y)], o.at[:, pair(1 - zf, c, y)], side))

    start_ffn(0)
    go_in = [link.remote(go_own, o_go.at[row(r, t)], group[r]) for r in (1, 2)]
    go_core = [link.remote(go_own, o_go.at[row(0, t)], core)]
    link.here(go_own, o_go.at[row(0, t)], keep=True)

    for c in side_mix + n1_core + aux_in:
        c.wait_recv()

    def core_copy(r):
        return pltpu.make_async_remote_copy(
            src_ref=part.at[row(r, 1 - t)],
            dst_ref=core_in.at[at(r * share, share, share)],
            send_sem=core_send.at[r],
            recv_sem=core_recv.at[r],
            device_id=core,
            device_id_type=MESH,
        )

    def sq_copy(r):
        return pltpu.make_async_remote_copy(
            src_ref=sq.at[row(r, 1 - t)],
            dst_ref=sq_core.at[at(r * share, share, share)],
            send_sem=sqc_send.at[r],
            recv_sem=sqc_recv.at[r],
            device_id=core,
            device_id_type=MESH,
        )

    bound = par[0:1, :]
    gain = par[1:2, :]

    def to_x(slot, r):
        from_rows, to_rows = at(r * share, share, share), at(slot * share, share, share)
        return [
            pltpu.make_async_remote_copy(
                src_ref=a.at[from_rows],
                dst_ref=b.at[to_rows],
                send_sem=x_send.at[i * 2 + slot],
                recv_sem=x_recv.at[i * 2 + slot],
                device_id=group[1],
                device_id_type=MESH,
            )
            for i, (a, b) in enumerate(((half, peer_in), (sq_half, sq_peer)))
        ]

    def hand_over(r):
        core_copy(r).wait()
        sq_copy(r).wait()

        def some(j, carry):
            to = at(r * share + j * 16, 16, 16)
            mine_rows = at(r * rows + t * share + j * 16, 16, 16)
            half[to, :] = (part[mine_rows, :].astype(f32) + core_in[to, :].astype(f32)).astype(bf16)
            sq_half[to, :] = sq[mine_rows, :] + sq_core[to, :]
            return carry

        lax.fori_loop(0, share // 16, some, 0)

    def piece(i, carry):
        r = 3 - 2 * i + 3 * (i // 2)
        here = at(r * rows, rows, rows)
        pre[here, :] = jnp.dot(n1[here, :], w_mix[...], preferred_element_type=f32)
        masks = aux[r].T
        valid = masks[:, 0:1]
        keep = masks[:, 1:2]
        forget = bound + (1.0 - bound) * jax.nn.sigmoid(pre[here, feat : 2 * feat])
        input_pre = pre[here, 0:feat]
        add[...] = input_pre * jax.nn.sigmoid(input_pre) * (1.0 - forget) * valid
        decay[...] = forget * keep
        scan_rows(decay, add, state.at[here, :], False)
        held = state[here, :]
        outgate_pre = pre[here, 2 * feat :]
        raw[here, :] = (held * gain * (outgate_pre * jax.nn.sigmoid(outgate_pre))).astype(bf16)
        sq[here, :] = fold_lanes(held * held)
        part[here, :] = jnp.dot(raw[here, :], w_out[...], preferred_element_type=f32).astype(bf16)
        core_copy(r).start()
        sq_copy(r).start()

        @pl.when(i > 0)
        def _():
            before = 5 - 2 * i + 3 * ((i - 1) // 2)
            hand_over(before)

            @pl.when(i < 3)
            def _():
                for c in to_x(i - 1, before):
                    c.start()

        return carry

    lax.fori_loop(0, 4, piece, 0)
    start_ffn(1)

    link.here(w_mix, o_mix, keep=True)
    link.here(w_out, o_out, keep=True)
    link.here(n1, o_n1, keep=True)
    link.here(pre, o_pre, keep=True)
    link.here(state, o_state, keep=True)
    link.here(raw, o_raw, keep=True)
    link.here(aux, o_aux, keep=True)
    link.here(par, o_par, keep=True)

    def spread(o, incoming, cores):
        incoming[1].wait_recv()
        incoming.append(link.remote(o.at[row(2, t)], o.at[row(3, t)], group[1]))
        cores.append(link.remote(o.at[row(2, t)], o.at[row(2, t)], core))
        incoming[0].wait_recv()
        cores.append(link.remote(o.at[row(1, t)], o.at[row(1, t)], core))

    def spread_last(o, incoming, cores):
        incoming[2].wait_recv()
        cores.append(link.remote(o.at[row(3, t)], o.at[row(3, t)], core))

    hand_over(0)
    for c in to_x(0, 3):
        c.wait()

    def pass_on(j, carry):
        two = at(2 * share + j * 16, 16, 16)
        half[two, :] = (half[two, :].astype(f32) + peer_in[at(j * 16, 16, 16), :].astype(f32)).astype(bf16)
        sq_half[two, :] = sq_half[two, :] + sq_peer[at(j * 16, 16, 16), :]
        return carry

    lax.fori_loop(0, share // 16, pass_on, 0)
    third = pl.ds(2 * share, share)
    to_z = [
        link.remote(half.at[third], peer_in.at[third], group[2]),
        link.remote(sq_half.at[third], sq_peer.at[third], group[2]),
    ]
    spread(o_go, go_in, go_core)
    forward_ffn(0)
    for c in to_x(1, 1):
        c.wait()
    for c in to_z:
        c.wait_recv()
    total_sq = sq_half[0:share, :] + sq_peer[share : 2 * share, :] + sq_peer[2 * share : 3 * share, :]
    scale = lax.rsqrt(jnp.sum(total_sq, axis=1, keepdims=True) / width + epsilon)
    sc[...] = jnp.broadcast_to(scale, sc.shape)
    chunk = min(share, 16)

    def finish(i, carry):
        to = at(i * chunk, chunk, chunk)
        total = part[at(t * share + i * chunk, chunk, chunk), :].astype(f32) + core_in[to, :].astype(f32)
        for r in (1, 2):
            total = total + peer_in[at(r * share + i * chunk, chunk, chunk), :].astype(f32)
        mixed = total * sc[to, 0:1]
        value = tok[at(t * share + i * chunk, chunk, chunk), :].astype(f32) + mixed
        mo[to, :] = mixed
        res[to, :] = value
        scale_two = lax.rsqrt(jnp.mean(value * value, axis=1, keepdims=True) + epsilon)
        n2[to, :] = (value * scale_two * gains[2:3, :]).astype(bf16)
        return carry

    lax.fori_loop(0, share // chunk, finish, 0)
    n2_in = [link.remote(n2, o_n2.at[row(r, t)], group[r]) for r in (1, 2)]
    n2_core = [link.remote(n2, o_n2.at[row(0, t)], core)]
    n2_here = link.here(n2, o_n2.at[row(0, t)])
    link.here(res, o_res, keep=True)
    link.here(mo, o_mo, keep=True)
    link.here(sc, o_sc, keep=True)
    start_ffn(2)
    spread_last(o_go, go_in, go_core)
    forward_ffn(1)
    spread(o_n2, n2_in, n2_core)
    spread_last(o_n2, n2_in, n2_core)

    forward_ffn(2)

    for c in side_ffn[0]:
        c.wait_recv()
    get_full = link.here(o_g, full_g)
    for c in n2_core:
        c.wait_recv()
    n2_here.wait()
    get_rows = link.here(o_n2, part)
    get_full.wait()
    get_rows.wait()

    def product(full, made):
        def some(j, carry):
            to = at(j * rows, rows, rows)
            made[:, to] = lax.dot_general(
                full[...], part[to, :], (((1,), (1,)), ((), ())), preferred_element_type=f32
            )
            return carry

        lax.fori_loop(0, 4, some, 0)

    product(full_g, gate)
    link.here(gate, o_gate, keep=True)
    for c in side_ffn[1]:
        c.wait_recv()
    get_full = link.here(o_u, full_u)
    get_full.wait()
    product(full_u, up)
    link.here(up, o_up, keep=True)
    for c in side_ffn[2] + go_core:
        c.wait_recv()
    link.close()


def front(s_in, s_fg, s_og, s_out, w_g, w_u, s_d, cot, tok, gains, table, sizes):
    rows, width = tok.shape
    share, group_rows = rows // 2, 4 * rows
    block = s_out.shape[0]
    feat, hid = 2 * block, s_d.shape[0] // 4
    lanes = 128 if feat % 128 == 0 else feat
    any_spec = pl.BlockSpec(memory_space=pl.ANY)
    vmem_spec = pl.BlockSpec(memory_space=pltpu.VMEM)
    made = jax.ShapeDtypeStruct
    outs = [
        made((width, 3 * feat), bf16),
        made((feat, width), bf16),
        made((hid, width), bf16),
        made((hid, width), bf16),
        made((hid, width), bf16),
        made((group_rows, width), bf16),
        made((group_rows, width), bf16),
        made((group_rows, width), bf16),
        made((group_rows, 3 * feat), f32),
        made((group_rows, feat), f32),
        made((group_rows, feat), bf16),
        made((share, width), f32),
        made((share, width), f32),
        made((share, 128), f32),
        made((4, 8, rows), f32),
        made((2, feat), f32),
        made((hid, group_rows), f32),
        made((hid, group_rows), f32),
        made((table.shape[0], block), f32),
    ]
    scratch = [
        pltpu.VMEM((width, 3 * feat), bf16),
        pltpu.VMEM((feat, width), bf16),
        pltpu.VMEM((group_rows, width), bf16),
        pltpu.VMEM((4, 8, rows), f32),
        pltpu.VMEM((group_rows, 3 * feat), f32),
        pltpu.VMEM((group_rows, feat), f32),
        pltpu.VMEM((group_rows, feat), bf16),
        pltpu.VMEM((group_rows, width), bf16),
        pltpu.VMEM((4 * share, width), bf16),
        pltpu.VMEM((4 * share, width), bf16),
        pltpu.VMEM((4 * share, width), bf16),
        pltpu.VMEM((2, feat), f32),
        pltpu.VMEM(w_g.shape, bf16),
        pltpu.VMEM(w_u.shape, bf16),
        pltpu.VMEM((4 * hid, block), bf16),
        pltpu.VMEM((4 * hid, block), bf16),
        pltpu.VMEM((share, width), bf16),
        pltpu.VMEM((8, width), f32),
        pltpu.VMEM((hid, width), bf16),
        pltpu.VMEM((hid, width), bf16),
        pltpu.VMEM((hid, group_rows), f32),
        pltpu.VMEM((hid, group_rows), f32),
        pltpu.VMEM(table.shape, f32),
        pltpu.VMEM((table.shape[0], block), f32),
        pltpu.VMEM((group_rows, lanes), f32),
        pltpu.VMEM((4 * share, lanes), f32),
        pltpu.VMEM((4 * share, lanes), f32),
        pltpu.VMEM((4 * share, lanes), f32),
        pltpu.VMEM((share, width), f32),
        pltpu.VMEM((share, width), f32),
        pltpu.VMEM((share, 128), f32),
        pltpu.VMEM((share, width), bf16),
        pltpu.VMEM((rows, feat), f32),
        pltpu.VMEM((rows, feat), f32),
        pltpu.SemaphoreType.DMA((88,)),
        pltpu.SemaphoreType.DMA((88,)),
        pltpu.SemaphoreType.DMA((32,)),
    ] + [pltpu.SemaphoreType.DMA((4,))] * 8
    return pl.pallas_call(
        front_kernel,
        in_specs=[any_spec] * 8 + [vmem_spec] * 3 + [pl.BlockSpec(memory_space=pltpu.SMEM)],
        out_specs=[any_spec] * len(outs),
        out_shape=outs,
        scratch_shapes=scratch,
        compiler_params=pltpu.CompilerParams(
            collective_id=1, has_side_effects=True, vmem_limit_bytes=56 << 20
        ),
        name="front",
    )(s_in, s_fg, s_og, s_out, w_g, w_u, s_d, cot, tok, gains, table, sizes)


def back_kernel(
    h_d, h_g, h_u, n2, go, w_g, w_u, w_d, n1, w_mix_in, w_out_in, pre, state, raw, aux_in,
    par, tok, res, mo, sc, gains,
    o_g, o_u, o_d, o_mix, o_out, o_tok, o_blk, o_vec,
    left, right, gmix, dw_d, dw_g, dw_u, dw_mix, yr_d, yr_g, yr_u, yr_mix, zr_d, zr_g, zr_u, zr_mix,
    own, half, core_in, core_blk, peer_in, peer_blk, w_mix, w_out, aux, pre_b, state_b, raw_b,
    grads, grads_t, decay, add, yr_out, zr_out, hid_a, hid_b,
    gres, gm_own, scalars, scal_all, sums, vec, vec_in,
    send, recv, local, core_send, core_recv, out_send, out_recv, piece_sem,
):
    me, t, (zf, zn, y, x), q, group, far, side, core = position()
    rows, width = tok.shape
    share = rows // 2
    block = width // 16
    feat = par.shape[1]
    link = Copies(send, recv, local)
    meet(group[1:] + [far, side, core])

    def at(start, size, unit):
        return pl.ds(pl.multiple_of(start, unit), size)

    def pair(fz, c, fy):
        return at(fz * (8 * block) + c * (4 * block) + fy * (2 * block), 2 * block, 2 * block)

    def row(r, tt):
        return at(r * rows + tt * share, share, share)

    def rel(r):
        return pl.ds(r * share, share)

    hid_rows = pl.ds(0, w_g.shape[0])
    full_g, full_u = left.at[hid_rows], gmix.at[hid_rows]
    get_g = [link.here(h_g, hid_a), link.here(n2, right)]
    get_u = link.here(h_u, hid_b)
    get_two = [link.here(w_g, full_g), link.here(w_u, full_u)]
    get_go = [link.here(go.at[row(0, t)], gm_own)]
    get_w_d = link.here(w_d, dw_d)
    get_aux = [link.here(aux_in, aux), link.here(w_mix_in, w_mix)]
    order = (3, 1, 2, 0)

    def stage(r):
        i = order.index(r)
        return w_out if i == 3 else dw_mix.at[i]

    def staged(r, tt):
        return w_out.at[at(tt * share, share, share)] if r == 0 else stage(r).at[tt]

    def products(terms):
        wide = 4 * block

        def at_piece(r, store):
            here = at(r * rows, rows, rows)

            def some(j, carry):
                to = at(j * wide, wide, wide)
                total = None
                for hid, weight in terms:
                    one = lax.dot_general(
                        hid[:, here], weight[:, to], (((0,), (0,)), ((), ())), preferred_element_type=f32
                    )
                    total = one if total is None else total + one
                store(to, total.astype(bf16))
                return carry

            lax.fori_loop(0, width // wide, some, 0)

        return at_piece

    def all_pieces(terms, incoming):
        at_piece = products(terms)
        copies = {}
        for i, r in enumerate(order):
            if r:

                def store(to, value):
                    dw_mix[i, 0, :, to] = value[:share]
                    dw_mix[i, 1, :, to] = value[share:]

            else:

                def store(to, value):
                    w_out[:, to] = value

            at_piece(r, store)
            copies[r] = link.remote(staged(r, 1 - t), incoming.at[rel(r)], core)
        return copies

    def two_rows(r, j):
        if r == 0:
            return w_out[at(t * share + j * 16, 16, 16), :].astype(f32)
        return dw_mix[order.index(r), t, at(j * 16, 16, 16), :].astype(f32)

    def own_rows(r, j):
        return own[at(r * share + j * 16, 16, 16), :].astype(f32)

    def add_half(r, source, incoming, held):
        def some(j, carry):
            to = at(r * share + j * 16, 16, 16)
            held[to, :] = (source(r, j) + incoming[to, :].astype(f32)).astype(bf16)
            return carry

        lax.fori_loop(0, share // 16, some, 0)

    def over_cores(arrived, source, incoming, held, peers):
        sent = []
        for r in (3, 1, 2, 0):
            arrived[r].wait_recv()
            if r:
                add_half(r, source, incoming, held)
            if r % 2:
                sent.append(link.remote(held.at[rel(r)], peers.at[rel(len(sent))], group[1]))
        return sent

    def pass_on(sent, held, peers):
        sent[0].wait_recv()

        def some(j, carry):
            two = at(2 * share + j * 16, 16, 16)
            held[two, :] = (held[two, :].astype(f32) + peers[at(j * 16, 16, 16), :].astype(f32)).astype(bf16)
            return carry

        lax.fori_loop(0, share // 16, some, 0)
        sent.append(link.remote(held.at[rel(2)], peers.at[rel(2)], group[2]))


    def weight_grad(hid, other, dw, first, count):
        wide = 4 * block

        def columns(i, carry):
            to = at(((1 - zf) * 2 + i - (i // 2) * 4 * (1 - zf)) * wide, wide, wide)
            made = jnp.dot(hid[...], other[:, to], preferred_element_type=f32).astype(bf16)
            if len(dw.shape) == 2:
                dw[:, to] = made
            else:
                dw[:, :, :, to] = made.reshape(dw.shape[:3] + (wide,))
            return carry

        lax.fori_loop(first, first + count, columns, 0)

    def cut(ref, cols):
        return ref.at[:, cols] if len(ref.shape) == 2 else ref.at[:, :, :, cols]

    def side_send(dw, yr, slot):
        fz = 1 - zf if slot == 0 else zf
        return [
            link.remote(cut(dw, pair(fz, c, 1 - y)), cut(yr, pl.ds((slot * 2 + c) * 2 * block, 2 * block)), side)
            for c in (0, 1)
        ]

    def add_columns(dw, to, others):
        if len(dw.shape) == 2:
            size = 64 if dw.shape[0] % 64 == 0 else dw.shape[0]
            steps = dw.shape[0] // size
        else:
            steps = dw.shape[0] * dw.shape[1]

        def some(j, carry):
            if len(dw.shape) == 2:
                lead = (at(j * size, size, size),)
            else:
                lead = (j // dw.shape[1], j % dw.shape[1], slice(None))
            total = dw[lead + (to,)].astype(f32)
            for ref, cols in others:
                total = total + ref[lead + (cols,)].astype(f32)
            dw[lead + (to,)] = total.astype(bf16)
            return carry

        lax.fori_loop(0, steps, some, 0)

    def part_of(i):
        return pl.ds(i * 2 * block, 2 * block)

    def second_hop(hop, dw, yr, zr):
        sent = []
        for c in (0, 1):
            hop[c].wait_recv()
            add_columns(dw, pair(1 - zf, c, y), [(yr, part_of(c))])
            sent.append(link.remote(cut(dw, pair(1 - zf, c, y)), cut(zr, part_of(c)), far))
        return sent

    def last_hop(near, sent, dw, yr, zr, out):
        for c in (0, 1):
            near[c].wait_recv()
            sent[c].wait_recv()
            add_columns(dw, pair(zf, c, y), [(yr, part_of(2 + c)), (zr, part_of(c))])

        def owner(r):
            fx = x if r in (0, 2) else 1 - x
            fzn = zn if r in (0, 1) else 1 - zn
            return at((zf * 8 + fzn * 4 + y * 2 + fx) * block, block, block)

        if len(dw.shape) == 2:
            place = out.at[q[0]]
            link.here(dw.at[:, owner(0)], place, keep=True)
            return [link.remote(dw.at[:, owner(r)], place, group[r]) for r in (1, 2, 3)]
        place = out.at[:, :, zn, t, x]
        kept = link.here(cut(dw, owner(0)), place)
        sent = [link.remote(cut(dw, owner(r)), place, group[r]) for r in (1, 2, 3)]
        kept.wait()
        return sent

    for c in get_g:
        c.wait()
    weight_grad(hid_a, right, dw_g, 0, 2)
    hop_g = side_send(dw_g, yr_g, 0)
    get_u.wait()
    for c in get_two:
        c.wait()
    two_core = all_pieces([(hid_a, full_g), (hid_b, full_u)], core_in)

    two_peer = over_cores(two_core, two_rows, core_in, half, peer_in)
    weight_grad(hid_b, right, dw_u, 0, 2)
    get_left = link.here(go, left)
    weight_grad(hid_a, right, dw_g, 2, 2)
    get_d = link.here(h_d, hid_a)
    far_g = second_hop(hop_g, dw_g, yr_g, zr_g)
    hop_u = side_send(dw_u, yr_u, 0)
    pass_on(two_peer, half, peer_in)
    weight_grad(hid_b, right, dw_u, 2, 2)

    for c in two_peer[1:]:
        c.wait_recv()
    for c in get_go:
        c.wait()
    gain_two = gains[2:3, :]
    sums[...] = jnp.zeros_like(sums)
    step = 16

    def residual_rows(j, carry):
        to = at(j * step, step, step)
        total = two_rows(0, j) + core_in[to, :].astype(f32)
        for r in (1, 2):
            total = total + peer_in[at(r * share + j * step, step, step), :].astype(f32)
        value = res[to, :]
        s = lax.rsqrt(jnp.mean(value * value, axis=1, keepdims=True) + epsilon)
        weighted = total * gain_two
        grad = (
            gm_own[to, :].astype(f32)
            + s * weighted
            - value * (s * s * s) * jnp.mean(weighted * value, axis=1, keepdims=True)
        )
        gres[to, :] = grad
        low = grad.astype(bf16)
        gm_own[to, :] = low
        dot = jnp.sum(low.astype(f32) * mo[to, :], axis=1, keepdims=True)
        scale = sc[to, 0:1]
        sc[to, 1:2] = dot / (scale * width)
        sums[1:2, :] += jnp.sum(total * value * s, axis=0, keepdims=True)
        return carry

    lax.fori_loop(0, share // step, residual_rows, 0)
    scalars[...] = sc[...].T[0:8, :]

    def scal(r, tt):
        return scal_all.at[r * 2 + tt]

    gm_in = [link.remote(gm_own, gmix.at[row(r, t)], group[r]) for r in (1, 2)]
    sc_in = [link.remote(scalars, scal(r, t), group[r]) for r in (1, 2, 3)]
    gm_core = [link.remote(gm_own, gmix.at[row(0, t)], core), link.remote(scalars, scal(0, t), core)]
    gm_here = [link.here(gm_own, gmix.at[row(0, t)]), link.here(scalars, scal(0, t))]
    for c in (get_d, get_w_d, get_left):
        c.wait()
    link.sent(two_core.values())
    blk_core = all_pieces([(hid_a, dw_d)], core_blk)
    blk_own = [link.here(staged(r, t), own.at[rel(r)]) for r in order]
    weight_grad(hid_a, left, dw_d, 0, 2)
    hop_d = side_send(dw_d, yr_d, 0)
    far_u = second_hop(hop_u, dw_u, yr_u, zr_u)
    near_g = side_send(dw_g, yr_g, 1)
    gm_in[1].wait_recv()
    gm_in.append(link.remote(gmix.at[row(2, t)], gmix.at[row(3, t)], group[1]))
    gm_core.append(link.remote(gmix.at[row(2, t)], gmix.at[row(2, t)], core))
    gm_in[0].wait_recv()
    gm_core.append(link.remote(gmix.at[row(1, t)], gmix.at[row(1, t)], core))
    for i, r in enumerate((1, 2, 3)):
        sc_in[i].wait_recv()
        gm_core.append(link.remote(scal(r, t), scal(r, t), core))
    weight_grad(hid_a, left, dw_d, 2, 2)
    get_n1 = link.here(n1, left)
    near_u = side_send(dw_u, yr_u, 1)
    for c in blk_own:
        c.wait()
    gm_in[2].wait_recv()
    gm_core.append(link.remote(gmix.at[row(3, t)], gmix.at[row(3, t)], core))
    far_d = second_hop(hop_d, dw_d, yr_d, zr_d)
    near_d = side_send(dw_d, yr_d, 1)
    blk_peer = over_cores(blk_core, own_rows, core_blk, own, peer_blk)
    link.sent(blk_core.values())
    link.sent(two_peer)
    get_aux.append(link.here(w_out_in, w_out))
    for c in get_aux + [get_n1] + gm_here:
        c.wait()
    for c in gm_core:
        c.wait_recv()

    def one_core(r):
        return pltpu.make_async_remote_copy(
            src_ref=right.at[row(r, 1 - t)],
            dst_ref=core_in.at[at(r * share, share, share)],
            send_sem=core_send.at[r],
            recv_sem=core_recv.at[r],
            device_id=core,
            device_id_type=MESH,
        )

    def fetch(r):
        here = at(r * rows, rows, rows)
        return [
            pltpu.make_async_copy(pre.at[here], pre_b, piece_sem.at[0]),
            pltpu.make_async_copy(state.at[here], state_b, piece_sem.at[1]),
            pltpu.make_async_copy(raw.at[here], raw_b, piece_sem.at[2]),
        ]

    bound = par[0:1, :]
    gain = par[1:2, :]
    gain_sums = sums.at[2:4, 0:feat]
    mixed_t = hid_b.at[0:feat]
    dw_out = w_out

    def one_rows(r, j):
        return right[at(r * rows + t * share + j * 16, 16, 16), :].astype(f32)

    def one_x(slot, r):
        return pltpu.make_async_remote_copy(
            src_ref=half.at[at(r * share, share, share)],
            dst_ref=peer_in.at[at(slot * share, share, share)],
            send_sem=core_send.at[4 + slot],
            recv_sem=core_recv.at[4 + slot],
            device_id=group[1],
            device_id_type=MESH,
        )

    def hand_over(r):
        one_core(r).wait()
        add_half(r, one_rows, core_in, half)

    def piece(i, carry):
        r = 3 - 2 * i + 3 * (i // 2)
        here = at(r * rows, rows, rows)
        copies = fetch(r)
        for c in copies:
            c.start()
        up = lax.dot_general(
            gmix[here, :], w_out[...], (((1,), (1,)), ((), ())), preferred_element_type=f32
        )
        masks = aux[r].T
        valid = masks[:, 0:1]
        keep = masks[:, 1:2]
        scale_parts = [scal_all[r * 2 + tt].T for tt in (0, 1)]
        scale = jnp.concatenate([p[:, 0:1] for p in scale_parts], axis=0)
        dot_mean = jnp.concatenate([p[:, 1:2] for p in scale_parts], axis=0)
        for c in copies:
            c.wait()
        at_row = lax.broadcasted_iota(jnp.int32, (rows, feat), 0)
        input_pre = pre_b[:, :feat]
        outgate_pre = pre_b[:, 2 * feat :]
        held = state_b[...]
        sig_out = jax.nn.sigmoid(outgate_pre)
        act_out = outgate_pre * sig_out
        scaled = up * (held * scale)
        grads[:, 2 * feat :] = scaled * gain * (sig_out * (1.0 + outgate_pre * (1.0 - sig_out)))
        add[...] = scale * (gain * act_out * up) - held * (scale * scale * scale * dot_mean)
        gain_sums[0:1, :] += jnp.sum(scaled * act_out, axis=0, keepdims=True)
        sig_forget = jax.nn.sigmoid(pre_b[:, feat : 2 * feat])
        forget = bound + (1.0 - bound) * sig_forget
        decay[...] = jnp.where(at_row < rows - 1, pltpu.roll(forget * keep, rows - 1, 0), 0.0)
        scan_rows(decay, add, add, True)
        grad_state = add[...]
        before = jnp.where(at_row > 0, pltpu.roll(held, 1, 0), 0.0)
        sig_in = jax.nn.sigmoid(input_pre)
        grad_forget = grad_state * (before * keep - input_pre * sig_in * valid)
        grads[:, :feat] = (
            grad_state * (1.0 - forget) * valid * (sig_in * (1.0 + input_pre * (1.0 - sig_in)))
        )
        grads[:, feat : 2 * feat] = grad_forget * (1.0 - bound) * sig_forget * (1.0 - sig_forget)
        gain_sums[1:2, :] += jnp.sum(grad_forget * (1.0 - sig_forget), axis=0, keepdims=True)
        low = grads[...].astype(bf16)
        right[here, :] = lax.dot_general(
            low, w_mix[...], (((1,), (1,)), ((), ())), preferred_element_type=f32
        ).astype(bf16)
        one_core(r).start()
        grads_t[:, here] = grads[...].T.astype(bf16)
        mixed_t[:, here] = (raw_b[...].astype(f32) * scale).T.astype(bf16)

        @pl.when(i > 0)
        def _():
            before_r = 5 - 2 * i + 3 * ((i - 1) // 2)
            hand_over(before_r)

            @pl.when(i < 3)
            def _():
                one_x(i - 1, before_r).start()

        return carry

    lax.fori_loop(0, 4, piece, 0)

    one_core(0).wait()
    pass_on(blk_peer, own, peer_blk)

    weight_grad(grads_t, left, dw_mix, 0, 2)
    hop_mix = side_send(dw_mix, yr_mix, 0)
    weight_grad(grads_t, left, dw_mix, 2, 2)

    def out_columns(i, carry):
        to = at(i * (4 * block), 4 * block, 4 * block)
        dw_out[:, to] = jnp.dot(mixed_t[...], gmix[:, to], preferred_element_type=f32).astype(bf16)
        return carry

    lax.fori_loop(0, 4, out_columns, 0)
    near_rows = at(zf * block, block, block)
    far_rows = at((1 - zf) * block, block, block)

    def out_copy(k, src, dst, device):
        return pltpu.make_async_remote_copy(
            src_ref=src,
            dst_ref=dst,
            send_sem=out_send.at[k],
            recv_sem=out_recv.at[k],
            device_id=device,
            device_id_type=MESH,
        )

    out_side = out_copy(0, dw_out, yr_out, side)
    out_far = out_copy(1, dw_out.at[far_rows], zr_out, far)
    out_core = out_copy(2, dw_out.at[near_rows], o_out, core)
    out_here = pltpu.make_async_copy(dw_out.at[near_rows], o_out, out_send.at[3])

    @pl.when(t != y)
    def _():
        out_side.start()

    one_x(0, 3).wait()

    def one_on(j, carry):
        two = at(2 * share + j * 16, 16, 16)
        half[two, :] = (half[two, :].astype(f32) + peer_in[at(j * 16, 16, 16), :].astype(f32)).astype(bf16)
        return carry

    lax.fori_loop(0, share // 16, one_on, 0)
    one_z = link.remote(half.at[rel(2)], peer_in.at[rel(2)], group[2])
    near_mix = side_send(dw_mix, yr_mix, 1)
    back_g = last_hop(near_g, far_g, dw_g, yr_g, zr_g, o_g)
    back_u = last_hop(near_u, far_u, dw_u, yr_u, zr_u, o_u)
    far_mix = second_hop(hop_mix, dw_mix, yr_mix, zr_mix)

    @pl.when(t == y)
    def _():
        out_side.wait_recv()
        add_columns(dw_out, pl.ds(0, width), [(yr_out, pl.ds(0, width))])
        out_far.start()

    one_x(1, 1).wait()
    one_z.wait_recv()
    gain_one = gains[0:1, :]

    def token_rows(j, carry):
        to = at(j * step, step, step)
        total = one_rows(0, j) + core_in[to, :].astype(f32)
        for r in (1, 2):
            total = total + peer_in[at(r * share + j * step, step, step), :].astype(f32)
        value = tok[at(t * share + j * step, step, step), :].astype(f32)
        s = lax.rsqrt(jnp.mean(value * value, axis=1, keepdims=True) + epsilon)
        weighted = total * gain_one
        gres[to, :] = (
            gres[to, :]
            + s * weighted
            - value * (s * s * s) * jnp.mean(weighted * value, axis=1, keepdims=True)
        )
        sums[0:1, :] += jnp.sum(total * value * s, axis=0, keepdims=True)
        return carry

    lax.fori_loop(0, share // step, token_rows, 0)
    tok_rows = at(t * share, share, share)
    tok_core = link.remote(gres, o_tok.at[tok_rows], core)
    link.here(gres, o_tok.at[tok_rows], keep=True)

    vec[0] = jnp.zeros(vec.shape[1:], f32)
    for k in (0, 1):
        for i in range(16):
            vec[0, k * 16 + i : k * 16 + i + 1, :] = sums[k : k + 1, i * block : (i + 1) * block]
    for k in (2, 3):
        for i in (0, 1):
            vec[0, pl.ds(k * 16 + i * 8 + zn * 4 + t * 2 + x, 1), :] = sums[
                k : k + 1, i * block : (i + 1) * block
            ]
    partners = [group[1], group[2], side, far, core]
    turn = [link.remote(vec.at[0], vec_in.at[0], partners[0])]

    def next_turn():
        k = len(turn)
        turn[k - 1].wait_recv()
        vec[k] = vec[k - 1] + vec_in[k - 1]
        if k < len(partners):
            turn.append(link.remote(vec.at[k], vec_in.at[k], partners[k]))

    next_turn()
    back_d = last_hop(near_d, far_d, dw_d, yr_d, zr_d, o_d)
    next_turn()
    next_turn()
    for c in blk_peer[1:]:
        c.wait_recv()

    def block_rows(j, carry):
        to = at(j * step, step, step)
        total = own_rows(0, j) + core_blk[to, :].astype(f32)
        for r in (1, 2):
            total = total + peer_blk[at(r * share + j * step, step, step), :].astype(f32)
        gm_own[to, :] = (res[to, :] + total).astype(bf16)
        return carry

    link.sent(gm_in[:2] + gm_core[:1])
    lax.fori_loop(0, share // step, block_rows, 0)
    link.here(gm_own, o_blk, keep=True)
    next_turn()
    next_turn()
    link.here(vec.at[5], o_vec, keep=True)
    back_mix = last_hop(near_mix, far_mix, dw_mix, yr_mix, zr_mix, o_mix)

    @pl.when(t == y)
    def _():
        out_far.wait_recv()

        def some(j, carry):
            to = at(zf * block + j * 16, 16, 16)
            dw_out[to, :] = (
                dw_out[to, :].astype(f32) + zr_out[at(j * 16, 16, 16), :].astype(f32)
            ).astype(bf16)
            return carry

        lax.fori_loop(0, block // 16, some, 0)
        out_core.start()
        out_here.start()
        out_far.wait_send()
        out_core.wait_send()
        out_here.wait()

    @pl.when(t != y)
    def _():
        out_side.wait_send()
        out_core.wait_recv()

    for c in back_mix:
        c.wait_recv()
    mix_core = link.remote(o_mix.at[:, :, :, t], o_mix.at[:, :, :, t], core)
    for c in back_d + back_g + back_u + [mix_core, tok_core]:
        c.wait_recv()
    link.close()


def back(*arrays):
    par, tok = arrays[15], arrays[16]
    rows, width = tok.shape
    share, group_rows = rows // 2, 4 * rows
    feat, hid, block = par.shape[1], arrays[0].shape[0], width // 16
    made = jax.ShapeDtypeStruct
    vm = pltpu.VMEM
    outs = [
        made((4, hid, block), bf16),
        made((4, hid, block), bf16),
        made((4, hid, block), bf16),
        made((3, 2, 2, 2, 2, block, block), bf16),
        made((block, width), bf16),
        made((rows, width), f32),
        made((share, width), bf16),
        made((64, block), f32),
    ]
    scratch = (
        [vm((group_rows, width), bf16)] * 3
        + [vm((hid, width), bf16)] * 3
        + [vm((3, 2, block, width), bf16)]
        + [vm((hid, width // 2), bf16)] * 3
        + [vm((3, 2, block, width // 2), bf16)]
        + [vm((hid, width // 4), bf16)] * 3
        + [vm((3, 2, block, width // 4), bf16)]
        + [vm((4 * share, width), bf16)] * 4
        + [vm((3 * share, width), bf16)] * 2
        + [
            vm((width, 3 * feat), bf16),
            vm((feat, width), bf16),
            vm(arrays[14].shape, f32),
            vm((rows, 3 * feat), f32),
            vm((rows, feat), f32),
            vm((rows, feat), bf16),
            vm((rows, 3 * feat), f32),
            vm((3 * feat, group_rows), bf16),
            vm((rows, feat), f32),
            vm((rows, feat), f32),
            vm((feat, width), bf16),
            vm((block, width), bf16),
            vm((hid, group_rows), bf16),
            vm((hid, group_rows), bf16),
            vm((share, width), f32),
            vm((share, width), bf16),
            vm((8, share), f32),
            vm((8, 8, share), f32),
            vm((4, width), f32),
            vm((6, 64, block), f32),
            vm((5, 64, block), f32),
            pltpu.SemaphoreType.DMA((96,)),
            pltpu.SemaphoreType.DMA((96,)),
            pltpu.SemaphoreType.DMA((32,)),
        ]
        + [pltpu.SemaphoreType.DMA((6,))] * 5
    )
    any_spec = pl.BlockSpec(memory_space=pl.ANY)
    vmem_spec = pl.BlockSpec(memory_space=pltpu.VMEM)
    return pl.pallas_call(
        back_kernel,
        in_specs=[any_spec] * 15 + [vmem_spec] * 6,
        out_specs=[any_spec] * len(outs),
        out_shape=outs,
        scratch_shapes=scratch,
        compiler_params=pltpu.CompilerParams(
            collective_id=2, has_side_effects=True, vmem_limit_bytes=63 << 20
        ),
        name="back",
    )(*arrays)


def body(
    n_dp,
    n_t,
    tokens_in,
    input_proj,
    forget_proj,
    outgate_proj,
    output_proj,
    glu_gate,
    glu_up,
    glu_down,
    norm_gain,
    mixer_gain,
    ffn_gain,
    bound_table,
    lengths,
    bucket,
    cotangent,
):
    depth = n_dp.bit_length() - 1
    tp_bits = (2, 0)
    fs_bits = tuple(b for b in reversed(range(depth)) if b not in tp_bits)
    t_depth = n_t.bit_length() - 1
    own_bits, free_bits = fs_bits[len(fs_bits) - t_depth :], fs_bits[: len(fs_bits) - t_depth]
    n_tp = 4
    tp_mask = (0, 1, 4, 5)
    axis_of = {b: depth - 1 - b for b in range(depth)}

    me = lax.axis_index("dp")
    t = lax.axis_index("tensor")
    bit = {b: (me >> b) & 1 for b in range(depth)}
    t_bit = {b: (t >> (t_depth - 1 - i)) & 1 for i, b in enumerate(own_bits)}
    q = bit[2] * 2 + bit[0]

    rows, width = tokens_in.shape
    share = cotangent.shape[0]
    block = width // n_dp
    free = 2 ** len(free_bits)
    feat = free * block

    def swap(values, mask):
        return lax.ppermute(values, "dp", [(i, i ^ mask) for i in range(n_dp)])

    def t_swap(values):
        return lax.ppermute(values, "tensor", [(0, 1), (1, 0)])

    def by_bit(which, own, other):
        return jnp.where(which == 0, own, other), jnp.where(which == 0, other, own)

    def in_order(parts, bits):
        parts = list(parts)
        for i, b in enumerate(reversed(bits)):
            step = 1 << i
            for r in range(len(parts)):
                if not r & step:
                    parts[r], parts[r | step] = by_bit(bit[b], parts[r], parts[r | step])
        return parts

    def t_gather(values):
        if n_t == 2:
            return jnp.stack(by_bit(t, values, t_swap(values)))
        return lax.all_gather(values, "tensor", axis=0)

    def t_scatter(values):
        if n_t == 2:
            return pick(values, t, 0).astype(f32) + t_swap(pick(values, 1 - t, 0)).astype(f32)
        return lax.psum_scatter(values, "tensor", scatter_dimension=0, tiled=False).astype(f32)

    def tp_gather(values):
        return [t_gather(values if r == 0 else swap(values, tp_mask[r])) for r in range(n_tp)]

    def tp_scatter(parts, kind):
        halves = [t_scatter(part) for part in parts]
        total = halves[0]
        for r in range(1, n_tp):
            total = total + swap(halves[r].astype(kind), tp_mask[r]).astype(f32)
        return total

    def exchange(values):
        parts = [pick(values, q, 0)]
        for r in range(1, n_tp):
            parts.append(swap(pick(values, q ^ r, 0), tp_mask[r]))
        return in_order(parts, tp_bits)

    def fs_gather(values):
        parts = [values]
        for b in fs_bits:
            parts = parts + [None] * 0 + [swap(v, 1 << b) for v in parts]
        return parts

    def weight_parts(shards):
        return fs_gather(jnp.stack(exchange(shards)))

    def weight_whole(parts):
        count = len(parts)
        flip = [0] * count
        for r in range(count):
            flip[sum(((r >> i) & 1) << (len(fs_bits) - 1 - i) for i in range(len(fs_bits)))] = parts[r]
        ordered = jnp.stack(in_order(flip, fs_bits))
        cols = ordered.shape[-1]
        ordered = ordered.reshape((2,) * depth + (block, cols))
        have = fs_bits + tp_bits
        axes = [have.index(b) for b in reversed(range(depth))]
        return ordered.transpose(axes + [depth, depth + 1]).reshape(width, cols)

    def weight_back(grad):
        cols = grad.shape[1]
        grad = grad.reshape((2,) * depth + (block, cols))
        for b in reversed(fs_bits):
            send = lax.dynamic_slice_in_dim(grad, 1 - bit[b], 1, axis_of[b]).astype(bf16)
            hold = lax.dynamic_slice_in_dim(grad, bit[b], 1, axis_of[b]).astype(f32)
            grad = hold + swap(send, 1 << b).astype(f32)
        return exchange(grad.reshape(n_tp, block, cols).astype(bf16))

    def my_columns(values):
        lead = values.shape[:-1]
        n = len(lead)
        values = values.reshape(lead + (2,) * depth + (block,))
        bits = list(reversed(range(depth)))
        for b in own_bits:
            values = pick(values, t_bit[b], n + bits.index(b))
            bits.remove(b)
        order = [n + bits.index(b) for b in tp_bits] + list(range(n)) + [n + bits.index(b) for b in free_bits]
        return values.transpose(order + [n + len(bits)]).reshape((n_tp,) + lead + (feat,))

    def my_half(values):
        return lax.dynamic_slice_in_dim(values, t * share, share, 0)

    hid = glu_gate.shape[1] // n_tp
    if n_dp == 16 and n_t == 2:
        gains = jnp.stack([norm_gain, mixer_gain, ffn_gain])
        (
            mix_full, out_full, gate_full, up_full, down_full, normed_one, grad_out_all, normed_two,
            pre, state, mix_raw, residual, mixed_out, scale_lanes, aux_rows, par, gate_pre, up_pre,
            coef,
        ) = front(
            input_proj, forget_proj, outgate_proj, output_proj, glu_gate, glu_up, glu_down, cotangent,
            tokens_in, gains, bound_table, jnp.concatenate([lengths, bucket]),
        )
    else:
        inputs = tokens_in.astype(f32)
        scale_one = rms_scale(inputs)
        normed_mine = (inputs * scale_one * norm_gain).astype(bf16)
        inputs_half = my_half(inputs)
        scale_one_half = my_half(scale_one)
        mix_shards = jnp.concatenate(
            [my_columns(w) for w in (input_proj, forget_proj, outgate_proj)], axis=-1
        )
        gate_shards = glu_gate.T.reshape(n_tp, hid, block)
        up_shards = glu_up.T.reshape(n_tp, hid, block)
        down_shards = glu_down.reshape(n_tp, hid, block)
        my_table = pick(my_columns(bound_table), q, 0)
        par = jnp.stack([bound_parts(my_table)[2], pick(my_columns(mixer_gain), q, 0)])
        valid_own, keep_own = layout(lengths, bucket, rows)
        grad_out_rows = (cotangent.astype(f32) * my_half(valid_own)).astype(bf16)
        normed_half = my_half(normed_mine)
        normed_parts = [normed_mine] + [
            t_gather(swap(normed_half, tp_mask[r])).reshape(rows, width) for r in range(1, n_tp)
        ]
        normed_one = jnp.concatenate(normed_parts)
        aux_own = jnp.concatenate([valid_own, keep_own], axis=1)
        aux = jnp.concatenate([aux_own] + [swap(aux_own, tp_mask[r]) for r in range(1, n_tp)])
        mix_full = weight_whole(weight_parts(mix_shards))
        out_piece = output_proj
        for b in own_bits:
            out_piece = jnp.where(t_bit[b] == bit[b], out_piece, swap(out_piece, 1 << b))
        out_pieces = [out_piece]
        for b in reversed(free_bits):
            out_pieces = out_pieces + [swap(v, 1 << b) for v in out_pieces]
        out_full = jnp.concatenate(in_order(out_pieces, free_bits))
        gate_full, up_full, down_full = (
            weight_whole(weight_parts(w.transpose(0, 2, 1))).T
            for w in (gate_shards, up_shards, down_shards)
        )
        grad_out_all = jnp.stack(tp_gather(grad_out_rows)).reshape(n_tp * rows, width)
        pre = matmul(normed_one, mix_full)
        state, mix_raw, square = mixer_forward(pre, aux, par, rows)
        out_parts = matmul(mix_raw, out_full).astype(bf16).reshape(n_tp, n_t, share, width)
        square_parts = square.reshape(n_tp, n_t, share)
        square_sum = tp_scatter([square_parts[r] for r in range(n_tp)], f32)
        out_sum = tp_scatter([out_parts[r] for r in range(n_tp)], bf16)
        scale_state = lax.rsqrt(square_sum / width + epsilon)[:, None]
        mixed_out = out_sum * scale_state
        residual = inputs_half + mixed_out
        normed_two_half = (residual * rms_scale(residual) * ffn_gain).astype(bf16)
        normed_two = jnp.stack(tp_gather(normed_two_half)).reshape(n_tp * rows, width)

    if n_dp == 16 and n_t == 2:
        grad_hidden = cross_cols(down_full, grad_out_all)
        gate_act = jax.nn.silu(gate_pre)
        hidden = (gate_act * up_pre).astype(bf16)
        grad_up = (grad_hidden * gate_act).astype(bf16)
        grad_gate = (grad_hidden * up_pre * silu_slope(gate_pre)).astype(bf16)
        grad_g, grad_u, grad_d, grad_mix_w, grad_out_w, grad_tokens, block_out, vec = back(
            hidden, grad_gate, grad_up, normed_two, grad_out_all, gate_full, up_full, down_full,
            normed_one, mix_full, out_full, pre, state, mix_raw, aux_rows, par, tokens_in, residual, mixed_out,
            scale_lanes, gains,
        )
        mix_all = grad_mix_w.reshape(3, width, block)
        mine = lambda k: lax.dynamic_slice_in_dim(vec, k * n_dp + me, 1, 0)
        return (
            block_out,
            grad_tokens,
            mix_all[0].T.astype(f32),
            mix_all[1].T.astype(f32),
            mix_all[2].T.astype(f32),
            grad_out_w.astype(f32),
            grad_g.reshape(n_tp * hid, block).T.astype(f32),
            grad_u.reshape(n_tp * hid, block).T.astype(f32),
            grad_d.reshape(n_tp * hid, block).astype(f32),
            mine(0)[0],
            mine(2)[0],
            mine(1)[0],
            coef * mine(3),
        )

    scale_two = rms_scale(residual)
    gate_pre = cross_cols(normed_two, gate_full)
    up_pre = cross_cols(normed_two, up_full)
    grad_hidden = cross_cols(grad_out_all, down_full)
    gate_act = jax.nn.silu(gate_pre)
    hidden = (gate_act * up_pre).astype(bf16)
    grad_up = (grad_hidden * gate_act).astype(bf16)
    grad_gate = (grad_hidden * up_pre * silu_slope(gate_pre)).astype(bf16)
    grad_two_parts = (
        (matmul(grad_gate, gate_full) + matmul(grad_up, up_full))
        .astype(bf16)
        .reshape(n_tp, n_t, share, width)
    )
    grad_normed_two = tp_scatter([grad_two_parts[r] for r in range(n_tp)], bf16)
    block_parts = matmul(hidden, down_full).astype(bf16).reshape(n_tp, n_t, share, width)
    block_out = (residual + tp_scatter([block_parts[r] for r in range(n_tp)], bf16)).astype(bf16)
    grad_down_t = jnp.stack(weight_back(cross_rows(grad_out_all, hidden).astype(bf16)))
    grad_w_gate = jnp.stack(weight_back(cross_rows(normed_two, grad_gate).astype(bf16)))
    grad_w_up = jnp.stack(weight_back(cross_rows(normed_two, grad_up).astype(bf16)))
    grad_glu_down = grad_down_t.transpose(0, 2, 1).reshape(glu_down.shape).astype(f32)
    grad_glu_gate = grad_w_gate.transpose(1, 0, 2).reshape(glu_gate.shape).astype(f32)
    grad_glu_up = grad_w_up.transpose(1, 0, 2).reshape(glu_up.shape).astype(f32)

    grad_residual = grad_out_rows.astype(f32) + norm_back(
        residual, scale_two, ffn_gain, grad_normed_two
    )
    ffn_gain_sum = jnp.sum(grad_normed_two * residual * scale_two, axis=0)
    grad_mix_half = grad_residual.astype(bf16)
    dot_mean = jnp.sum(grad_mix_half.astype(f32) * mixed_out, axis=1, keepdims=True) / (
        scale_state * width
    )
    row_values = jnp.concatenate([scale_state, dot_mean], axis=1).T
    row_all = jnp.stack(tp_gather(row_values)).transpose(0, 1, 3, 2).reshape(n_tp * rows, 2)
    grad_mix = jnp.stack(tp_gather(grad_mix_half)).reshape(n_tp * rows, width)
    grad_mixed = cross_cols(grad_mix, out_full)
    aux_back = jnp.concatenate([aux, row_all], axis=1)
    grads, sums = mixer_backward(pre, state, grad_mixed, aux_back, par, rows)
    one_parts = cross_cols(grads, mix_full).astype(bf16).reshape(n_tp, n_t, share, width)
    grad_normed_one = tp_scatter([one_parts[r] for r in range(n_tp)], bf16)
    grad_mix_w = jnp.stack(weight_back(cross_rows(normed_one, grads).astype(bf16)))

    mixed = (mix_raw.astype(f32) * row_all[:, :1]).astype(bf16)
    grad_out_w = cross_rows(mixed, grad_mix).astype(bf16).reshape((2,) * len(free_bits) + (block, width))
    for i, b in enumerate(free_bits):
        send = lax.dynamic_slice_in_dim(grad_out_w, 1 - bit[b], 1, i)
        hold = lax.dynamic_slice_in_dim(grad_out_w, bit[b], 1, i)
        grad_out_w = (hold.astype(f32) + swap(send, 1 << b).astype(f32)).astype(bf16)
    grad_out_w = grad_out_w.reshape(block, width)
    for b in own_bits:
        grad_out_w = (grad_out_w.astype(f32) + swap(grad_out_w, 1 << b).astype(f32)).astype(bf16)
    mine_t = jnp.int32(0)
    for b in own_bits:
        mine_t = mine_t * 2 + bit[b]
    if n_t == 2:
        other = t_swap(grad_out_w)
        grad_output_proj = jnp.where(mine_t == t, grad_out_w, other).astype(f32)
    else:
        grad_output_proj = pick(lax.all_gather(grad_out_w, "tensor", axis=0), mine_t, 0).astype(f32)

    mix_all = t_gather(grad_mix_w)
    mix_all = mix_all.reshape((2,) * t_depth + (2, 2) + (block, 3) + (2,) * len(free_bits) + (block,))
    order = list(own_bits) + list(tp_bits) + ["row", "which"] + list(free_bits) + ["col"]
    axes = [order.index(k) for k in ["which", "row"] + list(reversed(range(depth))) + ["col"]]
    mix_all = mix_all.transpose(axes).reshape(3, block, width).astype(f32)

    grad_tokens_half = my_half_residual = grad_residual + norm_back(
        inputs_half, scale_one_half, norm_gain, grad_normed_one
    )
    grad_tokens = t_gather(grad_tokens_half).reshape(rows, width)
    norm_gain_sum = jnp.sum(grad_normed_one * inputs_half * scale_one_half, axis=0)

    gains = jnp.stack([norm_gain_sum, ffn_gain_sum]).reshape((2,) + (2,) * depth + (block,))
    for b in reversed(range(depth)):
        at = 1 + axis_of[b]
        send = lax.dynamic_slice_in_dim(gains, 1 - bit[b], 1, at)
        hold = lax.dynamic_slice_in_dim(gains, bit[b], 1, at)
        gains = hold + swap(send, 1 << b)
    gains = gains.reshape(2, block)
    gains = gains + t_swap(gains) if n_t == 2 else lax.psum(gains, "tensor")

    for b in fs_bits:
        sums = sums + swap(sums, 1 << b)
    sums = t_gather(sums)
    sums = pick(sums, mine_t, 0).reshape((2,) + (2,) * len(free_bits) + (block,))
    for b in free_bits:
        sums = pick(sums, bit[b], 1)
    shares, picked, lower = bound_parts(lax.dynamic_slice_in_dim(bound_table, me * block, block, 1))
    grad_table = shares * (picked - lower[None, :]) * sums[1][None, :]

    return (
        block_out,
        grad_tokens,
        mix_all[0],
        mix_all[1],
        mix_all[2],
        grad_output_proj,
        grad_glu_gate,
        grad_glu_up,
        grad_glu_down,
        gains[0],
        sums[0],
        gains[1],
        grad_table,
    )


def solution(mesh):
    return jax.shard_map(
        functools.partial(body, mesh.shape["dp"], mesh.shape["tensor"]),
        mesh=mesh,
        in_specs=(
            P("dp", None),
            P("dp", None),
            P("dp", None),
            P("dp", None),
            P("dp", None),
            P("dp", "tensor"),
            P("dp", "tensor"),
            P("tensor", "dp"),
            P(),
            P(),
            P(),
            P(),
            P("dp"),
            P("dp"),
            P(("dp", "tensor"), None),
        ),
        out_specs=(
            P(("dp", "tensor"), None),
            P("dp", None),
            P("dp", None),
            P("dp", None),
            P("dp", None),
            P("dp", None),
            P("dp", "tensor"),
            P("dp", "tensor"),
            P("tensor", "dp"),
            P("dp"),
            P("dp"),
            P("dp"),
            P(None, "dp"),
        ),
        check_vma=False,
    )
```

```python
import functools

import jax
import jax.numpy as jnp
from jax import lax
from jax.experimental import pallas as pl
from jax.experimental.pallas import tpu as pltpu
from jax.sharding import PartitionSpec as P

LAYER = 12
epsilon = 1e-06
bf16 = jnp.bfloat16
f32 = jnp.float32


def rms_scale(values):
    return lax.rsqrt(jnp.mean(values * values, axis=-1, keepdims=True) + epsilon)


def norm_back(values, row_scale, gain_row, incoming):
    weighted = incoming * gain_row
    cubed = row_scale * row_scale * row_scale
    return row_scale * weighted - values * cubed * jnp.mean(
        weighted * values, axis=-1, keepdims=True
    )


def silu_slope(values):
    logistic = jax.nn.sigmoid(values)
    return logistic * (1.0 + values * (1.0 - logistic))


def matmul(first_op, second_op):
    return jnp.dot(first_op, second_op, preferred_element_type=f32)


def cross_rows(first_op, second_op):
    return lax.dot_general(
        first_op, second_op, (((0,), (0,)), ((), ())), preferred_element_type=f32
    )


def cross_cols(first_op, second_op):
    return lax.dot_general(
        first_op, second_op, (((1,), (1,)), ((), ())), preferred_element_type=f32
    )


def pick(values, index, axis):
    return lax.dynamic_index_in_dim(values, index, axis, keepdims=False)


def layout(lengths, bucket, row_count):
    slot_len = row_count // jnp.left_shift(jnp.int32(1), bucket)
    position = jnp.arange(row_count, dtype=jnp.int32)
    slot_index = position // slot_len
    offset = position - slot_index * slot_len
    slot_ids = jnp.arange(lengths.shape[0], dtype=jnp.int32)
    chosen = (slot_index[:, None] == slot_ids[None, :]).astype(jnp.int32)
    slot_limit = jnp.sum(chosen * lengths[None, :], axis=1)
    valid_mask = (offset < slot_limit).astype(f32)[:, None]
    keep_mask = (offset > 0).astype(f32)[:, None]
    return (valid_mask, keep_mask)


def bound_parts(bound_table):
    shares = jax.nn.softmax(bound_table, axis=0)
    layer_ids = jnp.arange(bound_table.shape[0], dtype=jnp.int32)[:, None]
    picked = ((layer_ids >= 1) & (layer_ids <= LAYER)).astype(f32)
    return (shares, picked, jnp.sum(shares * picked, axis=0))


def scan_rows(decay_ref, add_ref, out_ref, reverse):
    rows, width = out_ref.shape
    tiles = rows // 8
    sub = lax.broadcasted_iota(jnp.int32, (8, width), 0)

    def step(i, carry):
        j = tiles - 1 - i if reverse else i
        at = pl.ds(pl.multiple_of(j * 8, 8), 8)
        a = decay_ref[at, :]
        b = add_ref[at, :]
        for s in (1, 2, 4):
            shift = 8 - s if reverse else s
            inside = sub < 8 - s if reverse else sub >= s
            b = jnp.where(inside, b + a * pltpu.roll(b, shift, 0), b)
            a = jnp.where(inside, a * pltpu.roll(a, shift, 0), a)
        h = b + a * carry
        out_ref[at, :] = h
        edge = h[0:1, :] if reverse else h[7:8, :]
        return jnp.broadcast_to(edge, (8, width))

    lax.fori_loop(0, tiles, step, jnp.zeros((8, width), f32), unroll=4)


def mixer_forward_kernel(pre_ref, aux_ref, par_ref, state_ref, mix_ref, sq_ref, decay_ref, add_ref):
    width = state_ref.shape[1]
    input_pre = pre_ref[:, :width]
    forget_pre = pre_ref[:, width : 2 * width]
    outgate_pre = pre_ref[:, 2 * width :]
    valid = aux_ref[:, 0:1]
    keep = aux_ref[:, 1:2]
    bound = par_ref[0:1, :]
    gain = par_ref[1:2, :]
    forget = bound + (1.0 - bound) * jax.nn.sigmoid(forget_pre)
    add_ref[...] = input_pre * jax.nn.sigmoid(input_pre) * (1.0 - forget) * valid
    decay_ref[...] = forget * keep
    scan_rows(decay_ref, add_ref, state_ref, False)
    state = state_ref[...]
    mix_ref[...] = (state * gain * (outgate_pre * jax.nn.sigmoid(outgate_pre))).astype(bf16)
    sq_ref[...] = jnp.sum(state * state, axis=1, keepdims=True)


def mixer_forward(pre, aux, par, seq_rows):
    rows, width = pre.shape[0], pre.shape[1] // 3
    row_block = lambda n: pl.BlockSpec((seq_rows, n), lambda i: (i, 0))
    return pl.pallas_call(
        mixer_forward_kernel,
        grid=(rows // seq_rows,),
        in_specs=[
            row_block(3 * width),
            row_block(aux.shape[1]),
            pl.BlockSpec(par.shape, lambda i: (0, 0)),
        ],
        out_specs=[row_block(width), row_block(width), row_block(1)],
        out_shape=[
            jax.ShapeDtypeStruct((rows, width), f32),
            jax.ShapeDtypeStruct((rows, width), bf16),
            jax.ShapeDtypeStruct((rows, 1), f32),
        ],
        scratch_shapes=[pltpu.VMEM((seq_rows, width), f32)] * 2,
        cost_estimate=pl.CostEstimate(
            flops=rows * width * 60, bytes_accessed=rows * width * 20, transcendentals=rows * width * 3
        ),
        name="mixer_forward",
    )(pre, aux, par)


def mixer_backward_kernel(
    pre_ref, state_ref, up_ref, aux_ref, par_ref, grad_ref, sums_ref, decay_ref, add_ref, out_ref
):
    rows, width = state_ref.shape
    input_pre = pre_ref[:, :width]
    forget_pre = pre_ref[:, width : 2 * width]
    outgate_pre = pre_ref[:, 2 * width :]
    valid = aux_ref[:, 0:1]
    keep = aux_ref[:, 1:2]
    scale = aux_ref[:, 2:3]
    dot_mean = aux_ref[:, 3:4]
    bound = par_ref[0:1, :]
    gain = par_ref[1:2, :]
    state = state_ref[...]
    incoming = up_ref[...]
    at_row = lax.broadcasted_iota(jnp.int32, (rows, width), 0)
    sig_out = jax.nn.sigmoid(outgate_pre)
    act_out = outgate_pre * sig_out
    scaled = incoming * (state * scale)
    grad_ref[:, 2 * width :] = (
        scaled * gain * (sig_out * (1.0 + outgate_pre * (1.0 - sig_out)))
    ).astype(bf16)
    add_ref[...] = scale * (gain * act_out * incoming) - state * (scale * scale * scale * dot_mean)
    sig_forget = jax.nn.sigmoid(forget_pre)
    forget = bound + (1.0 - bound) * sig_forget
    decay_ref[...] = jnp.where(
        at_row < rows - 1, pltpu.roll(forget * keep, rows - 1, 0), 0.0
    )
    scan_rows(decay_ref, add_ref, out_ref, True)
    grad_state = out_ref[...]
    before = jnp.where(at_row > 0, pltpu.roll(state, 1, 0), 0.0)
    sig_in = jax.nn.sigmoid(input_pre)
    grad_forget = grad_state * (before * keep - input_pre * sig_in * valid)
    grad_ref[:, :width] = (
        grad_state * (1.0 - forget) * valid * (sig_in * (1.0 + input_pre * (1.0 - sig_in)))
    ).astype(bf16)
    grad_ref[:, width : 2 * width] = (
        grad_forget * (1.0 - bound) * sig_forget * (1.0 - sig_forget)
    ).astype(bf16)

    @pl.when(pl.program_id(0) == 0)
    def _():
        sums_ref[...] = jnp.zeros_like(sums_ref)

    sums_ref[0:1, :] += jnp.sum(scaled * act_out, axis=0, keepdims=True)
    sums_ref[1:2, :] += jnp.sum(grad_forget * (1.0 - sig_forget), axis=0, keepdims=True)


def mixer_backward(pre, state, incoming, aux, par, seq_rows):
    rows, width = state.shape
    row_block = lambda n: pl.BlockSpec((seq_rows, n), lambda i: (i, 0))
    whole = lambda shape: pl.BlockSpec(shape, lambda i: (0, 0))
    return pl.pallas_call(
        mixer_backward_kernel,
        grid=(rows // seq_rows,),
        in_specs=[
            row_block(3 * width),
            row_block(width),
            row_block(width),
            row_block(aux.shape[1]),
            whole(par.shape),
        ],
        out_specs=[row_block(3 * width), whole((2, width))],
        out_shape=[
            jax.ShapeDtypeStruct((rows, 3 * width), bf16),
            jax.ShapeDtypeStruct((2, width), f32),
        ],
        scratch_shapes=[pltpu.VMEM((seq_rows, width), f32)] * 3,
        cost_estimate=pl.CostEstimate(
            flops=rows * width * 90, bytes_accessed=rows * width * 26, transcendentals=rows * width * 3
        ),
        name="mixer_backward",
    )(pre, state, incoming, aux, par)


MESH = pl.DeviceIdType.MESH


class Copies:
    def __init__(self, send, recv, local):
        self.send, self.recv, self.local = send, recv, local
        self.n_remote = self.n_local = 0
        self.open = []

    def remote(self, src, dst, device):
        k = self.n_remote
        self.n_remote += 1
        copy = pltpu.make_async_remote_copy(
            src_ref=src,
            dst_ref=dst,
            send_sem=self.send.at[k],
            recv_sem=self.recv.at[k],
            device_id=device,
            device_id_type=MESH,
        )
        copy.start()
        self.open.append(copy.wait_send)
        return copy

    def here(self, src, dst, keep=False):
        k = self.n_local
        self.n_local += 1
        copy = pltpu.make_async_copy(src, dst, self.local.at[k])
        copy.start()
        if keep:
            self.open.append(copy.wait)
        return copy

    def sent(self, copies):
        for copy in copies:
            copy.wait_send()
            self.open.remove(copy.wait_send)

    def close(self):
        assert self.n_remote <= self.send.shape[0] and self.n_local <= self.local.shape[0]
        for wait in self.open:
            wait()


def position():
    me = lax.axis_index("dp")
    t = lax.axis_index("tensor")
    zf, zn, y, x = me // 8, (me // 4) % 2, (me // 2) % 2, me % 2
    to_x, to_zn = 1 - 2 * x, 4 - 8 * zn
    group = [None, (me + to_x, t), (me + to_zn, t), (me + to_x + to_zn, t)]
    q = [zn * 2 + x, zn * 2 + 1 - x, (1 - zn) * 2 + x, (1 - zn) * 2 + 1 - x]
    far = (me + 8 - 16 * zf, t)
    side = (me + 2 - 4 * y, t)
    core = (me, 1 - t)
    return me, t, (zf, zn, y, x), q, group, far, side, core


def meet(devices):
    barrier = pltpu.get_barrier_semaphore()
    for device in devices:
        pl.semaphore_signal(barrier, inc=1, device_id=device, device_id_type=MESH)
    pl.semaphore_wait(barrier, len(devices))


def fold_lanes(values):
    width = values.shape[1]
    if width % 128:
        return values
    total = values[:, :128]
    for i in range(128, width, 128):
        total = total + values[:, i : i + 128]
    return total


def front_kernel(
    s_in, s_fg, s_og, s_out, w_g, w_u, s_d, cot, tok, gain_one, gain_mix, gain_two, table, lengths, bucket,
    o_mix, o_out, o_g, o_u, o_d, o_n1, o_go, o_n2, o_pre, o_state, o_raw, o_res, o_mo, o_sc, o_aux, o_par, o_hid, o_hg, o_hu, o_coef,
    w_mix, w_out, n1, aux, pre, state, raw, part, core_in, half, peer_in, par, wide_g, wide_u, s_g, s_u, go_own, bound_row, full_g, full_u, gate, up, hid_v, hid_g, hid_u, all_powers, coef,
    sq, sq_core, sq_half, sq_peer, res, mo, sc, n2, decay, add,
    send, recv, local, core_send, core_recv, sqc_send, sqc_recv, out_send, out_recv, x_send, x_recv,
):
    me, t, (zf, zn, y, x), q, group, far, side, core = position()
    rows, width = tok.shape
    share = rows // 2
    block = s_out.shape[0]
    feat = par.shape[1]
    hid = s_d.shape[0] // 4
    link = Copies(send, recv, local)
    get_g, get_u, get_cot = link.here(w_g, wide_g), link.here(w_u, wide_u), link.here(cot, go_own)
    meet(group[1:] + [far, side, core])

    def at(start, size, unit):
        return pl.ds(pl.multiple_of(start, unit), size)

    def pair(fz, c, fy):
        return at(fz * (8 * block) + c * (4 * block) + fy * (2 * block), 2 * block, 2 * block)

    mine = at(me * block, block, block)

    def row(r, tt):
        return at(r * rows + tt * share, share, share)

    def columns(r, fz):
        fx = x if r in (0, 2) else 1 - x
        fzn = zn if r in (0, 1) else 1 - zn
        return at((fz * 8 + fzn * 4 + t * 2 + fx) * block, block, block)

    mix_in, mix_own = [], []
    for k, s in enumerate((s_in, s_fg, s_og)):
        for fz in (0, 1):
            to = w_mix.at[mine, pl.ds(k * feat + fz * block, block)]
            mix_in += [link.remote(s.at[:, columns(r, fz)], to, group[r]) for r in (1, 2, 3)]
            mix_own.append(link.here(s.at[:, columns(0, fz)], to))
    out_rows = [at(z * block, block, block) for z in (zf, 1 - zf)]

    def out_copy(k, src, dst, device):
        return pltpu.make_async_remote_copy(
            src_ref=src,
            dst_ref=w_out.at[dst],
            send_sem=out_send.at[k],
            recv_sem=out_recv.at[k],
            device_id=device,
            device_id_type=MESH,
        )

    out_far = out_copy(0, s_out, out_rows[0], far)
    out_side = out_copy(1, s_out, out_rows[0], side)
    out_next = out_copy(2, w_out.at[out_rows[1]], out_rows[1], side)
    out_here = pltpu.make_async_copy(s_out, w_out.at[out_rows[0]], out_send.at[3])

    @pl.when(t == y)
    def _():
        out_far.start()
        out_side.start()
        out_here.start()

    norm_row = gain_one[...]

    def norm_rows(first):
        def some(j, carry):
            to = at(first + j * 16, 16, 16)
            value = tok[to, :].astype(f32)
            s = lax.rsqrt(jnp.mean(value * value, axis=1, keepdims=True) + epsilon)
            n1[to, :] = (value * s * norm_row).astype(bf16)
            return carry

        lax.fori_loop(0, share // 16, some, 0)

    norm_rows(t * share)
    n1_in = [link.remote(n1.at[row(0, t)], n1.at[row(r, t)], group[r]) for r in (1, 2)]

    count = lengths.shape[0]
    slot_len = lax.shift_right_logical(jnp.int32(rows), bucket[0])
    position_row = lax.broadcasted_iota(jnp.int32, (1, rows), 1)
    slot = jnp.zeros((1, rows), jnp.int32)
    for j in range(1, count):
        slot = slot + (position_row >= j * slot_len).astype(jnp.int32)
    limit = jnp.zeros((1, rows), jnp.int32)
    for j in range(count):
        limit = limit + jnp.where(slot == j, lengths[j], 0)
    offset = position_row - slot * slot_len
    aux[0] = jnp.zeros(aux.shape[1:], f32)
    aux[0, 0:1, :] = (offset < limit).astype(f32)
    aux[0, 1:2, :] = (offset > 0).astype(f32)
    aux_in = [link.remote(aux.at[0], aux.at[r], group[r]) for r in (1, 2, 3)]

    norm_rows((1 - t) * share)
    for c in mix_own:
        c.wait()
    for c in mix_in:
        c.wait_recv()
    far_mix = [link.remote(w_mix.at[pair(zf, c, y)], w_mix.at[pair(zf, c, y)], far) for c in (0, 1)]
    side_mix = [link.remote(w_mix.at[pair(zf, c, y)], w_mix.at[pair(zf, c, y)], side) for c in (0, 1)]
    n1_in[1].wait_recv()
    n1_in.append(link.remote(n1.at[row(2, t)], n1.at[row(3, t)], group[1]))
    n1_core = [link.remote(n1.at[row(2, t)], n1.at[row(2, t)], core)]
    n1_in[0].wait_recv()
    n1_core.append(link.remote(n1.at[row(1, t)], n1.at[row(1, t)], core))
    shards = ((s_g, o_g), (s_u, o_u), (s_d, o_d))
    ffn_in, ffn_own = [], []

    def turn_round(wide, tall):
        size = min(128, wide.shape[1])

        def some(j, carry):
            to = at(j * size, size, size)
            tall[to, :] = wide[:, to].astype(f32).T.astype(bf16)
            return carry

        lax.fori_loop(0, wide.shape[1] // size, some, 0)

    def leave(s, o):
        units = [at(q[r] * hid, hid, 16) for r in range(4)]
        ffn_in.extend(link.remote(s.at[units[r]], o.at[:, mine], group[r]) for r in (1, 2, 3))
        ffn_own.append(link.here(s.at[units[0]], o.at[:, mine]))

    get_g.wait()
    turn_round(wide_g, s_g)
    leave(s_g, o_g)
    get_u.wait()
    turn_round(wide_u, s_u)
    leave(s_u, o_u)
    leave(s_d, o_d)

    logits = table[...]
    powers = jnp.exp(logits - jnp.max(logits, axis=0, keepdims=True))
    layer_ids = lax.broadcasted_iota(jnp.int32, logits.shape, 0)
    picked = jnp.where((layer_ids >= 1) & (layer_ids <= LAYER), powers, 0.0)
    bound_row[0:1, :] = jnp.sum(picked, axis=0, keepdims=True) / jnp.sum(powers, axis=0, keepdims=True)
    all_powers[...] = powers
    mine_powers = all_powers[:, mine]
    mine_shares = mine_powers / jnp.sum(mine_powers, axis=0, keepdims=True)
    ids = lax.broadcasted_iota(jnp.int32, mine_shares.shape, 0)
    mine_picked = ((ids >= 1) & (ids <= LAYER)).astype(f32)
    coef[...] = mine_shares * (mine_picked - jnp.sum(mine_shares * mine_picked, axis=0, keepdims=True))
    link.here(coef, o_coef, keep=True)
    for fz in (0, 1):
        par[0:1, fz * block : (fz + 1) * block] = bound_row[0:1, columns(0, fz)]
        par[1:2, fz * block : (fz + 1) * block] = gain_mix[0:1, columns(0, fz)]
    get_cot.wait()
    valid_rows = aux[0].T[:, 0:1]
    first_half = lax.broadcasted_iota(jnp.int32, (share, 1), 0) * 0 + t
    valid_half = jnp.where(first_half == 0, valid_rows[:share], valid_rows[share:])
    go_own[...] = (go_own[...].astype(f32) * valid_half).astype(bf16)
    n1_in[2].wait_recv()
    n1_core.append(link.remote(n1.at[row(3, t)], n1.at[row(3, t)], core))
    for c in (0, 1):
        far_mix[c].wait_recv()
        side_mix.append(link.remote(w_mix.at[pair(1 - zf, c, y)], w_mix.at[pair(1 - zf, c, y)], side))

    @pl.when(t == y)
    def _():
        out_far.wait_recv()
        out_next.start()
        out_far.wait_send()
        out_side.wait_send()
        out_here.wait()
        out_next.wait_send()

    @pl.when(t != y)
    def _():
        out_side.wait_recv()
        out_next.wait_recv()

    far_ffn, side_ffn = [], ([], [], [])

    def start_ffn(i):
        o = shards[i][1]
        ffn_own[i].wait()
        for c in ffn_in[3 * i : 3 * i + 3]:
            c.wait_recv()
        far_ffn.append([link.remote(o.at[:, pair(zf, c, y)], o.at[:, pair(zf, c, y)], far) for c in (0, 1)])
        side_ffn[i].extend(link.remote(o.at[:, pair(zf, c, y)], o.at[:, pair(zf, c, y)], side) for c in (0, 1))

    def forward_ffn(i):
        o = shards[i][1]
        for c in (0, 1):
            far_ffn[i][c].wait_recv()
            side_ffn[i].append(link.remote(o.at[:, pair(1 - zf, c, y)], o.at[:, pair(1 - zf, c, y)], side))

    start_ffn(0)
    go_in = [link.remote(go_own, o_go.at[row(r, t)], group[r]) for r in (1, 2)]
    go_core = [link.remote(go_own, o_go.at[row(0, t)], core)]
    go_here = link.here(go_own, o_go.at[row(0, t)])

    for c in side_mix + n1_core + aux_in:
        c.wait_recv()

    def core_copy(r):
        return pltpu.make_async_remote_copy(
            src_ref=part.at[row(r, 1 - t)],
            dst_ref=core_in.at[at(r * share, share, share)],
            send_sem=core_send.at[r],
            recv_sem=core_recv.at[r],
            device_id=core,
            device_id_type=MESH,
        )

    def sq_copy(r):
        return pltpu.make_async_remote_copy(
            src_ref=sq.at[row(r, 1 - t)],
            dst_ref=sq_core.at[at(r * share, share, share)],
            send_sem=sqc_send.at[r],
            recv_sem=sqc_recv.at[r],
            device_id=core,
            device_id_type=MESH,
        )

    bound = par[0:1, :]
    gain = par[1:2, :]

    def to_x(slot, r):
        from_rows, to_rows = at(r * share, share, share), at(slot * share, share, share)
        return [
            pltpu.make_async_remote_copy(
                src_ref=a.at[from_rows],
                dst_ref=b.at[to_rows],
                send_sem=x_send.at[i * 2 + slot],
                recv_sem=x_recv.at[i * 2 + slot],
                device_id=group[1],
                device_id_type=MESH,
            )
            for i, (a, b) in enumerate(((half, peer_in), (sq_half, sq_peer)))
        ]

    def hand_over(r):
        core_copy(r).wait()
        sq_copy(r).wait()

        def some(j, carry):
            to = at(r * share + j * 16, 16, 16)
            mine_rows = at(r * rows + t * share + j * 16, 16, 16)
            half[to, :] = (part[mine_rows, :].astype(f32) + core_in[to, :].astype(f32)).astype(bf16)
            sq_half[to, :] = sq[mine_rows, :] + sq_core[to, :]
            return carry

        lax.fori_loop(0, share // 16, some, 0)

    def piece(i, carry):
        r = 3 - 2 * i + 3 * (i // 2)
        here = at(r * rows, rows, rows)
        pre[here, :] = jnp.dot(n1[here, :], w_mix[...], preferred_element_type=f32)
        masks = aux[r].T
        valid = masks[:, 0:1]
        keep = masks[:, 1:2]
        forget = bound + (1.0 - bound) * jax.nn.sigmoid(pre[here, feat : 2 * feat])
        input_pre = pre[here, 0:feat]
        add[...] = input_pre * jax.nn.sigmoid(input_pre) * (1.0 - forget) * valid
        decay[...] = forget * keep
        scan_rows(decay, add, state.at[here, :], False)
        held = state[here, :]
        outgate_pre = pre[here, 2 * feat :]
        raw[here, :] = (held * gain * (outgate_pre * jax.nn.sigmoid(outgate_pre))).astype(bf16)
        sq[here, :] = fold_lanes(held * held)
        part[here, :] = jnp.dot(raw[here, :], w_out[...], preferred_element_type=f32).astype(bf16)
        core_copy(r).start()
        sq_copy(r).start()

        @pl.when(i > 0)
        def _():
            before = 5 - 2 * i + 3 * ((i - 1) // 2)
            hand_over(before)

            @pl.when(i < 3)
            def _():
                for c in to_x(i - 1, before):
                    c.start()

        return carry

    lax.fori_loop(0, 4, piece, 0)
    start_ffn(1)

    link.here(w_mix, o_mix, keep=True)
    link.here(w_out, o_out, keep=True)
    n1_out = link.here(n1, o_n1)
    link.here(pre, o_pre, keep=True)
    link.here(state, o_state, keep=True)
    link.here(raw, o_raw, keep=True)
    link.here(aux, o_aux, keep=True)
    link.here(par, o_par, keep=True)

    def spread(o, incoming, cores):
        incoming[1].wait_recv()
        incoming.append(link.remote(o.at[row(2, t)], o.at[row(3, t)], group[1]))
        cores.append(link.remote(o.at[row(2, t)], o.at[row(2, t)], core))
        incoming[0].wait_recv()
        cores.append(link.remote(o.at[row(1, t)], o.at[row(1, t)], core))

    def spread_last(o, incoming, cores):
        incoming[2].wait_recv()
        cores.append(link.remote(o.at[row(3, t)], o.at[row(3, t)], core))

    hand_over(0)
    for c in to_x(0, 3):
        c.wait()

    def pass_on(j, carry):
        two = at(2 * share + j * 16, 16, 16)
        half[two, :] = (half[two, :].astype(f32) + peer_in[at(j * 16, 16, 16), :].astype(f32)).astype(bf16)
        sq_half[two, :] = sq_half[two, :] + sq_peer[at(j * 16, 16, 16), :]
        return carry

    lax.fori_loop(0, share // 16, pass_on, 0)
    third = pl.ds(2 * share, share)
    to_z = [
        link.remote(half.at[third], peer_in.at[third], group[2]),
        link.remote(sq_half.at[third], sq_peer.at[third], group[2]),
    ]
    spread(o_go, go_in, go_core)
    forward_ffn(0)
    for c in to_x(1, 1):
        c.wait()
    for c in to_z:
        c.wait_recv()
    total_sq = sq_half[0:share, :] + sq_peer[share : 2 * share, :] + sq_peer[2 * share : 3 * share, :]
    scale = lax.rsqrt(jnp.sum(total_sq, axis=1, keepdims=True) / width + epsilon)
    sc[...] = jnp.broadcast_to(scale, sc.shape)
    chunk = min(share, 16)

    def finish(i, carry):
        to = at(i * chunk, chunk, chunk)
        total = part[at(t * share + i * chunk, chunk, chunk), :].astype(f32) + core_in[to, :].astype(f32)
        for r in (1, 2):
            total = total + peer_in[at(r * share + i * chunk, chunk, chunk), :].astype(f32)
        mixed = total * sc[to, 0:1]
        value = tok[at(t * share + i * chunk, chunk, chunk), :].astype(f32) + mixed
        mo[to, :] = mixed
        res[to, :] = value
        scale_two = lax.rsqrt(jnp.mean(value * value, axis=1, keepdims=True) + epsilon)
        n2[to, :] = (value * scale_two * gain_two[...]).astype(bf16)
        return carry

    lax.fori_loop(0, share // chunk, finish, 0)
    n2_in = [link.remote(n2, o_n2.at[row(r, t)], group[r]) for r in (1, 2)]
    n2_core = [link.remote(n2, o_n2.at[row(0, t)], core)]
    n2_here = link.here(n2, o_n2.at[row(0, t)])
    link.here(res, o_res, keep=True)
    link.here(mo, o_mo, keep=True)
    link.here(sc, o_sc, keep=True)
    start_ffn(2)
    spread_last(o_go, go_in, go_core)
    forward_ffn(1)
    spread(o_n2, n2_in, n2_core)
    spread_last(o_n2, n2_in, n2_core)

    forward_ffn(2)

    for c in side_ffn[0]:
        c.wait_recv()
    get_full = link.here(o_g, full_g)
    for c in n2_core:
        c.wait_recv()
    n2_here.wait()
    get_rows = link.here(o_n2, part)
    get_full.wait()
    get_rows.wait()

    def product(full, made):
        def some(j, carry):
            to = at(j * rows, rows, rows)
            made[:, to] = lax.dot_general(
                full[...], part[to, :], (((1,), (1,)), ((), ())), preferred_element_type=f32
            )
            return carry

        lax.fori_loop(0, 4, some, 0)

    product(full_g, gate)
    for c in side_ffn[1]:
        c.wait_recv()
    get_full = link.here(o_u, full_u)
    get_full.wait()
    for c in go_core:
        c.wait_recv()
    go_here.wait()
    n1_out.wait()
    link.sent(n1_in + n1_core)
    get_rows = link.here(o_go, n1)
    product(full_u, up)
    for c in side_ffn[2]:
        c.wait_recv()
    get_full = link.here(o_d, full_g)
    get_full.wait()
    get_rows.wait()

    def hidden_rows(j, carry):
        to = at(j * rows, rows, rows)
        grad = lax.dot_general(
            full_g[...], n1[to, :], (((1,), (1,)), ((), ())), preferred_element_type=f32
        )
        value, other = gate[:, to], up[:, to]
        sig = jax.nn.sigmoid(value)
        act = value * sig
        hid_v[:, to] = (act * other).astype(bf16)
        hid_u[:, to] = (grad * act).astype(bf16)
        hid_g[:, to] = (grad * other * (sig * (1.0 + value * (1.0 - sig)))).astype(bf16)
        return carry

    lax.fori_loop(0, 4, hidden_rows, 0)
    for made, out in ((hid_v, o_hid), (hid_g, o_hg), (hid_u, o_hu)):
        link.here(made, out, keep=True)
    link.close()


def front(s_in, s_fg, s_og, s_out, w_g, w_u, s_d, cot, tok, gain_one, gain_mix, gain_two, table, lengths, bucket):
    rows, width = tok.shape
    share, group_rows = rows // 2, 4 * rows
    block = s_out.shape[0]
    feat, hid = 2 * block, s_d.shape[0] // 4
    lanes = 128 if feat % 128 == 0 else feat
    any_spec = pl.BlockSpec(memory_space=pl.ANY)
    vmem_spec = pl.BlockSpec(memory_space=pltpu.VMEM)
    made = jax.ShapeDtypeStruct
    outs = [
        made((width, 3 * feat), bf16),
        made((feat, width), bf16),
        made((hid, width), bf16),
        made((hid, width), bf16),
        made((hid, width), bf16),
        made((group_rows, width), bf16),
        made((group_rows, width), bf16),
        made((group_rows, width), bf16),
        made((group_rows, 3 * feat), f32),
        made((group_rows, feat), f32),
        made((group_rows, feat), bf16),
        made((share, width), f32),
        made((share, width), f32),
        made((share, 128), f32),
        made((4, 8, rows), f32),
        made((2, feat), f32),
        made((hid, group_rows), bf16),
        made((hid, group_rows), bf16),
        made((hid, group_rows), bf16),
        made((table.shape[0], block), f32),
    ]
    scratch = [
        pltpu.VMEM((width, 3 * feat), bf16),
        pltpu.VMEM((feat, width), bf16),
        pltpu.VMEM((group_rows, width), bf16),
        pltpu.VMEM((4, 8, rows), f32),
        pltpu.VMEM((group_rows, 3 * feat), f32),
        pltpu.VMEM((group_rows, feat), f32),
        pltpu.VMEM((group_rows, feat), bf16),
        pltpu.VMEM((group_rows, width), bf16),
        pltpu.VMEM((4 * share, width), bf16),
        pltpu.VMEM((4 * share, width), bf16),
        pltpu.VMEM((4 * share, width), bf16),
        pltpu.VMEM((2, feat), f32),
        pltpu.VMEM(w_g.shape, bf16),
        pltpu.VMEM(w_u.shape, bf16),
        pltpu.VMEM((4 * hid, block), bf16),
        pltpu.VMEM((4 * hid, block), bf16),
        pltpu.VMEM((share, width), bf16),
        pltpu.VMEM((8, width), f32),
        pltpu.VMEM((hid, width), bf16),
        pltpu.VMEM((hid, width), bf16),
        pltpu.VMEM((hid, group_rows), f32),
        pltpu.VMEM((hid, group_rows), f32),
        pltpu.VMEM((hid, group_rows), bf16),
        pltpu.VMEM((hid, group_rows), bf16),
        pltpu.VMEM((hid, group_rows), bf16),
        pltpu.VMEM(table.shape, f32),
        pltpu.VMEM((table.shape[0], block), f32),
        pltpu.VMEM((group_rows, lanes), f32),
        pltpu.VMEM((4 * share, lanes), f32),
        pltpu.VMEM((4 * share, lanes), f32),
        pltpu.VMEM((4 * share, lanes), f32),
        pltpu.VMEM((share, width), f32),
        pltpu.VMEM((share, width), f32),
        pltpu.VMEM((share, 128), f32),
        pltpu.VMEM((share, width), bf16),
        pltpu.VMEM((rows, feat), f32),
        pltpu.VMEM((rows, feat), f32),
        pltpu.SemaphoreType.DMA((88,)),
        pltpu.SemaphoreType.DMA((88,)),
        pltpu.SemaphoreType.DMA((40,)),
    ] + [pltpu.SemaphoreType.DMA((4,))] * 8
    return pl.pallas_call(
        front_kernel,
        in_specs=[any_spec] * 8 + [vmem_spec] * 5 + [pl.BlockSpec(memory_space=pltpu.SMEM)] * 2,
        out_specs=[any_spec] * len(outs),
        out_shape=outs,
        scratch_shapes=scratch,
        compiler_params=pltpu.CompilerParams(
            collective_id=1, has_side_effects=True, vmem_limit_bytes=56 << 20
        ),
        name="front",
    )(s_in, s_fg, s_og, s_out, w_g, w_u, s_d, cot, tok, gain_one, gain_mix, gain_two, table, lengths, bucket)


def back_kernel(
    h_d, h_g, h_u, n2, go, w_g, w_u, w_d, n1, w_mix_in, w_out_in, pre, state, raw, aux_in,
    par, tok, res, mo, sc, first_gain, second_gain,
    o_g, o_u, o_d, o_mix, o_out, o_tok, o_blk, o_vec,
    left, right, gmix, dw_d, dw_g, dw_u, dw_mix, yr_d, yr_g, yr_u, yr_mix, zr_d, zr_g, zr_u, zr_mix,
    own, half, core_in, core_blk, peer_in, peer_blk, w_mix, w_out, aux, pre_b, state_b, raw_b,
    grads, grads_t, decay, add, yr_out, zr_out, hid_a, hid_b,
    gres, gm_own, scalars, scal_all, sums, vec, vec_in,
    send, recv, local, core_send, core_recv, out_send, out_recv, piece_sem,
):
    me, t, (zf, zn, y, x), q, group, far, side, core = position()
    rows, width = tok.shape
    share = rows // 2
    block = width // 16
    feat = par.shape[1]
    link = Copies(send, recv, local)
    meet(group[1:] + [far, side, core])

    def at(start, size, unit):
        return pl.ds(pl.multiple_of(start, unit), size)

    def pair(fz, c, fy):
        return at(fz * (8 * block) + c * (4 * block) + fy * (2 * block), 2 * block, 2 * block)

    def row(r, tt):
        return at(r * rows + tt * share, share, share)

    def rel(r):
        return pl.ds(r * share, share)

    hid_rows = pl.ds(0, w_g.shape[0])
    full_g, full_u = left.at[hid_rows], gmix.at[hid_rows]
    get_g = [link.here(h_g, hid_a), link.here(n2, right)]
    get_u = link.here(h_u, hid_b)
    get_two = [link.here(w_g, full_g), link.here(w_u, full_u)]
    get_go = [link.here(go.at[row(0, t)], gm_own)]
    get_w_d = link.here(w_d, dw_d)
    get_aux = [link.here(aux_in, aux), link.here(w_mix_in, w_mix)]
    order = (3, 1, 2, 0)

    def stage(r):
        i = order.index(r)
        return w_out if i == 3 else dw_mix.at[i]

    def staged(r, tt):
        return w_out.at[at(tt * share, share, share)] if r == 0 else stage(r).at[tt]

    def products(terms):
        wide = 4 * block

        def at_piece(r, store):
            here = at(r * rows, rows, rows)

            def some(j, carry):
                to = at(j * wide, wide, wide)
                total = None
                for hid, weight in terms:
                    one = lax.dot_general(
                        hid[:, here], weight[:, to], (((0,), (0,)), ((), ())), preferred_element_type=f32
                    )
                    total = one if total is None else total + one
                store(to, total.astype(bf16))
                return carry

            lax.fori_loop(0, width // wide, some, 0)

        return at_piece

    def all_pieces(terms, incoming):
        at_piece = products(terms)
        copies = {}
        for i, r in enumerate(order):
            if r:

                def store(to, value):
                    dw_mix[i, 0, :, to] = value[:share]
                    dw_mix[i, 1, :, to] = value[share:]

            else:

                def store(to, value):
                    w_out[:, to] = value

            at_piece(r, store)
            copies[r] = link.remote(staged(r, 1 - t), incoming.at[rel(r)], core)
        return copies

    def two_rows(r, j):
        if r == 0:
            return w_out[at(t * share + j * 16, 16, 16), :].astype(f32)
        return dw_mix[order.index(r), t, at(j * 16, 16, 16), :].astype(f32)

    def own_rows(r, j):
        return own[at(r * share + j * 16, 16, 16), :].astype(f32)

    def add_half(r, source, incoming, held):
        def some(j, carry):
            to = at(r * share + j * 16, 16, 16)
            held[to, :] = (source(r, j) + incoming[to, :].astype(f32)).astype(bf16)
            return carry

        lax.fori_loop(0, share // 16, some, 0)

    def over_cores(arrived, source, incoming, held, peers):
        sent = []
        for r in (3, 1, 2, 0):
            arrived[r].wait_recv()
            if r:
                add_half(r, source, incoming, held)
            if r % 2:
                sent.append(link.remote(held.at[rel(r)], peers.at[rel(len(sent))], group[1]))
        return sent

    def pass_on(sent, held, peers):
        sent[0].wait_recv()

        def some(j, carry):
            two = at(2 * share + j * 16, 16, 16)
            held[two, :] = (held[two, :].astype(f32) + peers[at(j * 16, 16, 16), :].astype(f32)).astype(bf16)
            return carry

        lax.fori_loop(0, share // 16, some, 0)
        sent.append(link.remote(held.at[rel(2)], peers.at[rel(2)], group[2]))


    def weight_grad(hid, other, dw, first, count):
        wide = 4 * block

        def columns(i, carry):
            to = at(((1 - zf) * 2 + i - (i // 2) * 4 * (1 - zf)) * wide, wide, wide)
            made = jnp.dot(hid[...], other[:, to], preferred_element_type=f32).astype(bf16)
            if len(dw.shape) == 2:
                dw[:, to] = made
            else:
                dw[:, :, :, to] = made.reshape(dw.shape[:3] + (wide,))
            return carry

        lax.fori_loop(first, first + count, columns, 0)

    def cut(ref, cols):
        return ref.at[:, cols] if len(ref.shape) == 2 else ref.at[:, :, :, cols]

    def side_send(dw, yr, slot):
        fz = 1 - zf if slot == 0 else zf
        return [
            link.remote(cut(dw, pair(fz, c, 1 - y)), cut(yr, pl.ds((slot * 2 + c) * 2 * block, 2 * block)), side)
            for c in (0, 1)
        ]

    def add_columns(dw, to, others):
        if len(dw.shape) == 2:
            size = 64 if dw.shape[0] % 64 == 0 else dw.shape[0]
            steps = dw.shape[0] // size
        else:
            steps = dw.shape[0] * dw.shape[1]

        def some(j, carry):
            if len(dw.shape) == 2:
                lead = (at(j * size, size, size),)
            else:
                lead = (j // dw.shape[1], j % dw.shape[1], slice(None))
            total = dw[lead + (to,)].astype(f32)
            for ref, cols in others:
                total = total + ref[lead + (cols,)].astype(f32)
            dw[lead + (to,)] = total.astype(bf16)
            return carry

        lax.fori_loop(0, steps, some, 0)

    def part_of(i):
        return pl.ds(i * 2 * block, 2 * block)

    def second_hop(hop, dw, yr, zr):
        sent = []
        for c in (0, 1):
            hop[c].wait_recv()
            add_columns(dw, pair(1 - zf, c, y), [(yr, part_of(c))])
            sent.append(link.remote(cut(dw, pair(1 - zf, c, y)), cut(zr, part_of(c)), far))
        return sent

    def last_hop(near, sent, dw, yr, zr, out):
        for c in (0, 1):
            near[c].wait_recv()
            sent[c].wait_recv()
            add_columns(dw, pair(zf, c, y), [(yr, part_of(2 + c)), (zr, part_of(c))])

        def owner(r):
            fx = x if r in (0, 2) else 1 - x
            fzn = zn if r in (0, 1) else 1 - zn
            return at((zf * 8 + fzn * 4 + y * 2 + fx) * block, block, block)

        if len(dw.shape) == 2:
            place = out.at[q[0]]
            link.here(dw.at[:, owner(0)], place, keep=True)
            return [link.remote(dw.at[:, owner(r)], place, group[r]) for r in (1, 2, 3)]
        place = out.at[:, :, zn, t, x]
        kept = link.here(cut(dw, owner(0)), place)
        sent = [link.remote(cut(dw, owner(r)), place, group[r]) for r in (1, 2, 3)]
        kept.wait()
        return sent

    for c in get_g:
        c.wait()
    weight_grad(hid_a, right, dw_g, 0, 2)
    hop_g = side_send(dw_g, yr_g, 0)
    get_u.wait()
    for c in get_two:
        c.wait()
    two_core = all_pieces([(hid_a, full_g), (hid_b, full_u)], core_in)

    two_peer = over_cores(two_core, two_rows, core_in, half, peer_in)
    weight_grad(hid_b, right, dw_u, 0, 2)
    get_left = link.here(go, left)
    weight_grad(hid_a, right, dw_g, 2, 2)
    get_d = link.here(h_d, hid_a)
    far_g = second_hop(hop_g, dw_g, yr_g, zr_g)
    hop_u = side_send(dw_u, yr_u, 0)
    pass_on(two_peer, half, peer_in)
    weight_grad(hid_b, right, dw_u, 2, 2)

    for c in two_peer[1:]:
        c.wait_recv()
    for c in get_go:
        c.wait()
    gain_two = second_gain[...]
    sums[...] = jnp.zeros_like(sums)
    step = 16

    def residual_rows(j, carry):
        to = at(j * step, step, step)
        total = two_rows(0, j) + core_in[to, :].astype(f32)
        for r in (1, 2):
            total = total + peer_in[at(r * share + j * step, step, step), :].astype(f32)
        value = res[to, :]
        s = lax.rsqrt(jnp.mean(value * value, axis=1, keepdims=True) + epsilon)
        weighted = total * gain_two
        grad = (
            gm_own[to, :].astype(f32)
            + s * weighted
            - value * (s * s * s) * jnp.mean(weighted * value, axis=1, keepdims=True)
        )
        gres[to, :] = grad
        low = grad.astype(bf16)
        gm_own[to, :] = low
        dot = jnp.sum(low.astype(f32) * mo[to, :], axis=1, keepdims=True)
        scale = sc[to, 0:1]
        sc[to, 1:2] = dot / (scale * width)
        sums[1:2, :] += jnp.sum(total * value * s, axis=0, keepdims=True)
        return carry

    lax.fori_loop(0, share // step, residual_rows, 0)
    scalars[...] = sc[...].T[0:8, :]

    def scal(r, tt):
        return scal_all.at[r * 2 + tt]

    gm_in = [link.remote(gm_own, gmix.at[row(r, t)], group[r]) for r in (1, 2)]
    sc_in = [link.remote(scalars, scal(r, t), group[r]) for r in (1, 2, 3)]
    gm_core = [link.remote(gm_own, gmix.at[row(0, t)], core), link.remote(scalars, scal(0, t), core)]
    gm_here = [link.here(gm_own, gmix.at[row(0, t)]), link.here(scalars, scal(0, t))]
    for c in (get_d, get_w_d, get_left):
        c.wait()
    link.sent(two_core.values())
    blk_core = all_pieces([(hid_a, dw_d)], core_blk)
    blk_own = [link.here(staged(r, t), own.at[rel(r)]) for r in order]
    weight_grad(hid_a, left, dw_d, 0, 2)
    hop_d = side_send(dw_d, yr_d, 0)
    far_u = second_hop(hop_u, dw_u, yr_u, zr_u)
    near_g = side_send(dw_g, yr_g, 1)
    gm_in[1].wait_recv()
    gm_in.append(link.remote(gmix.at[row(2, t)], gmix.at[row(3, t)], group[1]))
    gm_core.append(link.remote(gmix.at[row(2, t)], gmix.at[row(2, t)], core))
    gm_in[0].wait_recv()
    gm_core.append(link.remote(gmix.at[row(1, t)], gmix.at[row(1, t)], core))
    for i, r in enumerate((1, 2, 3)):
        sc_in[i].wait_recv()
        gm_core.append(link.remote(scal(r, t), scal(r, t), core))
    weight_grad(hid_a, left, dw_d, 2, 2)
    get_n1 = link.here(n1, left)
    near_u = side_send(dw_u, yr_u, 1)
    for c in blk_own:
        c.wait()
    gm_in[2].wait_recv()
    gm_core.append(link.remote(gmix.at[row(3, t)], gmix.at[row(3, t)], core))
    far_d = second_hop(hop_d, dw_d, yr_d, zr_d)
    near_d = side_send(dw_d, yr_d, 1)
    blk_peer = over_cores(blk_core, own_rows, core_blk, own, peer_blk)
    link.sent(blk_core.values())
    link.sent(two_peer)
    get_aux.append(link.here(w_out_in, w_out))
    for c in get_aux + [get_n1] + gm_here:
        c.wait()
    for c in gm_core:
        c.wait_recv()

    def one_core(r):
        return pltpu.make_async_remote_copy(
            src_ref=right.at[row(r, 1 - t)],
            dst_ref=core_in.at[at(r * share, share, share)],
            send_sem=core_send.at[r],
            recv_sem=core_recv.at[r],
            device_id=core,
            device_id_type=MESH,
        )

    def fetch(r):
        here = at(r * rows, rows, rows)
        return [
            pltpu.make_async_copy(pre.at[here], pre_b, piece_sem.at[0]),
            pltpu.make_async_copy(state.at[here], state_b, piece_sem.at[1]),
            pltpu.make_async_copy(raw.at[here], raw_b, piece_sem.at[2]),
        ]

    bound = par[0:1, :]
    gain = par[1:2, :]
    gain_sums = sums.at[2:4, 0:feat]
    mixed_t = hid_b.at[0:feat]
    dw_out = w_out

    def one_rows(r, j):
        return right[at(r * rows + t * share + j * 16, 16, 16), :].astype(f32)

    def one_x(slot, r):
        return pltpu.make_async_remote_copy(
            src_ref=half.at[at(r * share, share, share)],
            dst_ref=peer_in.at[at(slot * share, share, share)],
            send_sem=core_send.at[4 + slot],
            recv_sem=core_recv.at[4 + slot],
            device_id=group[1],
            device_id_type=MESH,
        )

    def hand_over(r):
        one_core(r).wait()
        add_half(r, one_rows, core_in, half)

    def piece(i, carry):
        r = 3 - 2 * i + 3 * (i // 2)
        here = at(r * rows, rows, rows)
        copies = fetch(r)
        for c in copies:
            c.start()
        up = lax.dot_general(
            gmix[here, :], w_out[...], (((1,), (1,)), ((), ())), preferred_element_type=f32
        )
        masks = aux[r].T
        valid = masks[:, 0:1]
        keep = masks[:, 1:2]
        scale_parts = [scal_all[r * 2 + tt].T for tt in (0, 1)]
        scale = jnp.concatenate([p[:, 0:1] for p in scale_parts], axis=0)
        dot_mean = jnp.concatenate([p[:, 1:2] for p in scale_parts], axis=0)
        for c in copies:
            c.wait()
        at_row = lax.broadcasted_iota(jnp.int32, (rows, feat), 0)
        input_pre = pre_b[:, :feat]
        outgate_pre = pre_b[:, 2 * feat :]
        held = state_b[...]
        sig_out = jax.nn.sigmoid(outgate_pre)
        act_out = outgate_pre * sig_out
        scaled = up * (held * scale)
        grads[:, 2 * feat :] = scaled * gain * (sig_out * (1.0 + outgate_pre * (1.0 - sig_out)))
        add[...] = scale * (gain * act_out * up) - held * (scale * scale * scale * dot_mean)
        gain_sums[0:1, :] += jnp.sum(scaled * act_out, axis=0, keepdims=True)
        sig_forget = jax.nn.sigmoid(pre_b[:, feat : 2 * feat])
        forget = bound + (1.0 - bound) * sig_forget
        decay[...] = jnp.where(at_row < rows - 1, pltpu.roll(forget * keep, rows - 1, 0), 0.0)
        scan_rows(decay, add, add, True)
        grad_state = add[...]
        before = jnp.where(at_row > 0, pltpu.roll(held, 1, 0), 0.0)
        sig_in = jax.nn.sigmoid(input_pre)
        grad_forget = grad_state * (before * keep - input_pre * sig_in * valid)
        grads[:, :feat] = (
            grad_state * (1.0 - forget) * valid * (sig_in * (1.0 + input_pre * (1.0 - sig_in)))
        )
        grads[:, feat : 2 * feat] = grad_forget * (1.0 - bound) * sig_forget * (1.0 - sig_forget)
        gain_sums[1:2, :] += jnp.sum(grad_forget * (1.0 - sig_forget), axis=0, keepdims=True)
        low = grads[...].astype(bf16)
        right[here, :] = lax.dot_general(
            low, w_mix[...], (((1,), (1,)), ((), ())), preferred_element_type=f32
        ).astype(bf16)
        one_core(r).start()
        grads_t[:, here] = grads[...].T.astype(bf16)
        mixed_t[:, here] = (raw_b[...].astype(f32) * scale).T.astype(bf16)

        @pl.when(i > 0)
        def _():
            before_r = 5 - 2 * i + 3 * ((i - 1) // 2)
            hand_over(before_r)

            @pl.when(i < 3)
            def _():
                one_x(i - 1, before_r).start()

        return carry

    lax.fori_loop(0, 4, piece, 0)

    one_core(0).wait()
    pass_on(blk_peer, own, peer_blk)

    weight_grad(grads_t, left, dw_mix, 0, 2)
    hop_mix = side_send(dw_mix, yr_mix, 0)
    weight_grad(grads_t, left, dw_mix, 2, 2)

    def out_columns(i, carry):
        to = at(i * (4 * block), 4 * block, 4 * block)
        dw_out[:, to] = jnp.dot(mixed_t[...], gmix[:, to], preferred_element_type=f32).astype(bf16)
        return carry

    lax.fori_loop(0, 4, out_columns, 0)
    near_rows = at(zf * block, block, block)
    far_rows = at((1 - zf) * block, block, block)

    def out_copy(k, src, dst, device):
        return pltpu.make_async_remote_copy(
            src_ref=src,
            dst_ref=dst,
            send_sem=out_send.at[k],
            recv_sem=out_recv.at[k],
            device_id=device,
            device_id_type=MESH,
        )

    out_side = out_copy(0, dw_out, yr_out, side)
    out_far = out_copy(1, dw_out.at[far_rows], zr_out, far)
    out_core = out_copy(2, dw_out.at[near_rows], o_out, core)
    out_here = pltpu.make_async_copy(dw_out.at[near_rows], o_out, out_send.at[3])

    @pl.when(t != y)
    def _():
        out_side.start()

    one_x(0, 3).wait()

    def one_on(j, carry):
        two = at(2 * share + j * 16, 16, 16)
        half[two, :] = (half[two, :].astype(f32) + peer_in[at(j * 16, 16, 16), :].astype(f32)).astype(bf16)
        return carry

    lax.fori_loop(0, share // 16, one_on, 0)
    one_z = link.remote(half.at[rel(2)], peer_in.at[rel(2)], group[2])
    near_mix = side_send(dw_mix, yr_mix, 1)
    back_g = last_hop(near_g, far_g, dw_g, yr_g, zr_g, o_g)
    back_u = last_hop(near_u, far_u, dw_u, yr_u, zr_u, o_u)
    far_mix = second_hop(hop_mix, dw_mix, yr_mix, zr_mix)

    @pl.when(t == y)
    def _():
        out_side.wait_recv()
        add_columns(dw_out, pl.ds(0, width), [(yr_out, pl.ds(0, width))])
        out_far.start()

    one_x(1, 1).wait()
    one_z.wait_recv()
    gain_one = first_gain[...]

    def token_rows(j, carry):
        to = at(j * step, step, step)
        total = one_rows(0, j) + core_in[to, :].astype(f32)
        for r in (1, 2):
            total = total + peer_in[at(r * share + j * step, step, step), :].astype(f32)
        value = tok[at(t * share + j * step, step, step), :].astype(f32)
        s = lax.rsqrt(jnp.mean(value * value, axis=1, keepdims=True) + epsilon)
        weighted = total * gain_one
        gres[to, :] = (
            gres[to, :]
            + s * weighted
            - value * (s * s * s) * jnp.mean(weighted * value, axis=1, keepdims=True)
        )
        sums[0:1, :] += jnp.sum(total * value * s, axis=0, keepdims=True)
        return carry

    lax.fori_loop(0, share // step, token_rows, 0)
    tok_rows = at(t * share, share, share)
    tok_core = link.remote(gres, o_tok.at[tok_rows], core)
    link.here(gres, o_tok.at[tok_rows], keep=True)

    vec[0] = jnp.zeros(vec.shape[1:], f32)
    for k in (0, 1):
        for i in range(16):
            vec[0, k * 16 + i : k * 16 + i + 1, :] = sums[k : k + 1, i * block : (i + 1) * block]
    for k in (2, 3):
        for i in (0, 1):
            vec[0, pl.ds(k * 16 + i * 8 + zn * 4 + t * 2 + x, 1), :] = sums[
                k : k + 1, i * block : (i + 1) * block
            ]
    partners = [group[1], group[2], side, far, core]
    turn = [link.remote(vec.at[0], vec_in.at[0], partners[0])]

    def next_turn():
        k = len(turn)
        turn[k - 1].wait_recv()
        vec[k] = vec[k - 1] + vec_in[k - 1]
        if k < len(partners):
            turn.append(link.remote(vec.at[k], vec_in.at[k], partners[k]))

    next_turn()
    back_d = last_hop(near_d, far_d, dw_d, yr_d, zr_d, o_d)
    next_turn()
    next_turn()
    for c in blk_peer[1:]:
        c.wait_recv()

    def block_rows(j, carry):
        to = at(j * step, step, step)
        total = own_rows(0, j) + core_blk[to, :].astype(f32)
        for r in (1, 2):
            total = total + peer_blk[at(r * share + j * step, step, step), :].astype(f32)
        gm_own[to, :] = (res[to, :] + total).astype(bf16)
        return carry

    link.sent(gm_in[:2] + gm_core[:1])
    lax.fori_loop(0, share // step, block_rows, 0)
    link.here(gm_own, o_blk, keep=True)
    next_turn()
    next_turn()
    link.here(vec.at[5], o_vec, keep=True)
    back_mix = last_hop(near_mix, far_mix, dw_mix, yr_mix, zr_mix, o_mix)

    @pl.when(t == y)
    def _():
        out_far.wait_recv()

        def some(j, carry):
            to = at(zf * block + j * 16, 16, 16)
            dw_out[to, :] = (
                dw_out[to, :].astype(f32) + zr_out[at(j * 16, 16, 16), :].astype(f32)
            ).astype(bf16)
            return carry

        lax.fori_loop(0, block // 16, some, 0)
        out_core.start()
        out_here.start()
        out_far.wait_send()
        out_core.wait_send()
        out_here.wait()

    @pl.when(t != y)
    def _():
        out_side.wait_send()
        out_core.wait_recv()

    for c in back_mix:
        c.wait_recv()
    mix_core = link.remote(o_mix.at[:, :, :, t], o_mix.at[:, :, :, t], core)
    for c in back_d + back_g + back_u + [mix_core, tok_core]:
        c.wait_recv()
    link.close()


def back(*arrays):
    par, tok = arrays[15], arrays[16]
    rows, width = tok.shape
    share, group_rows = rows // 2, 4 * rows
    feat, hid, block = par.shape[1], arrays[0].shape[0], width // 16
    made = jax.ShapeDtypeStruct
    vm = pltpu.VMEM
    outs = [
        made((4, hid, block), bf16),
        made((4, hid, block), bf16),
        made((4, hid, block), bf16),
        made((3, 2, 2, 2, 2, block, block), bf16),
        made((block, width), bf16),
        made((rows, width), f32),
        made((share, width), bf16),
        made((64, block), f32),
    ]
    scratch = (
        [vm((group_rows, width), bf16)] * 3
        + [vm((hid, width), bf16)] * 3
        + [vm((3, 2, block, width), bf16)]
        + [vm((hid, width // 2), bf16)] * 3
        + [vm((3, 2, block, width // 2), bf16)]
        + [vm((hid, width // 4), bf16)] * 3
        + [vm((3, 2, block, width // 4), bf16)]
        + [vm((4 * share, width), bf16)] * 4
        + [vm((3 * share, width), bf16)] * 2
        + [
            vm((width, 3 * feat), bf16),
            vm((feat, width), bf16),
            vm(arrays[14].shape, f32),
            vm((rows, 3 * feat), f32),
            vm((rows, feat), f32),
            vm((rows, feat), bf16),
            vm((rows, 3 * feat), f32),
            vm((3 * feat, group_rows), bf16),
            vm((rows, feat), f32),
            vm((rows, feat), f32),
            vm((feat, width), bf16),
            vm((block, width), bf16),
            vm((hid, group_rows), bf16),
            vm((hid, group_rows), bf16),
            vm((share, width), f32),
            vm((share, width), bf16),
            vm((8, share), f32),
            vm((8, 8, share), f32),
            vm((4, width), f32),
            vm((6, 64, block), f32),
            vm((5, 64, block), f32),
            pltpu.SemaphoreType.DMA((96,)),
            pltpu.SemaphoreType.DMA((96,)),
            pltpu.SemaphoreType.DMA((32,)),
        ]
        + [pltpu.SemaphoreType.DMA((6,))] * 5
    )
    any_spec = pl.BlockSpec(memory_space=pl.ANY)
    vmem_spec = pl.BlockSpec(memory_space=pltpu.VMEM)
    return pl.pallas_call(
        back_kernel,
        in_specs=[any_spec] * 15 + [vmem_spec] * 7,
        out_specs=[any_spec] * len(outs),
        out_shape=outs,
        scratch_shapes=scratch,
        compiler_params=pltpu.CompilerParams(
            collective_id=2, has_side_effects=True, vmem_limit_bytes=63 << 20
        ),
        name="back",
    )(*arrays)


def body(
    n_dp,
    n_t,
    tokens_in,
    input_proj,
    forget_proj,
    outgate_proj,
    output_proj,
    glu_gate,
    glu_up,
    glu_down,
    norm_gain,
    mixer_gain,
    ffn_gain,
    bound_table,
    lengths,
    bucket,
    cotangent,
):
    depth = n_dp.bit_length() - 1
    tp_bits = (2, 0)
    fs_bits = tuple(b for b in reversed(range(depth)) if b not in tp_bits)
    t_depth = n_t.bit_length() - 1
    own_bits, free_bits = fs_bits[len(fs_bits) - t_depth :], fs_bits[: len(fs_bits) - t_depth]
    n_tp = 4
    tp_mask = (0, 1, 4, 5)
    axis_of = {b: depth - 1 - b for b in range(depth)}

    me = lax.axis_index("dp")
    t = lax.axis_index("tensor")
    bit = {b: (me >> b) & 1 for b in range(depth)}
    t_bit = {b: (t >> (t_depth - 1 - i)) & 1 for i, b in enumerate(own_bits)}
    q = bit[2] * 2 + bit[0]

    rows, width = tokens_in.shape
    share = cotangent.shape[0]
    block = width // n_dp
    free = 2 ** len(free_bits)
    feat = free * block

    def swap(values, mask):
        return lax.ppermute(values, "dp", [(i, i ^ mask) for i in range(n_dp)])

    def t_swap(values):
        return lax.ppermute(values, "tensor", [(0, 1), (1, 0)])

    def by_bit(which, own, other):
        return jnp.where(which == 0, own, other), jnp.where(which == 0, other, own)

    def in_order(parts, bits):
        parts = list(parts)
        for i, b in enumerate(reversed(bits)):
            step = 1 << i
            for r in range(len(parts)):
                if not r & step:
                    parts[r], parts[r | step] = by_bit(bit[b], parts[r], parts[r | step])
        return parts

    def t_gather(values):
        if n_t == 2:
            return jnp.stack(by_bit(t, values, t_swap(values)))
        return lax.all_gather(values, "tensor", axis=0)

    def t_scatter(values):
        if n_t == 2:
            return pick(values, t, 0).astype(f32) + t_swap(pick(values, 1 - t, 0)).astype(f32)
        return lax.psum_scatter(values, "tensor", scatter_dimension=0, tiled=False).astype(f32)

    def tp_gather(values):
        return [t_gather(values if r == 0 else swap(values, tp_mask[r])) for r in range(n_tp)]

    def tp_scatter(parts, kind):
        halves = [t_scatter(part) for part in parts]
        total = halves[0]
        for r in range(1, n_tp):
            total = total + swap(halves[r].astype(kind), tp_mask[r]).astype(f32)
        return total

    def exchange(values):
        parts = [pick(values, q, 0)]
        for r in range(1, n_tp):
            parts.append(swap(pick(values, q ^ r, 0), tp_mask[r]))
        return in_order(parts, tp_bits)

    def fs_gather(values):
        parts = [values]
        for b in fs_bits:
            parts = parts + [None] * 0 + [swap(v, 1 << b) for v in parts]
        return parts

    def weight_parts(shards):
        return fs_gather(jnp.stack(exchange(shards)))

    def weight_whole(parts):
        count = len(parts)
        flip = [0] * count
        for r in range(count):
            flip[sum(((r >> i) & 1) << (len(fs_bits) - 1 - i) for i in range(len(fs_bits)))] = parts[r]
        ordered = jnp.stack(in_order(flip, fs_bits))
        cols = ordered.shape[-1]
        ordered = ordered.reshape((2,) * depth + (block, cols))
        have = fs_bits + tp_bits
        axes = [have.index(b) for b in reversed(range(depth))]
        return ordered.transpose(axes + [depth, depth + 1]).reshape(width, cols)

    def weight_back(grad):
        cols = grad.shape[1]
        grad = grad.reshape((2,) * depth + (block, cols))
        for b in reversed(fs_bits):
            send = lax.dynamic_slice_in_dim(grad, 1 - bit[b], 1, axis_of[b]).astype(bf16)
            hold = lax.dynamic_slice_in_dim(grad, bit[b], 1, axis_of[b]).astype(f32)
            grad = hold + swap(send, 1 << b).astype(f32)
        return exchange(grad.reshape(n_tp, block, cols).astype(bf16))

    def my_columns(values):
        lead = values.shape[:-1]
        n = len(lead)
        values = values.reshape(lead + (2,) * depth + (block,))
        bits = list(reversed(range(depth)))
        for b in own_bits:
            values = pick(values, t_bit[b], n + bits.index(b))
            bits.remove(b)
        order = [n + bits.index(b) for b in tp_bits] + list(range(n)) + [n + bits.index(b) for b in free_bits]
        return values.transpose(order + [n + len(bits)]).reshape((n_tp,) + lead + (feat,))

    def my_half(values):
        return lax.dynamic_slice_in_dim(values, t * share, share, 0)

    hid = glu_gate.shape[1] // n_tp
    if n_dp == 16 and n_t == 2:
        (
            mix_full, out_full, gate_full, up_full, down_full, normed_one, grad_out_all, normed_two,
            pre, state, mix_raw, residual, mixed_out, scale_lanes, aux_rows, par, hidden, grad_gate,
            grad_up, coef,
        ) = front(
            input_proj, forget_proj, outgate_proj, output_proj, glu_gate, glu_up, glu_down, cotangent,
            tokens_in, norm_gain[None, :], mixer_gain[None, :], ffn_gain[None, :], bound_table, lengths, bucket,
        )
    else:
        inputs = tokens_in.astype(f32)
        scale_one = rms_scale(inputs)
        normed_mine = (inputs * scale_one * norm_gain).astype(bf16)
        inputs_half = my_half(inputs)
        scale_one_half = my_half(scale_one)
        mix_shards = jnp.concatenate(
            [my_columns(w) for w in (input_proj, forget_proj, outgate_proj)], axis=-1
        )
        gate_shards = glu_gate.T.reshape(n_tp, hid, block)
        up_shards = glu_up.T.reshape(n_tp, hid, block)
        down_shards = glu_down.reshape(n_tp, hid, block)
        my_table = pick(my_columns(bound_table), q, 0)
        par = jnp.stack([bound_parts(my_table)[2], pick(my_columns(mixer_gain), q, 0)])
        valid_own, keep_own = layout(lengths, bucket, rows)
        grad_out_rows = (cotangent.astype(f32) * my_half(valid_own)).astype(bf16)
        normed_half = my_half(normed_mine)
        normed_parts = [normed_mine] + [
            t_gather(swap(normed_half, tp_mask[r])).reshape(rows, width) for r in range(1, n_tp)
        ]
        normed_one = jnp.concatenate(normed_parts)
        aux_own = jnp.concatenate([valid_own, keep_own], axis=1)
        aux = jnp.concatenate([aux_own] + [swap(aux_own, tp_mask[r]) for r in range(1, n_tp)])
        mix_full = weight_whole(weight_parts(mix_shards))
        out_piece = output_proj
        for b in own_bits:
            out_piece = jnp.where(t_bit[b] == bit[b], out_piece, swap(out_piece, 1 << b))
        out_pieces = [out_piece]
        for b in reversed(free_bits):
            out_pieces = out_pieces + [swap(v, 1 << b) for v in out_pieces]
        out_full = jnp.concatenate(in_order(out_pieces, free_bits))
        gate_full, up_full, down_full = (
            weight_whole(weight_parts(w.transpose(0, 2, 1))).T
            for w in (gate_shards, up_shards, down_shards)
        )
        grad_out_all = jnp.stack(tp_gather(grad_out_rows)).reshape(n_tp * rows, width)
        pre = matmul(normed_one, mix_full)
        state, mix_raw, square = mixer_forward(pre, aux, par, rows)
        out_parts = matmul(mix_raw, out_full).astype(bf16).reshape(n_tp, n_t, share, width)
        square_parts = square.reshape(n_tp, n_t, share)
        square_sum = tp_scatter([square_parts[r] for r in range(n_tp)], f32)
        out_sum = tp_scatter([out_parts[r] for r in range(n_tp)], bf16)
        scale_state = lax.rsqrt(square_sum / width + epsilon)[:, None]
        mixed_out = out_sum * scale_state
        residual = inputs_half + mixed_out
        normed_two_half = (residual * rms_scale(residual) * ffn_gain).astype(bf16)
        normed_two = jnp.stack(tp_gather(normed_two_half)).reshape(n_tp * rows, width)

    if n_dp == 16 and n_t == 2:
        grad_g, grad_u, grad_d, grad_mix_w, grad_out_w, grad_tokens, block_out, vec = back(
            hidden, grad_gate, grad_up, normed_two, grad_out_all, gate_full, up_full, down_full,
            normed_one, mix_full, out_full, pre, state, mix_raw, aux_rows, par, tokens_in, residual, mixed_out,
            scale_lanes, norm_gain[None, :], ffn_gain[None, :],
        )
        mix_all = grad_mix_w.reshape(3, width, block)
        mine = lambda k: lax.dynamic_slice_in_dim(vec, k * n_dp + me, 1, 0)
        return (
            block_out,
            grad_tokens,
            mix_all[0].T.astype(f32),
            mix_all[1].T.astype(f32),
            mix_all[2].T.astype(f32),
            grad_out_w.astype(f32),
            grad_g.reshape(n_tp * hid, block).T.astype(f32),
            grad_u.reshape(n_tp * hid, block).T.astype(f32),
            grad_d.reshape(n_tp * hid, block).astype(f32),
            mine(0)[0],
            mine(2)[0],
            mine(1)[0],
            coef * mine(3),
        )

    scale_two = rms_scale(residual)
    gate_pre = cross_cols(normed_two, gate_full)
    up_pre = cross_cols(normed_two, up_full)
    grad_hidden = cross_cols(grad_out_all, down_full)
    gate_act = jax.nn.silu(gate_pre)
    hidden = (gate_act * up_pre).astype(bf16)
    grad_up = (grad_hidden * gate_act).astype(bf16)
    grad_gate = (grad_hidden * up_pre * silu_slope(gate_pre)).astype(bf16)
    grad_two_parts = (
        (matmul(grad_gate, gate_full) + matmul(grad_up, up_full))
        .astype(bf16)
        .reshape(n_tp, n_t, share, width)
    )
    grad_normed_two = tp_scatter([grad_two_parts[r] for r in range(n_tp)], bf16)
    block_parts = matmul(hidden, down_full).astype(bf16).reshape(n_tp, n_t, share, width)
    block_out = (residual + tp_scatter([block_parts[r] for r in range(n_tp)], bf16)).astype(bf16)
    grad_down_t = jnp.stack(weight_back(cross_rows(grad_out_all, hidden).astype(bf16)))
    grad_w_gate = jnp.stack(weight_back(cross_rows(normed_two, grad_gate).astype(bf16)))
    grad_w_up = jnp.stack(weight_back(cross_rows(normed_two, grad_up).astype(bf16)))
    grad_glu_down = grad_down_t.transpose(0, 2, 1).reshape(glu_down.shape).astype(f32)
    grad_glu_gate = grad_w_gate.transpose(1, 0, 2).reshape(glu_gate.shape).astype(f32)
    grad_glu_up = grad_w_up.transpose(1, 0, 2).reshape(glu_up.shape).astype(f32)

    grad_residual = grad_out_rows.astype(f32) + norm_back(
        residual, scale_two, ffn_gain, grad_normed_two
    )
    ffn_gain_sum = jnp.sum(grad_normed_two * residual * scale_two, axis=0)
    grad_mix_half = grad_residual.astype(bf16)
    dot_mean = jnp.sum(grad_mix_half.astype(f32) * mixed_out, axis=1, keepdims=True) / (
        scale_state * width
    )
    row_values = jnp.concatenate([scale_state, dot_mean], axis=1).T
    row_all = jnp.stack(tp_gather(row_values)).transpose(0, 1, 3, 2).reshape(n_tp * rows, 2)
    grad_mix = jnp.stack(tp_gather(grad_mix_half)).reshape(n_tp * rows, width)
    grad_mixed = cross_cols(grad_mix, out_full)
    aux_back = jnp.concatenate([aux, row_all], axis=1)
    grads, sums = mixer_backward(pre, state, grad_mixed, aux_back, par, rows)
    one_parts = cross_cols(grads, mix_full).astype(bf16).reshape(n_tp, n_t, share, width)
    grad_normed_one = tp_scatter([one_parts[r] for r in range(n_tp)], bf16)
    grad_mix_w = jnp.stack(weight_back(cross_rows(normed_one, grads).astype(bf16)))

    mixed = (mix_raw.astype(f32) * row_all[:, :1]).astype(bf16)
    grad_out_w = cross_rows(mixed, grad_mix).astype(bf16).reshape((2,) * len(free_bits) + (block, width))
    for i, b in enumerate(free_bits):
        send = lax.dynamic_slice_in_dim(grad_out_w, 1 - bit[b], 1, i)
        hold = lax.dynamic_slice_in_dim(grad_out_w, bit[b], 1, i)
        grad_out_w = (hold.astype(f32) + swap(send, 1 << b).astype(f32)).astype(bf16)
    grad_out_w = grad_out_w.reshape(block, width)
    for b in own_bits:
        grad_out_w = (grad_out_w.astype(f32) + swap(grad_out_w, 1 << b).astype(f32)).astype(bf16)
    mine_t = jnp.int32(0)
    for b in own_bits:
        mine_t = mine_t * 2 + bit[b]
    if n_t == 2:
        other = t_swap(grad_out_w)
        grad_output_proj = jnp.where(mine_t == t, grad_out_w, other).astype(f32)
    else:
        grad_output_proj = pick(lax.all_gather(grad_out_w, "tensor", axis=0), mine_t, 0).astype(f32)

    mix_all = t_gather(grad_mix_w)
    mix_all = mix_all.reshape((2,) * t_depth + (2, 2) + (block, 3) + (2,) * len(free_bits) + (block,))
    order = list(own_bits) + list(tp_bits) + ["row", "which"] + list(free_bits) + ["col"]
    axes = [order.index(k) for k in ["which", "row"] + list(reversed(range(depth))) + ["col"]]
    mix_all = mix_all.transpose(axes).reshape(3, block, width).astype(f32)

    grad_tokens_half = my_half_residual = grad_residual + norm_back(
        inputs_half, scale_one_half, norm_gain, grad_normed_one
    )
    grad_tokens = t_gather(grad_tokens_half).reshape(rows, width)
    norm_gain_sum = jnp.sum(grad_normed_one * inputs_half * scale_one_half, axis=0)

    gains = jnp.stack([norm_gain_sum, ffn_gain_sum]).reshape((2,) + (2,) * depth + (block,))
    for b in reversed(range(depth)):
        at = 1 + axis_of[b]
        send = lax.dynamic_slice_in_dim(gains, 1 - bit[b], 1, at)
        hold = lax.dynamic_slice_in_dim(gains, bit[b], 1, at)
        gains = hold + swap(send, 1 << b)
    gains = gains.reshape(2, block)
    gains = gains + t_swap(gains) if n_t == 2 else lax.psum(gains, "tensor")

    for b in fs_bits:
        sums = sums + swap(sums, 1 << b)
    sums = t_gather(sums)
    sums = pick(sums, mine_t, 0).reshape((2,) + (2,) * len(free_bits) + (block,))
    for b in free_bits:
        sums = pick(sums, bit[b], 1)
    shares, picked, lower = bound_parts(lax.dynamic_slice_in_dim(bound_table, me * block, block, 1))
    grad_table = shares * (picked - lower[None, :]) * sums[1][None, :]

    return (
        block_out,
        grad_tokens,
        mix_all[0],
        mix_all[1],
        mix_all[2],
        grad_output_proj,
        grad_glu_gate,
        grad_glu_up,
        grad_glu_down,
        gains[0],
        sums[0],
        gains[1],
        grad_table,
    )


def solution(mesh):
    return jax.shard_map(
        functools.partial(body, mesh.shape["dp"], mesh.shape["tensor"]),
        mesh=mesh,
        in_specs=(
            P("dp", None),
            P("dp", None),
            P("dp", None),
            P("dp", None),
            P("dp", None),
            P("dp", "tensor"),
            P("dp", "tensor"),
            P("tensor", "dp"),
            P(),
            P(),
            P(),
            P(),
            P("dp"),
            P("dp"),
            P(("dp", "tensor"), None),
        ),
        out_specs=(
            P(("dp", "tensor"), None),
            P("dp", None),
            P("dp", None),
            P("dp", None),
            P("dp", None),
            P("dp", None),
            P("dp", "tensor"),
            P("dp", "tensor"),
            P("tensor", "dp"),
            P("dp"),
            P("dp"),
            P("dp"),
            P(None, "dp"),
        ),
        check_vma=False,
    )
```

```python
import functools

import jax
import jax.numpy as jnp
from jax import lax
from jax.experimental import pallas as pl
from jax.experimental.pallas import tpu as pltpu
from jax.sharding import PartitionSpec as P

LAYER = 12
epsilon = 1e-06
bf16 = jnp.bfloat16
f32 = jnp.float32


def rms_scale(values):
    return lax.rsqrt(jnp.mean(values * values, axis=-1, keepdims=True) + epsilon)


def norm_back(values, row_scale, gain_row, incoming):
    weighted = incoming * gain_row
    cubed = row_scale * row_scale * row_scale
    return row_scale * weighted - values * cubed * jnp.mean(
        weighted * values, axis=-1, keepdims=True
    )


def silu_slope(values):
    logistic = jax.nn.sigmoid(values)
    return logistic * (1.0 + values * (1.0 - logistic))


def matmul(first_op, second_op):
    return jnp.dot(first_op, second_op, preferred_element_type=f32)


def cross_rows(first_op, second_op):
    return lax.dot_general(
        first_op, second_op, (((0,), (0,)), ((), ())), preferred_element_type=f32
    )


def cross_cols(first_op, second_op):
    return lax.dot_general(
        first_op, second_op, (((1,), (1,)), ((), ())), preferred_element_type=f32
    )


def pick(values, index, axis):
    return lax.dynamic_index_in_dim(values, index, axis, keepdims=False)


def layout(lengths, bucket, row_count):
    slot_len = row_count // jnp.left_shift(jnp.int32(1), bucket)
    position = jnp.arange(row_count, dtype=jnp.int32)
    slot_index = position // slot_len
    offset = position - slot_index * slot_len
    slot_ids = jnp.arange(lengths.shape[0], dtype=jnp.int32)
    chosen = (slot_index[:, None] == slot_ids[None, :]).astype(jnp.int32)
    slot_limit = jnp.sum(chosen * lengths[None, :], axis=1)
    valid_mask = (offset < slot_limit).astype(f32)[:, None]
    keep_mask = (offset > 0).astype(f32)[:, None]
    return (valid_mask, keep_mask)


def bound_parts(bound_table):
    shares = jax.nn.softmax(bound_table, axis=0)
    layer_ids = jnp.arange(bound_table.shape[0], dtype=jnp.int32)[:, None]
    picked = ((layer_ids >= 1) & (layer_ids <= LAYER)).astype(f32)
    return (shares, picked, jnp.sum(shares * picked, axis=0))


def scan_rows(decay_ref, add_ref, out_ref, reverse):
    rows, width = out_ref.shape
    tiles = rows // 8
    sub = lax.broadcasted_iota(jnp.int32, (8, width), 0)

    def step(i, carry):
        j = tiles - 1 - i if reverse else i
        at = pl.ds(pl.multiple_of(j * 8, 8), 8)
        a = decay_ref[at, :]
        b = add_ref[at, :]
        for s in (1, 2, 4):
            shift = 8 - s if reverse else s
            inside = sub < 8 - s if reverse else sub >= s
            b = jnp.where(inside, b + a * pltpu.roll(b, shift, 0), b)
            a = jnp.where(inside, a * pltpu.roll(a, shift, 0), a)
        h = b + a * carry
        out_ref[at, :] = h
        edge = h[0:1, :] if reverse else h[7:8, :]
        return jnp.broadcast_to(edge, (8, width))

    lax.fori_loop(0, tiles, step, jnp.zeros((8, width), f32), unroll=4)


def mixer_forward_kernel(pre_ref, aux_ref, par_ref, state_ref, mix_ref, sq_ref, decay_ref, add_ref):
    width = state_ref.shape[1]
    input_pre = pre_ref[:, :width]
    forget_pre = pre_ref[:, width : 2 * width]
    outgate_pre = pre_ref[:, 2 * width :]
    valid = aux_ref[:, 0:1]
    keep = aux_ref[:, 1:2]
    bound = par_ref[0:1, :]
    gain = par_ref[1:2, :]
    forget = bound + (1.0 - bound) * jax.nn.sigmoid(forget_pre)
    add_ref[...] = input_pre * jax.nn.sigmoid(input_pre) * (1.0 - forget) * valid
    decay_ref[...] = forget * keep
    scan_rows(decay_ref, add_ref, state_ref, False)
    state = state_ref[...]
    mix_ref[...] = (state * gain * (outgate_pre * jax.nn.sigmoid(outgate_pre))).astype(bf16)
    sq_ref[...] = jnp.sum(state * state, axis=1, keepdims=True)


def mixer_forward(pre, aux, par, seq_rows):
    rows, width = pre.shape[0], pre.shape[1] // 3
    row_block = lambda n: pl.BlockSpec((seq_rows, n), lambda i: (i, 0))
    return pl.pallas_call(
        mixer_forward_kernel,
        grid=(rows // seq_rows,),
        in_specs=[
            row_block(3 * width),
            row_block(aux.shape[1]),
            pl.BlockSpec(par.shape, lambda i: (0, 0)),
        ],
        out_specs=[row_block(width), row_block(width), row_block(1)],
        out_shape=[
            jax.ShapeDtypeStruct((rows, width), f32),
            jax.ShapeDtypeStruct((rows, width), bf16),
            jax.ShapeDtypeStruct((rows, 1), f32),
        ],
        scratch_shapes=[pltpu.VMEM((seq_rows, width), f32)] * 2,
        cost_estimate=pl.CostEstimate(
            flops=rows * width * 60, bytes_accessed=rows * width * 20, transcendentals=rows * width * 3
        ),
        name="mixer_forward",
    )(pre, aux, par)


def mixer_backward_kernel(
    pre_ref, state_ref, up_ref, aux_ref, par_ref, grad_ref, sums_ref, decay_ref, add_ref, out_ref
):
    rows, width = state_ref.shape
    input_pre = pre_ref[:, :width]
    forget_pre = pre_ref[:, width : 2 * width]
    outgate_pre = pre_ref[:, 2 * width :]
    valid = aux_ref[:, 0:1]
    keep = aux_ref[:, 1:2]
    scale = aux_ref[:, 2:3]
    dot_mean = aux_ref[:, 3:4]
    bound = par_ref[0:1, :]
    gain = par_ref[1:2, :]
    state = state_ref[...]
    incoming = up_ref[...]
    at_row = lax.broadcasted_iota(jnp.int32, (rows, width), 0)
    sig_out = jax.nn.sigmoid(outgate_pre)
    act_out = outgate_pre * sig_out
    scaled = incoming * (state * scale)
    grad_ref[:, 2 * width :] = (
        scaled * gain * (sig_out * (1.0 + outgate_pre * (1.0 - sig_out)))
    ).astype(bf16)
    add_ref[...] = scale * (gain * act_out * incoming) - state * (scale * scale * scale * dot_mean)
    sig_forget = jax.nn.sigmoid(forget_pre)
    forget = bound + (1.0 - bound) * sig_forget
    decay_ref[...] = jnp.where(
        at_row < rows - 1, pltpu.roll(forget * keep, rows - 1, 0), 0.0
    )
    scan_rows(decay_ref, add_ref, out_ref, True)
    grad_state = out_ref[...]
    before = jnp.where(at_row > 0, pltpu.roll(state, 1, 0), 0.0)
    sig_in = jax.nn.sigmoid(input_pre)
    grad_forget = grad_state * (before * keep - input_pre * sig_in * valid)
    grad_ref[:, :width] = (
        grad_state * (1.0 - forget) * valid * (sig_in * (1.0 + input_pre * (1.0 - sig_in)))
    ).astype(bf16)
    grad_ref[:, width : 2 * width] = (
        grad_forget * (1.0 - bound) * sig_forget * (1.0 - sig_forget)
    ).astype(bf16)

    @pl.when(pl.program_id(0) == 0)
    def _():
        sums_ref[...] = jnp.zeros_like(sums_ref)

    sums_ref[0:1, :] += jnp.sum(scaled * act_out, axis=0, keepdims=True)
    sums_ref[1:2, :] += jnp.sum(grad_forget * (1.0 - sig_forget), axis=0, keepdims=True)


def mixer_backward(pre, state, incoming, aux, par, seq_rows):
    rows, width = state.shape
    row_block = lambda n: pl.BlockSpec((seq_rows, n), lambda i: (i, 0))
    whole = lambda shape: pl.BlockSpec(shape, lambda i: (0, 0))
    return pl.pallas_call(
        mixer_backward_kernel,
        grid=(rows // seq_rows,),
        in_specs=[
            row_block(3 * width),
            row_block(width),
            row_block(width),
            row_block(aux.shape[1]),
            whole(par.shape),
        ],
        out_specs=[row_block(3 * width), whole((2, width))],
        out_shape=[
            jax.ShapeDtypeStruct((rows, 3 * width), bf16),
            jax.ShapeDtypeStruct((2, width), f32),
        ],
        scratch_shapes=[pltpu.VMEM((seq_rows, width), f32)] * 3,
        cost_estimate=pl.CostEstimate(
            flops=rows * width * 90, bytes_accessed=rows * width * 26, transcendentals=rows * width * 3
        ),
        name="mixer_backward",
    )(pre, state, incoming, aux, par)


MESH = pl.DeviceIdType.MESH


class Copies:
    def __init__(self, send, recv, local):
        self.send, self.recv, self.local = send, recv, local
        self.n_remote = self.n_local = 0
        self.open = []

    def remote(self, src, dst, device):
        k = self.n_remote
        self.n_remote += 1
        copy = pltpu.make_async_remote_copy(
            src_ref=src,
            dst_ref=dst,
            send_sem=self.send.at[k],
            recv_sem=self.recv.at[k],
            device_id=device,
            device_id_type=MESH,
        )
        copy.start()
        self.open.append(copy.wait_send)
        return copy

    def here(self, src, dst, keep=False):
        k = self.n_local
        self.n_local += 1
        copy = pltpu.make_async_copy(src, dst, self.local.at[k])
        copy.start()
        if keep:
            self.open.append(copy.wait)
        return copy

    def sent(self, copies):
        for copy in copies:
            copy.wait_send()
            self.open.remove(copy.wait_send)

    def close(self):
        assert self.n_remote <= self.send.shape[0] and self.n_local <= self.local.shape[0]
        for wait in self.open:
            wait()


def position():
    me = lax.axis_index("dp")
    t = lax.axis_index("tensor")
    zf, zn, y, x = me // 8, (me // 4) % 2, (me // 2) % 2, me % 2
    to_x, to_zn = 1 - 2 * x, 4 - 8 * zn
    group = [None, (me + to_x, t), (me + to_zn, t), (me + to_x + to_zn, t)]
    q = [zn * 2 + x, zn * 2 + 1 - x, (1 - zn) * 2 + x, (1 - zn) * 2 + 1 - x]
    far = (me + 8 - 16 * zf, t)
    side = (me + 2 - 4 * y, t)
    core = (me, 1 - t)
    return me, t, (zf, zn, y, x), q, group, far, side, core


def meet(devices):
    barrier = pltpu.get_barrier_semaphore()
    for device in devices:
        pl.semaphore_signal(barrier, inc=1, device_id=device, device_id_type=MESH)
    pl.semaphore_wait(barrier, len(devices))


def fold_lanes(values):
    width = values.shape[1]
    if width % 128:
        return values
    total = values[:, :128]
    for i in range(128, width, 128):
        total = total + values[:, i : i + 128]
    return total


def front_kernel(
    s_in, s_fg, s_og, s_out, w_g, w_u, s_d, cot, tok, gain_one, gain_mix, gain_two, table, lengths, bucket,
    o_mix, o_out, o_g, o_u, o_d, o_n1, o_go, o_n2, o_pre, o_state, o_raw, o_res, o_mo, o_sc, o_aux, o_par, o_hid, o_hg, o_hu, o_coef,
    w_mix, w_out, n1, aux, pre, state, raw, part, core_in, half, peer_in, par, wide_g, wide_u, s_g, s_u, go_own, bound_row, full_g, full_u, gate, up, into, hid_v, hid_g, hid_u, all_powers, coef,
    sq, sq_core, sq_half, sq_peer, res, mo, sc, n2, decay, add,
    send, recv, local, core_send, core_recv, sqc_send, sqc_recv, out_send, out_recv, x_send, x_recv,
):
    me, t, (zf, zn, y, x), q, group, far, side, core = position()
    rows, width = tok.shape
    share = rows // 2
    block = s_out.shape[0]
    feat = par.shape[1]
    hid = s_d.shape[0] // 4
    link = Copies(send, recv, local)
    get_g, get_u, get_cot = link.here(w_g, wide_g), link.here(w_u, wide_u), link.here(cot, go_own)
    meet(group[1:] + [far, side, core])

    def at(start, size, unit):
        return pl.ds(pl.multiple_of(start, unit), size)

    def pair(fz, c, fy):
        return at(fz * (8 * block) + c * (4 * block) + fy * (2 * block), 2 * block, 2 * block)

    mine = at(me * block, block, block)

    def row(r, tt):
        return at(r * rows + tt * share, share, share)

    def columns(r, fz):
        fx = x if r in (0, 2) else 1 - x
        fzn = zn if r in (0, 1) else 1 - zn
        return at((fz * 8 + fzn * 4 + t * 2 + fx) * block, block, block)

    mix_in, mix_own = [], []
    for k, s in enumerate((s_in, s_fg, s_og)):
        for fz in (0, 1):
            to = w_mix.at[mine, pl.ds(k * feat + fz * block, block)]
            mix_in += [link.remote(s.at[:, columns(r, fz)], to, group[r]) for r in (1, 2, 3)]
            mix_own.append(link.here(s.at[:, columns(0, fz)], to))
    out_rows = [at(z * block, block, block) for z in (zf, 1 - zf)]

    def out_copy(k, src, dst, device):
        return pltpu.make_async_remote_copy(
            src_ref=src,
            dst_ref=w_out.at[dst],
            send_sem=out_send.at[k],
            recv_sem=out_recv.at[k],
            device_id=device,
            device_id_type=MESH,
        )

    out_far = out_copy(0, s_out, out_rows[0], far)
    out_side = out_copy(1, s_out, out_rows[0], side)
    out_next = out_copy(2, w_out.at[out_rows[1]], out_rows[1], side)
    out_here = pltpu.make_async_copy(s_out, w_out.at[out_rows[0]], out_send.at[3])

    @pl.when(t == y)
    def _():
        out_far.start()
        out_side.start()
        out_here.start()

    norm_row = gain_one[...]

    def norm_rows(first):
        def some(j, carry):
            to = at(first + j * 16, 16, 16)
            value = tok[to, :].astype(f32)
            s = lax.rsqrt(jnp.mean(value * value, axis=1, keepdims=True) + epsilon)
            n1[to, :] = (value * s * norm_row).astype(bf16)
            return carry

        lax.fori_loop(0, share // 16, some, 0)

    norm_rows(t * share)
    n1_in = [link.remote(n1.at[row(0, t)], n1.at[row(r, t)], group[r]) for r in (1, 2)]

    count = lengths.shape[0]
    slot_len = lax.shift_right_logical(jnp.int32(rows), bucket[0])
    position_row = lax.broadcasted_iota(jnp.int32, (1, rows), 1)
    slot = jnp.zeros((1, rows), jnp.int32)
    for j in range(1, count):
        slot = slot + (position_row >= j * slot_len).astype(jnp.int32)
    limit = jnp.zeros((1, rows), jnp.int32)
    for j in range(count):
        limit = limit + jnp.where(slot == j, lengths[j], 0)
    offset = position_row - slot * slot_len
    aux[0] = jnp.zeros(aux.shape[1:], f32)
    aux[0, 0:1, :] = (offset < limit).astype(f32)
    aux[0, 1:2, :] = (offset > 0).astype(f32)
    aux_in = [link.remote(aux.at[0], aux.at[r], group[r]) for r in (1, 2, 3)]

    norm_rows((1 - t) * share)
    for c in mix_own:
        c.wait()
    for c in mix_in:
        c.wait_recv()
    far_mix = [link.remote(w_mix.at[pair(zf, c, y)], w_mix.at[pair(zf, c, y)], far) for c in (0, 1)]
    side_mix = [link.remote(w_mix.at[pair(zf, c, y)], w_mix.at[pair(zf, c, y)], side) for c in (0, 1)]
    n1_in[1].wait_recv()
    n1_in.append(link.remote(n1.at[row(2, t)], n1.at[row(3, t)], group[1]))
    n1_core = [link.remote(n1.at[row(2, t)], n1.at[row(2, t)], core)]
    n1_in[0].wait_recv()
    n1_core.append(link.remote(n1.at[row(1, t)], n1.at[row(1, t)], core))
    shards = ((s_g, o_g), (s_u, o_u), (s_d, o_d))
    ffn_in, ffn_own = [], []

    def turn_round(wide, tall):
        size = min(128, wide.shape[1])

        def some(j, carry):
            to = at(j * size, size, size)
            tall[to, :] = wide[:, to].astype(f32).T.astype(bf16)
            return carry

        lax.fori_loop(0, wide.shape[1] // size, some, 0)

    def leave(s, o):
        units = [at(q[r] * hid, hid, 16) for r in range(4)]
        ffn_in.extend(link.remote(s.at[units[r]], o.at[:, mine], group[r]) for r in (1, 2, 3))
        ffn_own.append(link.here(s.at[units[0]], o.at[:, mine]))

    get_g.wait()
    turn_round(wide_g, s_g)
    leave(s_g, o_g)
    get_u.wait()
    turn_round(wide_u, s_u)
    leave(s_u, o_u)
    leave(s_d, o_d)

    logits = table[...]
    powers = jnp.exp(logits - jnp.max(logits, axis=0, keepdims=True))
    layer_ids = lax.broadcasted_iota(jnp.int32, logits.shape, 0)
    picked = jnp.where((layer_ids >= 1) & (layer_ids <= LAYER), powers, 0.0)
    bound_row[0:1, :] = jnp.sum(picked, axis=0, keepdims=True) / jnp.sum(powers, axis=0, keepdims=True)
    all_powers[...] = powers
    mine_powers = all_powers[:, mine]
    mine_shares = mine_powers / jnp.sum(mine_powers, axis=0, keepdims=True)
    ids = lax.broadcasted_iota(jnp.int32, mine_shares.shape, 0)
    mine_picked = ((ids >= 1) & (ids <= LAYER)).astype(f32)
    coef[...] = mine_shares * (mine_picked - jnp.sum(mine_shares * mine_picked, axis=0, keepdims=True))
    link.here(coef, o_coef, keep=True)
    for fz in (0, 1):
        par[0:1, fz * block : (fz + 1) * block] = bound_row[0:1, columns(0, fz)]
        par[1:2, fz * block : (fz + 1) * block] = gain_mix[0:1, columns(0, fz)]
    get_cot.wait()
    valid_rows = aux[0].T[:, 0:1]
    first_half = lax.broadcasted_iota(jnp.int32, (share, 1), 0) * 0 + t
    valid_half = jnp.where(first_half == 0, valid_rows[:share], valid_rows[share:])
    go_own[...] = (go_own[...].astype(f32) * valid_half).astype(bf16)
    n1_in[2].wait_recv()
    n1_core.append(link.remote(n1.at[row(3, t)], n1.at[row(3, t)], core))
    for c in (0, 1):
        far_mix[c].wait_recv()
        side_mix.append(link.remote(w_mix.at[pair(1 - zf, c, y)], w_mix.at[pair(1 - zf, c, y)], side))

    @pl.when(t == y)
    def _():
        out_far.wait_recv()
        out_next.start()
        out_far.wait_send()
        out_side.wait_send()
        out_here.wait()
        out_next.wait_send()

    @pl.when(t != y)
    def _():
        out_side.wait_recv()
        out_next.wait_recv()

    far_ffn, side_ffn = [], ([], [], [])

    def start_ffn(i):
        o = shards[i][1]
        ffn_own[i].wait()
        for c in ffn_in[3 * i : 3 * i + 3]:
            c.wait_recv()
        far_ffn.append([link.remote(o.at[:, pair(zf, c, y)], o.at[:, pair(zf, c, y)], far) for c in (0, 1)])
        side_ffn[i].extend(link.remote(o.at[:, pair(zf, c, y)], o.at[:, pair(zf, c, y)], side) for c in (0, 1))

    def forward_ffn(i):
        o = shards[i][1]
        for c in (0, 1):
            far_ffn[i][c].wait_recv()
            side_ffn[i].append(link.remote(o.at[:, pair(1 - zf, c, y)], o.at[:, pair(1 - zf, c, y)], side))

    start_ffn(0)
    go_in = [link.remote(go_own, o_go.at[row(r, t)], group[r]) for r in (1, 2)]
    go_core = [link.remote(go_own, o_go.at[row(0, t)], core)]
    go_here = link.here(go_own, o_go.at[row(0, t)])

    for c in side_mix + n1_core + aux_in:
        c.wait_recv()

    def core_copy(r):
        return pltpu.make_async_remote_copy(
            src_ref=part.at[row(r, 1 - t)],
            dst_ref=core_in.at[at(r * share, share, share)],
            send_sem=core_send.at[r],
            recv_sem=core_recv.at[r],
            device_id=core,
            device_id_type=MESH,
        )

    def sq_copy(r):
        return pltpu.make_async_remote_copy(
            src_ref=sq.at[row(r, 1 - t)],
            dst_ref=sq_core.at[at(r * share, share, share)],
            send_sem=sqc_send.at[r],
            recv_sem=sqc_recv.at[r],
            device_id=core,
            device_id_type=MESH,
        )

    bound = par[0:1, :]
    gain = par[1:2, :]

    def to_x(slot, r):
        from_rows, to_rows = at(r * share, share, share), at(slot * share, share, share)
        return [
            pltpu.make_async_remote_copy(
                src_ref=a.at[from_rows],
                dst_ref=b.at[to_rows],
                send_sem=x_send.at[i * 2 + slot],
                recv_sem=x_recv.at[i * 2 + slot],
                device_id=group[1],
                device_id_type=MESH,
            )
            for i, (a, b) in enumerate(((half, peer_in), (sq_half, sq_peer)))
        ]

    def hand_over(r):
        core_copy(r).wait()
        sq_copy(r).wait()

        def some(j, carry):
            to = at(r * share + j * 16, 16, 16)
            mine_rows = at(r * rows + t * share + j * 16, 16, 16)
            half[to, :] = (part[mine_rows, :].astype(f32) + core_in[to, :].astype(f32)).astype(bf16)
            sq_half[to, :] = sq[mine_rows, :] + sq_core[to, :]
            return carry

        lax.fori_loop(0, share // 16, some, 0)

    def piece(i, carry):
        r = 3 - 2 * i + 3 * (i // 2)
        here = at(r * rows, rows, rows)
        pre[here, :] = jnp.dot(n1[here, :], w_mix[...], preferred_element_type=f32)
        masks = aux[r].T
        valid = masks[:, 0:1]
        keep = masks[:, 1:2]
        forget = bound + (1.0 - bound) * jax.nn.sigmoid(pre[here, feat : 2 * feat])
        input_pre = pre[here, 0:feat]
        add[...] = input_pre * jax.nn.sigmoid(input_pre) * (1.0 - forget) * valid
        decay[...] = forget * keep
        scan_rows(decay, add, state.at[here, :], False)
        held = state[here, :]
        outgate_pre = pre[here, 2 * feat :]
        raw[here, :] = (held * gain * (outgate_pre * jax.nn.sigmoid(outgate_pre))).astype(bf16)
        sq[here, :] = fold_lanes(held * held)
        part[here, :] = jnp.dot(raw[here, :], w_out[...], preferred_element_type=f32).astype(bf16)
        core_copy(r).start()
        sq_copy(r).start()

        @pl.when(i > 0)
        def _():
            before = 5 - 2 * i + 3 * ((i - 1) // 2)
            hand_over(before)

            @pl.when(i < 3)
            def _():
                for c in to_x(i - 1, before):
                    c.start()

        return carry

    lax.fori_loop(0, 4, piece, 0)
    start_ffn(1)

    link.here(w_mix, o_mix, keep=True)
    link.here(w_out, o_out, keep=True)
    n1_out = link.here(n1, o_n1)
    link.here(pre, o_pre, keep=True)
    link.here(state, o_state, keep=True)
    link.here(raw, o_raw, keep=True)
    link.here(aux, o_aux, keep=True)
    link.here(par, o_par, keep=True)

    def spread(o, incoming, cores):
        incoming[1].wait_recv()
        incoming.append(link.remote(o.at[row(2, t)], o.at[row(3, t)], group[1]))
        cores.append(link.remote(o.at[row(2, t)], o.at[row(2, t)], core))
        incoming[0].wait_recv()
        cores.append(link.remote(o.at[row(1, t)], o.at[row(1, t)], core))

    def spread_last(o, incoming, cores):
        incoming[2].wait_recv()
        cores.append(link.remote(o.at[row(3, t)], o.at[row(3, t)], core))

    hand_over(0)
    for c in to_x(0, 3):
        c.wait()

    def pass_on(j, carry):
        two = at(2 * share + j * 16, 16, 16)
        half[two, :] = (half[two, :].astype(f32) + peer_in[at(j * 16, 16, 16), :].astype(f32)).astype(bf16)
        sq_half[two, :] = sq_half[two, :] + sq_peer[at(j * 16, 16, 16), :]
        return carry

    lax.fori_loop(0, share // 16, pass_on, 0)
    third = pl.ds(2 * share, share)
    to_z = [
        link.remote(half.at[third], peer_in.at[third], group[2]),
        link.remote(sq_half.at[third], sq_peer.at[third], group[2]),
    ]
    spread(o_go, go_in, go_core)
    forward_ffn(0)
    for c in to_x(1, 1):
        c.wait()
    for c in to_z:
        c.wait_recv()
    total_sq = sq_half[0:share, :] + sq_peer[share : 2 * share, :] + sq_peer[2 * share : 3 * share, :]
    scale = lax.rsqrt(jnp.sum(total_sq, axis=1, keepdims=True) / width + epsilon)
    sc[...] = jnp.broadcast_to(scale, sc.shape)
    chunk = min(share, 16)

    def finish(i, carry):
        to = at(i * chunk, chunk, chunk)
        total = part[at(t * share + i * chunk, chunk, chunk), :].astype(f32) + core_in[to, :].astype(f32)
        for r in (1, 2):
            total = total + peer_in[at(r * share + i * chunk, chunk, chunk), :].astype(f32)
        mixed = total * sc[to, 0:1]
        value = tok[at(t * share + i * chunk, chunk, chunk), :].astype(f32) + mixed
        mo[to, :] = mixed
        res[to, :] = value
        scale_two = lax.rsqrt(jnp.mean(value * value, axis=1, keepdims=True) + epsilon)
        n2[to, :] = (value * scale_two * gain_two[...]).astype(bf16)
        return carry

    lax.fori_loop(0, share // chunk, finish, 0)
    n2_in = [link.remote(n2, o_n2.at[row(r, t)], group[r]) for r in (1, 2)]
    n2_core = [link.remote(n2, o_n2.at[row(0, t)], core)]
    n2_here = link.here(n2, o_n2.at[row(0, t)])
    link.here(res, o_res, keep=True)
    link.here(mo, o_mo, keep=True)
    link.here(sc, o_sc, keep=True)
    start_ffn(2)
    spread_last(o_go, go_in, go_core)
    forward_ffn(1)
    spread(o_n2, n2_in, n2_core)
    spread_last(o_n2, n2_in, n2_core)

    forward_ffn(2)

    for c in side_ffn[0]:
        c.wait_recv()
    get_full = link.here(o_g, full_g)
    for c in n2_core:
        c.wait_recv()
    n2_here.wait()
    get_rows = link.here(o_n2, part)
    get_full.wait()
    get_rows.wait()

    def product(full, made):
        def some(j, carry):
            to = at(j * rows, rows, rows)
            made[:, to] = lax.dot_general(
                full[...], part[to, :], (((1,), (1,)), ((), ())), preferred_element_type=f32
            )
            return carry

        lax.fori_loop(0, 4, some, 0)

    product(full_g, gate)
    for c in side_ffn[1]:
        c.wait_recv()
    get_full = link.here(o_u, full_u)
    get_full.wait()
    for c in go_core:
        c.wait_recv()
    go_here.wait()
    n1_out.wait()
    link.sent(n1_in + n1_core)
    get_rows = link.here(o_go, n1)
    for c in side_ffn[2][:2]:
        c.wait_recv()
    early = [pair(fz, c, fy) for fz, fy in ((zf, y), (zf, 1 - y), (1 - zf, y)) for c in (0, 1)]
    get_early = [link.here(o_d.at[:, cols], full_g.at[:, cols]) for cols in early]
    product(full_u, up)
    for c in get_early + [get_rows]:
        c.wait()

    def contribution(cols, to):
        return lax.dot_general(
            full_g[:, cols], n1[to, cols], (((1,), (1,)), ((), ())), preferred_element_type=f32
        )

    def early_rows(j, carry):
        to = at(j * rows, rows, rows)
        total = contribution(early[0], to)
        for cols in early[1:]:
            total = total + contribution(cols, to)
        into[:, to] = total
        return carry

    lax.fori_loop(0, 4, early_rows, 0)
    late = [pair(1 - zf, c, 1 - y) for c in (0, 1)]
    get_late = []
    for c, cols in zip(side_ffn[2][2:], late):
        c.wait_recv()
        get_late.append(link.here(o_d.at[:, cols], full_g.at[:, cols]))
    for c in get_late:
        c.wait()

    def hidden_rows(j, carry):
        to = at(j * rows, rows, rows)
        grad = into[:, to] + contribution(late[0], to) + contribution(late[1], to)
        value, other = gate[:, to], up[:, to]
        sig = jax.nn.sigmoid(value)
        act = value * sig
        hid_v[:, to] = (act * other).astype(bf16)
        hid_u[:, to] = (grad * act).astype(bf16)
        hid_g[:, to] = (grad * other * (sig * (1.0 + value * (1.0 - sig)))).astype(bf16)
        return carry

    lax.fori_loop(0, 4, hidden_rows, 0)
    for made, out in ((hid_v, o_hid), (hid_g, o_hg), (hid_u, o_hu)):
        link.here(made, out, keep=True)
    link.close()


def front(s_in, s_fg, s_og, s_out, w_g, w_u, s_d, cot, tok, gain_one, gain_mix, gain_two, table, lengths, bucket):
    rows, width = tok.shape
    share, group_rows = rows // 2, 4 * rows
    block = s_out.shape[0]
    feat, hid = 2 * block, s_d.shape[0] // 4
    lanes = 128 if feat % 128 == 0 else feat
    any_spec = pl.BlockSpec(memory_space=pl.ANY)
    vmem_spec = pl.BlockSpec(memory_space=pltpu.VMEM)
    made = jax.ShapeDtypeStruct
    outs = [
        made((width, 3 * feat), bf16),
        made((feat, width), bf16),
        made((hid, width), bf16),
        made((hid, width), bf16),
        made((hid, width), bf16),
        made((group_rows, width), bf16),
        made((group_rows, width), bf16),
        made((group_rows, width), bf16),
        made((group_rows, 3 * feat), f32),
        made((group_rows, feat), f32),
        made((group_rows, feat), bf16),
        made((share, width), f32),
        made((share, width), f32),
        made((share, 128), f32),
        made((4, 8, rows), f32),
        made((2, feat), f32),
        made((hid, group_rows), bf16),
        made((hid, group_rows), bf16),
        made((hid, group_rows), bf16),
        made((table.shape[0], block), f32),
    ]
    scratch = [
        pltpu.VMEM((width, 3 * feat), bf16),
        pltpu.VMEM((feat, width), bf16),
        pltpu.VMEM((group_rows, width), bf16),
        pltpu.VMEM((4, 8, rows), f32),
        pltpu.VMEM((group_rows, 3 * feat), f32),
        pltpu.VMEM((group_rows, feat), f32),
        pltpu.VMEM((group_rows, feat), bf16),
        pltpu.VMEM((group_rows, width), bf16),
        pltpu.VMEM((4 * share, width), bf16),
        pltpu.VMEM((4 * share, width), bf16),
        pltpu.VMEM((4 * share, width), bf16),
        pltpu.VMEM((2, feat), f32),
        pltpu.VMEM(w_g.shape, bf16),
        pltpu.VMEM(w_u.shape, bf16),
        pltpu.VMEM((4 * hid, block), bf16),
        pltpu.VMEM((4 * hid, block), bf16),
        pltpu.VMEM((share, width), bf16),
        pltpu.VMEM((8, width), f32),
        pltpu.VMEM((hid, width), bf16),
        pltpu.VMEM((hid, width), bf16),
        pltpu.VMEM((hid, group_rows), f32),
        pltpu.VMEM((hid, group_rows), f32),
        pltpu.VMEM((hid, group_rows), f32),
        pltpu.VMEM((hid, group_rows), bf16),
        pltpu.VMEM((hid, group_rows), bf16),
        pltpu.VMEM((hid, group_rows), bf16),
        pltpu.VMEM(table.shape, f32),
        pltpu.VMEM((table.shape[0], block), f32),
        pltpu.VMEM((group_rows, lanes), f32),
        pltpu.VMEM((4 * share, lanes), f32),
        pltpu.VMEM((4 * share, lanes), f32),
        pltpu.VMEM((4 * share, lanes), f32),
        pltpu.VMEM((share, width), f32),
        pltpu.VMEM((share, width), f32),
        pltpu.VMEM((share, 128), f32),
        pltpu.VMEM((share, width), bf16),
        pltpu.VMEM((rows, feat), f32),
        pltpu.VMEM((rows, feat), f32),
        pltpu.SemaphoreType.DMA((88,)),
        pltpu.SemaphoreType.DMA((88,)),
        pltpu.SemaphoreType.DMA((48,)),
    ] + [pltpu.SemaphoreType.DMA((4,))] * 8
    return pl.pallas_call(
        front_kernel,
        in_specs=[any_spec] * 8 + [vmem_spec] * 5 + [pl.BlockSpec(memory_space=pltpu.SMEM)] * 2,
        out_specs=[any_spec] * len(outs),
        out_shape=outs,
        scratch_shapes=scratch,
        compiler_params=pltpu.CompilerParams(
            collective_id=1, has_side_effects=True, vmem_limit_bytes=60 << 20
        ),
        name="front",
    )(s_in, s_fg, s_og, s_out, w_g, w_u, s_d, cot, tok, gain_one, gain_mix, gain_two, table, lengths, bucket)


def back_kernel(
    h_d, h_g, h_u, n2, go, w_g, w_u, w_d, n1, w_mix_in, w_out_in, pre, state, raw, aux_in,
    par, tok, res, mo, sc, first_gain, second_gain,
    o_g, o_u, o_d, o_mix, o_out, o_tok, o_blk, o_vec,
    left, right, gmix, dw_d, dw_g, dw_u, dw_mix, yr_d, yr_g, yr_u, yr_mix, zr_d, zr_g, zr_u, zr_mix,
    own, half, core_in, core_blk, peer_in, peer_blk, w_mix, w_out, aux, pre_b, state_b, raw_b,
    grads, grads_t, decay, add, yr_out, zr_out, hid_a, hid_b,
    gres, gm_own, scalars, scal_all, sums, vec, vec_in,
    send, recv, local, core_send, core_recv, out_send, out_recv, piece_sem,
):
    me, t, (zf, zn, y, x), q, group, far, side, core = position()
    rows, width = tok.shape
    share = rows // 2
    block = width // 16
    feat = par.shape[1]
    link = Copies(send, recv, local)
    meet(group[1:] + [far, side, core])

    def at(start, size, unit):
        return pl.ds(pl.multiple_of(start, unit), size)

    def pair(fz, c, fy):
        return at(fz * (8 * block) + c * (4 * block) + fy * (2 * block), 2 * block, 2 * block)

    def row(r, tt):
        return at(r * rows + tt * share, share, share)

    def rel(r):
        return pl.ds(r * share, share)

    hid_rows = pl.ds(0, w_g.shape[0])
    full_g, full_u = left.at[hid_rows], gmix.at[hid_rows]
    get_g = [link.here(h_g, hid_a), link.here(n2, right)]
    get_u = link.here(h_u, hid_b)
    get_two = [link.here(w_g, full_g), link.here(w_u, full_u)]
    get_go = [link.here(go.at[row(0, t)], gm_own)]
    get_w_d = link.here(w_d, dw_d)
    get_aux = [link.here(aux_in, aux), link.here(w_mix_in, w_mix)]
    order = (3, 1, 2, 0)

    def stage(r):
        i = order.index(r)
        return w_out if i == 3 else dw_mix.at[i]

    def staged(r, tt):
        return w_out.at[at(tt * share, share, share)] if r == 0 else stage(r).at[tt]

    def products(terms):
        wide = 4 * block

        def at_piece(r, store):
            here = at(r * rows, rows, rows)

            def some(j, carry):
                to = at(j * wide, wide, wide)
                total = None
                for hid, weight in terms:
                    one = lax.dot_general(
                        hid[:, here], weight[:, to], (((0,), (0,)), ((), ())), preferred_element_type=f32
                    )
                    total = one if total is None else total + one
                store(to, total.astype(bf16))
                return carry

            lax.fori_loop(0, width // wide, some, 0)

        return at_piece

    def all_pieces(terms, incoming):
        at_piece = products(terms)
        copies = {}
        for i, r in enumerate(order):
            if r:

                def store(to, value):
                    dw_mix[i, 0, :, to] = value[:share]
                    dw_mix[i, 1, :, to] = value[share:]

            else:

                def store(to, value):
                    w_out[:, to] = value

            at_piece(r, store)
            copies[r] = link.remote(staged(r, 1 - t), incoming.at[rel(r)], core)
        return copies

    def two_rows(r, j):
        if r == 0:
            return w_out[at(t * share + j * 16, 16, 16), :].astype(f32)
        return dw_mix[order.index(r), t, at(j * 16, 16, 16), :].astype(f32)

    def own_rows(r, j):
        return own[at(r * share + j * 16, 16, 16), :].astype(f32)

    def add_half(r, source, incoming, held):
        def some(j, carry):
            to = at(r * share + j * 16, 16, 16)
            held[to, :] = (source(r, j) + incoming[to, :].astype(f32)).astype(bf16)
            return carry

        lax.fori_loop(0, share // 16, some, 0)

    def over_cores(arrived, source, incoming, held, peers):
        sent = []
        for r in (3, 1, 2, 0):
            arrived[r].wait_recv()
            if r:
                add_half(r, source, incoming, held)
            if r % 2:
                sent.append(link.remote(held.at[rel(r)], peers.at[rel(len(sent))], group[1]))
        return sent

    def pass_on(sent, held, peers):
        sent[0].wait_recv()

        def some(j, carry):
            two = at(2 * share + j * 16, 16, 16)
            held[two, :] = (held[two, :].astype(f32) + peers[at(j * 16, 16, 16), :].astype(f32)).astype(bf16)
            return carry

        lax.fori_loop(0, share // 16, some, 0)
        sent.append(link.remote(held.at[rel(2)], peers.at[rel(2)], group[2]))


    def weight_grad(hid, other, dw, first, count):
        wide = 4 * block

        def columns(i, carry):
            to = at(((1 - zf) * 2 + i - (i // 2) * 4 * (1 - zf)) * wide, wide, wide)
            made = jnp.dot(hid[...], other[:, to], preferred_element_type=f32).astype(bf16)
            if len(dw.shape) == 2:
                dw[:, to] = made
            else:
                dw[:, :, :, to] = made.reshape(dw.shape[:3] + (wide,))
            return carry

        lax.fori_loop(first, first + count, columns, 0)

    def cut(ref, cols):
        return ref.at[:, cols] if len(ref.shape) == 2 else ref.at[:, :, :, cols]

    def side_send(dw, yr, slot):
        fz = 1 - zf if slot == 0 else zf
        return [
            link.remote(cut(dw, pair(fz, c, 1 - y)), cut(yr, pl.ds((slot * 2 + c) * 2 * block, 2 * block)), side)
            for c in (0, 1)
        ]

    def add_columns(dw, to, others):
        if len(dw.shape) == 2:
            size = 64 if dw.shape[0] % 64 == 0 else dw.shape[0]
            steps = dw.shape[0] // size
        else:
            steps = dw.shape[0] * dw.shape[1]

        def some(j, carry):
            if len(dw.shape) == 2:
                lead = (at(j * size, size, size),)
            else:
                lead = (j // dw.shape[1], j % dw.shape[1], slice(None))
            total = dw[lead + (to,)].astype(f32)
            for ref, cols in others:
                total = total + ref[lead + (cols,)].astype(f32)
            dw[lead + (to,)] = total.astype(bf16)
            return carry

        lax.fori_loop(0, steps, some, 0)

    def part_of(i):
        return pl.ds(i * 2 * block, 2 * block)

    def second_hop(hop, dw, yr, zr):
        sent = []
        for c in (0, 1):
            hop[c].wait_recv()
            add_columns(dw, pair(1 - zf, c, y), [(yr, part_of(c))])
            sent.append(link.remote(cut(dw, pair(1 - zf, c, y)), cut(zr, part_of(c)), far))
        return sent

    def last_hop(near, sent, dw, yr, zr, out):
        for c in (0, 1):
            near[c].wait_recv()
            sent[c].wait_recv()
            add_columns(dw, pair(zf, c, y), [(yr, part_of(2 + c)), (zr, part_of(c))])

        def owner(r):
            fx = x if r in (0, 2) else 1 - x
            fzn = zn if r in (0, 1) else 1 - zn
            return at((zf * 8 + fzn * 4 + y * 2 + fx) * block, block, block)

        if len(dw.shape) == 2:
            place = out.at[q[0]]
            link.here(dw.at[:, owner(0)], place, keep=True)
            return [link.remote(dw.at[:, owner(r)], place, group[r]) for r in (1, 2, 3)]
        place = out.at[:, :, zn, t, x]
        kept = link.here(cut(dw, owner(0)), place)
        sent = [link.remote(cut(dw, owner(r)), place, group[r]) for r in (1, 2, 3)]
        kept.wait()
        return sent

    for c in get_g:
        c.wait()
    weight_grad(hid_a, right, dw_g, 0, 2)
    hop_g = side_send(dw_g, yr_g, 0)
    get_u.wait()
    for c in get_two:
        c.wait()
    two_core = all_pieces([(hid_a, full_g), (hid_b, full_u)], core_in)

    two_peer = over_cores(two_core, two_rows, core_in, half, peer_in)
    weight_grad(hid_b, right, dw_u, 0, 2)
    get_left = link.here(go, left)
    weight_grad(hid_a, right, dw_g, 2, 2)
    get_d = link.here(h_d, hid_a)
    far_g = second_hop(hop_g, dw_g, yr_g, zr_g)
    hop_u = side_send(dw_u, yr_u, 0)
    pass_on(two_peer, half, peer_in)
    weight_grad(hid_b, right, dw_u, 2, 2)

    for c in two_peer[1:]:
        c.wait_recv()
    for c in get_go:
        c.wait()
    gain_two = second_gain[...]
    sums[...] = jnp.zeros_like(sums)
    step = 16

    def residual_rows(j, carry):
        to = at(j * step, step, step)
        total = two_rows(0, j) + core_in[to, :].astype(f32)
        for r in (1, 2):
            total = total + peer_in[at(r * share + j * step, step, step), :].astype(f32)
        value = res[to, :]
        s = lax.rsqrt(jnp.mean(value * value, axis=1, keepdims=True) + epsilon)
        weighted = total * gain_two
        grad = (
            gm_own[to, :].astype(f32)
            + s * weighted
            - value * (s * s * s) * jnp.mean(weighted * value, axis=1, keepdims=True)
        )
        gres[to, :] = grad
        low = grad.astype(bf16)
        gm_own[to, :] = low
        dot = jnp.sum(low.astype(f32) * mo[to, :], axis=1, keepdims=True)
        scale = sc[to, 0:1]
        sc[to, 1:2] = dot / (scale * width)
        sums[1:2, :] += jnp.sum(total * value * s, axis=0, keepdims=True)
        return carry

    lax.fori_loop(0, share // step, residual_rows, 0)
    scalars[...] = sc[...].T[0:8, :]

    def scal(r, tt):
        return scal_all.at[r * 2 + tt]

    gm_in = [link.remote(gm_own, gmix.at[row(r, t)], group[r]) for r in (1, 2)]
    sc_in = [link.remote(scalars, scal(r, t), group[r]) for r in (1, 2, 3)]
    gm_core = [link.remote(gm_own, gmix.at[row(0, t)], core), link.remote(scalars, scal(0, t), core)]
    gm_here = [link.here(gm_own, gmix.at[row(0, t)]), link.here(scalars, scal(0, t))]
    for c in (get_d, get_w_d, get_left):
        c.wait()
    link.sent(two_core.values())
    blk_core = all_pieces([(hid_a, dw_d)], core_blk)
    blk_own = [link.here(staged(r, t), own.at[rel(r)]) for r in order]
    weight_grad(hid_a, left, dw_d, 0, 2)
    hop_d = side_send(dw_d, yr_d, 0)
    far_u = second_hop(hop_u, dw_u, yr_u, zr_u)
    near_g = side_send(dw_g, yr_g, 1)
    gm_in[1].wait_recv()
    gm_in.append(link.remote(gmix.at[row(2, t)], gmix.at[row(3, t)], group[1]))
    gm_core.append(link.remote(gmix.at[row(2, t)], gmix.at[row(2, t)], core))
    gm_in[0].wait_recv()
    gm_core.append(link.remote(gmix.at[row(1, t)], gmix.at[row(1, t)], core))
    for i, r in enumerate((1, 2, 3)):
        sc_in[i].wait_recv()
        gm_core.append(link.remote(scal(r, t), scal(r, t), core))
    weight_grad(hid_a, left, dw_d, 2, 2)
    get_n1 = link.here(n1, left)
    near_u = side_send(dw_u, yr_u, 1)
    for c in blk_own:
        c.wait()
    gm_in[2].wait_recv()
    gm_core.append(link.remote(gmix.at[row(3, t)], gmix.at[row(3, t)], core))
    far_d = second_hop(hop_d, dw_d, yr_d, zr_d)
    near_d = side_send(dw_d, yr_d, 1)
    blk_peer = over_cores(blk_core, own_rows, core_blk, own, peer_blk)
    link.sent(blk_core.values())
    link.sent(two_peer)
    get_aux.append(link.here(w_out_in, w_out))
    for c in get_aux + [get_n1] + gm_here:
        c.wait()
    for c in gm_core:
        c.wait_recv()

    def one_core(r):
        return pltpu.make_async_remote_copy(
            src_ref=right.at[row(r, 1 - t)],
            dst_ref=core_in.at[at(r * share, share, share)],
            send_sem=core_send.at[r],
            recv_sem=core_recv.at[r],
            device_id=core,
            device_id_type=MESH,
        )

    def fetch(r):
        here = at(r * rows, rows, rows)
        return [
            pltpu.make_async_copy(pre.at[here], pre_b, piece_sem.at[0]),
            pltpu.make_async_copy(state.at[here], state_b, piece_sem.at[1]),
            pltpu.make_async_copy(raw.at[here], raw_b, piece_sem.at[2]),
        ]

    bound = par[0:1, :]
    gain = par[1:2, :]
    gain_sums = sums.at[2:4, 0:feat]
    mixed_t = hid_b.at[0:feat]
    dw_out = w_out

    def one_rows(r, j):
        return right[at(r * rows + t * share + j * 16, 16, 16), :].astype(f32)

    def one_x(slot, r):
        return pltpu.make_async_remote_copy(
            src_ref=half.at[at(r * share, share, share)],
            dst_ref=peer_in.at[at(slot * share, share, share)],
            send_sem=core_send.at[4 + slot],
            recv_sem=core_recv.at[4 + slot],
            device_id=group[1],
            device_id_type=MESH,
        )

    def hand_over(r):
        one_core(r).wait()
        add_half(r, one_rows, core_in, half)

    def piece(i, carry):
        r = 3 - 2 * i + 3 * (i // 2)
        here = at(r * rows, rows, rows)
        copies = fetch(r)
        for c in copies:
            c.start()
        up = lax.dot_general(
            gmix[here, :], w_out[...], (((1,), (1,)), ((), ())), preferred_element_type=f32
        )
        masks = aux[r].T
        valid = masks[:, 0:1]
        keep = masks[:, 1:2]
        scale_parts = [scal_all[r * 2 + tt].T for tt in (0, 1)]
        scale = jnp.concatenate([p[:, 0:1] for p in scale_parts], axis=0)
        dot_mean = jnp.concatenate([p[:, 1:2] for p in scale_parts], axis=0)
        for c in copies:
            c.wait()
        at_row = lax.broadcasted_iota(jnp.int32, (rows, feat), 0)
        input_pre = pre_b[:, :feat]
        outgate_pre = pre_b[:, 2 * feat :]
        held = state_b[...]
        sig_out = jax.nn.sigmoid(outgate_pre)
        act_out = outgate_pre * sig_out
        scaled = up * (held * scale)
        grads[:, 2 * feat :] = scaled * gain * (sig_out * (1.0 + outgate_pre * (1.0 - sig_out)))
        add[...] = scale * (gain * act_out * up) - held * (scale * scale * scale * dot_mean)
        gain_sums[0:1, :] += jnp.sum(scaled * act_out, axis=0, keepdims=True)
        sig_forget = jax.nn.sigmoid(pre_b[:, feat : 2 * feat])
        forget = bound + (1.0 - bound) * sig_forget
        decay[...] = jnp.where(at_row < rows - 1, pltpu.roll(forget * keep, rows - 1, 0), 0.0)
        scan_rows(decay, add, add, True)
        grad_state = add[...]
        before = jnp.where(at_row > 0, pltpu.roll(held, 1, 0), 0.0)
        sig_in = jax.nn.sigmoid(input_pre)
        grad_forget = grad_state * (before * keep - input_pre * sig_in * valid)
        grads[:, :feat] = (
            grad_state * (1.0 - forget) * valid * (sig_in * (1.0 + input_pre * (1.0 - sig_in)))
        )
        grads[:, feat : 2 * feat] = grad_forget * (1.0 - bound) * sig_forget * (1.0 - sig_forget)
        gain_sums[1:2, :] += jnp.sum(grad_forget * (1.0 - sig_forget), axis=0, keepdims=True)
        low = grads[...].astype(bf16)
        right[here, :] = lax.dot_general(
            low, w_mix[...], (((1,), (1,)), ((), ())), preferred_element_type=f32
        ).astype(bf16)
        one_core(r).start()
        grads_t[:, here] = grads[...].T.astype(bf16)
        mixed_t[:, here] = (raw_b[...].astype(f32) * scale).T.astype(bf16)

        @pl.when(i > 0)
        def _():
            before_r = 5 - 2 * i + 3 * ((i - 1) // 2)
            hand_over(before_r)

            @pl.when(i < 3)
            def _():
                one_x(i - 1, before_r).start()

        return carry

    lax.fori_loop(0, 4, piece, 0)

    one_core(0).wait()
    pass_on(blk_peer, own, peer_blk)

    weight_grad(grads_t, left, dw_mix, 0, 2)
    hop_mix = side_send(dw_mix, yr_mix, 0)
    weight_grad(grads_t, left, dw_mix, 2, 2)

    def out_columns(i, carry):
        to = at(i * (4 * block), 4 * block, 4 * block)
        dw_out[:, to] = jnp.dot(mixed_t[...], gmix[:, to], preferred_element_type=f32).astype(bf16)
        return carry

    lax.fori_loop(0, 4, out_columns, 0)
    near_rows = at(zf * block, block, block)
    far_rows = at((1 - zf) * block, block, block)

    def out_copy(k, src, dst, device):
        return pltpu.make_async_remote_copy(
            src_ref=src,
            dst_ref=dst,
            send_sem=out_send.at[k],
            recv_sem=out_recv.at[k],
            device_id=device,
            device_id_type=MESH,
        )

    out_side = out_copy(0, dw_out, yr_out, side)
    out_far = out_copy(1, dw_out.at[far_rows], zr_out, far)
    out_core = out_copy(2, dw_out.at[near_rows], o_out, core)
    out_here = pltpu.make_async_copy(dw_out.at[near_rows], o_out, out_send.at[3])

    @pl.when(t != y)
    def _():
        out_side.start()

    one_x(0, 3).wait()

    def one_on(j, carry):
        two = at(2 * share + j * 16, 16, 16)
        half[two, :] = (half[two, :].astype(f32) + peer_in[at(j * 16, 16, 16), :].astype(f32)).astype(bf16)
        return carry

    lax.fori_loop(0, share // 16, one_on, 0)
    one_z = link.remote(half.at[rel(2)], peer_in.at[rel(2)], group[2])
    near_mix = side_send(dw_mix, yr_mix, 1)
    back_g = last_hop(near_g, far_g, dw_g, yr_g, zr_g, o_g)
    back_u = last_hop(near_u, far_u, dw_u, yr_u, zr_u, o_u)
    far_mix = second_hop(hop_mix, dw_mix, yr_mix, zr_mix)

    @pl.when(t == y)
    def _():
        out_side.wait_recv()
        add_columns(dw_out, pl.ds(0, width), [(yr_out, pl.ds(0, width))])
        out_far.start()

    one_x(1, 1).wait()
    one_z.wait_recv()
    gain_one = first_gain[...]

    def token_rows(j, carry):
        to = at(j * step, step, step)
        total = one_rows(0, j) + core_in[to, :].astype(f32)
        for r in (1, 2):
            total = total + peer_in[at(r * share + j * step, step, step), :].astype(f32)
        value = tok[at(t * share + j * step, step, step), :].astype(f32)
        s = lax.rsqrt(jnp.mean(value * value, axis=1, keepdims=True) + epsilon)
        weighted = total * gain_one
        gres[to, :] = (
            gres[to, :]
            + s * weighted
            - value * (s * s * s) * jnp.mean(weighted * value, axis=1, keepdims=True)
        )
        sums[0:1, :] += jnp.sum(total * value * s, axis=0, keepdims=True)
        return carry

    lax.fori_loop(0, share // step, token_rows, 0)
    tok_rows = at(t * share, share, share)
    tok_core = link.remote(gres, o_tok.at[tok_rows], core)
    link.here(gres, o_tok.at[tok_rows], keep=True)

    vec[0] = jnp.zeros(vec.shape[1:], f32)
    for k in (0, 1):
        for i in range(16):
            vec[0, k * 16 + i : k * 16 + i + 1, :] = sums[k : k + 1, i * block : (i + 1) * block]
    for k in (2, 3):
        for i in (0, 1):
            vec[0, pl.ds(k * 16 + i * 8 + zn * 4 + t * 2 + x, 1), :] = sums[
                k : k + 1, i * block : (i + 1) * block
            ]
    partners = [group[1], group[2], side, far, core]
    turn = [link.remote(vec.at[0], vec_in.at[0], partners[0])]

    def next_turn():
        k = len(turn)
        turn[k - 1].wait_recv()
        vec[k] = vec[k - 1] + vec_in[k - 1]
        if k < len(partners):
            turn.append(link.remote(vec.at[k], vec_in.at[k], partners[k]))

    next_turn()
    back_d = last_hop(near_d, far_d, dw_d, yr_d, zr_d, o_d)
    next_turn()
    next_turn()
    for c in blk_peer[1:]:
        c.wait_recv()

    def block_rows(j, carry):
        to = at(j * step, step, step)
        total = own_rows(0, j) + core_blk[to, :].astype(f32)
        for r in (1, 2):
            total = total + peer_blk[at(r * share + j * step, step, step), :].astype(f32)
        gm_own[to, :] = (res[to, :] + total).astype(bf16)
        return carry

    link.sent(gm_in[:2] + gm_core[:1])
    lax.fori_loop(0, share // step, block_rows, 0)
    link.here(gm_own, o_blk, keep=True)
    next_turn()
    next_turn()
    link.here(vec.at[5], o_vec, keep=True)
    back_mix = last_hop(near_mix, far_mix, dw_mix, yr_mix, zr_mix, o_mix)

    @pl.when(t == y)
    def _():
        out_far.wait_recv()

        def some(j, carry):
            to = at(zf * block + j * 16, 16, 16)
            dw_out[to, :] = (
                dw_out[to, :].astype(f32) + zr_out[at(j * 16, 16, 16), :].astype(f32)
            ).astype(bf16)
            return carry

        lax.fori_loop(0, block // 16, some, 0)
        out_core.start()
        out_here.start()
        out_far.wait_send()
        out_core.wait_send()
        out_here.wait()

    @pl.when(t != y)
    def _():
        out_side.wait_send()
        out_core.wait_recv()

    for c in back_mix:
        c.wait_recv()
    mix_core = link.remote(o_mix.at[:, :, :, t], o_mix.at[:, :, :, t], core)
    for c in back_d + back_g + back_u + [mix_core, tok_core]:
        c.wait_recv()
    link.close()


def back(*arrays):
    par, tok = arrays[15], arrays[16]
    rows, width = tok.shape
    share, group_rows = rows // 2, 4 * rows
    feat, hid, block = par.shape[1], arrays[0].shape[0], width // 16
    made = jax.ShapeDtypeStruct
    vm = pltpu.VMEM
    outs = [
        made((4, hid, block), bf16),
        made((4, hid, block), bf16),
        made((4, hid, block), bf16),
        made((3, 2, 2, 2, 2, block, block), bf16),
        made((block, width), bf16),
        made((rows, width), f32),
        made((share, width), bf16),
        made((64, block), f32),
    ]
    scratch = (
        [vm((group_rows, width), bf16)] * 3
        + [vm((hid, width), bf16)] * 3
        + [vm((3, 2, block, width), bf16)]
        + [vm((hid, width // 2), bf16)] * 3
        + [vm((3, 2, block, width // 2), bf16)]
        + [vm((hid, width // 4), bf16)] * 3
        + [vm((3, 2, block, width // 4), bf16)]
        + [vm((4 * share, width), bf16)] * 4
        + [vm((3 * share, width), bf16)] * 2
        + [
            vm((width, 3 * feat), bf16),
            vm((feat, width), bf16),
            vm(arrays[14].shape, f32),
            vm((rows, 3 * feat), f32),
            vm((rows, feat), f32),
            vm((rows, feat), bf16),
            vm((rows, 3 * feat), f32),
            vm((3 * feat, group_rows), bf16),
            vm((rows, feat), f32),
            vm((rows, feat), f32),
            vm((feat, width), bf16),
            vm((block, width), bf16),
            vm((hid, group_rows), bf16),
            vm((hid, group_rows), bf16),
            vm((share, width), f32),
            vm((share, width), bf16),
            vm((8, share), f32),
            vm((8, 8, share), f32),
            vm((4, width), f32),
            vm((6, 64, block), f32),
            vm((5, 64, block), f32),
            pltpu.SemaphoreType.DMA((96,)),
            pltpu.SemaphoreType.DMA((96,)),
            pltpu.SemaphoreType.DMA((32,)),
        ]
        + [pltpu.SemaphoreType.DMA((6,))] * 5
    )
    any_spec = pl.BlockSpec(memory_space=pl.ANY)
    vmem_spec = pl.BlockSpec(memory_space=pltpu.VMEM)
    return pl.pallas_call(
        back_kernel,
        in_specs=[any_spec] * 15 + [vmem_spec] * 7,
        out_specs=[any_spec] * len(outs),
        out_shape=outs,
        scratch_shapes=scratch,
        compiler_params=pltpu.CompilerParams(
            collective_id=2, has_side_effects=True, vmem_limit_bytes=63 << 20
        ),
        name="back",
    )(*arrays)


def body(
    n_dp,
    n_t,
    tokens_in,
    input_proj,
    forget_proj,
    outgate_proj,
    output_proj,
    glu_gate,
    glu_up,
    glu_down,
    norm_gain,
    mixer_gain,
    ffn_gain,
    bound_table,
    lengths,
    bucket,
    cotangent,
):
    depth = n_dp.bit_length() - 1
    tp_bits = (2, 0)
    fs_bits = tuple(b for b in reversed(range(depth)) if b not in tp_bits)
    t_depth = n_t.bit_length() - 1
    own_bits, free_bits = fs_bits[len(fs_bits) - t_depth :], fs_bits[: len(fs_bits) - t_depth]
    n_tp = 4
    tp_mask = (0, 1, 4, 5)
    axis_of = {b: depth - 1 - b for b in range(depth)}

    me = lax.axis_index("dp")
    t = lax.axis_index("tensor")
    bit = {b: (me >> b) & 1 for b in range(depth)}
    t_bit = {b: (t >> (t_depth - 1 - i)) & 1 for i, b in enumerate(own_bits)}
    q = bit[2] * 2 + bit[0]

    rows, width = tokens_in.shape
    share = cotangent.shape[0]
    block = width // n_dp
    free = 2 ** len(free_bits)
    feat = free * block

    def swap(values, mask):
        return lax.ppermute(values, "dp", [(i, i ^ mask) for i in range(n_dp)])

    def t_swap(values):
        return lax.ppermute(values, "tensor", [(0, 1), (1, 0)])

    def by_bit(which, own, other):
        return jnp.where(which == 0, own, other), jnp.where(which == 0, other, own)

    def in_order(parts, bits):
        parts = list(parts)
        for i, b in enumerate(reversed(bits)):
            step = 1 << i
            for r in range(len(parts)):
                if not r & step:
                    parts[r], parts[r | step] = by_bit(bit[b], parts[r], parts[r | step])
        return parts

    def t_gather(values):
        if n_t == 2:
            return jnp.stack(by_bit(t, values, t_swap(values)))
        return lax.all_gather(values, "tensor", axis=0)

    def t_scatter(values):
        if n_t == 2:
            return pick(values, t, 0).astype(f32) + t_swap(pick(values, 1 - t, 0)).astype(f32)
        return lax.psum_scatter(values, "tensor", scatter_dimension=0, tiled=False).astype(f32)

    def tp_gather(values):
        return [t_gather(values if r == 0 else swap(values, tp_mask[r])) for r in range(n_tp)]

    def tp_scatter(parts, kind):
        halves = [t_scatter(part) for part in parts]
        total = halves[0]
        for r in range(1, n_tp):
            total = total + swap(halves[r].astype(kind), tp_mask[r]).astype(f32)
        return total

    def exchange(values):
        parts = [pick(values, q, 0)]
        for r in range(1, n_tp):
            parts.append(swap(pick(values, q ^ r, 0), tp_mask[r]))
        return in_order(parts, tp_bits)

    def fs_gather(values):
        parts = [values]
        for b in fs_bits:
            parts = parts + [None] * 0 + [swap(v, 1 << b) for v in parts]
        return parts

    def weight_parts(shards):
        return fs_gather(jnp.stack(exchange(shards)))

    def weight_whole(parts):
        count = len(parts)
        flip = [0] * count
        for r in range(count):
            flip[sum(((r >> i) & 1) << (len(fs_bits) - 1 - i) for i in range(len(fs_bits)))] = parts[r]
        ordered = jnp.stack(in_order(flip, fs_bits))
        cols = ordered.shape[-1]
        ordered = ordered.reshape((2,) * depth + (block, cols))
        have = fs_bits + tp_bits
        axes = [have.index(b) for b in reversed(range(depth))]
        return ordered.transpose(axes + [depth, depth + 1]).reshape(width, cols)

    def weight_back(grad):
        cols = grad.shape[1]
        grad = grad.reshape((2,) * depth + (block, cols))
        for b in reversed(fs_bits):
            send = lax.dynamic_slice_in_dim(grad, 1 - bit[b], 1, axis_of[b]).astype(bf16)
            hold = lax.dynamic_slice_in_dim(grad, bit[b], 1, axis_of[b]).astype(f32)
            grad = hold + swap(send, 1 << b).astype(f32)
        return exchange(grad.reshape(n_tp, block, cols).astype(bf16))

    def my_columns(values):
        lead = values.shape[:-1]
        n = len(lead)
        values = values.reshape(lead + (2,) * depth + (block,))
        bits = list(reversed(range(depth)))
        for b in own_bits:
            values = pick(values, t_bit[b], n + bits.index(b))
            bits.remove(b)
        order = [n + bits.index(b) for b in tp_bits] + list(range(n)) + [n + bits.index(b) for b in free_bits]
        return values.transpose(order + [n + len(bits)]).reshape((n_tp,) + lead + (feat,))

    def my_half(values):
        return lax.dynamic_slice_in_dim(values, t * share, share, 0)

    hid = glu_gate.shape[1] // n_tp
    if n_dp == 16 and n_t == 2:
        (
            mix_full, out_full, gate_full, up_full, down_full, normed_one, grad_out_all, normed_two,
            pre, state, mix_raw, residual, mixed_out, scale_lanes, aux_rows, par, hidden, grad_gate,
            grad_up, coef,
        ) = front(
            input_proj, forget_proj, outgate_proj, output_proj, glu_gate, glu_up, glu_down, cotangent,
            tokens_in, norm_gain[None, :], mixer_gain[None, :], ffn_gain[None, :], bound_table, lengths, bucket,
        )
    else:
        inputs = tokens_in.astype(f32)
        scale_one = rms_scale(inputs)
        normed_mine = (inputs * scale_one * norm_gain).astype(bf16)
        inputs_half = my_half(inputs)
        scale_one_half = my_half(scale_one)
        mix_shards = jnp.concatenate(
            [my_columns(w) for w in (input_proj, forget_proj, outgate_proj)], axis=-1
        )
        gate_shards = glu_gate.T.reshape(n_tp, hid, block)
        up_shards = glu_up.T.reshape(n_tp, hid, block)
        down_shards = glu_down.reshape(n_tp, hid, block)
        my_table = pick(my_columns(bound_table), q, 0)
        par = jnp.stack([bound_parts(my_table)[2], pick(my_columns(mixer_gain), q, 0)])
        valid_own, keep_own = layout(lengths, bucket, rows)
        grad_out_rows = (cotangent.astype(f32) * my_half(valid_own)).astype(bf16)
        normed_half = my_half(normed_mine)
        normed_parts = [normed_mine] + [
            t_gather(swap(normed_half, tp_mask[r])).reshape(rows, width) for r in range(1, n_tp)
        ]
        normed_one = jnp.concatenate(normed_parts)
        aux_own = jnp.concatenate([valid_own, keep_own], axis=1)
        aux = jnp.concatenate([aux_own] + [swap(aux_own, tp_mask[r]) for r in range(1, n_tp)])
        mix_full = weight_whole(weight_parts(mix_shards))
        out_piece = output_proj
        for b in own_bits:
            out_piece = jnp.where(t_bit[b] == bit[b], out_piece, swap(out_piece, 1 << b))
        out_pieces = [out_piece]
        for b in reversed(free_bits):
            out_pieces = out_pieces + [swap(v, 1 << b) for v in out_pieces]
        out_full = jnp.concatenate(in_order(out_pieces, free_bits))
        gate_full, up_full, down_full = (
            weight_whole(weight_parts(w.transpose(0, 2, 1))).T
            for w in (gate_shards, up_shards, down_shards)
        )
        grad_out_all = jnp.stack(tp_gather(grad_out_rows)).reshape(n_tp * rows, width)
        pre = matmul(normed_one, mix_full)
        state, mix_raw, square = mixer_forward(pre, aux, par, rows)
        out_parts = matmul(mix_raw, out_full).astype(bf16).reshape(n_tp, n_t, share, width)
        square_parts = square.reshape(n_tp, n_t, share)
        square_sum = tp_scatter([square_parts[r] for r in range(n_tp)], f32)
        out_sum = tp_scatter([out_parts[r] for r in range(n_tp)], bf16)
        scale_state = lax.rsqrt(square_sum / width + epsilon)[:, None]
        mixed_out = out_sum * scale_state
        residual = inputs_half + mixed_out
        normed_two_half = (residual * rms_scale(residual) * ffn_gain).astype(bf16)
        normed_two = jnp.stack(tp_gather(normed_two_half)).reshape(n_tp * rows, width)

    if n_dp == 16 and n_t == 2:
        grad_g, grad_u, grad_d, grad_mix_w, grad_out_w, grad_tokens, block_out, vec = back(
            hidden, grad_gate, grad_up, normed_two, grad_out_all, gate_full, up_full, down_full,
            normed_one, mix_full, out_full, pre, state, mix_raw, aux_rows, par, tokens_in, residual, mixed_out,
            scale_lanes, norm_gain[None, :], ffn_gain[None, :],
        )
        mix_all = grad_mix_w.reshape(3, width, block)
        mine = lambda k: lax.dynamic_slice_in_dim(vec, k * n_dp + me, 1, 0)
        return (
            block_out,
            grad_tokens,
            mix_all[0].T.astype(f32),
            mix_all[1].T.astype(f32),
            mix_all[2].T.astype(f32),
            grad_out_w.astype(f32),
            grad_g.reshape(n_tp * hid, block).T.astype(f32),
            grad_u.reshape(n_tp * hid, block).T.astype(f32),
            grad_d.reshape(n_tp * hid, block).astype(f32),
            mine(0)[0],
            mine(2)[0],
            mine(1)[0],
            coef * mine(3),
        )

    scale_two = rms_scale(residual)
    gate_pre = cross_cols(normed_two, gate_full)
    up_pre = cross_cols(normed_two, up_full)
    grad_hidden = cross_cols(grad_out_all, down_full)
    gate_act = jax.nn.silu(gate_pre)
    hidden = (gate_act * up_pre).astype(bf16)
    grad_up = (grad_hidden * gate_act).astype(bf16)
    grad_gate = (grad_hidden * up_pre * silu_slope(gate_pre)).astype(bf16)
    grad_two_parts = (
        (matmul(grad_gate, gate_full) + matmul(grad_up, up_full))
        .astype(bf16)
        .reshape(n_tp, n_t, share, width)
    )
    grad_normed_two = tp_scatter([grad_two_parts[r] for r in range(n_tp)], bf16)
    block_parts = matmul(hidden, down_full).astype(bf16).reshape(n_tp, n_t, share, width)
    block_out = (residual + tp_scatter([block_parts[r] for r in range(n_tp)], bf16)).astype(bf16)
    grad_down_t = jnp.stack(weight_back(cross_rows(grad_out_all, hidden).astype(bf16)))
    grad_w_gate = jnp.stack(weight_back(cross_rows(normed_two, grad_gate).astype(bf16)))
    grad_w_up = jnp.stack(weight_back(cross_rows(normed_two, grad_up).astype(bf16)))
    grad_glu_down = grad_down_t.transpose(0, 2, 1).reshape(glu_down.shape).astype(f32)
    grad_glu_gate = grad_w_gate.transpose(1, 0, 2).reshape(glu_gate.shape).astype(f32)
    grad_glu_up = grad_w_up.transpose(1, 0, 2).reshape(glu_up.shape).astype(f32)

    grad_residual = grad_out_rows.astype(f32) + norm_back(
        residual, scale_two, ffn_gain, grad_normed_two
    )
    ffn_gain_sum = jnp.sum(grad_normed_two * residual * scale_two, axis=0)
    grad_mix_half = grad_residual.astype(bf16)
    dot_mean = jnp.sum(grad_mix_half.astype(f32) * mixed_out, axis=1, keepdims=True) / (
        scale_state * width
    )
    row_values = jnp.concatenate([scale_state, dot_mean], axis=1).T
    row_all = jnp.stack(tp_gather(row_values)).transpose(0, 1, 3, 2).reshape(n_tp * rows, 2)
    grad_mix = jnp.stack(tp_gather(grad_mix_half)).reshape(n_tp * rows, width)
    grad_mixed = cross_cols(grad_mix, out_full)
    aux_back = jnp.concatenate([aux, row_all], axis=1)
    grads, sums = mixer_backward(pre, state, grad_mixed, aux_back, par, rows)
    one_parts = cross_cols(grads, mix_full).astype(bf16).reshape(n_tp, n_t, share, width)
    grad_normed_one = tp_scatter([one_parts[r] for r in range(n_tp)], bf16)
    grad_mix_w = jnp.stack(weight_back(cross_rows(normed_one, grads).astype(bf16)))

    mixed = (mix_raw.astype(f32) * row_all[:, :1]).astype(bf16)
    grad_out_w = cross_rows(mixed, grad_mix).astype(bf16).reshape((2,) * len(free_bits) + (block, width))
    for i, b in enumerate(free_bits):
        send = lax.dynamic_slice_in_dim(grad_out_w, 1 - bit[b], 1, i)
        hold = lax.dynamic_slice_in_dim(grad_out_w, bit[b], 1, i)
        grad_out_w = (hold.astype(f32) + swap(send, 1 << b).astype(f32)).astype(bf16)
    grad_out_w = grad_out_w.reshape(block, width)
    for b in own_bits:
        grad_out_w = (grad_out_w.astype(f32) + swap(grad_out_w, 1 << b).astype(f32)).astype(bf16)
    mine_t = jnp.int32(0)
    for b in own_bits:
        mine_t = mine_t * 2 + bit[b]
    if n_t == 2:
        other = t_swap(grad_out_w)
        grad_output_proj = jnp.where(mine_t == t, grad_out_w, other).astype(f32)
    else:
        grad_output_proj = pick(lax.all_gather(grad_out_w, "tensor", axis=0), mine_t, 0).astype(f32)

    mix_all = t_gather(grad_mix_w)
    mix_all = mix_all.reshape((2,) * t_depth + (2, 2) + (block, 3) + (2,) * len(free_bits) + (block,))
    order = list(own_bits) + list(tp_bits) + ["row", "which"] + list(free_bits) + ["col"]
    axes = [order.index(k) for k in ["which", "row"] + list(reversed(range(depth))) + ["col"]]
    mix_all = mix_all.transpose(axes).reshape(3, block, width).astype(f32)

    grad_tokens_half = my_half_residual = grad_residual + norm_back(
        inputs_half, scale_one_half, norm_gain, grad_normed_one
    )
    grad_tokens = t_gather(grad_tokens_half).reshape(rows, width)
    norm_gain_sum = jnp.sum(grad_normed_one * inputs_half * scale_one_half, axis=0)

    gains = jnp.stack([norm_gain_sum, ffn_gain_sum]).reshape((2,) + (2,) * depth + (block,))
    for b in reversed(range(depth)):
        at = 1 + axis_of[b]
        send = lax.dynamic_slice_in_dim(gains, 1 - bit[b], 1, at)
        hold = lax.dynamic_slice_in_dim(gains, bit[b], 1, at)
        gains = hold + swap(send, 1 << b)
    gains = gains.reshape(2, block)
    gains = gains + t_swap(gains) if n_t == 2 else lax.psum(gains, "tensor")

    for b in fs_bits:
        sums = sums + swap(sums, 1 << b)
    sums = t_gather(sums)
    sums = pick(sums, mine_t, 0).reshape((2,) + (2,) * len(free_bits) + (block,))
    for b in free_bits:
        sums = pick(sums, bit[b], 1)
    shares, picked, lower = bound_parts(lax.dynamic_slice_in_dim(bound_table, me * block, block, 1))
    grad_table = shares * (picked - lower[None, :]) * sums[1][None, :]

    return (
        block_out,
        grad_tokens,
        mix_all[0],
        mix_all[1],
        mix_all[2],
        grad_output_proj,
        grad_glu_gate,
        grad_glu_up,
        grad_glu_down,
        gains[0],
        sums[0],
        gains[1],
        grad_table,
    )


def solution(mesh):
    return jax.shard_map(
        functools.partial(body, mesh.shape["dp"], mesh.shape["tensor"]),
        mesh=mesh,
        in_specs=(
            P("dp", None),
            P("dp", None),
            P("dp", None),
            P("dp", None),
            P("dp", None),
            P("dp", "tensor"),
            P("dp", "tensor"),
            P("tensor", "dp"),
            P(),
            P(),
            P(),
            P(),
            P("dp"),
            P("dp"),
            P(("dp", "tensor"), None),
        ),
        out_specs=(
            P(("dp", "tensor"), None),
            P("dp", None),
            P("dp", None),
            P("dp", None),
            P("dp", None),
            P("dp", None),
            P("dp", "tensor"),
            P("dp", "tensor"),
            P("tensor", "dp"),
            P("dp"),
            P("dp"),
            P("dp"),
            P(None, "dp"),
        ),
        check_vma=False,
    )
```

```python
import functools

import jax
import jax.numpy as jnp
from jax import lax
from jax.experimental import pallas as pl
from jax.experimental.pallas import tpu as pltpu
from jax.sharding import PartitionSpec as P

LAYER = 12
epsilon = 1e-06
bf16 = jnp.bfloat16
f32 = jnp.float32


def rms_scale(values):
    return lax.rsqrt(jnp.mean(values * values, axis=-1, keepdims=True) + epsilon)


def norm_back(values, row_scale, gain_row, incoming):
    weighted = incoming * gain_row
    cubed = row_scale * row_scale * row_scale
    return row_scale * weighted - values * cubed * jnp.mean(
        weighted * values, axis=-1, keepdims=True
    )


def silu_slope(values):
    logistic = jax.nn.sigmoid(values)
    return logistic * (1.0 + values * (1.0 - logistic))


def matmul(first_op, second_op):
    return jnp.dot(first_op, second_op, preferred_element_type=f32)


def cross_rows(first_op, second_op):
    return lax.dot_general(
        first_op, second_op, (((0,), (0,)), ((), ())), preferred_element_type=f32
    )


def cross_cols(first_op, second_op):
    return lax.dot_general(
        first_op, second_op, (((1,), (1,)), ((), ())), preferred_element_type=f32
    )


def pick(values, index, axis):
    return lax.dynamic_index_in_dim(values, index, axis, keepdims=False)


def layout(lengths, bucket, row_count):
    slot_len = row_count // jnp.left_shift(jnp.int32(1), bucket)
    position = jnp.arange(row_count, dtype=jnp.int32)
    slot_index = position // slot_len
    offset = position - slot_index * slot_len
    slot_ids = jnp.arange(lengths.shape[0], dtype=jnp.int32)
    chosen = (slot_index[:, None] == slot_ids[None, :]).astype(jnp.int32)
    slot_limit = jnp.sum(chosen * lengths[None, :], axis=1)
    valid_mask = (offset < slot_limit).astype(f32)[:, None]
    keep_mask = (offset > 0).astype(f32)[:, None]
    return (valid_mask, keep_mask)


def bound_parts(bound_table):
    shares = jax.nn.softmax(bound_table, axis=0)
    layer_ids = jnp.arange(bound_table.shape[0], dtype=jnp.int32)[:, None]
    picked = ((layer_ids >= 1) & (layer_ids <= LAYER)).astype(f32)
    return (shares, picked, jnp.sum(shares * picked, axis=0))


def scan_rows(decay_ref, add_ref, out_ref, reverse):
    rows, width = out_ref.shape
    tiles = rows // 8
    sub = lax.broadcasted_iota(jnp.int32, (8, width), 0)

    def step(i, carry):
        j = tiles - 1 - i if reverse else i
        at = pl.ds(pl.multiple_of(j * 8, 8), 8)
        a = decay_ref[at, :]
        b = add_ref[at, :]
        for s in (1, 2, 4):
            shift = 8 - s if reverse else s
            inside = sub < 8 - s if reverse else sub >= s
            b = jnp.where(inside, b + a * pltpu.roll(b, shift, 0), b)
            a = jnp.where(inside, a * pltpu.roll(a, shift, 0), a)
        h = b + a * carry
        out_ref[at, :] = h
        edge = h[0:1, :] if reverse else h[7:8, :]
        return jnp.broadcast_to(edge, (8, width))

    lax.fori_loop(0, tiles, step, jnp.zeros((8, width), f32), unroll=4)


def mixer_forward_kernel(pre_ref, aux_ref, par_ref, state_ref, mix_ref, sq_ref, decay_ref, add_ref):
    width = state_ref.shape[1]
    input_pre = pre_ref[:, :width]
    forget_pre = pre_ref[:, width : 2 * width]
    outgate_pre = pre_ref[:, 2 * width :]
    valid = aux_ref[:, 0:1]
    keep = aux_ref[:, 1:2]
    bound = par_ref[0:1, :]
    gain = par_ref[1:2, :]
    forget = bound + (1.0 - bound) * jax.nn.sigmoid(forget_pre)
    add_ref[...] = input_pre * jax.nn.sigmoid(input_pre) * (1.0 - forget) * valid
    decay_ref[...] = forget * keep
    scan_rows(decay_ref, add_ref, state_ref, False)
    state = state_ref[...]
    mix_ref[...] = (state * gain * (outgate_pre * jax.nn.sigmoid(outgate_pre))).astype(bf16)
    sq_ref[...] = jnp.sum(state * state, axis=1, keepdims=True)


def mixer_forward(pre, aux, par, seq_rows):
    rows, width = pre.shape[0], pre.shape[1] // 3
    row_block = lambda n: pl.BlockSpec((seq_rows, n), lambda i: (i, 0))
    return pl.pallas_call(
        mixer_forward_kernel,
        grid=(rows // seq_rows,),
        in_specs=[
            row_block(3 * width),
            row_block(aux.shape[1]),
            pl.BlockSpec(par.shape, lambda i: (0, 0)),
        ],
        out_specs=[row_block(width), row_block(width), row_block(1)],
        out_shape=[
            jax.ShapeDtypeStruct((rows, width), f32),
            jax.ShapeDtypeStruct((rows, width), bf16),
            jax.ShapeDtypeStruct((rows, 1), f32),
        ],
        scratch_shapes=[pltpu.VMEM((seq_rows, width), f32)] * 2,
        cost_estimate=pl.CostEstimate(
            flops=rows * width * 60, bytes_accessed=rows * width * 20, transcendentals=rows * width * 3
        ),
        name="mixer_forward",
    )(pre, aux, par)


def mixer_backward_kernel(
    pre_ref, state_ref, up_ref, aux_ref, par_ref, grad_ref, sums_ref, decay_ref, add_ref, out_ref
):
    rows, width = state_ref.shape
    input_pre = pre_ref[:, :width]
    forget_pre = pre_ref[:, width : 2 * width]
    outgate_pre = pre_ref[:, 2 * width :]
    valid = aux_ref[:, 0:1]
    keep = aux_ref[:, 1:2]
    scale = aux_ref[:, 2:3]
    dot_mean = aux_ref[:, 3:4]
    bound = par_ref[0:1, :]
    gain = par_ref[1:2, :]
    state = state_ref[...]
    incoming = up_ref[...]
    at_row = lax.broadcasted_iota(jnp.int32, (rows, width), 0)
    sig_out = jax.nn.sigmoid(outgate_pre)
    act_out = outgate_pre * sig_out
    scaled = incoming * (state * scale)
    grad_ref[:, 2 * width :] = (
        scaled * gain * (sig_out * (1.0 + outgate_pre * (1.0 - sig_out)))
    ).astype(bf16)
    add_ref[...] = scale * (gain * act_out * incoming) - state * (scale * scale * scale * dot_mean)
    sig_forget = jax.nn.sigmoid(forget_pre)
    forget = bound + (1.0 - bound) * sig_forget
    decay_ref[...] = jnp.where(
        at_row < rows - 1, pltpu.roll(forget * keep, rows - 1, 0), 0.0
    )
    scan_rows(decay_ref, add_ref, out_ref, True)
    grad_state = out_ref[...]
    before = jnp.where(at_row > 0, pltpu.roll(state, 1, 0), 0.0)
    sig_in = jax.nn.sigmoid(input_pre)
    grad_forget = grad_state * (before * keep - input_pre * sig_in * valid)
    grad_ref[:, :width] = (
        grad_state * (1.0 - forget) * valid * (sig_in * (1.0 + input_pre * (1.0 - sig_in)))
    ).astype(bf16)
    grad_ref[:, width : 2 * width] = (
        grad_forget * (1.0 - bound) * sig_forget * (1.0 - sig_forget)
    ).astype(bf16)

    @pl.when(pl.program_id(0) == 0)
    def _():
        sums_ref[...] = jnp.zeros_like(sums_ref)

    sums_ref[0:1, :] += jnp.sum(scaled * act_out, axis=0, keepdims=True)
    sums_ref[1:2, :] += jnp.sum(grad_forget * (1.0 - sig_forget), axis=0, keepdims=True)


def mixer_backward(pre, state, incoming, aux, par, seq_rows):
    rows, width = state.shape
    row_block = lambda n: pl.BlockSpec((seq_rows, n), lambda i: (i, 0))
    whole = lambda shape: pl.BlockSpec(shape, lambda i: (0, 0))
    return pl.pallas_call(
        mixer_backward_kernel,
        grid=(rows // seq_rows,),
        in_specs=[
            row_block(3 * width),
            row_block(width),
            row_block(width),
            row_block(aux.shape[1]),
            whole(par.shape),
        ],
        out_specs=[row_block(3 * width), whole((2, width))],
        out_shape=[
            jax.ShapeDtypeStruct((rows, 3 * width), bf16),
            jax.ShapeDtypeStruct((2, width), f32),
        ],
        scratch_shapes=[pltpu.VMEM((seq_rows, width), f32)] * 3,
        cost_estimate=pl.CostEstimate(
            flops=rows * width * 90, bytes_accessed=rows * width * 26, transcendentals=rows * width * 3
        ),
        name="mixer_backward",
    )(pre, state, incoming, aux, par)


MESH = pl.DeviceIdType.MESH


class Copies:
    def __init__(self, send, recv, local):
        self.send, self.recv, self.local = send, recv, local
        self.n_remote = self.n_local = 0
        self.open = []

    def remote(self, src, dst, device):
        k = self.n_remote
        self.n_remote += 1
        copy = pltpu.make_async_remote_copy(
            src_ref=src,
            dst_ref=dst,
            send_sem=self.send.at[k],
            recv_sem=self.recv.at[k],
            device_id=device,
            device_id_type=MESH,
        )
        copy.start()
        self.open.append(copy.wait_send)
        return copy

    def here(self, src, dst, keep=False):
        k = self.n_local
        self.n_local += 1
        copy = pltpu.make_async_copy(src, dst, self.local.at[k])
        copy.start()
        if keep:
            self.open.append(copy.wait)
        return copy

    def sent(self, copies):
        for copy in copies:
            copy.wait_send()
            self.open.remove(copy.wait_send)

    def close(self):
        assert self.n_remote <= self.send.shape[0] and self.n_local <= self.local.shape[0]
        for wait in self.open:
            wait()


def position():
    me = lax.axis_index("dp")
    t = lax.axis_index("tensor")
    zf, zn, y, x = me // 8, (me // 4) % 2, (me // 2) % 2, me % 2
    to_x, to_zn = 1 - 2 * x, 4 - 8 * zn
    group = [None, (me + to_x, t), (me + to_zn, t), (me + to_x + to_zn, t)]
    q = [zn * 2 + x, zn * 2 + 1 - x, (1 - zn) * 2 + x, (1 - zn) * 2 + 1 - x]
    far = (me + 8 - 16 * zf, t)
    side = (me + 2 - 4 * y, t)
    core = (me, 1 - t)
    return me, t, (zf, zn, y, x), q, group, far, side, core


def meet(devices):
    barrier = pltpu.get_barrier_semaphore()
    for device in devices:
        pl.semaphore_signal(barrier, inc=1, device_id=device, device_id_type=MESH)
    pl.semaphore_wait(barrier, len(devices))


def fold_lanes(values):
    width = values.shape[1]
    if width % 128:
        return values
    total = values[:, :128]
    for i in range(128, width, 128):
        total = total + values[:, i : i + 128]
    return total


def front_kernel(
    s_in, s_fg, s_og, s_out, w_g, w_u, s_d, cot, tok, gain_one, gain_mix, gain_two, table, lengths, bucket,
    o_mix, o_out, o_g, o_u, o_d, o_n1, o_go, o_n2, o_pre, o_state, o_raw, o_res, o_mo, o_sc, o_aux, o_par, o_hid, o_hg, o_hu, o_coef,
    w_mix, w_out, n1, aux, pre, state, raw, part, core_in, half, peer_in, par, wide_g, wide_u, s_g, s_u, go_own, bound_row, full_g, full_u, gate, up, into, hid_v, hid_g, hid_u, all_powers, coef,
    sq, sq_core, sq_half, sq_peer, res, mo, sc, n2, decay, add,
    send, recv, local, core_send, core_recv, sqc_send, sqc_recv, out_send, out_recv, x_send, x_recv,
):
    me, t, (zf, zn, y, x), q, group, far, side, core = position()
    rows, width = tok.shape
    share = rows // 2
    block = s_out.shape[0]
    feat = par.shape[1]
    hid = s_d.shape[0] // 4
    link = Copies(send, recv, local)
    get_g, get_u, get_cot = link.here(w_g, wide_g), link.here(w_u, wide_u), link.here(cot, go_own)
    meet(group[1:] + [far, side, core])

    def at(start, size, unit):
        return pl.ds(pl.multiple_of(start, unit), size)

    def pair(fz, c, fy):
        return at(fz * (8 * block) + c * (4 * block) + fy * (2 * block), 2 * block, 2 * block)

    mine = at(me * block, block, block)

    def row(r, tt):
        return at(r * rows + tt * share, share, share)

    def columns(r, fz):
        fx = x if r in (0, 2) else 1 - x
        fzn = zn if r in (0, 1) else 1 - zn
        return at((fz * 8 + fzn * 4 + t * 2 + fx) * block, block, block)

    mix_in, mix_own = [], []
    for k, s in enumerate((s_in, s_fg, s_og)):
        for fz in (0, 1):
            to = w_mix.at[mine, pl.ds(k * feat + fz * block, block)]
            mix_in += [link.remote(s.at[:, columns(r, fz)], to, group[r]) for r in (1, 2, 3)]
            mix_own.append(link.here(s.at[:, columns(0, fz)], to))
    out_rows = [at(z * block, block, block) for z in (zf, 1 - zf)]

    def out_copy(k, src, dst, device):
        return pltpu.make_async_remote_copy(
            src_ref=src,
            dst_ref=w_out.at[dst],
            send_sem=out_send.at[k],
            recv_sem=out_recv.at[k],
            device_id=device,
            device_id_type=MESH,
        )

    out_far = out_copy(0, s_out, out_rows[0], far)
    out_side = out_copy(1, s_out, out_rows[0], side)
    out_next = out_copy(2, w_out.at[out_rows[1]], out_rows[1], side)
    out_here = pltpu.make_async_copy(s_out, w_out.at[out_rows[0]], out_send.at[3])

    @pl.when(t == y)
    def _():
        out_far.start()
        out_side.start()
        out_here.start()

    norm_row = gain_one[...]

    def norm_rows(first):
        def some(j, carry):
            to = at(first + j * 16, 16, 16)
            value = tok[to, :].astype(f32)
            s = lax.rsqrt(jnp.mean(value * value, axis=1, keepdims=True) + epsilon)
            n1[to, :] = (value * s * norm_row).astype(bf16)
            return carry

        lax.fori_loop(0, share // 16, some, 0)

    norm_rows(t * share)
    n1_in = [link.remote(n1.at[row(0, t)], n1.at[row(r, t)], group[r]) for r in (1, 2)]

    count = lengths.shape[0]
    slot_len = lax.shift_right_logical(jnp.int32(rows), bucket[0])
    position_row = lax.broadcasted_iota(jnp.int32, (1, rows), 1)
    slot = jnp.zeros((1, rows), jnp.int32)
    for j in range(1, count):
        slot = slot + (position_row >= j * slot_len).astype(jnp.int32)
    limit = jnp.zeros((1, rows), jnp.int32)
    for j in range(count):
        limit = limit + jnp.where(slot == j, lengths[j], 0)
    offset = position_row - slot * slot_len
    aux[0] = jnp.zeros(aux.shape[1:], f32)
    aux[0, 0:1, :] = (offset < limit).astype(f32)
    aux[0, 1:2, :] = (offset > 0).astype(f32)
    aux_in = [link.remote(aux.at[0], aux.at[r], group[r]) for r in (1, 2, 3)]

    norm_rows((1 - t) * share)
    for c in mix_own:
        c.wait()
    for c in mix_in:
        c.wait_recv()
    far_mix = [link.remote(w_mix.at[pair(zf, c, y)], w_mix.at[pair(zf, c, y)], far) for c in (0, 1)]
    side_mix = [link.remote(w_mix.at[pair(zf, c, y)], w_mix.at[pair(zf, c, y)], side) for c in (0, 1)]
    n1_in[1].wait_recv()
    n1_in.append(link.remote(n1.at[row(2, t)], n1.at[row(3, t)], group[1]))
    n1_core = [link.remote(n1.at[row(2, t)], n1.at[row(2, t)], core)]
    n1_in[0].wait_recv()
    n1_core.append(link.remote(n1.at[row(1, t)], n1.at[row(1, t)], core))
    shards = ((s_g, o_g), (s_u, o_u), (s_d, o_d))
    ffn_in, ffn_own = [], []

    def turn_round(wide, tall):
        size = min(128, wide.shape[1])

        def some(j, carry):
            to = at(j * size, size, size)
            tall[to, :] = wide[:, to].astype(f32).T.astype(bf16)
            return carry

        lax.fori_loop(0, wide.shape[1] // size, some, 0)

    def leave(s, o):
        units = [at(q[r] * hid, hid, 16) for r in range(4)]
        ffn_in.extend(link.remote(s.at[units[r]], o.at[:, mine], group[r]) for r in (1, 2, 3))
        ffn_own.append(link.here(s.at[units[0]], o.at[:, mine]))

    get_g.wait()
    turn_round(wide_g, s_g)
    leave(s_g, o_g)
    get_u.wait()
    turn_round(wide_u, s_u)
    leave(s_u, o_u)
    leave(s_d, o_d)

    logits = table[...]
    powers = jnp.exp(logits - jnp.max(logits, axis=0, keepdims=True))
    layer_ids = lax.broadcasted_iota(jnp.int32, logits.shape, 0)
    picked = jnp.where((layer_ids >= 1) & (layer_ids <= LAYER), powers, 0.0)
    bound_row[0:1, :] = jnp.sum(picked, axis=0, keepdims=True) / jnp.sum(powers, axis=0, keepdims=True)
    all_powers[...] = powers
    mine_powers = all_powers[:, mine]
    mine_shares = mine_powers / jnp.sum(mine_powers, axis=0, keepdims=True)
    ids = lax.broadcasted_iota(jnp.int32, mine_shares.shape, 0)
    mine_picked = ((ids >= 1) & (ids <= LAYER)).astype(f32)
    coef[...] = mine_shares * (mine_picked - jnp.sum(mine_shares * mine_picked, axis=0, keepdims=True))
    link.here(coef, o_coef, keep=True)
    for fz in (0, 1):
        par[0:1, fz * block : (fz + 1) * block] = bound_row[0:1, columns(0, fz)]
        par[1:2, fz * block : (fz + 1) * block] = gain_mix[0:1, columns(0, fz)]
    get_cot.wait()
    valid_rows = aux[0].T[:, 0:1]
    first_half = lax.broadcasted_iota(jnp.int32, (share, 1), 0) * 0 + t
    valid_half = jnp.where(first_half == 0, valid_rows[:share], valid_rows[share:])
    go_own[...] = (go_own[...].astype(f32) * valid_half).astype(bf16)
    n1_in[2].wait_recv()
    n1_core.append(link.remote(n1.at[row(3, t)], n1.at[row(3, t)], core))
    for c in (0, 1):
        far_mix[c].wait_recv()
        side_mix.append(link.remote(w_mix.at[pair(1 - zf, c, y)], w_mix.at[pair(1 - zf, c, y)], side))

    @pl.when(t == y)
    def _():
        out_far.wait_recv()
        out_next.start()
        out_far.wait_send()
        out_side.wait_send()
        out_here.wait()
        out_next.wait_send()

    @pl.when(t != y)
    def _():
        out_side.wait_recv()
        out_next.wait_recv()

    far_ffn, side_ffn = [], ([], [], [])

    def start_ffn(i):
        o = shards[i][1]
        ffn_own[i].wait()
        for c in ffn_in[3 * i : 3 * i + 3]:
            c.wait_recv()
        far_ffn.append([link.remote(o.at[:, pair(zf, c, y)], o.at[:, pair(zf, c, y)], far) for c in (0, 1)])
        side_ffn[i].extend(link.remote(o.at[:, pair(zf, c, y)], o.at[:, pair(zf, c, y)], side) for c in (0, 1))

    def forward_ffn(i):
        o = shards[i][1]
        for c in (0, 1):
            far_ffn[i][c].wait_recv()
            side_ffn[i].append(link.remote(o.at[:, pair(1 - zf, c, y)], o.at[:, pair(1 - zf, c, y)], side))

    start_ffn(0)
    go_in = [link.remote(go_own, o_go.at[row(r, t)], group[r]) for r in (1, 2)]
    go_core = [link.remote(go_own, o_go.at[row(0, t)], core)]
    go_here = link.here(go_own, o_go.at[row(0, t)])

    for c in side_mix + n1_core + aux_in:
        c.wait_recv()

    def core_copy(r):
        return pltpu.make_async_remote_copy(
            src_ref=part.at[row(r, 1 - t)],
            dst_ref=core_in.at[at(r * share, share, share)],
            send_sem=core_send.at[r],
            recv_sem=core_recv.at[r],
            device_id=core,
            device_id_type=MESH,
        )

    def sq_copy(r):
        return pltpu.make_async_remote_copy(
            src_ref=sq.at[row(r, 1 - t)],
            dst_ref=sq_core.at[at(r * share, share, share)],
            send_sem=sqc_send.at[r],
            recv_sem=sqc_recv.at[r],
            device_id=core,
            device_id_type=MESH,
        )

    bound = par[0:1, :]
    gain = par[1:2, :]

    def to_x(slot, r):
        from_rows, to_rows = at(r * share, share, share), at(slot * share, share, share)
        return [
            pltpu.make_async_remote_copy(
                src_ref=a.at[from_rows],
                dst_ref=b.at[to_rows],
                send_sem=x_send.at[i * 2 + slot],
                recv_sem=x_recv.at[i * 2 + slot],
                device_id=group[1],
                device_id_type=MESH,
            )
            for i, (a, b) in enumerate(((half, peer_in), (sq_half, sq_peer)))
        ]

    def hand_over(r):
        core_copy(r).wait()
        sq_copy(r).wait()

        def some(j, carry):
            to = at(r * share + j * 16, 16, 16)
            mine_rows = at(r * rows + t * share + j * 16, 16, 16)
            half[to, :] = (part[mine_rows, :].astype(f32) + core_in[to, :].astype(f32)).astype(bf16)
            sq_half[to, :] = sq[mine_rows, :] + sq_core[to, :]
            return carry

        lax.fori_loop(0, share // 16, some, 0)

    def piece(i, carry):
        r = 3 - 2 * i + 3 * (i // 2)
        here = at(r * rows, rows, rows)
        pre[here, :] = jnp.dot(n1[here, :], w_mix[...], preferred_element_type=f32)
        masks = aux[r].T
        valid = masks[:, 0:1]
        keep = masks[:, 1:2]
        forget = bound + (1.0 - bound) * jax.nn.sigmoid(pre[here, feat : 2 * feat])
        input_pre = pre[here, 0:feat]
        add[...] = input_pre * jax.nn.sigmoid(input_pre) * (1.0 - forget) * valid
        decay[...] = forget * keep
        scan_rows(decay, add, state.at[here, :], False)
        held = state[here, :]
        outgate_pre = pre[here, 2 * feat :]
        raw[here, :] = (held * gain * (outgate_pre * jax.nn.sigmoid(outgate_pre))).astype(bf16)
        sq[here, :] = fold_lanes(held * held)
        part[here, :] = jnp.dot(raw[here, :], w_out[...], preferred_element_type=f32).astype(bf16)
        core_copy(r).start()
        sq_copy(r).start()

        @pl.when(i > 0)
        def _():
            before = 5 - 2 * i + 3 * ((i - 1) // 2)
            hand_over(before)

            @pl.when(i < 3)
            def _():
                for c in to_x(i - 1, before):
                    c.start()

        return carry

    lax.fori_loop(0, 4, piece, 0)
    start_ffn(1)

    link.here(w_mix, o_mix, keep=True)
    link.here(w_out, o_out, keep=True)
    n1_out = link.here(n1, o_n1)
    link.here(pre, o_pre, keep=True)
    link.here(state, o_state, keep=True)
    link.here(raw, o_raw, keep=True)
    link.here(aux, o_aux, keep=True)
    link.here(par, o_par, keep=True)

    def spread(o, incoming, cores):
        incoming[1].wait_recv()
        incoming.append(link.remote(o.at[row(2, t)], o.at[row(3, t)], group[1]))
        cores.append(link.remote(o.at[row(2, t)], o.at[row(2, t)], core))
        incoming[0].wait_recv()
        cores.append(link.remote(o.at[row(1, t)], o.at[row(1, t)], core))

    def spread_last(o, incoming, cores):
        incoming[2].wait_recv()
        cores.append(link.remote(o.at[row(3, t)], o.at[row(3, t)], core))

    hand_over(0)
    for c in to_x(0, 3):
        c.wait()

    def pass_on(j, carry):
        two = at(2 * share + j * 16, 16, 16)
        half[two, :] = (half[two, :].astype(f32) + peer_in[at(j * 16, 16, 16), :].astype(f32)).astype(bf16)
        sq_half[two, :] = sq_half[two, :] + sq_peer[at(j * 16, 16, 16), :]
        return carry

    lax.fori_loop(0, share // 16, pass_on, 0)
    third = pl.ds(2 * share, share)
    to_z = [
        link.remote(half.at[third], peer_in.at[third], group[2]),
        link.remote(sq_half.at[third], sq_peer.at[third], group[2]),
    ]
    spread(o_go, go_in, go_core)
    forward_ffn(0)
    for c in to_x(1, 1):
        c.wait()
    for c in to_z:
        c.wait_recv()
    total_sq = sq_half[0:share, :] + sq_peer[share : 2 * share, :] + sq_peer[2 * share : 3 * share, :]
    scale = lax.rsqrt(jnp.sum(total_sq, axis=1, keepdims=True) / width + epsilon)
    sc[...] = jnp.broadcast_to(scale, sc.shape)
    chunk = min(share, 16)

    def finish(i, carry):
        to = at(i * chunk, chunk, chunk)
        total = part[at(t * share + i * chunk, chunk, chunk), :].astype(f32) + core_in[to, :].astype(f32)
        for r in (1, 2):
            total = total + peer_in[at(r * share + i * chunk, chunk, chunk), :].astype(f32)
        mixed = total * sc[to, 0:1]
        value = tok[at(t * share + i * chunk, chunk, chunk), :].astype(f32) + mixed
        mo[to, :] = mixed
        res[to, :] = value
        scale_two = lax.rsqrt(jnp.mean(value * value, axis=1, keepdims=True) + epsilon)
        n2[to, :] = (value * scale_two * gain_two[...]).astype(bf16)
        return carry

    lax.fori_loop(0, share // chunk, finish, 0)
    n2_in = [link.remote(n2, o_n2.at[row(r, t)], group[r]) for r in (1, 2)]
    n2_core = [link.remote(n2, o_n2.at[row(0, t)], core)]
    n2_here = link.here(n2, o_n2.at[row(0, t)])
    link.here(res, o_res, keep=True)
    link.here(mo, o_mo, keep=True)
    link.here(sc, o_sc, keep=True)
    start_ffn(2)
    spread_last(o_go, go_in, go_core)
    forward_ffn(1)
    spread(o_n2, n2_in, n2_core)
    spread_last(o_n2, n2_in, n2_core)

    forward_ffn(2)

    for c in side_ffn[0]:
        c.wait_recv()
    get_full = link.here(o_g, full_g)
    for c in n2_core:
        c.wait_recv()
    n2_here.wait()
    get_rows = link.here(o_n2, part)
    get_full.wait()
    get_rows.wait()

    def product(full, made):
        def some(j, carry):
            to = at(j * rows, rows, rows)
            made[:, to] = lax.dot_general(
                full[...], part[to, :], (((1,), (1,)), ((), ())), preferred_element_type=f32
            )
            return carry

        lax.fori_loop(0, 4, some, 0)

    product(full_g, gate)
    for c in side_ffn[1]:
        c.wait_recv()
    get_full = link.here(o_u, full_u)
    get_full.wait()
    for c in go_core:
        c.wait_recv()
    go_here.wait()
    n1_out.wait()
    link.sent(n1_in + n1_core)
    get_rows = link.here(o_go, n1)
    for c in side_ffn[2][:2]:
        c.wait_recv()
    early = [pair(fz, c, fy) for fz, fy in ((zf, y), (zf, 1 - y), (1 - zf, y)) for c in (0, 1)]
    get_early = [link.here(o_d.at[:, cols], full_g.at[:, cols]) for cols in early]
    product(full_u, up)
    for c in get_early + [get_rows]:
        c.wait()

    def contribution(cols, to):
        return lax.dot_general(
            full_g[:, cols], n1[to, cols], (((1,), (1,)), ((), ())), preferred_element_type=f32
        )

    def early_rows(j, carry):
        to = at(j * rows, rows, rows)
        total = contribution(early[0], to)
        for cols in early[1:]:
            total = total + contribution(cols, to)
        into[:, to] = total
        return carry

    lax.fori_loop(0, 4, early_rows, 0)
    late = [pair(1 - zf, c, 1 - y) for c in (0, 1)]
    get_late = []
    for c, cols in zip(side_ffn[2][2:], late):
        c.wait_recv()
        get_late.append(link.here(o_d.at[:, cols], full_g.at[:, cols]))
    for c in get_late:
        c.wait()

    def hidden_rows(j, carry):
        to = at(j * rows, rows, rows)
        grad = into[:, to] + contribution(late[0], to) + contribution(late[1], to)
        value, other = gate[:, to], up[:, to]
        sig = jax.nn.sigmoid(value)
        act = value * sig
        hid_v[:, to] = (act * other).astype(bf16)
        hid_u[:, to] = (grad * act).astype(bf16)
        hid_g[:, to] = (grad * other * (sig * (1.0 + value * (1.0 - sig)))).astype(bf16)
        return carry

    lax.fori_loop(0, 4, hidden_rows, 0)
    for made, out in ((hid_v, o_hid), (hid_g, o_hg), (hid_u, o_hu)):
        link.here(made, out, keep=True)
    link.close()


def front(s_in, s_fg, s_og, s_out, w_g, w_u, s_d, cot, tok, gain_one, gain_mix, gain_two, table, lengths, bucket):
    rows, width = tok.shape
    share, group_rows = rows // 2, 4 * rows
    block = s_out.shape[0]
    feat, hid = 2 * block, s_d.shape[0] // 4
    lanes = 128 if feat % 128 == 0 else feat
    any_spec = pl.BlockSpec(memory_space=pl.ANY)
    vmem_spec = pl.BlockSpec(memory_space=pltpu.VMEM)
    made = jax.ShapeDtypeStruct
    outs = [
        made((width, 3 * feat), bf16),
        made((feat, width), bf16),
        made((hid, width), bf16),
        made((hid, width), bf16),
        made((hid, width), bf16),
        made((group_rows, width), bf16),
        made((group_rows, width), bf16),
        made((group_rows, width), bf16),
        made((group_rows, 3 * feat), f32),
        made((group_rows, feat), f32),
        made((group_rows, feat), bf16),
        made((share, width), f32),
        made((share, width), f32),
        made((share, 128), f32),
        made((4, 8, rows), f32),
        made((2, feat), f32),
        made((hid, group_rows), bf16),
        made((hid, group_rows), bf16),
        made((hid, group_rows), bf16),
        made((table.shape[0], block), f32),
    ]
    scratch = [
        pltpu.VMEM((width, 3 * feat), bf16),
        pltpu.VMEM((feat, width), bf16),
        pltpu.VMEM((group_rows, width), bf16),
        pltpu.VMEM((4, 8, rows), f32),
        pltpu.VMEM((group_rows, 3 * feat), f32),
        pltpu.VMEM((group_rows, feat), f32),
        pltpu.VMEM((group_rows, feat), bf16),
        pltpu.VMEM((group_rows, width), bf16),
        pltpu.VMEM((4 * share, width), bf16),
        pltpu.VMEM((4 * share, width), bf16),
        pltpu.VMEM((4 * share, width), bf16),
        pltpu.VMEM((2, feat), f32),
        pltpu.VMEM(w_g.shape, bf16),
        pltpu.VMEM(w_u.shape, bf16),
        pltpu.VMEM((4 * hid, block), bf16),
        pltpu.VMEM((4 * hid, block), bf16),
        pltpu.VMEM((share, width), bf16),
        pltpu.VMEM((8, width), f32),
        pltpu.VMEM((hid, width), bf16),
        pltpu.VMEM((hid, width), bf16),
        pltpu.VMEM((hid, group_rows), f32),
        pltpu.VMEM((hid, group_rows), f32),
        pltpu.VMEM((hid, group_rows), f32),
        pltpu.VMEM((hid, group_rows), bf16),
        pltpu.VMEM((hid, group_rows), bf16),
        pltpu.VMEM((hid, group_rows), bf16),
        pltpu.VMEM(table.shape, f32),
        pltpu.VMEM((table.shape[0], block), f32),
        pltpu.VMEM((group_rows, lanes), f32),
        pltpu.VMEM((4 * share, lanes), f32),
        pltpu.VMEM((4 * share, lanes), f32),
        pltpu.VMEM((4 * share, lanes), f32),
        pltpu.VMEM((share, width), f32),
        pltpu.VMEM((share, width), f32),
        pltpu.VMEM((share, 128), f32),
        pltpu.VMEM((share, width), bf16),
        pltpu.VMEM((rows, feat), f32),
        pltpu.VMEM((rows, feat), f32),
        pltpu.SemaphoreType.DMA((88,)),
        pltpu.SemaphoreType.DMA((88,)),
        pltpu.SemaphoreType.DMA((48,)),
    ] + [pltpu.SemaphoreType.DMA((4,))] * 8
    return pl.pallas_call(
        front_kernel,
        in_specs=[any_spec] * 8 + [vmem_spec] * 5 + [pl.BlockSpec(memory_space=pltpu.SMEM)] * 2,
        out_specs=[any_spec] * len(outs),
        out_shape=outs,
        scratch_shapes=scratch,
        compiler_params=pltpu.CompilerParams(
            collective_id=1, has_side_effects=True, vmem_limit_bytes=60 << 20
        ),
        name="front",
    )(s_in, s_fg, s_og, s_out, w_g, w_u, s_d, cot, tok, gain_one, gain_mix, gain_two, table, lengths, bucket)


def back_kernel(
    h_d, h_g, h_u, n2, go, w_g, w_u, w_d, n1, w_mix_in, w_out_in, pre, state, raw, aux_in,
    par, tok, res, mo, sc, first_gain, second_gain,
    o_g, o_u, o_d, o_mix, o_out, o_tok, o_blk, o_vec,
    left, right, gmix, dw_d, dw_g, dw_u, dw_mix, yr_d, yr_g, yr_u, yr_mix, zr_d, zr_g, zr_u, zr_mix,
    own, half, core_in, core_blk, peer_in, peer_blk, w_mix, w_out, aux, pre_b, state_b, raw_b,
    grads, grads_t, decay, add, yr_out, zr_out, hid_a, hid_b,
    gres, gm_own, scalars, scal_all, sums, vec, vec_in,
    send, recv, local, core_send, core_recv, out_send, out_recv, piece_sem,
):
    me, t, (zf, zn, y, x), q, group, far, side, core = position()
    rows, width = tok.shape
    share = rows // 2
    block = width // 16
    feat = par.shape[1]
    link = Copies(send, recv, local)
    meet(group[1:] + [far, side, core])

    def at(start, size, unit):
        return pl.ds(pl.multiple_of(start, unit), size)

    def pair(fz, c, fy):
        return at(fz * (8 * block) + c * (4 * block) + fy * (2 * block), 2 * block, 2 * block)

    def row(r, tt):
        return at(r * rows + tt * share, share, share)

    def rel(r):
        return pl.ds(r * share, share)

    hid_rows = pl.ds(0, w_g.shape[0])
    full_g, full_u = left.at[hid_rows], gmix.at[hid_rows]
    get_g = [link.here(h_g, hid_a), link.here(n2, right)]
    get_u = link.here(h_u, hid_b)
    get_two = [link.here(w_g, full_g), link.here(w_u, full_u)]
    get_go = [link.here(go.at[row(0, t)], gm_own)]
    get_w_d = link.here(w_d, dw_d)
    get_aux = [link.here(aux_in, aux), link.here(w_mix_in, w_mix)]
    order = (3, 1, 2, 0)

    def stage(r):
        i = order.index(r)
        return w_out if i == 3 else dw_mix.at[i]

    def staged(r, tt):
        return w_out.at[at(tt * share, share, share)] if r == 0 else stage(r).at[tt]

    def products(terms):
        wide = 4 * block

        def at_piece(r, store):
            here = at(r * rows, rows, rows)

            def some(j, carry):
                to = at(j * wide, wide, wide)
                total = None
                for hid, weight in terms:
                    one = lax.dot_general(
                        hid[:, here], weight[:, to], (((0,), (0,)), ((), ())), preferred_element_type=f32
                    )
                    total = one if total is None else total + one
                store(to, total.astype(bf16))
                return carry

            lax.fori_loop(0, width // wide, some, 0)

        return at_piece

    def all_pieces(terms, incoming):
        at_piece = products(terms)
        copies = {}
        for i, r in enumerate(order):
            if r:

                def store(to, value):
                    dw_mix[i, 0, :, to] = value[:share]
                    dw_mix[i, 1, :, to] = value[share:]

            else:

                def store(to, value):
                    w_out[:, to] = value

            at_piece(r, store)
            copies[r] = link.remote(staged(r, 1 - t), incoming.at[rel(r)], core)
        return copies

    def two_rows(r, j):
        if r == 0:
            return w_out[at(t * share + j * 16, 16, 16), :].astype(f32)
        return dw_mix[order.index(r), t, at(j * 16, 16, 16), :].astype(f32)

    def own_rows(r, j):
        return own[at(r * share + j * 16, 16, 16), :].astype(f32)

    def add_half(r, source, incoming, held):
        def some(j, carry):
            to = at(r * share + j * 16, 16, 16)
            held[to, :] = (source(r, j) + incoming[to, :].astype(f32)).astype(bf16)
            return carry

        lax.fori_loop(0, share // 16, some, 0)

    def over_cores(arrived, source, incoming, held, peers):
        sent = []
        for r in (3, 1, 2, 0):
            arrived[r].wait_recv()
            if r:
                add_half(r, source, incoming, held)
            if r % 2:
                sent.append(link.remote(held.at[rel(r)], peers.at[rel(len(sent))], group[1]))
        return sent

    def pass_on(sent, held, peers):
        sent[0].wait_recv()

        def some(j, carry):
            two = at(2 * share + j * 16, 16, 16)
            held[two, :] = (held[two, :].astype(f32) + peers[at(j * 16, 16, 16), :].astype(f32)).astype(bf16)
            return carry

        lax.fori_loop(0, share // 16, some, 0)
        sent.append(link.remote(held.at[rel(2)], peers.at[rel(2)], group[2]))


    def weight_grad(hid, other, dw, first, count):
        wide = 4 * block

        def columns(i, carry):
            to = at(((1 - zf) * 2 + i - (i // 2) * 4 * (1 - zf)) * wide, wide, wide)
            made = jnp.dot(hid[...], other[:, to], preferred_element_type=f32).astype(bf16)
            if len(dw.shape) == 2:
                dw[:, to] = made
            else:
                dw[:, :, :, to] = made.reshape(dw.shape[:3] + (wide,))
            return carry

        lax.fori_loop(first, first + count, columns, 0)

    def cut(ref, cols):
        return ref.at[:, cols] if len(ref.shape) == 2 else ref.at[:, :, :, cols]

    def side_part(dw, yr, slot, c):
        fz = 1 - zf if slot == 0 else zf
        to = cut(yr, pl.ds((slot * 2 + c) * 2 * block, 2 * block))
        return link.remote(cut(dw, pair(fz, c, 1 - y)), to, side)

    def side_send(dw, yr, slot):
        return [side_part(dw, yr, slot, c) for c in (0, 1)]

    def far_half(hid, other, dw, yr):
        sent = []
        for c in (0, 1):
            weight_grad(hid, other, dw, c, 1)
            sent.append(side_part(dw, yr, 0, c))
        return sent

    def add_columns(dw, to, others):
        if len(dw.shape) == 2:
            size = 64 if dw.shape[0] % 64 == 0 else dw.shape[0]
            steps = dw.shape[0] // size
        else:
            steps = dw.shape[0] * dw.shape[1]

        def some(j, carry):
            if len(dw.shape) == 2:
                lead = (at(j * size, size, size),)
            else:
                lead = (j // dw.shape[1], j % dw.shape[1], slice(None))
            total = dw[lead + (to,)].astype(f32)
            for ref, cols in others:
                total = total + ref[lead + (cols,)].astype(f32)
            dw[lead + (to,)] = total.astype(bf16)
            return carry

        lax.fori_loop(0, steps, some, 0)

    def part_of(i):
        return pl.ds(i * 2 * block, 2 * block)

    def second_hop(hop, dw, yr, zr):
        sent = []
        for c in (0, 1):
            hop[c].wait_recv()
            add_columns(dw, pair(1 - zf, c, y), [(yr, part_of(c))])
            sent.append(link.remote(cut(dw, pair(1 - zf, c, y)), cut(zr, part_of(c)), far))
        return sent

    def last_hop(near, sent, dw, yr, zr, out):
        for c in (0, 1):
            near[c].wait_recv()
            sent[c].wait_recv()
            add_columns(dw, pair(zf, c, y), [(yr, part_of(2 + c)), (zr, part_of(c))])

        def owner(r):
            fx = x if r in (0, 2) else 1 - x
            fzn = zn if r in (0, 1) else 1 - zn
            return at((zf * 8 + fzn * 4 + y * 2 + fx) * block, block, block)

        if len(dw.shape) == 2:
            place = out.at[q[0]]
            link.here(dw.at[:, owner(0)], place, keep=True)
            return [link.remote(dw.at[:, owner(r)], place, group[r]) for r in (1, 2, 3)]
        place = out.at[:, :, zn, t, x]
        kept = link.here(cut(dw, owner(0)), place)
        sent = [link.remote(cut(dw, owner(r)), place, group[r]) for r in (1, 2, 3)]
        kept.wait()
        return sent

    for c in get_g:
        c.wait()
    hop_g = far_half(hid_a, right, dw_g, yr_g)
    get_u.wait()
    for c in get_two:
        c.wait()
    two_core = all_pieces([(hid_a, full_g), (hid_b, full_u)], core_in)

    two_peer = over_cores(two_core, two_rows, core_in, half, peer_in)
    weight_grad(hid_b, right, dw_u, 0, 2)
    get_left = link.here(go, left)
    weight_grad(hid_a, right, dw_g, 2, 2)
    get_d = link.here(h_d, hid_a)
    far_g = second_hop(hop_g, dw_g, yr_g, zr_g)
    hop_u = side_send(dw_u, yr_u, 0)
    pass_on(two_peer, half, peer_in)
    weight_grad(hid_b, right, dw_u, 2, 2)

    for c in two_peer[1:]:
        c.wait_recv()
    for c in get_go:
        c.wait()
    gain_two = second_gain[...]
    sums[...] = jnp.zeros_like(sums)
    step = 16

    def residual_rows(j, carry):
        to = at(j * step, step, step)
        total = two_rows(0, j) + core_in[to, :].astype(f32)
        for r in (1, 2):
            total = total + peer_in[at(r * share + j * step, step, step), :].astype(f32)
        value = res[to, :]
        s = lax.rsqrt(jnp.mean(value * value, axis=1, keepdims=True) + epsilon)
        weighted = total * gain_two
        grad = (
            gm_own[to, :].astype(f32)
            + s * weighted
            - value * (s * s * s) * jnp.mean(weighted * value, axis=1, keepdims=True)
        )
        gres[to, :] = grad
        low = grad.astype(bf16)
        gm_own[to, :] = low
        dot = jnp.sum(low.astype(f32) * mo[to, :], axis=1, keepdims=True)
        scale = sc[to, 0:1]
        sc[to, 1:2] = dot / (scale * width)
        sums[1:2, :] += jnp.sum(total * value * s, axis=0, keepdims=True)
        return carry

    lax.fori_loop(0, share // step, residual_rows, 0)
    scalars[...] = sc[...].T[0:8, :]

    def scal(r, tt):
        return scal_all.at[r * 2 + tt]

    gm_in = [link.remote(gm_own, gmix.at[row(r, t)], group[r]) for r in (1, 2)]
    sc_in = [link.remote(scalars, scal(r, t), group[r]) for r in (1, 2, 3)]
    gm_core = [link.remote(gm_own, gmix.at[row(0, t)], core), link.remote(scalars, scal(0, t), core)]
    gm_here = [link.here(gm_own, gmix.at[row(0, t)]), link.here(scalars, scal(0, t))]
    for c in (get_d, get_w_d, get_left):
        c.wait()
    link.sent(two_core.values())
    blk_core = all_pieces([(hid_a, dw_d)], core_blk)
    blk_own = [link.here(staged(r, t), own.at[rel(r)]) for r in order]
    weight_grad(hid_a, left, dw_d, 0, 2)
    hop_d = side_send(dw_d, yr_d, 0)
    far_u = second_hop(hop_u, dw_u, yr_u, zr_u)
    near_g = side_send(dw_g, yr_g, 1)
    gm_in[1].wait_recv()
    gm_in.append(link.remote(gmix.at[row(2, t)], gmix.at[row(3, t)], group[1]))
    gm_core.append(link.remote(gmix.at[row(2, t)], gmix.at[row(2, t)], core))
    gm_in[0].wait_recv()
    gm_core.append(link.remote(gmix.at[row(1, t)], gmix.at[row(1, t)], core))
    for i, r in enumerate((1, 2, 3)):
        sc_in[i].wait_recv()
        gm_core.append(link.remote(scal(r, t), scal(r, t), core))
    weight_grad(hid_a, left, dw_d, 2, 2)
    get_n1 = link.here(n1, left)
    near_u = side_send(dw_u, yr_u, 1)
    for c in blk_own:
        c.wait()
    gm_in[2].wait_recv()
    gm_core.append(link.remote(gmix.at[row(3, t)], gmix.at[row(3, t)], core))
    far_d = second_hop(hop_d, dw_d, yr_d, zr_d)
    near_d = side_send(dw_d, yr_d, 1)
    blk_peer = over_cores(blk_core, own_rows, core_blk, own, peer_blk)
    link.sent(blk_core.values())
    link.sent(two_peer)
    get_aux.append(link.here(w_out_in, w_out))
    for c in get_aux + [get_n1] + gm_here:
        c.wait()
    for c in gm_core:
        c.wait_recv()

    def one_core(r):
        return pltpu.make_async_remote_copy(
            src_ref=right.at[row(r, 1 - t)],
            dst_ref=core_in.at[at(r * share, share, share)],
            send_sem=core_send.at[r],
            recv_sem=core_recv.at[r],
            device_id=core,
            device_id_type=MESH,
        )

    def fetch(r):
        here = at(r * rows, rows, rows)
        return [
            pltpu.make_async_copy(pre.at[here], pre_b, piece_sem.at[0]),
            pltpu.make_async_copy(state.at[here], state_b, piece_sem.at[1]),
            pltpu.make_async_copy(raw.at[here], raw_b, piece_sem.at[2]),
        ]

    bound = par[0:1, :]
    gain = par[1:2, :]
    gain_sums = sums.at[2:4, 0:feat]
    mixed_t = hid_b.at[0:feat]
    dw_out = w_out

    def one_rows(r, j):
        return right[at(r * rows + t * share + j * 16, 16, 16), :].astype(f32)

    def one_x(slot, r):
        return pltpu.make_async_remote_copy(
            src_ref=half.at[at(r * share, share, share)],
            dst_ref=peer_in.at[at(slot * share, share, share)],
            send_sem=core_send.at[4 + slot],
            recv_sem=core_recv.at[4 + slot],
            device_id=group[1],
            device_id_type=MESH,
        )

    def hand_over(r):
        one_core(r).wait()
        add_half(r, one_rows, core_in, half)

    def piece(i, carry):
        r = 3 - 2 * i + 3 * (i // 2)
        here = at(r * rows, rows, rows)
        copies = fetch(r)
        for c in copies:
            c.start()
        up = lax.dot_general(
            gmix[here, :], w_out[...], (((1,), (1,)), ((), ())), preferred_element_type=f32
        )
        masks = aux[r].T
        valid = masks[:, 0:1]
        keep = masks[:, 1:2]
        scale_parts = [scal_all[r * 2 + tt].T for tt in (0, 1)]
        scale = jnp.concatenate([p[:, 0:1] for p in scale_parts], axis=0)
        dot_mean = jnp.concatenate([p[:, 1:2] for p in scale_parts], axis=0)
        for c in copies:
            c.wait()
        at_row = lax.broadcasted_iota(jnp.int32, (rows, feat), 0)
        input_pre = pre_b[:, :feat]
        outgate_pre = pre_b[:, 2 * feat :]
        held = state_b[...]
        sig_out = jax.nn.sigmoid(outgate_pre)
        act_out = outgate_pre * sig_out
        scaled = up * (held * scale)
        grads[:, 2 * feat :] = scaled * gain * (sig_out * (1.0 + outgate_pre * (1.0 - sig_out)))
        add[...] = scale * (gain * act_out * up) - held * (scale * scale * scale * dot_mean)
        gain_sums[0:1, :] += jnp.sum(scaled * act_out, axis=0, keepdims=True)
        sig_forget = jax.nn.sigmoid(pre_b[:, feat : 2 * feat])
        forget = bound + (1.0 - bound) * sig_forget
        decay[...] = jnp.where(at_row < rows - 1, pltpu.roll(forget * keep, rows - 1, 0), 0.0)
        scan_rows(decay, add, add, True)
        grad_state = add[...]
        before = jnp.where(at_row > 0, pltpu.roll(held, 1, 0), 0.0)
        sig_in = jax.nn.sigmoid(input_pre)
        grad_forget = grad_state * (before * keep - input_pre * sig_in * valid)
        grads[:, :feat] = (
            grad_state * (1.0 - forget) * valid * (sig_in * (1.0 + input_pre * (1.0 - sig_in)))
        )
        grads[:, feat : 2 * feat] = grad_forget * (1.0 - bound) * sig_forget * (1.0 - sig_forget)
        gain_sums[1:2, :] += jnp.sum(grad_forget * (1.0 - sig_forget), axis=0, keepdims=True)
        low = grads[...].astype(bf16)
        right[here, :] = lax.dot_general(
            low, w_mix[...], (((1,), (1,)), ((), ())), preferred_element_type=f32
        ).astype(bf16)
        one_core(r).start()
        grads_t[:, here] = grads[...].T.astype(bf16)
        mixed_t[:, here] = (raw_b[...].astype(f32) * scale).T.astype(bf16)

        @pl.when(i > 0)
        def _():
            before_r = 5 - 2 * i + 3 * ((i - 1) // 2)
            hand_over(before_r)

            @pl.when(i < 3)
            def _():
                one_x(i - 1, before_r).start()

        return carry

    lax.fori_loop(0, 4, piece, 0)

    one_core(0).wait()
    pass_on(blk_peer, own, peer_blk)

    hop_mix = far_half(grads_t, left, dw_mix, yr_mix)
    weight_grad(grads_t, left, dw_mix, 2, 2)

    def out_columns(i, carry):
        to = at(i * (4 * block), 4 * block, 4 * block)
        dw_out[:, to] = jnp.dot(mixed_t[...], gmix[:, to], preferred_element_type=f32).astype(bf16)
        return carry

    lax.fori_loop(0, 4, out_columns, 0)
    near_rows = at(zf * block, block, block)
    far_rows = at((1 - zf) * block, block, block)

    def out_copy(k, src, dst, device):
        return pltpu.make_async_remote_copy(
            src_ref=src,
            dst_ref=dst,
            send_sem=out_send.at[k],
            recv_sem=out_recv.at[k],
            device_id=device,
            device_id_type=MESH,
        )

    out_side = out_copy(0, dw_out, yr_out, side)
    out_far = out_copy(1, dw_out.at[far_rows], zr_out, far)
    out_core = out_copy(2, dw_out.at[near_rows], o_out, core)
    out_here = pltpu.make_async_copy(dw_out.at[near_rows], o_out, out_send.at[3])

    @pl.when(t != y)
    def _():
        out_side.start()

    one_x(0, 3).wait()

    def one_on(j, carry):
        two = at(2 * share + j * 16, 16, 16)
        half[two, :] = (half[two, :].astype(f32) + peer_in[at(j * 16, 16, 16), :].astype(f32)).astype(bf16)
        return carry

    lax.fori_loop(0, share // 16, one_on, 0)
    one_z = link.remote(half.at[rel(2)], peer_in.at[rel(2)], group[2])
    near_mix = side_send(dw_mix, yr_mix, 1)
    back_g = last_hop(near_g, far_g, dw_g, yr_g, zr_g, o_g)
    back_u = last_hop(near_u, far_u, dw_u, yr_u, zr_u, o_u)
    far_mix = second_hop(hop_mix, dw_mix, yr_mix, zr_mix)

    @pl.when(t == y)
    def _():
        out_side.wait_recv()
        add_columns(dw_out, pl.ds(0, width), [(yr_out, pl.ds(0, width))])
        out_far.start()

    one_x(1, 1).wait()
    one_z.wait_recv()
    gain_one = first_gain[...]

    def token_rows(j, carry):
        to = at(j * step, step, step)
        total = one_rows(0, j) + core_in[to, :].astype(f32)
        for r in (1, 2):
            total = total + peer_in[at(r * share + j * step, step, step), :].astype(f32)
        value = tok[at(t * share + j * step, step, step), :].astype(f32)
        s = lax.rsqrt(jnp.mean(value * value, axis=1, keepdims=True) + epsilon)
        weighted = total * gain_one
        gres[to, :] = (
            gres[to, :]
            + s * weighted
            - value * (s * s * s) * jnp.mean(weighted * value, axis=1, keepdims=True)
        )
        sums[0:1, :] += jnp.sum(total * value * s, axis=0, keepdims=True)
        return carry

    lax.fori_loop(0, share // step, token_rows, 0)
    tok_rows = at(t * share, share, share)
    tok_core = link.remote(gres, o_tok.at[tok_rows], core)
    link.here(gres, o_tok.at[tok_rows], keep=True)

    vec[0] = jnp.zeros(vec.shape[1:], f32)
    for k in (0, 1):
        for i in range(16):
            vec[0, k * 16 + i : k * 16 + i + 1, :] = sums[k : k + 1, i * block : (i + 1) * block]
    for k in (2, 3):
        for i in (0, 1):
            vec[0, pl.ds(k * 16 + i * 8 + zn * 4 + t * 2 + x, 1), :] = sums[
                k : k + 1, i * block : (i + 1) * block
            ]
    partners = [group[1], group[2], side, far, core]
    turn = [link.remote(vec.at[0], vec_in.at[0], partners[0])]

    def next_turn():
        k = len(turn)
        turn[k - 1].wait_recv()
        vec[k] = vec[k - 1] + vec_in[k - 1]
        if k < len(partners):
            turn.append(link.remote(vec.at[k], vec_in.at[k], partners[k]))

    next_turn()
    back_d = last_hop(near_d, far_d, dw_d, yr_d, zr_d, o_d)
    next_turn()
    next_turn()
    for c in blk_peer[1:]:
        c.wait_recv()

    def block_rows(j, carry):
        to = at(j * step, step, step)
        total = own_rows(0, j) + core_blk[to, :].astype(f32)
        for r in (1, 2):
            total = total + peer_blk[at(r * share + j * step, step, step), :].astype(f32)
        gm_own[to, :] = (res[to, :] + total).astype(bf16)
        return carry

    link.sent(gm_in[:2] + gm_core[:1])
    lax.fori_loop(0, share // step, block_rows, 0)
    link.here(gm_own, o_blk, keep=True)
    next_turn()
    next_turn()
    link.here(vec.at[5], o_vec, keep=True)
    back_mix = last_hop(near_mix, far_mix, dw_mix, yr_mix, zr_mix, o_mix)

    @pl.when(t == y)
    def _():
        out_far.wait_recv()

        def some(j, carry):
            to = at(zf * block + j * 16, 16, 16)
            dw_out[to, :] = (
                dw_out[to, :].astype(f32) + zr_out[at(j * 16, 16, 16), :].astype(f32)
            ).astype(bf16)
            return carry

        lax.fori_loop(0, block // 16, some, 0)
        out_core.start()
        out_here.start()
        out_far.wait_send()
        out_core.wait_send()
        out_here.wait()

    @pl.when(t != y)
    def _():
        out_side.wait_send()
        out_core.wait_recv()

    for c in back_mix:
        c.wait_recv()
    mix_core = link.remote(o_mix.at[:, :, :, t], o_mix.at[:, :, :, t], core)
    for c in back_d + back_g + back_u + [mix_core, tok_core]:
        c.wait_recv()
    link.close()


def back(*arrays):
    par, tok = arrays[15], arrays[16]
    rows, width = tok.shape
    share, group_rows = rows // 2, 4 * rows
    feat, hid, block = par.shape[1], arrays[0].shape[0], width // 16
    made = jax.ShapeDtypeStruct
    vm = pltpu.VMEM
    outs = [
        made((4, hid, block), bf16),
        made((4, hid, block), bf16),
        made((4, hid, block), bf16),
        made((3, 2, 2, 2, 2, block, block), bf16),
        made((block, width), bf16),
        made((rows, width), f32),
        made((share, width), bf16),
        made((64, block), f32),
    ]
    scratch = (
        [vm((group_rows, width), bf16)] * 3
        + [vm((hid, width), bf16)] * 3
        + [vm((3, 2, block, width), bf16)]
        + [vm((hid, width // 2), bf16)] * 3
        + [vm((3, 2, block, width // 2), bf16)]
        + [vm((hid, width // 4), bf16)] * 3
        + [vm((3, 2, block, width // 4), bf16)]
        + [vm((4 * share, width), bf16)] * 4
        + [vm((3 * share, width), bf16)] * 2
        + [
            vm((width, 3 * feat), bf16),
            vm((feat, width), bf16),
            vm(arrays[14].shape, f32),
            vm((rows, 3 * feat), f32),
            vm((rows, feat), f32),
            vm((rows, feat), bf16),
            vm((rows, 3 * feat), f32),
            vm((3 * feat, group_rows), bf16),
            vm((rows, feat), f32),
            vm((rows, feat), f32),
            vm((feat, width), bf16),
            vm((block, width), bf16),
            vm((hid, group_rows), bf16),
            vm((hid, group_rows), bf16),
            vm((share, width), f32),
            vm((share, width), bf16),
            vm((8, share), f32),
            vm((8, 8, share), f32),
            vm((4, width), f32),
            vm((6, 64, block), f32),
            vm((5, 64, block), f32),
            pltpu.SemaphoreType.DMA((96,)),
            pltpu.SemaphoreType.DMA((96,)),
            pltpu.SemaphoreType.DMA((32,)),
        ]
        + [pltpu.SemaphoreType.DMA((6,))] * 5
    )
    any_spec = pl.BlockSpec(memory_space=pl.ANY)
    vmem_spec = pl.BlockSpec(memory_space=pltpu.VMEM)
    return pl.pallas_call(
        back_kernel,
        in_specs=[any_spec] * 15 + [vmem_spec] * 7,
        out_specs=[any_spec] * len(outs),
        out_shape=outs,
        scratch_shapes=scratch,
        compiler_params=pltpu.CompilerParams(
            collective_id=2, has_side_effects=True, vmem_limit_bytes=127 << 19
        ),
        name="back",
    )(*arrays)


def body(
    n_dp,
    n_t,
    tokens_in,
    input_proj,
    forget_proj,
    outgate_proj,
    output_proj,
    glu_gate,
    glu_up,
    glu_down,
    norm_gain,
    mixer_gain,
    ffn_gain,
    bound_table,
    lengths,
    bucket,
    cotangent,
):
    depth = n_dp.bit_length() - 1
    tp_bits = (2, 0)
    fs_bits = tuple(b for b in reversed(range(depth)) if b not in tp_bits)
    t_depth = n_t.bit_length() - 1
    own_bits, free_bits = fs_bits[len(fs_bits) - t_depth :], fs_bits[: len(fs_bits) - t_depth]
    n_tp = 4
    tp_mask = (0, 1, 4, 5)
    axis_of = {b: depth - 1 - b for b in range(depth)}

    me = lax.axis_index("dp")
    t = lax.axis_index("tensor")
    bit = {b: (me >> b) & 1 for b in range(depth)}
    t_bit = {b: (t >> (t_depth - 1 - i)) & 1 for i, b in enumerate(own_bits)}
    q = bit[2] * 2 + bit[0]

    rows, width = tokens_in.shape
    share = cotangent.shape[0]
    block = width // n_dp
    free = 2 ** len(free_bits)
    feat = free * block

    def swap(values, mask):
        return lax.ppermute(values, "dp", [(i, i ^ mask) for i in range(n_dp)])

    def t_swap(values):
        return lax.ppermute(values, "tensor", [(0, 1), (1, 0)])

    def by_bit(which, own, other):
        return jnp.where(which == 0, own, other), jnp.where(which == 0, other, own)

    def in_order(parts, bits):
        parts = list(parts)
        for i, b in enumerate(reversed(bits)):
            step = 1 << i
            for r in range(len(parts)):
                if not r & step:
                    parts[r], parts[r | step] = by_bit(bit[b], parts[r], parts[r | step])
        return parts

    def t_gather(values):
        if n_t == 2:
            return jnp.stack(by_bit(t, values, t_swap(values)))
        return lax.all_gather(values, "tensor", axis=0)

    def t_scatter(values):
        if n_t == 2:
            return pick(values, t, 0).astype(f32) + t_swap(pick(values, 1 - t, 0)).astype(f32)
        return lax.psum_scatter(values, "tensor", scatter_dimension=0, tiled=False).astype(f32)

    def tp_gather(values):
        return [t_gather(values if r == 0 else swap(values, tp_mask[r])) for r in range(n_tp)]

    def tp_scatter(parts, kind):
        halves = [t_scatter(part) for part in parts]
        total = halves[0]
        for r in range(1, n_tp):
            total = total + swap(halves[r].astype(kind), tp_mask[r]).astype(f32)
        return total

    def exchange(values):
        parts = [pick(values, q, 0)]
        for r in range(1, n_tp):
            parts.append(swap(pick(values, q ^ r, 0), tp_mask[r]))
        return in_order(parts, tp_bits)

    def fs_gather(values):
        parts = [values]
        for b in fs_bits:
            parts = parts + [None] * 0 + [swap(v, 1 << b) for v in parts]
        return parts

    def weight_parts(shards):
        return fs_gather(jnp.stack(exchange(shards)))

    def weight_whole(parts):
        count = len(parts)
        flip = [0] * count
        for r in range(count):
            flip[sum(((r >> i) & 1) << (len(fs_bits) - 1 - i) for i in range(len(fs_bits)))] = parts[r]
        ordered = jnp.stack(in_order(flip, fs_bits))
        cols = ordered.shape[-1]
        ordered = ordered.reshape((2,) * depth + (block, cols))
        have = fs_bits + tp_bits
        axes = [have.index(b) for b in reversed(range(depth))]
        return ordered.transpose(axes + [depth, depth + 1]).reshape(width, cols)

    def weight_back(grad):
        cols = grad.shape[1]
        grad = grad.reshape((2,) * depth + (block, cols))
        for b in reversed(fs_bits):
            send = lax.dynamic_slice_in_dim(grad, 1 - bit[b], 1, axis_of[b]).astype(bf16)
            hold = lax.dynamic_slice_in_dim(grad, bit[b], 1, axis_of[b]).astype(f32)
            grad = hold + swap(send, 1 << b).astype(f32)
        return exchange(grad.reshape(n_tp, block, cols).astype(bf16))

    def my_columns(values):
        lead = values.shape[:-1]
        n = len(lead)
        values = values.reshape(lead + (2,) * depth + (block,))
        bits = list(reversed(range(depth)))
        for b in own_bits:
            values = pick(values, t_bit[b], n + bits.index(b))
            bits.remove(b)
        order = [n + bits.index(b) for b in tp_bits] + list(range(n)) + [n + bits.index(b) for b in free_bits]
        return values.transpose(order + [n + len(bits)]).reshape((n_tp,) + lead + (feat,))

    def my_half(values):
        return lax.dynamic_slice_in_dim(values, t * share, share, 0)

    hid = glu_gate.shape[1] // n_tp
    if n_dp == 16 and n_t == 2:
        (
            mix_full, out_full, gate_full, up_full, down_full, normed_one, grad_out_all, normed_two,
            pre, state, mix_raw, residual, mixed_out, scale_lanes, aux_rows, par, hidden, grad_gate,
            grad_up, coef,
        ) = front(
            input_proj, forget_proj, outgate_proj, output_proj, glu_gate, glu_up, glu_down, cotangent,
            tokens_in, norm_gain[None, :], mixer_gain[None, :], ffn_gain[None, :], bound_table, lengths, bucket,
        )
    else:
        inputs = tokens_in.astype(f32)
        scale_one = rms_scale(inputs)
        normed_mine = (inputs * scale_one * norm_gain).astype(bf16)
        inputs_half = my_half(inputs)
        scale_one_half = my_half(scale_one)
        mix_shards = jnp.concatenate(
            [my_columns(w) for w in (input_proj, forget_proj, outgate_proj)], axis=-1
        )
        gate_shards = glu_gate.T.reshape(n_tp, hid, block)
        up_shards = glu_up.T.reshape(n_tp, hid, block)
        down_shards = glu_down.reshape(n_tp, hid, block)
        my_table = pick(my_columns(bound_table), q, 0)
        par = jnp.stack([bound_parts(my_table)[2], pick(my_columns(mixer_gain), q, 0)])
        valid_own, keep_own = layout(lengths, bucket, rows)
        grad_out_rows = (cotangent.astype(f32) * my_half(valid_own)).astype(bf16)
        normed_half = my_half(normed_mine)
        normed_parts = [normed_mine] + [
            t_gather(swap(normed_half, tp_mask[r])).reshape(rows, width) for r in range(1, n_tp)
        ]
        normed_one = jnp.concatenate(normed_parts)
        aux_own = jnp.concatenate([valid_own, keep_own], axis=1)
        aux = jnp.concatenate([aux_own] + [swap(aux_own, tp_mask[r]) for r in range(1, n_tp)])
        mix_full = weight_whole(weight_parts(mix_shards))
        out_piece = output_proj
        for b in own_bits:
            out_piece = jnp.where(t_bit[b] == bit[b], out_piece, swap(out_piece, 1 << b))
        out_pieces = [out_piece]
        for b in reversed(free_bits):
            out_pieces = out_pieces + [swap(v, 1 << b) for v in out_pieces]
        out_full = jnp.concatenate(in_order(out_pieces, free_bits))
        gate_full, up_full, down_full = (
            weight_whole(weight_parts(w.transpose(0, 2, 1))).T
            for w in (gate_shards, up_shards, down_shards)
        )
        grad_out_all = jnp.stack(tp_gather(grad_out_rows)).reshape(n_tp * rows, width)
        pre = matmul(normed_one, mix_full)
        state, mix_raw, square = mixer_forward(pre, aux, par, rows)
        out_parts = matmul(mix_raw, out_full).astype(bf16).reshape(n_tp, n_t, share, width)
        square_parts = square.reshape(n_tp, n_t, share)
        square_sum = tp_scatter([square_parts[r] for r in range(n_tp)], f32)
        out_sum = tp_scatter([out_parts[r] for r in range(n_tp)], bf16)
        scale_state = lax.rsqrt(square_sum / width + epsilon)[:, None]
        mixed_out = out_sum * scale_state
        residual = inputs_half + mixed_out
        normed_two_half = (residual * rms_scale(residual) * ffn_gain).astype(bf16)
        normed_two = jnp.stack(tp_gather(normed_two_half)).reshape(n_tp * rows, width)

    if n_dp == 16 and n_t == 2:
        grad_g, grad_u, grad_d, grad_mix_w, grad_out_w, grad_tokens, block_out, vec = back(
            hidden, grad_gate, grad_up, normed_two, grad_out_all, gate_full, up_full, down_full,
            normed_one, mix_full, out_full, pre, state, mix_raw, aux_rows, par, tokens_in, residual, mixed_out,
            scale_lanes, norm_gain[None, :], ffn_gain[None, :],
        )
        mix_all = grad_mix_w.reshape(3, width, block)
        mine = lambda k: lax.dynamic_slice_in_dim(vec, k * n_dp + me, 1, 0)
        return (
            block_out,
            grad_tokens,
            mix_all[0].T.astype(f32),
            mix_all[1].T.astype(f32),
            mix_all[2].T.astype(f32),
            grad_out_w.astype(f32),
            grad_g.reshape(n_tp * hid, block).T.astype(f32),
            grad_u.reshape(n_tp * hid, block).T.astype(f32),
            grad_d.reshape(n_tp * hid, block).astype(f32),
            mine(0)[0],
            mine(2)[0],
            mine(1)[0],
            coef * mine(3),
        )

    scale_two = rms_scale(residual)
    gate_pre = cross_cols(normed_two, gate_full)
    up_pre = cross_cols(normed_two, up_full)
    grad_hidden = cross_cols(grad_out_all, down_full)
    gate_act = jax.nn.silu(gate_pre)
    hidden = (gate_act * up_pre).astype(bf16)
    grad_up = (grad_hidden * gate_act).astype(bf16)
    grad_gate = (grad_hidden * up_pre * silu_slope(gate_pre)).astype(bf16)
    grad_two_parts = (
        (matmul(grad_gate, gate_full) + matmul(grad_up, up_full))
        .astype(bf16)
        .reshape(n_tp, n_t, share, width)
    )
    grad_normed_two = tp_scatter([grad_two_parts[r] for r in range(n_tp)], bf16)
    block_parts = matmul(hidden, down_full).astype(bf16).reshape(n_tp, n_t, share, width)
    block_out = (residual + tp_scatter([block_parts[r] for r in range(n_tp)], bf16)).astype(bf16)
    grad_down_t = jnp.stack(weight_back(cross_rows(grad_out_all, hidden).astype(bf16)))
    grad_w_gate = jnp.stack(weight_back(cross_rows(normed_two, grad_gate).astype(bf16)))
    grad_w_up = jnp.stack(weight_back(cross_rows(normed_two, grad_up).astype(bf16)))
    grad_glu_down = grad_down_t.transpose(0, 2, 1).reshape(glu_down.shape).astype(f32)
    grad_glu_gate = grad_w_gate.transpose(1, 0, 2).reshape(glu_gate.shape).astype(f32)
    grad_glu_up = grad_w_up.transpose(1, 0, 2).reshape(glu_up.shape).astype(f32)

    grad_residual = grad_out_rows.astype(f32) + norm_back(
        residual, scale_two, ffn_gain, grad_normed_two
    )
    ffn_gain_sum = jnp.sum(grad_normed_two * residual * scale_two, axis=0)
    grad_mix_half = grad_residual.astype(bf16)
    dot_mean = jnp.sum(grad_mix_half.astype(f32) * mixed_out, axis=1, keepdims=True) / (
        scale_state * width
    )
    row_values = jnp.concatenate([scale_state, dot_mean], axis=1).T
    row_all = jnp.stack(tp_gather(row_values)).transpose(0, 1, 3, 2).reshape(n_tp * rows, 2)
    grad_mix = jnp.stack(tp_gather(grad_mix_half)).reshape(n_tp * rows, width)
    grad_mixed = cross_cols(grad_mix, out_full)
    aux_back = jnp.concatenate([aux, row_all], axis=1)
    grads, sums = mixer_backward(pre, state, grad_mixed, aux_back, par, rows)
    one_parts = cross_cols(grads, mix_full).astype(bf16).reshape(n_tp, n_t, share, width)
    grad_normed_one = tp_scatter([one_parts[r] for r in range(n_tp)], bf16)
    grad_mix_w = jnp.stack(weight_back(cross_rows(normed_one, grads).astype(bf16)))

    mixed = (mix_raw.astype(f32) * row_all[:, :1]).astype(bf16)
    grad_out_w = cross_rows(mixed, grad_mix).astype(bf16).reshape((2,) * len(free_bits) + (block, width))
    for i, b in enumerate(free_bits):
        send = lax.dynamic_slice_in_dim(grad_out_w, 1 - bit[b], 1, i)
        hold = lax.dynamic_slice_in_dim(grad_out_w, bit[b], 1, i)
        grad_out_w = (hold.astype(f32) + swap(send, 1 << b).astype(f32)).astype(bf16)
    grad_out_w = grad_out_w.reshape(block, width)
    for b in own_bits:
        grad_out_w = (grad_out_w.astype(f32) + swap(grad_out_w, 1 << b).astype(f32)).astype(bf16)
    mine_t = jnp.int32(0)
    for b in own_bits:
        mine_t = mine_t * 2 + bit[b]
    if n_t == 2:
        other = t_swap(grad_out_w)
        grad_output_proj = jnp.where(mine_t == t, grad_out_w, other).astype(f32)
    else:
        grad_output_proj = pick(lax.all_gather(grad_out_w, "tensor", axis=0), mine_t, 0).astype(f32)

    mix_all = t_gather(grad_mix_w)
    mix_all = mix_all.reshape((2,) * t_depth + (2, 2) + (block, 3) + (2,) * len(free_bits) + (block,))
    order = list(own_bits) + list(tp_bits) + ["row", "which"] + list(free_bits) + ["col"]
    axes = [order.index(k) for k in ["which", "row"] + list(reversed(range(depth))) + ["col"]]
    mix_all = mix_all.transpose(axes).reshape(3, block, width).astype(f32)

    grad_tokens_half = my_half_residual = grad_residual + norm_back(
        inputs_half, scale_one_half, norm_gain, grad_normed_one
    )
    grad_tokens = t_gather(grad_tokens_half).reshape(rows, width)
    norm_gain_sum = jnp.sum(grad_normed_one * inputs_half * scale_one_half, axis=0)

    gains = jnp.stack([norm_gain_sum, ffn_gain_sum]).reshape((2,) + (2,) * depth + (block,))
    for b in reversed(range(depth)):
        at = 1 + axis_of[b]
        send = lax.dynamic_slice_in_dim(gains, 1 - bit[b], 1, at)
        hold = lax.dynamic_slice_in_dim(gains, bit[b], 1, at)
        gains = hold + swap(send, 1 << b)
    gains = gains.reshape(2, block)
    gains = gains + t_swap(gains) if n_t == 2 else lax.psum(gains, "tensor")

    for b in fs_bits:
        sums = sums + swap(sums, 1 << b)
    sums = t_gather(sums)
    sums = pick(sums, mine_t, 0).reshape((2,) + (2,) * len(free_bits) + (block,))
    for b in free_bits:
        sums = pick(sums, bit[b], 1)
    shares, picked, lower = bound_parts(lax.dynamic_slice_in_dim(bound_table, me * block, block, 1))
    grad_table = shares * (picked - lower[None, :]) * sums[1][None, :]

    return (
        block_out,
        grad_tokens,
        mix_all[0],
        mix_all[1],
        mix_all[2],
        grad_output_proj,
        grad_glu_gate,
        grad_glu_up,
        grad_glu_down,
        gains[0],
        sums[0],
        gains[1],
        grad_table,
    )


def solution(mesh):
    return jax.shard_map(
        functools.partial(body, mesh.shape["dp"], mesh.shape["tensor"]),
        mesh=mesh,
        in_specs=(
            P("dp", None),
            P("dp", None),
            P("dp", None),
            P("dp", None),
            P("dp", None),
            P("dp", "tensor"),
            P("dp", "tensor"),
            P("tensor", "dp"),
            P(),
            P(),
            P(),
            P(),
            P("dp"),
            P("dp"),
            P(("dp", "tensor"), None),
        ),
        out_specs=(
            P(("dp", "tensor"), None),
            P("dp", None),
            P("dp", None),
            P("dp", None),
            P("dp", None),
            P("dp", None),
            P("dp", "tensor"),
            P("dp", "tensor"),
            P("tensor", "dp"),
            P("dp"),
            P("dp"),
            P("dp"),
            P(None, "dp"),
        ),
        check_vma=False,
    )
```
